32 devices in a mesh: head: 4 (over y, x), blk: 8 (over z, core).
Axes of the slice: x: 2, y: 2, z: 4, core: 2. Of those that a mesh axis runs over, the one named last changes fastest.
Arguments:
- tokens: bfloat16 [8, 6144, 512], P('blk', 'head'), may hold values from -6 to 6
- cotangent: bfloat16 [8, 6144, 512], P('blk', 'head'), may hold values from -6 to 6
- doc_lengths: int32 [49], replicated, may hold values from 1 to 62, 1536 in all
- norm_gain1: bfloat16 [512], P(('head', 'blk')), may hold values from 0.25 to 1.75
- w_qkv: bfloat16 [512, 1536], P('head', 'blk'), may hold values from -0.25 to 0.25
- w_out: bfloat16 [512, 512], P('head', 'blk'), may hold values from -0.75 to 0.75
- b_out: bfloat16 [512], P(('head', 'blk')), may hold values from -3 to 3
- norm_gain2: bfloat16 [512], P(('head', 'blk')), may hold values from 0.25 to 1.75
- w_in: bfloat16 [512, 2048], P('head', 'blk'), may hold values from -0.25 to 0.25
- b_in: bfloat16 [2048], P(('head', 'blk')), may hold values from -3 to 3
- w_down: bfloat16 [2048, 512], P('head', 'blk'), may hold values from -0.125 to 0.125
- b_down: bfloat16 [512], P(('head', 'blk')), may hold values from -3 to 3
- w_sort: bfloat16 [512, 64], P('head', 'blk'), may hold values from -6 to 6
Outputs:
- output: bfloat16 [8, 6144, 512], P('blk', 'head')
- input_grad: float32 [8, 6144, 512], P('blk', 'head')
- grad_norm_gain1: float32 [512], P(('head', 'blk'))
- grad_w_qkv: float32 [512, 1536], P('head', 'blk')
- grad_w_out: float32 [512, 512], P('head', 'blk')
- grad_b_out: float32 [512], P(('head', 'blk'))
- grad_norm_gain2: float32 [512], P(('head', 'blk'))
- grad_w_in: float32 [512, 2048], P('head', 'blk')
- grad_b_in: float32 [2048], P(('head', 'blk'))
- grad_w_down: float32 [2048, 512], P('head', 'blk')
- grad_b_down: float32 [512], P(('head', 'blk'))
- grad_w_sort: float32 [512, 64], P('head', 'blk')
The draws below stay inside these ranges and needn't reach their ends.
Inputs may be any that keep to these rules, and one draw needn't show every extreme that they name: `doc_lengths`: document lengths in blocks of 32 tokens; they sum to 1536 and the longest has exactly 62 blocks.
All inputs are finite; a program needn't handle non-finite values.
Results may differ from the reference program's by a relative error of at most 0.02.
The reference program's roundings to bfloat16 on the way count: a program that leaves them out, or rounds other values in their place, can miss the bound.
Values may be sent and summed in bfloat16 or wider, within the bound.
No kernel may reach another device: no remote copies, remote signals or barrier semaphores. Data moves between devices by JAX's collectives and lax.ppermute only.
A program may use at most 192 MiB of HBM per device.

```python
import math
import jax
import jax.numpy as jnp
import numpy as np
from jax import lax

D = 512
HEADS = 8
HEAD_DIM = 64
FF = 2048
BLOCK = 32
SINK_ITERS = 8
DOC_MOST = 62
TOK_DEV = 1536
SPAN_TOK = 6144
TOKENS = 49152
TOTAL_BLOCKS = 1536
NDOC = 49
N_HEAD = 4
N_BLK = 8


def levels(stream_key, extent, pieces, least, top_value):
    def one(dim, parts):
        steps = jax.random.uniform(jax.random.fold_in(jax.random.fold_in(stream_key, 6), dim), (parts,), jnp.float32, least / len(pieces), top_value / len(pieces))
        return jnp.repeat(jnp.exp(steps), extent[dim] // parts).reshape((-1,) + (1,) * (len(extent) - dim - 1))

    level = one(*pieces[0])
    for cut in pieces[1:]:
        level = level * one(*cut)
    return level


def length_profile(amount, total, bound, skew):
    portions = [(1 << 20) // math.isqrt(standing ** skew) + 1 for standing in range(2, amount + 1)]
    spare, counts = total - bound - (amount - 1), [1] * (amount - 1)
    while spare > 0:
        movable = [i for i in range(amount - 1) if counts[i] < bound]
        mass, remaining = sum([portions[i] for i in movable]), spare
        for i in movable:
            extra = min(bound - counts[i], max(1, remaining * portions[i] // mass), spare)
            counts[i] = counts[i] + extra
            spare = spare - extra
    return np.array([bound] + counts)


def uneven_parts(stream_key, count, total, reach, slope):
    if count == 2:
        one = jax.random.randint(stream_key, (), max(1, total - reach), min(reach, total - 1) + 1)
        return jnp.stack([one, total - one])
    lengths = jnp.asarray(length_profile(count, total, reach, slope), jnp.int32)
    couples = (count - 1) // 2
    donor, sink = lengths[1:1 + 2 * couples:2], lengths[2:2 + 2 * couples:2]
    room = jnp.minimum(donor - 1, reach - sink)
    passed = jax.random.randint(jax.random.fold_in(stream_key, 1), (couples,), 0, 1 << 20) % (room + 1)
    lengths = lengths.at[1:1 + 2 * couples:2].set(donor - passed).at[2:2 + 2 * couples:2].set(sink + passed)
    return lengths[jax.random.permutation(jax.random.fold_in(stream_key, 2), count)]


def scatter_about(key, dims, scale, bound, split=(), held_as=jnp.bfloat16):
    drawn = scale * jax.random.normal(key, dims, jnp.float32)
    if split:
        drawn = drawn * levels(key, dims, split, -0.22, 0.18)
    return jnp.clip(drawn, -bound, bound).astype(held_as)


def setup_inputs(seed: int = 0) -> dict:
    seeds = jax.random.split(jax.random.key(seed), 14)
    tokens = scatter_about(seeds[0], (N_BLK, SPAN_TOK, D), 1.0, 6.0, ((0, 8), (1, 4)))
    cotangent = scatter_about(seeds[1], (N_BLK, SPAN_TOK, D), 1.0, 6.0, ((0, 8), (1, 4)))
    doc_lengths = uneven_parts(seeds[2], NDOC, TOTAL_BLOCKS, DOC_MOST, 1).astype(jnp.int32)
    norm_gain1 = jnp.clip(1.0 + 0.15 * jax.random.normal(seeds[3], (D,), jnp.float32), 0.25, 1.75).astype(jnp.bfloat16)
    w_qkv = scatter_about(seeds[4], (D, 3 * D), D ** -0.5, 0.25, ((0, 4), (1, 8)))
    w_out = scatter_about(seeds[5], (D, D), (D // 8) ** -0.5, 0.75, ((0, 4), (1, 8)))
    b_out = scatter_about(seeds[6], (D,), 0.5, 3.0, ((0, 32),))
    norm_gain2 = jnp.clip(1.0 + 0.15 * jax.random.normal(seeds[7], (D,), jnp.float32), 0.25, 1.75).astype(jnp.bfloat16)
    w_in = scatter_about(seeds[8], (D, FF), D ** -0.5, 0.25, ((0, 4), (1, 8)))
    b_in = scatter_about(seeds[9], (FF,), 0.5, 3.0, ((0, 32),))
    w_down = scatter_about(seeds[10], (FF, D), FF ** -0.5, 0.125, ((0, 4), (1, 8)))
    b_down = scatter_about(seeds[11], (D,), 0.5, 3.0, ((0, 32),))
    w_sort = scatter_about(seeds[12], (HEADS * HEAD_DIM, HEAD_DIM), (2 * BLOCK / HEAD_DIM), 6.0, ((0, 4), (1, 8)))
    return dict(tokens=tokens, cotangent=cotangent, doc_lengths=doc_lengths, norm_gain1=norm_gain1, w_qkv=w_qkv, w_out=w_out, b_out=b_out, norm_gain2=norm_gain2, w_in=w_in, b_in=b_in, w_down=w_down, b_down=b_down, w_sort=w_sort)


PRECISE = lax.Precision.HIGHEST
EPSILON = 1e-05
NEGATIVE = -1e+30

@jax.custom_vjp
def low(v):
    return lax.optimization_barrier(v.astype(jnp.bfloat16)).astype(jnp.float32)

@jax.custom_vjp
def low_back(v):
    return v

def low_keep(v):
    return (low(v), None)

def low_pass(kept, grad):
    return (grad,)

def back_keep(v):
    return (v, None)

def back_low(kept, grad):
    return (low(grad),)
low.defvjp(low_keep, low_pass)
low_back.defvjp(back_keep, back_low)

def round_both(values):
    return low(low_back(values))

def layer_norm(values, gain):
    centre = values - lax.optimization_barrier(jnp.mean(values, axis=-1, keepdims=True))
    spread = lax.optimization_barrier(jnp.mean(centre * centre, axis=-1, keepdims=True))
    return centre * lax.rsqrt(spread + EPSILON) * gain

def masked_logsum(values, permitted_blocks, axis):
    alive = jnp.any(permitted_blocks, axis=axis, keepdims=True)
    highest = lax.optimization_barrier(jnp.max(jnp.where(permitted_blocks, values, NEGATIVE), axis=axis, keepdims=True))
    highest = jnp.where(alive, highest, 0.0)
    shifted = jnp.exp(jnp.where(permitted_blocks, values, highest) - highest)
    total = lax.optimization_barrier(jnp.sum(jnp.where(permitted_blocks, shifted, 0.0), axis=axis, keepdims=True))
    return jnp.where(alive, highest + jnp.log(jnp.where(alive, total, 1.0)), 0.0)

def balanced_transport_plan(block_logits, permitted_blocks):
    values = jnp.where(permitted_blocks, block_logits, 0.0)
    for repeat in range(SINK_ITERS):
        values = jnp.where(permitted_blocks, values - masked_logsum(values, permitted_blocks, 2), 0.0)
        values = jnp.where(permitted_blocks, values - masked_logsum(values, permitted_blocks, 1), 0.0)
    return jnp.where(permitted_blocks, jnp.exp(values), 0.0)

def block_documents(first, number, doc_lengths, total):
    position = first + jnp.arange(number, dtype=jnp.int32)
    doc_ends = jnp.cumsum(doc_lengths, dtype=jnp.int32)
    ended = lax.optimization_barrier(jnp.sum((doc_ends[None, :] <= position[:, None]).astype(jnp.int32), axis=1, dtype=jnp.int32))
    inside = (position >= 0) & (position < total)
    return jnp.where(inside, ended, -1)

def sort_allowed(doc_ids):
    number = doc_ids.shape[0]
    later = jnp.arange(number)[:, None] > jnp.arange(number)[None, :]
    return (doc_ids[:, None] == doc_ids[None, :]) & (doc_ids[:, None] >= 0) & later

def reference(tokens, cotangent, doc_lengths, norm_gain1, w_qkv, w_out, b_out, norm_gain2, w_in, b_in, w_down, b_down, w_sort):
    attend_range = DOC_MOST - 1
    document_span_blocks = N_HEAD * TOK_DEV // BLOCK
    total_blocks = TOKENS // BLOCK
    span_count = total_blocks // document_span_blocks
    scale = HEAD_DIM ** (-0.5)

    def forward(stream, gain_one, weight_qkv, weight_out, bias_out, gain_two, weight_in, bias_in, weight_down, bias_down, weight_sort):
        normed = low(layer_norm(stream, gain_one))
        qkv = round_both(jnp.dot(normed, weight_qkv, precision=PRECISE))
        qkv = qkv.reshape(total_blocks, BLOCK, HEADS, 3 * HEAD_DIM)
        means = jnp.concatenate([lax.optimization_barrier(jnp.mean(qkv[..., :HEAD_DIM], axis=1)), lax.optimization_barrier(jnp.mean(qkv[..., HEAD_DIM:2 * HEAD_DIM], axis=1))], axis=-1)
        means_pad = jnp.pad(means, ((attend_range, 0), (0, 0), (0, 0)))
        keyval_pad = jnp.pad(qkv[..., HEAD_DIM:], ((attend_range, 0), (0, 0), (0, 0), (0, 0)))
        sort_weight = weight_sort.reshape(HEADS, HEAD_DIM, HEAD_DIM)

        def one_span(index):
            start = index * document_span_blocks
            beside_all = lax.dynamic_slice_in_dim(means_pad, start, document_span_blocks + attend_range, 0)
            doc_ids = block_documents(start - attend_range, document_span_blocks + attend_range, doc_lengths, total_blocks)
            permitted_blocks = sort_allowed(doc_ids)
            block_logits = jnp.einsum('nhi,hij,mhj->hnm', beside_all[..., :HEAD_DIM], sort_weight, beside_all[..., HEAD_DIM:], precision=PRECISE)
            block_permutation = balanced_transport_plan(block_logits, permitted_blocks[None])[:, attend_range:attend_range + document_span_blocks, :attend_range + document_span_blocks]
            sorting_low = low(block_permutation)
            context = lax.dynamic_slice_in_dim(keyval_pad, start, document_span_blocks + attend_range, 0)
            sorted_kv = round_both(jnp.einsum('hnm,mbhe->nbhe', sorting_low, context, precision=PRECISE))
            own = lax.dynamic_slice_in_dim(qkv, start, document_span_blocks, 0)
            query = own[..., :HEAD_DIM]
            key_local = own[..., HEAD_DIM:2 * HEAD_DIM]
            value_local = own[..., 2 * HEAD_DIM:]
            live_rows = jnp.any(permitted_blocks[attend_range:attend_range + document_span_blocks, :attend_range + document_span_blocks], axis=1)
            local_scores = low_back(jnp.einsum('nbhd,nchd->nhbc', query, key_local, precision=PRECISE) * scale)
            sorted_scores = low_back(jnp.einsum('nbhd,nchd->nhbc', query, sorted_kv[..., :HEAD_DIM], precision=PRECISE) * scale)
            causal = jnp.arange(BLOCK)[:, None] >= jnp.arange(BLOCK)[None, :]
            scores = jnp.concatenate([jnp.where(causal, local_scores, NEGATIVE), jnp.where(live_rows[:, None, None, None], sorted_scores, NEGATIVE)], axis=-1)
            weights = low(jax.nn.softmax(scores, axis=-1))
            mixed = jnp.einsum('nhbc,nche->nbhe', weights[..., :BLOCK], value_local, precision=PRECISE)
            mixed = mixed + jnp.einsum('nhbc,nche->nbhe', weights[..., BLOCK:], sorted_kv[..., HEAD_DIM:], precision=PRECISE)
            return round_both(mixed)
        attended = lax.map(jax.checkpoint(one_span), jnp.arange(span_count, dtype=jnp.int32))
        attended = attended.reshape(TOKENS, D)
        branch = low_back(jnp.dot(attended, weight_out, precision=PRECISE) + bias_out)
        middle = stream + branch
        normed_two = low(layer_norm(middle, gain_two))
        pre = low_back(jnp.dot(normed_two, weight_in, precision=PRECISE) + bias_in)
        hidden = low(jax.nn.gelu(pre, approximate=True))
        return middle + jnp.dot(hidden, weight_down, precision=PRECISE) + bias_down
    params = (tokens.reshape(TOKENS, D), norm_gain1, w_qkv, w_out, b_out, norm_gain2, w_in, b_in, w_down, b_down, w_sort)
    params = tuple((item.astype(jnp.float32) for item in params))
    result, pullback = jax.vjp(forward, *params)
    grads = pullback(cotangent.reshape(TOKENS, D).astype(jnp.float32))
    return (result.astype(jnp.bfloat16).reshape(N_BLK, SPAN_TOK, D), grads[0].reshape(N_BLK, SPAN_TOK, D), grads[1], grads[2], grads[3], grads[4], grads[5], grads[6], grads[7], grads[8], grads[9], grads[10])
```

```python
import functools

import jax
import jax.numpy as jnp
from jax import lax
from jax.experimental import pallas as pl
from jax.experimental.pallas import tpu as pltpu
from jax.sharding import PartitionSpec as P

D = 512
HEADS = 8
HEAD_DIM = 64
FF = 2048
BLOCK = 32
SINK_ITERS = 8
DOC_MOST = 62
LANES = 128
PAIRS = HEADS // 2
HALO = 64
UNROLL = 2
PRECISE = lax.Precision.HIGHEST
EPSILON = 1e-05
NEGATIVE = -1e30
F32 = jnp.float32
BF16 = jnp.bfloat16
NT = (((1,), (1,)), ((), ()))
NN = (((1,), (0,)), ((), ()))
TN = (((0,), (0,)), ((), ()))


def mm(a, b, dims=NN, precision=None):
    return lax.dot_general(a, b, dims, precision=precision, preferred_element_type=F32)


def vmem(limit=56):
    return pltpu.CompilerParams(vmem_limit_bytes=limit * 1024 * 1024)


def sink_mask(docn_ref, docc_ref, window, context):
    first = context
    fold = window - LANES
    lane = lax.broadcasted_iota(jnp.int32, (1, LANES), 1)
    docn = docn_ref[...]
    row = lax.broadcasted_iota(jnp.int32, (window, 1), 0)
    col = jnp.where((row >= first) & (lane < fold), lane + LANES, lane)
    docc = jnp.where(row >= first, docc_ref[1:2, :], docc_ref[0:1, :])
    return (docn == docc) & (docn >= 0) & (col < row)


def fold_pair(top, low, fold, join):
    lane = lax.broadcasted_iota(jnp.int32, (1, LANES), 1)
    both = join(top, low)
    return jnp.where(lane < fold, top, both), jnp.where(lane < fold, low, both)


def sink_weight(w_ref, head):
    pair = w_ref[head // 2]
    lane = lax.broadcasted_iota(jnp.int32, pair.shape, 1)
    zero = jnp.zeros_like(pair)
    if head % 2 == 0:
        return jnp.concatenate([jnp.where(lane < HEAD_DIM, pair, zero), zero], axis=0)
    return jnp.concatenate([zero, jnp.where(lane >= HEAD_DIM, pair, zero)], axis=0)


def sink_logits(queries, keys, weight, context, fold):
    projected = mm(queries, weight, NT, PRECISE)
    keys_two = jnp.concatenate([keys[LANES:], keys[fold:LANES]], axis=0)
    top = mm(projected[:context], keys[:LANES], NT, PRECISE)
    low = mm(projected[context:], keys_two, NT, PRECISE)
    return projected, keys_two, jnp.concatenate([top, low], axis=0)


def row_step(values):
    highest = jnp.max(values, axis=1, keepdims=True)
    alive = highest > 0.5 * NEGATIVE
    highest = jnp.where(alive, highest, 0.0)
    shifted = jnp.exp(values - highest)
    total = jnp.where(alive, jnp.sum(shifted, axis=1, keepdims=True), 1.0)
    return values - (highest + jnp.log(total)), shifted, total


def column_step(values, context, fold):
    top, low = values[:context], values[context:]
    h1, h2 = fold_pair(
        jnp.max(top, axis=0, keepdims=True),
        jnp.max(low, axis=0, keepdims=True),
        fold,
        jnp.maximum,
    )
    a1, a2 = h1 > 0.5 * NEGATIVE, h2 > 0.5 * NEGATIVE
    h1, h2 = jnp.where(a1, h1, 0.0), jnp.where(a2, h2, 0.0)
    e1, e2 = jnp.exp(top - h1), jnp.exp(low - h2)
    t1, t2 = fold_pair(
        jnp.sum(e1, axis=0, keepdims=True), jnp.sum(e2, axis=0, keepdims=True), fold, jnp.add
    )
    t1, t2 = jnp.where(a1, t1, 1.0), jnp.where(a2, t2, 1.0)
    moved = jnp.concatenate([top - (h1 + jnp.log(t1)), low - (h2 + jnp.log(t2))], axis=0)
    return moved, (e1, e2), (t1, t2)


def sink_start(q_ref, k_ref, w_ref, docn_ref, docc_ref, vals, proj, context):
    window = q_ref.shape[0]
    fold = window - LANES
    permitted = sink_mask(docn_ref, docc_ref, window, context)
    for head in range(HEADS):
        lanes = slice(head // 2 * LANES, (head // 2 + 1) * LANES)
        projected, _, logits = sink_logits(
            q_ref[:, lanes], k_ref[:, lanes], sink_weight(w_ref, head), context, fold
        )
        vals[head] = jnp.where(permitted, logits, NEGATIVE)
        if proj is not None:
            proj[head] = projected


def sink_forward_kernel(own, context, q_ref, k_ref, w_ref, docn_ref, docc_ref, plan_ref, vals):
    fold = q_ref.shape[0] - LANES
    sink_start(q_ref, k_ref, w_ref, docn_ref, docc_ref, vals, None, context)

    def step(_, carry):
        for head in range(HEADS):
            moved, _, _ = row_step(vals[head])
            moved, _, _ = column_step(moved, context, fold)
            vals[head] = moved
        return carry

    lax.fori_loop(0, SINK_ITERS, step, 0)
    for head in range(HEADS):
        plan_ref[head] = jnp.exp(vals[head, context - own : context, :]).astype(BF16)


def sink_backward_kernel(
    own, context, q_ref, k_ref, w_ref, docn_ref, docc_ref, gp_ref, gq_ref, gk_ref, gw_ref,
    vals, proj, kept,
):
    window = q_ref.shape[0]
    fold = window - LANES
    sink_start(q_ref, k_ref, w_ref, docn_ref, docc_ref, vals, proj, context)

    def step(at, carry):
        for head in range(HEADS):
            moved, shifted, total = row_step(vals[head])
            kept[2 * at, head] = shifted * (1.0 / total)
            moved, (e1, e2), (t1, t2) = column_step(moved, context, fold)
            kept[2 * at + 1, head, :context, :] = e1 * (1.0 / t1)
            kept[2 * at + 1, head, context:, :] = e2 * (1.0 / t2)
            vals[head] = moved
        return carry

    lax.fori_loop(0, SINK_ITERS, step, 0)
    for head in range(HEADS):
        vals[head] = jnp.concatenate(
            [
                jnp.zeros((context - own, LANES), F32),
                gp_ref[head] * kept[2 * SINK_ITERS - 1, head, context - own : context, :],
                jnp.zeros((window - context, LANES), F32),
            ],
            axis=0,
        )

    def back(turn, carry):
        at = SINK_ITERS - 1 - turn
        for head in range(HEADS):
            g1, g2 = vals[head, :context, :], vals[head, context:, :]
            s1, s2 = fold_pair(
                jnp.sum(g1, axis=0, keepdims=True),
                jnp.sum(g2, axis=0, keepdims=True),
                fold,
                jnp.add,
            )
            grad = jnp.concatenate(
                [
                    g1 - kept[2 * at + 1, head, :context, :] * s1,
                    g2 - kept[2 * at + 1, head, context:, :] * s2,
                ],
                axis=0,
            )
            vals[head] = grad - kept[2 * at, head] * jnp.sum(grad, axis=1, keepdims=True)
        return carry

    lax.fori_loop(0, SINK_ITERS, back, 0)
    for pair in range(PAIRS):
        lanes = slice(pair * LANES, (pair + 1) * LANES)
        queries, keys = q_ref[:, lanes], k_ref[:, lanes]
        keys_two = jnp.concatenate([keys[LANES:], keys[fold:LANES]], axis=0)
        gq_total = jnp.zeros((window, LANES), F32)
        gk_total = jnp.zeros((window, LANES), F32)
        turned = []
        for head in (2 * pair, 2 * pair + 1):
            g1, g2 = vals[head, :context, :], vals[head, context:, :]
            against = jnp.concatenate(
                [mm(g1, keys[:LANES], NN, PRECISE), mm(g2, keys_two, NN, PRECISE)], axis=0
            )
            gq_total = gq_total + mm(against, sink_weight(w_ref, head), NN, PRECISE)
            u1 = mm(g1, proj[head, :context, :], TN, PRECISE)
            u2 = mm(g2, proj[head, context:, :], TN, PRECISE)
            gk_total = gk_total + jnp.concatenate(
                [u1[:fold], u1[fold:] + u2[fold:], u2[:fold]], axis=0
            )
            turned.append(mm(against, queries, TN, PRECISE))
        half = lax.broadcasted_iota(jnp.int32, (HEAD_DIM, LANES), 1) < HEAD_DIM
        gw_ref[pair] = jnp.where(half, turned[0][:HEAD_DIM], turned[1][HEAD_DIM:])
        gq_ref[:, lanes] = gq_total
        gk_ref[:, lanes] = gk_total


def sink_forward(qmean, kmean, weight, docn, docc, own, context):
    window = qmean.shape[0]
    return pl.pallas_call(
        functools.partial(sink_forward_kernel, own, context),
        out_shape=jax.ShapeDtypeStruct((HEADS, own, LANES), BF16),
        scratch_shapes=[pltpu.VMEM((HEADS, window, LANES), F32)],
        compiler_params=vmem(),
        name="sink_forward",
    )(qmean, kmean, weight, docn, docc)


def sink_backward(qmean, kmean, weight, docn, docc, gplan, own, context):
    window = qmean.shape[0]
    return pl.pallas_call(
        functools.partial(sink_backward_kernel, own, context),
        out_shape=[
            jax.ShapeDtypeStruct((window, D), F32),
            jax.ShapeDtypeStruct((window, D), F32),
            jax.ShapeDtypeStruct((PAIRS, HEAD_DIM, LANES), F32),
        ],
        scratch_shapes=[
            pltpu.VMEM((HEADS, window, LANES), F32),
            pltpu.VMEM((HEADS, window, LANES), F32),
            pltpu.VMEM((2 * SINK_ITERS, HEADS, window, LANES), F32),
        ],
        compiler_params=vmem(),
        name="sink_backward",
    )(qmean, kmean, weight, docn, docc, gplan)


def normalise(values):
    centre = values - jnp.mean(values, axis=-1, keepdims=True)
    spread = jnp.mean(centre * centre, axis=-1, keepdims=True)
    return centre * lax.rsqrt(spread + EPSILON)


def context_kernel(halo_blocks, x_ref, gain_ref, w_ref, kvx_ref, nh_ref):
    blocks = x_ref.shape[0]
    normed = normalise(x_ref[...].astype(F32)) * gain_ref[...].reshape(1, 1, D)
    normed = normed.astype(BF16).reshape(blocks * 8, D)
    row = lax.broadcasted_iota(jnp.int32, (LANES, LANES), 0)
    lane = lax.broadcasted_iota(jnp.int32, (LANES, LANES), 1)
    turn = (lane == (row % 16) * 8 + row // 16).astype(F32).astype(BF16)
    turned = [
        mm(turn, normed[i * LANES : (i + 1) * LANES]).astype(BF16) for i in range(blocks // 16)
    ]
    for b in range(8):
        rows = jnp.concatenate([part[b * 16 : (b + 1) * 16] for part in turned], axis=0)
        nh_ref[b] = rows[:halo_blocks]
        out = mm(rows, w_ref[...], NT).astype(BF16)
        for head in range(HEADS):
            kvx_ref[head, :, b * LANES : (b + 1) * LANES] = out[
                :, head * LANES : (head + 1) * LANES
            ]


def context_project(x_context, gain, w_kv, halo_blocks):
    blocks = x_context.shape[0]
    return pl.pallas_call(
        functools.partial(context_kernel, halo_blocks),
        grid=(BLOCK // 8,),
        in_specs=[
            pl.BlockSpec((blocks, 8, D), lambda i: (0, i, 0)),
            pl.BlockSpec((1, D), lambda i: (0, 0)),
            pl.BlockSpec((2 * D, D), lambda i: (0, 0)),
        ],
        out_specs=[
            pl.BlockSpec((HEADS, blocks, 8 * LANES), lambda i: (0, 0, i)),
            pl.BlockSpec((8, halo_blocks, D), lambda i: (i, 0, 0)),
        ],
        out_shape=[
            jax.ShapeDtypeStruct((HEADS, blocks, BLOCK * LANES), BF16),
            jax.ShapeDtypeStruct((BLOCK, halo_blocks, D), BF16),
        ],
        compiler_params=vmem(),
        name="context_project",
    )(x_context, gain, w_kv)


def compact(values, lane_block):
    out = values[:BLOCK]
    for j in range(1, 4):
        out = jnp.where(lane_block == j, values[j * BLOCK : (j + 1) * BLOCK], out)
    return out


def spread(values, lane_block):
    zero = jnp.zeros_like(values)
    return jnp.concatenate([jnp.where(lane_block == j, values, zero) for j in range(4)], axis=0)


def softmax_pair(local, chosen, live):
    lane = lax.broadcasted_iota(jnp.int32, (BLOCK, LANES), 1)
    row = lax.broadcasted_iota(jnp.int32, (BLOCK, LANES), 0)
    local = jnp.where(row <= lax.rem(lane, BLOCK), local, NEGATIVE)
    chosen = jnp.where(live, chosen, NEGATIVE)
    highest = jnp.maximum(
        jnp.max(local, axis=0, keepdims=True), jnp.max(chosen, axis=0, keepdims=True)
    )
    el, es = jnp.exp(local - highest), jnp.exp(chosen - highest)
    total = jnp.sum(el, axis=0, keepdims=True) + jnp.sum(es, axis=0, keepdims=True)
    inverse = 1.0 / total
    return el * inverse, es * inverse


def half_mask(first):
    lane = lax.broadcasted_iota(jnp.int32, (LANES, LANES), 1)
    return (lane < HEAD_DIM) if first else (lane >= HEAD_DIM)


def attend_kernel(q_ref, kv_ref, kvx_ref, plan_ref, live_ref, att_ref, skv_ref, even_ref, odd_ref):
    own = plan_ref.shape[1]
    blocks = kvx_ref.shape[1]
    held = (even_ref, odd_ref)
    for e in range(2):
        plan = plan_ref[e][:, :blocks]
        for chunk in range(4):
            out = mm(plan, kvx_ref[e, :, chunk * 8 * LANES : (chunk + 1) * 8 * LANES])
            for b in range(8):
                at = (chunk * 8 + b) * (own + 1)
                held[e][at : at + own, :] = out[:, b * LANES : (b + 1) * LANES]
    lane_block = lax.broadcasted_iota(jnp.int32, (BLOCK, LANES), 1) // BLOCK
    lane_half = [half_mask(True), half_mask(False)]

    def group(g, carry):
        start = pl.multiple_of(g * LANES, LANES)
        live = live_ref[pl.ds(g, 1), :] > 0.0
        q = q_ref[pl.ds(start, LANES), :] * 0.125
        outs = []
        for e in range(2):
            local = kv_ref[pl.ds(start, LANES), e * LANES : (e + 1) * LANES]
            chosen = jnp.concatenate(
                [held[e][pl.ds(4 * g + i, BLOCK, stride=own + 1), :] for i in range(4)], axis=0
            ).astype(BF16)
            skv_ref[pl.ds(start, LANES), e * LANES : (e + 1) * LANES] = chosen
            both = jnp.concatenate([local, chosen], axis=0)
            qm = jnp.where(lane_half[e], q, jnp.zeros_like(q))
            scores = mm(both, qm, NT)
            wl, ws = softmax_pair(
                compact(scores[:LANES], lane_block), compact(scores[LANES:], lane_block), live
            )
            weights = jnp.concatenate(
                [spread(wl, lane_block), spread(ws, lane_block)], axis=0
            ).astype(BF16)
            turned = both.T
            values = turned[HEAD_DIM:] if e == 0 else turned[:HEAD_DIM]
            outs.append(mm(values, weights))
        att_ref[pl.ds(start, LANES), :] = jnp.concatenate(outs, axis=0).T.astype(BF16)
        return carry

    lax.fori_loop(0, own // 4, group, 0, unroll=UNROLL)


def attend(q, kv, kvx, plan, live):
    tok, own, blocks = q.shape[0], plan.shape[1], kvx.shape[1]
    return pl.pallas_call(
        attend_kernel,
        grid=(PAIRS,),
        in_specs=[
            pl.BlockSpec((tok, LANES), lambda j: (0, j)),
            pl.BlockSpec((tok, 2 * LANES), lambda j: (0, j)),
            pl.BlockSpec((2, blocks, BLOCK * LANES), lambda j: (j, 0, 0)),
            pl.BlockSpec((2, own, LANES), lambda j: (j, 0, 0)),
            pl.BlockSpec((tok // LANES, LANES), lambda j: (0, 0)),
        ],
        out_specs=[
            pl.BlockSpec((tok, LANES), lambda j: (0, j)),
            pl.BlockSpec((tok, 2 * LANES), lambda j: (0, j)),
        ],
        out_shape=[
            jax.ShapeDtypeStruct((tok, D), BF16),
            jax.ShapeDtypeStruct((tok, 2 * D), BF16),
        ],
        scratch_shapes=[pltpu.VMEM((BLOCK * (own + 1), LANES), F32)] * 2,
        compiler_params=vmem(),
        name="attend",
    )(q, kv, kvx, plan, live)


def attend_back_kernel(
    q_ref, kv_ref, skv_ref, go_ref, kvx_ref, plan_ref, live_ref,
    gq_ref, gkv_ref, gh_ref, gp_ref, even_ref, odd_ref, leven_ref, lodd_ref,
):
    own = plan_ref.shape[1]
    blocks = kvx_ref.shape[1]
    halo = blocks - own
    held = (even_ref, odd_ref)
    lheld = (leven_ref, lodd_ref)
    lane_block = lax.broadcasted_iota(jnp.int32, (BLOCK, LANES), 1) // BLOCK
    lane_half = [half_mask(True), half_mask(False)]

    def group(g, carry):
        start = pl.multiple_of(g * LANES, LANES)
        live = live_ref[pl.ds(g, 1), :] > 0.0
        q = q_ref[pl.ds(start, LANES), :] * 0.125
        go = go_ref[pl.ds(start, LANES), :]
        go = jnp.concatenate([go[:, HEAD_DIM:], go[:, :HEAD_DIM]], axis=1)
        outs = []
        for e in range(2):
            local = kv_ref[pl.ds(start, LANES), e * LANES : (e + 1) * LANES]
            chosen = skv_ref[pl.ds(start, LANES), e * LANES : (e + 1) * LANES]
            both = jnp.concatenate([local, chosen], axis=0)
            qm = jnp.where(lane_half[e], q, jnp.zeros_like(q))
            gm = jnp.where(lane_half[1 - e], go, jnp.zeros_like(go))
            right = jnp.concatenate([qm, gm], axis=0)
            scores = mm(both, right, NT)
            wl, ws = softmax_pair(
                compact(scores[:LANES, :LANES], lane_block),
                compact(scores[LANES:, :LANES], lane_block),
                live,
            )
            dl = compact(scores[:LANES, LANES:], lane_block)
            ds = compact(scores[LANES:, LANES:], lane_block)
            inner = jnp.sum(wl * dl, axis=0, keepdims=True) + jnp.sum(
                ws * ds, axis=0, keepdims=True
            )
            gl, gs = wl * (dl - inner), ws * (ds - inner)
            weights = jnp.concatenate(
                [spread(wl, lane_block), spread(ws, lane_block)], axis=0
            ).astype(BF16)
            gscore = jnp.concatenate(
                [spread(gl, lane_block), spread(gs, lane_block)], axis=0
            ).astype(BF16)
            gboth = mm(jnp.concatenate([gscore, weights], axis=1), right)
            lheld[e][pl.ds(start, LANES), :] = gboth[:LANES]
            gchosen = gboth[LANES:]
            for i in range(4):
                held[e][pl.ds(4 * g + i, BLOCK, stride=own + 1), :] = gchosen[
                    i * BLOCK : (i + 1) * BLOCK
                ]
            turned = both.T
            keys = turned[:HEAD_DIM] if e == 0 else turned[HEAD_DIM:]
            outs.append(mm(keys, gscore))
        gq_ref[pl.ds(start, LANES), :] = (jnp.concatenate(outs, axis=0).T * 0.125).astype(BF16)
        return carry

    lax.fori_loop(0, own // 4, group, 0, unroll=UNROLL)
    for e in range(2):
        plan = plan_ref[e][:, :blocks]
        gplan = jnp.zeros((own, blocks), F32)
        for chunk in range(4):
            lanes = slice(chunk * 8 * LANES, (chunk + 1) * 8 * LANES)
            grads = jnp.concatenate(
                [
                    held[e][(chunk * 8 + b) * (own + 1) : (chunk * 8 + b) * (own + 1) + own, :]
                    for b in range(8)
                ],
                axis=1,
            ).astype(BF16)
            gplan = gplan + mm(grads, kvx_ref[e, :, lanes], NT)
            gcontext = mm(plan, grads, TN)
            gh_ref[e, :, lanes] = gcontext[:halo].astype(BF16)
            for b in range(8):
                at = (chunk * 8 + b) * (own + 1)
                held[e][at : at + own, :] = gcontext[halo:, b * LANES : (b + 1) * LANES]
        gp_ref[e] = jnp.concatenate([gplan, jnp.zeros((own, LANES - blocks), F32)], axis=1)

    def finish(g, carry):
        start = pl.multiple_of(g * LANES, LANES)
        for e in range(2):
            rest = jnp.concatenate(
                [held[e][pl.ds(4 * g + i, BLOCK, stride=own + 1), :] for i in range(4)], axis=0
            )
            gkv_ref[pl.ds(start, LANES), e * LANES : (e + 1) * LANES] = (
                rest + lheld[e][pl.ds(start, LANES), :]
            ).astype(BF16)
        return carry

    lax.fori_loop(0, own // 4, finish, 0)


def attend_back(q, kv, skv, go, kvx, plan, live):
    tok, own, blocks = q.shape[0], plan.shape[1], kvx.shape[1]
    halo = blocks - own
    return pl.pallas_call(
        attend_back_kernel,
        grid=(PAIRS,),
        in_specs=[
            pl.BlockSpec((tok, LANES), lambda j: (0, j)),
            pl.BlockSpec((tok, 2 * LANES), lambda j: (0, j)),
            pl.BlockSpec((tok, 2 * LANES), lambda j: (0, j)),
            pl.BlockSpec((tok, LANES), lambda j: (0, j)),
            pl.BlockSpec((2, blocks, BLOCK * LANES), lambda j: (j, 0, 0)),
            pl.BlockSpec((2, own, LANES), lambda j: (j, 0, 0)),
            pl.BlockSpec((tok // LANES, LANES), lambda j: (0, 0)),
        ],
        out_specs=[
            pl.BlockSpec((tok, LANES), lambda j: (0, j)),
            pl.BlockSpec((tok, 2 * LANES), lambda j: (0, j)),
            pl.BlockSpec((2, halo, BLOCK * LANES), lambda j: (j, 0, 0)),
            pl.BlockSpec((2, own, LANES), lambda j: (j, 0, 0)),
        ],
        out_shape=[
            jax.ShapeDtypeStruct((tok, D), BF16),
            jax.ShapeDtypeStruct((tok, 2 * D), BF16),
            jax.ShapeDtypeStruct((HEADS, halo, BLOCK * LANES), BF16),
            jax.ShapeDtypeStruct((HEADS, own, LANES), F32),
        ],
        scratch_shapes=[pltpu.VMEM((BLOCK * (own + 1), LANES), F32)] * 4,
        compiler_params=vmem(),
        name="attend_back",
    )(q, kv, skv, go, kvx, plan, live)


def halo_kernel(gh_ref, nh_ref, w_ref, gn_ref, gw_ref):
    halo = gh_ref.shape[1]

    @pl.when(pl.program_id(0) == 0)
    def _():
        gw_ref[...] = jnp.zeros_like(gw_ref)

    rows = jnp.concatenate(
        [
            jnp.concatenate(
                [gh_ref[head, :, b * LANES : (b + 1) * LANES] for head in range(HEADS)], axis=1
            )
            for b in range(8)
        ],
        axis=0,
    )
    gn_ref[...] = mm(rows, w_ref[...]).astype(BF16).reshape(8, halo, D)
    gw_ref[...] += mm(rows, nh_ref[...].reshape(8 * halo, D), TN)


def halo_back(gh, nh, w_kv):
    halo = gh.shape[1]
    return pl.pallas_call(
        halo_kernel,
        grid=(BLOCK // 8,),
        in_specs=[
            pl.BlockSpec((HEADS, halo, 8 * LANES), lambda i: (0, 0, i)),
            pl.BlockSpec((8, halo, D), lambda i: (i, 0, 0)),
            pl.BlockSpec((2 * D, D), lambda i: (0, 0)),
        ],
        out_specs=[
            pl.BlockSpec((8, halo, D), lambda i: (i, 0, 0)),
            pl.BlockSpec((2 * D, D), lambda i: (0, 0)),
        ],
        out_shape=[
            jax.ShapeDtypeStruct((BLOCK, halo, D), BF16),
            jax.ShapeDtypeStruct((2 * D, D), F32),
        ],
        compiler_params=vmem(),
        name="halo_back",
    )(gh, nh, w_kv)


def project_kernel(x_ref, gain_ref, wq_ref, wkv_ref, n_ref, q_ref, kv_ref, qm_ref, km_ref):
    rows = x_ref.shape[0]
    blocks = rows // BLOCK
    normed = (normalise(x_ref[...].astype(F32)) * gain_ref[...]).astype(BF16)
    n_ref[...] = normed
    q = mm(normed, wq_ref[...], NT).astype(BF16)
    q_ref[...] = q
    kv = mm(normed, wkv_ref[...], NT).astype(BF16)
    kv_ref[...] = kv
    half = lax.broadcasted_iota(jnp.int32, (1, LANES), 1) < HEAD_DIM
    qm_ref[...] = jnp.mean(q.astype(F32).reshape(blocks, BLOCK, D), axis=1)
    for pair in range(PAIRS):
        even = kv[:, 2 * pair * LANES : (2 * pair + 1) * LANES]
        odd = kv[:, (2 * pair + 1) * LANES : (2 * pair + 2) * LANES]
        keys = jnp.where(half, even.astype(F32), odd.astype(F32))
        km_ref[:, pair * LANES : (pair + 1) * LANES] = jnp.mean(
            keys.reshape(blocks, BLOCK, LANES), axis=1
        )


def project(x, gain, wt_q, wt_kv):
    tok = x.shape[0]
    tile = 8 * BLOCK
    return pl.pallas_call(
        project_kernel,
        grid=(tok // tile,),
        in_specs=[
            pl.BlockSpec((tile, D), lambda i: (i, 0)),
            pl.BlockSpec((1, D), lambda i: (0, 0)),
            pl.BlockSpec((D, D), lambda i: (0, 0)),
            pl.BlockSpec((2 * D, D), lambda i: (0, 0)),
        ],
        out_specs=[
            pl.BlockSpec((tile, D), lambda i: (i, 0)),
            pl.BlockSpec((tile, D), lambda i: (i, 0)),
            pl.BlockSpec((tile, 2 * D), lambda i: (i, 0)),
            pl.BlockSpec((8, D), lambda i: (i, 0)),
            pl.BlockSpec((8, D), lambda i: (i, 0)),
        ],
        out_shape=[
            jax.ShapeDtypeStruct((tok, D), BF16),
            jax.ShapeDtypeStruct((tok, D), BF16),
            jax.ShapeDtypeStruct((tok, 2 * D), BF16),
            jax.ShapeDtypeStruct((tok // BLOCK, D), F32),
            jax.ShapeDtypeStruct((tok // BLOCK, D), F32),
        ],
        compiler_params=vmem(),
        name="project",
    )(x, gain, wt_q, wt_kv)


PIECE_ONE = 208
PIECE_TWO = 576
PARTS_TWO = 592


def turn(value):
    return value.astype(F32).T.astype(BF16)


def pack_kernel(wqkv_ref, wsort_ref, vec_ref, win_ref, wdown_ref, wout_ref, one_ref, two_ref):
    one_ref[...] = jnp.concatenate(
        [
            wqkv_ref[...].astype(F32).T,
            wsort_ref[...].astype(F32).T,
            vec_ref[...].astype(F32),
            jnp.zeros((PIECE_ONE - 201, LANES), F32),
        ],
        axis=0,
    ).astype(BF16)
    two_ref[:256, :] = turn(win_ref[...])
    for k in range(4):
        two_ref[256 + k * 64 : 256 + (k + 1) * 64, :] = turn(
            wdown_ref[k * LANES : (k + 1) * LANES, :]
        )
    two_ref[512:, :] = turn(wout_ref[...])


def pack(w_qkv, w_sort, vectors, w_in, w_down, w_out):
    return pl.pallas_call(
        pack_kernel,
        out_shape=[
            jax.ShapeDtypeStruct((PIECE_ONE, LANES), BF16),
            jax.ShapeDtypeStruct((PIECE_TWO, LANES), BF16),
        ],
        compiler_params=vmem(),
        name="pack",
    )(w_qkv, w_sort, vectors, w_in, w_down, w_out)


def each_piece(at_ref, mine_ref, other_ref, visit):
    for core in range(2):

        @pl.when(at_ref[2] == core)
        def _():
            for h in range(4):
                for z in range(4):
                    for c in range(2):
                        source = mine_ref if c == core else other_ref
                        visit(h, z, c, source.at[at_ref[1] ^ z, at_ref[0] ^ h])


def widen(vecs, start, size):
    total = 32 * size
    lane = lax.broadcasted_iota(jnp.int32, (LANES, total), 1)
    row = lax.broadcasted_iota(jnp.int32, (LANES, total), 0)
    pick = (row == start + lax.rem(lane, size)).astype(F32).astype(BF16)
    every = mm(vecs, pick)
    owner = lax.broadcasted_iota(jnp.int32, (32, total), 0)
    lane = lax.broadcasted_iota(jnp.int32, (32, total), 1)
    return jnp.sum(jnp.where(owner == lane // size, every, 0.0), axis=0, keepdims=True)


def assemble_kernel(
    at_ref, mine_ref, other_ref, wq_ref, wkv_ref, ws_ref, g1_ref, bo_ref, g2_ref, bi_ref, bd_ref,
    vecs_ref,
):
    def visit(h, z, c, piece):
        b = 2 * z + c
        lanes = slice(h * LANES, (h + 1) * LANES)
        wq_ref[b * 64 : (b + 1) * 64, lanes] = piece[:64, :]
        base = b * LANES
        wkv_ref[base : base + 64, lanes] = piece[64:128, :] if c == 0 else piece[128:192, :]
        wkv_ref[base + 64 : base + 128, lanes] = piece[128:192, :] if c == 0 else piece[64:128, :]
        tail = piece[192:208, :].astype(F32)
        ws_ref[h, b * 8 : (b + 1) * 8, :] = tail[:8]
        vecs_ref[h * 8 + b : h * 8 + b + 1, :] = tail[8:9]

    each_piece(at_ref, mine_ref, other_ref, visit)
    vecs = vecs_ref[...].astype(BF16)
    g1_ref[...] = widen(vecs, 0, 16)
    bo_ref[...] = widen(vecs, 16, 16)
    g2_ref[...] = widen(vecs, 32, 16)
    bi_ref[...] = widen(vecs, 48, 64)
    bd_ref[...] = widen(vecs, 112, 16)


SMEM = pl.BlockSpec(memory_space=pltpu.SMEM)
VMEM = pl.BlockSpec(memory_space=pltpu.VMEM)


def assemble(at, mine, other):
    row = jax.ShapeDtypeStruct((1, D), F32)
    return pl.pallas_call(
        assemble_kernel,
        in_specs=[SMEM, VMEM, VMEM],
        out_shape=[
            jax.ShapeDtypeStruct((D, D), BF16),
            jax.ShapeDtypeStruct((2 * D, D), BF16),
            jax.ShapeDtypeStruct((PAIRS, HEAD_DIM, LANES), F32),
            row, row, row, jax.ShapeDtypeStruct((1, FF), F32), row,
        ],
        scratch_shapes=[pltpu.VMEM((32, LANES), F32)],
        compiler_params=vmem(),
        name="assemble",
    )(at, mine, other)


GELU_A = 0.7978845608028654
GELU_B = 0.044715


def feed_tile(x, att, g, bo, g2, bi, bd, win, wdown, wout, acc_in, acc_down, acc_out, sums):
    middle = x.astype(F32) + mm(att, wout[...], NT) + bo
    centre = middle - jnp.mean(middle, axis=-1, keepdims=True)
    spread_ = jnp.mean(centre * centre, axis=-1, keepdims=True)
    inverse = lax.rsqrt(spread_ + EPSILON)
    hat = centre * inverse
    normed = (hat * g2).astype(BF16)
    normed_t = normed.T
    g_t = g.T
    out = jnp.zeros(middle.shape, F32)
    u = jnp.zeros(middle.shape, F32)
    cut = 512
    for k in range(FF // cut):
        cols = slice(k * cut, (k + 1) * cut)
        pre = mm(normed, win[cols, :], NT) + bi[:, cols]
        square = pre * pre
        t = jnp.tanh(GELU_A * pre * (1.0 + GELU_B * square))
        half = 0.5 * (1.0 + t)
        hidden = (pre * half).astype(BF16)
        slope = half + (0.5 * GELU_A) * pre * (1.0 - t * t) * (1.0 + (3.0 * GELU_B) * square)
        g_pre = (mm(g, wdown[:, cols], NN) * slope).astype(BF16)
        out = out + mm(hidden, wdown[:, cols], NT)
        u = u + mm(g_pre, win[cols, :], NN)
        acc_in[:, cols] += mm(normed_t, g_pre)
        acc_down[:, cols] += mm(g_t, hidden)
        sums[4:5, cols] += jnp.sum(g_pre.astype(F32), axis=0, keepdims=True)
    gf = g.astype(F32)
    sums[1:2, :D] += jnp.sum(u * hat, axis=0, keepdims=True)
    sums[3:4, :D] += jnp.sum(gf, axis=0, keepdims=True)
    du = u * g2
    inner = jnp.mean(du * hat, axis=-1, keepdims=True)
    g_middle = gf + inverse * (du - jnp.mean(du, axis=-1, keepdims=True) - hat * inner)
    branch = g_middle.astype(BF16)
    sums[0:1, :D] += jnp.sum(branch.astype(F32), axis=0, keepdims=True)
    acc_out[...] += mm(branch.T, att)
    return (middle + out + bd).astype(BF16), g_middle, mm(branch, wout[...], NN).astype(BF16)


def clear(*refs):
    for ref in refs:
        ref[...] = jnp.zeros_like(ref)


def narrow(sums, h, b):
    lane = lax.broadcasted_iota(jnp.int32, (1, LANES), 1)
    owner = h * 8 + b
    row = jnp.zeros((1, LANES), F32)
    for index, start, size in ((0, 16, 16), (1, 32, 16), (4, 48, 64), (3, 112, 16)):
        at = owner * size
        tile = sums[index : index + 1, at // LANES * LANES : at // LANES * LANES + LANES]
        tile = pltpu.roll(jnp.broadcast_to(tile, (8, LANES)), (start - at) % LANES, 1)[:1]
        row = jnp.where((lane >= start) & (lane < start + size), tile, row)
    return row


def feed_fast_kernel(
    at_ref, x_ref, att_ref, g_ref, bo_ref, g2_ref, bi_ref, bd_ref, mine_ref, other_ref,
    out_ref, gm_ref, ga_ref, keep_ref, send_ref,
    win, wdown, wout, acc_in, acc_down, acc_out, sums,
):
    @pl.when(pl.program_id(0) == 0)
    def _():
        def visit(h, z, c, piece):
            b = 2 * z + c
            win[b * 256 : (b + 1) * 256, h * LANES : (h + 1) * LANES] = piece[:256, :]
            for k in range(4):
                lanes = slice(h * 512 + k * LANES, h * 512 + (k + 1) * LANES)
                wdown[b * 64 : (b + 1) * 64, lanes] = piece[256 + k * 64 : 320 + k * 64, :]
            wout[b * 64 : (b + 1) * 64, h * LANES : (h + 1) * LANES] = piece[512:576, :]

        each_piece(at_ref, mine_ref, other_ref, visit)
        clear(acc_in, acc_down, acc_out, sums)

    out_ref[...], gm_ref[...], ga_ref[...] = feed_tile(
        x_ref[...], att_ref[...], g_ref[...], bo_ref[...], g2_ref[...], bi_ref[...], bd_ref[...],
        win, wdown, wout, acc_in, acc_down, acc_out, sums,
    )

    @pl.when(pl.program_id(0) == pl.num_programs(0) - 1)
    def _():
        for core in range(2):

            @pl.when(at_ref[2] == core)
            def _():
                for h in range(4):
                    for z in range(4):
                        for c in range(2):
                            ref = keep_ref if c == core else send_ref
                            b = 2 * z + c
                            for k in range(2):
                                ref[z, h, k * LANES : (k + 1) * LANES, :] = acc_in[
                                    h * LANES : (h + 1) * LANES,
                                    b * 256 + k * LANES : b * 256 + (k + 1) * LANES,
                                ].astype(BF16)
                            for k in range(4):
                                ref[z, h, 256 + k * 64 : 320 + k * 64, :] = acc_down[
                                    b * 64 : (b + 1) * 64,
                                    h * 512 + k * LANES : h * 512 + (k + 1) * LANES,
                                ].astype(BF16)
                            ref[z, h, 512:576, :] = acc_out[
                                b * 64 : (b + 1) * 64, h * LANES : (h + 1) * LANES
                            ].astype(BF16)
                            ref[z, h, 576:592, :] = jnp.broadcast_to(
                                narrow(sums, h, b), (16, LANES)
                            ).astype(BF16)


def once(shape):
    return pl.BlockSpec(shape, lambda *i: (0,) * len(shape), pipeline_mode=pl.Buffered(1))


def feed_fast(at, x, att, g, bo, g2, bi, bd, mine, other):
    tok = x.shape[0]
    tile = 512
    tiled = pl.BlockSpec((tile, D), lambda i: (i, 0))
    parts = (4, 4, PARTS_TWO, LANES)
    return pl.pallas_call(
        feed_fast_kernel,
        grid=(tok // tile,),
        in_specs=[
            SMEM, tiled, tiled, tiled, once((1, D)), once((1, D)), once((1, FF)), once((1, D)),
            once(mine.shape), once(other.shape),
        ],
        out_specs=[tiled, tiled, tiled, once(parts), once(parts)],
        out_shape=[
            jax.ShapeDtypeStruct((tok, D), BF16),
            jax.ShapeDtypeStruct((tok, D), F32),
            jax.ShapeDtypeStruct((tok, D), BF16),
            jax.ShapeDtypeStruct(parts, BF16),
            jax.ShapeDtypeStruct(parts, BF16),
        ],
        scratch_shapes=[
            pltpu.VMEM((FF, D), BF16), pltpu.VMEM((D, FF), BF16), pltpu.VMEM((D, D), BF16),
            pltpu.VMEM((D, FF), F32), pltpu.VMEM((D, FF), F32), pltpu.VMEM((D, D), F32),
            pltpu.VMEM((8, FF), F32),
        ],
        compiler_params=vmem(60),
        name="feed",
    )(at, x, att, g, bo, g2, bi, bd, mine, other)


def feed_slow_kernel(
    x_ref, att_ref, g_ref, bo_ref, g2_ref, bi_ref, bd_ref, win, wdown, wout,
    out_ref, gm_ref, ga_ref, acc_in, acc_down, acc_out, sums,
):
    @pl.when(pl.program_id(0) == 0)
    def _():
        clear(acc_in, acc_down, acc_out, sums)

    out_ref[...], gm_ref[...], ga_ref[...] = feed_tile(
        x_ref[...], att_ref[...], g_ref[...], bo_ref[...], g2_ref[...], bi_ref[...], bd_ref[...],
        win, wdown, wout, acc_in, acc_down, acc_out, sums,
    )


def feed_slow(x, att, g, bo, g2, bi, bd, win, wdown, wout):
    tok = x.shape[0]
    tile = 512
    tiled = pl.BlockSpec((tile, D), lambda i: (i, 0))
    wide, square, rows = (D, FF), (D, D), (8, FF)
    return pl.pallas_call(
        feed_slow_kernel,
        grid=(tok // tile,),
        in_specs=[
            tiled, tiled, tiled, once((1, D)), once((1, D)), once((1, FF)), once((1, D)),
            once((FF, D)), once(wide), once(square),
        ],
        out_specs=[tiled, tiled, tiled, once(wide), once(wide), once(square), once(rows)],
        out_shape=[
            jax.ShapeDtypeStruct((tok, D), BF16),
            jax.ShapeDtypeStruct((tok, D), F32),
            jax.ShapeDtypeStruct((tok, D), BF16),
            jax.ShapeDtypeStruct(wide, F32),
            jax.ShapeDtypeStruct(wide, F32),
            jax.ShapeDtypeStruct(square, F32),
            jax.ShapeDtypeStruct(rows, F32),
        ],
        compiler_params=vmem(60),
        name="feed_whole",
    )(x, att, g, bo, g2, bi, bd, win, wdown, wout)


def sum_planes_kernel(at_ref, keep_ref, got_ref, *outs):
    for r, out in enumerate(outs):
        z = at_ref[1] ^ r
        out[0] = (keep_ref[z, 0].astype(F32) + got_ref[z, 0].astype(F32)).astype(BF16)


def sum_planes(at, keep, got):
    planes, heads, rows, lanes = keep.shape
    block = pl.BlockSpec((planes, 1, rows, lanes), lambda i: (0, i, 0, 0))
    return pl.pallas_call(
        sum_planes_kernel,
        grid=(heads,),
        in_specs=[SMEM, block, block],
        out_specs=[pl.BlockSpec((1, rows, lanes), lambda i: (i, 0, 0))] * planes,
        out_shape=[jax.ShapeDtypeStruct((heads, rows, lanes), BF16)] * planes,
        compiler_params=vmem(),
        name="sum_planes",
    )(at, keep, got)


def sum_heads_kernel(at_ref, a_ref, b_ref, c_ref, d_ref, *outs):
    for r, out in enumerate(outs):
        h = at_ref[0] ^ r
        total = a_ref[h].astype(F32) + b_ref[h].astype(F32)
        out[...] = (total + c_ref[h].astype(F32) + d_ref[h].astype(F32)).astype(BF16)


def sum_heads(at, pieces):
    heads, rows, lanes = pieces[0].shape
    return pl.pallas_call(
        sum_heads_kernel,
        in_specs=[SMEM] + [VMEM] * 4,
        out_shape=[jax.ShapeDtypeStruct((rows, lanes), BF16)] * heads,
        compiler_params=vmem(),
        name="sum_heads",
    )(at, *pieces)


def last_two_kernel(a_ref, b_ref, c_ref, d_ref, gin_ref, gdown_ref, gout_ref, vec_ref):
    total = a_ref[...].astype(F32) + b_ref[...].astype(F32)
    total = total + c_ref[...].astype(F32) + d_ref[...].astype(F32)
    for k in range(2):
        gin_ref[:, k * LANES : (k + 1) * LANES] = total[k * LANES : (k + 1) * LANES]
    for k in range(4):
        gdown_ref[k * LANES : (k + 1) * LANES, :] = total[256 + k * 64 : 320 + k * 64].T
    gout_ref[...] = total[512:576].T
    vec_ref[...] = total[576:584]


def last_two(pieces):
    return pl.pallas_call(
        last_two_kernel,
        out_shape=[
            jax.ShapeDtypeStruct((LANES, 256), F32),
            jax.ShapeDtypeStruct((512, 64), F32),
            jax.ShapeDtypeStruct((LANES, 64), F32),
            jax.ShapeDtypeStruct((8, LANES), F32),
        ],
        compiler_params=vmem(),
        name="last_two",
    )(*pieces)


def last_one_kernel(a_ref, b_ref, c_ref, d_ref, gw_ref, gs_ref, vec_ref):
    total = a_ref[...].astype(F32) + b_ref[...].astype(F32)
    total = total + c_ref[...].astype(F32) + d_ref[...].astype(F32)
    gw_ref[...] = total[:192].T
    gs_ref[...] = total[192:200].T
    vec_ref[...] = total[200:208]


def last_one(pieces):
    return pl.pallas_call(
        last_one_kernel,
        out_shape=[
            jax.ShapeDtypeStruct((LANES, 192), F32),
            jax.ShapeDtypeStruct((LANES, 8), F32),
            jax.ShapeDtypeStruct((8, LANES), F32),
        ],
        compiler_params=vmem(),
        name="last_one",
    )(*pieces)


def weight_tile(gq, gkv, normed, wq_ref, wkv_ref, u_ref, gmq_ref, gmk_ref, acc_q, acc_kv, first):
    u_ref[...] = mm(gq, wq_ref[...]) + mm(gkv, wkv_ref[...])
    acc_q[...] += mm(gq.T, normed)
    acc_kv[...] += mm(gkv.T, normed)
    blocks = normed.shape[0] // BLOCK
    sums = jnp.sum(normed.astype(F32).reshape(blocks, BLOCK, D), axis=1).astype(BF16)
    rows = pl.ds(pl.multiple_of(first * blocks, blocks), blocks)
    gmq, gmk = gmq_ref[rows, :].astype(BF16), gmk_ref[rows, :].astype(BF16)
    zero = jnp.zeros((blocks, LANES), BF16)
    half = lax.broadcasted_iota(jnp.int32, (blocks, LANES), 1) < HEAD_DIM
    acc_q[...] += mm(gmq, sums, TN)
    wide = []
    for pair in range(PAIRS):
        tile = gmk[:, pair * LANES : (pair + 1) * LANES]
        wide += [jnp.where(half, tile, zero), jnp.where(half, zero, tile)]
    wide = jnp.concatenate(wide, axis=1)
    acc_kv[...] += mm(wide, sums, TN)
    block_u = mm(gmq, wq_ref[...]) + mm(wide, wkv_ref[...])
    for i in range(blocks):
        u_ref[i * BLOCK : (i + 1) * BLOCK, :] += block_u[i : i + 1]


def weight_kernel(
    fast, at_ref, gq_ref, gkv_ref, n_ref, wq_ref, wkv_ref, gmq_ref, gmk_ref, halo_ref, gain_ref,
    gs_ref, u_ref, keep_ref, send_ref, acc_q, acc_kv,
):
    @pl.when(pl.program_id(0) == 0)
    def _():
        clear(acc_q)
        acc_kv[...] = halo_ref[...]

    weight_tile(
        gq_ref[...], gkv_ref[...], n_ref[...], wq_ref, wkv_ref, u_ref, gmq_ref, gmk_ref,
        acc_q, acc_kv, pl.program_id(0),
    )

    @pl.when(pl.program_id(0) == pl.num_programs(0) - 1)
    def _():
        gain = jnp.sum(acc_q[...] * wq_ref[...].astype(F32), axis=0, keepdims=True)
        gain = gain + jnp.sum(acc_kv[...] * wkv_ref[...].astype(F32), axis=0, keepdims=True)
        gain = gain / gain_ref[...]
        if not fast:
            keep_ref[:D, :] = acc_q[...]
            keep_ref[D:, :] = acc_kv[...]
            send_ref[...] = jnp.broadcast_to(gain, (8, D))
            return
        for core in range(2):

            @pl.when(at_ref[2] == core)
            def _():
                lane = lax.broadcasted_iota(jnp.int32, (1, LANES), 1)
                for h in range(4):
                    lanes = slice(h * LANES, (h + 1) * LANES)
                    for z in range(4):
                        for c in range(2):
                            ref = keep_ref if c == core else send_ref
                            b = 2 * z + c
                            base = b * LANES
                            ref[z, h, :64, :] = acc_q[b * 64 : (b + 1) * 64, lanes].astype(BF16)
                            low = acc_kv[base : base + 64, lanes].astype(BF16)
                            high = acc_kv[base + 64 : base + 128, lanes].astype(BF16)
                            ref[z, h, 64:128, :] = low if c == 0 else high
                            ref[z, h, 128:192, :] = high if c == 0 else low
                            own = pltpu.roll(
                                jnp.broadcast_to(gain[:, lanes], (8, LANES)), -16 * b % LANES, 1
                            )
                            ref[z, h, 192:208, :] = jnp.concatenate(
                                [gs_ref[h, b * 8 : (b + 1) * 8, :], own], axis=0
                            ).astype(BF16)


def weight_back(at, gq, gkv, normed, wt_q, wt_kv, gmq, gmk, halo, gain, gsort, fast):
    tok = gq.shape[0]
    tile = 8 * BLOCK
    blocks = tok // BLOCK
    tiled = pl.BlockSpec((tile, D), lambda i: (i, 0))
    parts = (4, 4, PIECE_ONE, LANES)
    shapes = (parts, parts) if fast else ((3 * D, D), (8, D))
    kind = BF16 if fast else F32
    return pl.pallas_call(
        functools.partial(weight_kernel, fast),
        grid=(tok // tile,),
        in_specs=[
            SMEM, tiled, pl.BlockSpec((tile, 2 * D), lambda i: (i, 0)), tiled, once((D, D)),
            once((2 * D, D)), once((blocks, D)), once((blocks, D)), once((2 * D, D)),
            once((1, D)), once(gsort.shape),
        ],
        out_specs=[tiled, once(shapes[0]), once(shapes[1])],
        out_shape=[
            jax.ShapeDtypeStruct((tok, D), F32),
            jax.ShapeDtypeStruct(shapes[0], kind),
            jax.ShapeDtypeStruct(shapes[1], kind),
        ],
        scratch_shapes=[pltpu.VMEM((D, D), F32), pltpu.VMEM((2 * D, D), F32)],
        compiler_params=vmem(),
        name="weight_back",
    )(at, gq, gkv, normed, wt_q, wt_kv, gmq, gmk, halo, gain, gsort)


def finish_kernel(skip, x_ref, u_ref, one_ref, two_ref, gm_ref, gain_ref, out_ref, total):
    rows = x_ref.shape[0]
    at = lax.broadcasted_iota(jnp.int32, (rows, rows), 0)
    lane = lax.broadcasted_iota(jnp.int32, (rows, rows), 1)
    order = (lane == lax.rem(at, BLOCK) * 8 + at // BLOCK).astype(F32).astype(BF16)
    total[...] = u_ref[...] + mm(order, one_ref[...].reshape(rows, D))

    @pl.when(pl.program_id(0) >= skip)
    def _():
        total[...] += mm(order, two_ref[...].reshape(rows, D))

    x = x_ref[...].astype(F32)
    centre = x - jnp.mean(x, axis=-1, keepdims=True)
    inverse = lax.rsqrt(jnp.mean(centre * centre, axis=-1, keepdims=True) + EPSILON)
    hat = centre * inverse
    du = total[...] * gain_ref[...]
    inner = jnp.mean(du * hat, axis=-1, keepdims=True)
    out_ref[...] = gm_ref[...] + inverse * (
        du - jnp.mean(du, axis=-1, keepdims=True) - hat * inner
    )


def finish(x, u, one, two, gm, gain):
    tok = x.shape[0]
    tile = 8 * BLOCK
    skip = (tok // BLOCK - two.shape[1]) // 8
    tiled = pl.BlockSpec((tile, D), lambda i: (i, 0))
    return pl.pallas_call(
        functools.partial(finish_kernel, skip),
        grid=(tok // tile,),
        in_specs=[
            tiled, tiled,
            pl.BlockSpec((BLOCK, 8, D), lambda i: (0, i, 0)),
            pl.BlockSpec((BLOCK, 8, D), lambda i: (0, jnp.maximum(i - skip, 0), 0)),
            tiled, once((1, D)),
        ],
        out_specs=tiled,
        out_shape=jax.ShapeDtypeStruct((tok, D), F32),
        scratch_shapes=[pltpu.VMEM((tile, D), F32)],
        compiler_params=vmem(),
        name="finish",
    )(x, u, one, two, gm, gain)


class Grid:
    def __init__(self):
        self.heads = lax.axis_size("head")
        self.cycles = lax.axis_size("blk")
        self.planes = self.cycles // 2
        self.head = lax.axis_index("head")
        self.cycle = lax.axis_index("blk")
        self.plane = self.cycle // 2
        self.core = self.cycle % 2
        self.place = self.cycle * self.heads + self.head

    def send(self, value, pairs):
        return lax.ppermute(value, ("head", "blk"), pairs)

    def number(self, head, cycle):
        return head * self.cycles + cycle

    def along(self, steps):
        count = self.heads * self.cycles
        at = lambda place: self.number(place % self.heads, place // self.heads)
        return [(at(i), at(i + steps)) for i in range(count) if 0 <= i + steps < count]

    def swap_head(self, flip):
        return [
            (self.number(h, b), self.number(h ^ flip, b))
            for h in range(self.heads)
            for b in range(self.cycles)
        ]

    def swap_plane(self, flip):
        return [
            (self.number(h, b), self.number(h, b ^ (2 * flip)))
            for h in range(self.heads)
            for b in range(self.cycles)
        ]

    def swap_core(self):
        return [
            (self.number(h, b), self.number(h, b ^ 1))
            for h in range(self.heads)
            for b in range(self.cycles)
        ]


def in_order(pieces, index):
    stacked = jnp.stack(pieces)
    count = len(pieces)
    bit = 1
    while bit < count:
        swapped = jnp.stack([stacked[i ^ bit] for i in range(count)])
        stacked = jnp.where((index & bit) != 0, swapped, stacked)
        bit *= 2
    return stacked


def gather_all(grid, piece):
    got = [piece] + [grid.send(piece, grid.swap_plane(r)) for r in range(1, grid.planes)]
    got = in_order(got, grid.plane)
    got = [got] + [grid.send(got, grid.swap_head(r)) for r in range(1, grid.heads)]
    got = in_order(got, grid.head)
    got = in_order([got, grid.send(got, grid.swap_core())], grid.core)
    got = got.transpose(1, 2, 0, *range(3, got.ndim))
    return got.reshape(grid.heads, grid.cycles, *piece.shape)


def scatter_sum(grid, parts):
    mine = lax.dynamic_index_in_dim(parts, grid.core, 0, keepdims=False)
    other = lax.dynamic_index_in_dim(parts, 1 - grid.core, 0, keepdims=False)
    got = grid.send(other, grid.swap_core())
    total = (mine.astype(F32) + got.astype(F32)).astype(BF16)
    pick = lambda r: lax.dynamic_index_in_dim(total, grid.head ^ r, 0, keepdims=False)
    got = [pick(0)] + [grid.send(pick(r), grid.swap_head(r)) for r in range(1, grid.heads)]
    total = sum(item.astype(F32) for item in got).astype(BF16)
    pick = lambda r: lax.dynamic_index_in_dim(total, grid.plane ^ r, 0, keepdims=False)
    got = [pick(0)] + [grid.send(pick(r), grid.swap_plane(r)) for r in range(1, grid.planes)]
    return sum(item.astype(F32) for item in got)


def as_rows(value):
    flat = value.reshape(-1)
    short = -flat.shape[0] % LANES
    return jnp.pad(flat, (0, short)).reshape(-1, LANES)


def by_owner(grid, value):
    columns, rows = value.shape
    cut = value.reshape(grid.planes, 2, columns // grid.cycles, grid.heads, rows // grid.heads)
    return cut.transpose(1, 3, 0, 2, 4)


def vector_by_owner(grid, value):
    cut = value.reshape(grid.heads, grid.planes, 2, -1)
    return cut.transpose(2, 0, 1, 3)


def rows_of(value):
    lead = value.shape[:3]
    flat = value.reshape(*lead, -1)
    short = -flat.shape[-1] % LANES
    flat = jnp.pad(flat, ((0, 0),) * 3 + ((0, short),))
    return flat.reshape(*lead, -1, LANES)


def after(value, *others):
    return lax.optimization_barrier((value, *others))[0]


def weights_slow(grid, vectors, parameters):
    w_qkv, w_sort, w_in, w_down, w_out = parameters
    heads, cycles = grid.heads, grid.cycles
    first = jnp.concatenate([as_rows(w_qkv.T), as_rows(w_sort), as_rows(jnp.concatenate(vectors))])
    wide, sort_rows = as_rows(w_qkv.T).shape[0], as_rows(w_sort).shape[0]
    got = gather_all(grid, first)
    span = w_qkv.shape[1]
    wt_qkv = (
        got[:, :, :wide]
        .reshape(heads, cycles, span, D // heads)
        .transpose(1, 2, 0, 3)
        .reshape(HEADS, 3, HEAD_DIM, D)
    )
    wt_q = wt_qkv[:, 0].reshape(D, D)
    paired = wt_qkv.reshape(PAIRS, 2, 3, HEAD_DIM, D)
    wt_kv = jnp.stack(
        [paired[:, 0, 1], paired[:, 0, 2], paired[:, 1, 2], paired[:, 1, 1]], axis=1
    ).reshape(2 * D, D)
    size = w_sort.shape[0] * w_sort.shape[1]
    w_pairs = (
        got[:, :, wide : wide + sort_rows]
        .reshape(heads, cycles, -1)[:, :, :size]
        .reshape(heads, cycles, *w_sort.shape)
        .transpose(1, 3, 0, 2)
        .reshape(HEAD_DIM, PAIRS, LANES)
        .transpose(1, 0, 2)
        .astype(F32)
    )
    flat = got[:, :, wide + sort_rows :].reshape(heads, cycles, -1)
    sizes = [v.shape[0] for v in vectors]
    cuts = [sum(sizes[:i]) for i in range(len(sizes) + 1)]
    rows = [
        flat[:, :, cuts[i] : cuts[i + 1]].reshape(1, -1).astype(F32) for i in range(len(sizes))
    ]
    second = jnp.concatenate([as_rows(w_in.T), as_rows(w_down.T), as_rows(w_out.T)])
    in_rows, down_rows = as_rows(w_in.T).shape[0], as_rows(w_down.T).shape[0]
    got = gather_all(grid, second)

    def whole(depth, columns, part):
        return (
            part.reshape(heads, cycles, -1)[:, :, : columns // cycles * (depth // heads)]
            .reshape(heads, cycles, columns // cycles, depth // heads)
            .transpose(1, 2, 0, 3)
            .reshape(columns, depth)
        )

    feed = (
        whole(D, FF, got[:, :, :in_rows]),
        whole(FF, D, got[:, :, in_rows : in_rows + down_rows]),
        whole(D, D, got[:, :, in_rows + down_rows :]),
    )
    return wt_q, wt_kv, w_pairs, rows, feed


def matrix(rows, shape):
    flat = rows.reshape(-1)[: shape[0] * shape[1]]
    return flat.reshape(shape[1], shape[0]).T


def gradients_two_slow(grid, acc_in, acc_down, acc_out, sums, parameters, vectors):
    w_qkv, w_sort, w_in, w_down, w_out = parameters
    low = [
        rows_of(by_owner(grid, v.astype(BF16))) for v in (acc_in.T, acc_down, acc_out)
    ]
    order = ((0, D), (1, D), (4, FF), (3, D))
    small = [vector_by_owner(grid, sums[i, :n]) for i, n in order]
    low.append(rows_of(jnp.concatenate(small, axis=-1).astype(BF16)))
    total = scatter_sum(grid, jnp.concatenate(low, axis=3))
    cuts = [0]
    for item in low:
        cuts.append(cuts[-1] + item.shape[3])
    g_in, g_down, g_out = (
        matrix(total[cuts[i] : cuts[i + 1]], w.shape) for i, w in enumerate((w_in, w_down, w_out))
    )
    flat = total[cuts[3] :].reshape(-1)
    sizes = [v.shape[0] for v in vectors[1:]]
    at = [sum(sizes[:i]) for i in range(5)]
    return g_in, g_down, g_out, *(flat[at[i] : at[i + 1]] for i in range(4))


def gradients_one_slow(grid, both, gain, gsort, parameters, vectors):
    w_qkv, w_sort = parameters[:2]
    q = both[:D].reshape(HEADS, HEAD_DIM, D)
    kv = both[D:].reshape(PAIRS, 4, HEAD_DIM, D)
    k = jnp.stack([kv[:, 0], kv[:, 3]], axis=1).reshape(HEADS, HEAD_DIM, D)
    v = jnp.stack([kv[:, 1], kv[:, 2]], axis=1).reshape(HEADS, HEAD_DIM, D)
    wide = jnp.stack([q, k, v], axis=1).reshape(3 * D, D)
    sort = gsort.transpose(0, 2, 1).reshape(grid.heads, D // grid.heads, grid.planes, 2, -1)
    low = [
        rows_of(by_owner(grid, wide.astype(BF16))),
        rows_of(sort.transpose(3, 0, 2, 1, 4).astype(BF16)),
        rows_of(vector_by_owner(grid, gain[0]).astype(BF16)),
    ]
    total = scatter_sum(grid, jnp.concatenate(low, axis=3))
    one, two = low[0].shape[3], low[0].shape[3] + low[1].shape[3]
    size = w_sort.shape[0] * w_sort.shape[1]
    return (
        matrix(total[:one], w_qkv.shape),
        total[one:two].reshape(-1)[:size].reshape(w_sort.shape),
        total[two:].reshape(-1)[: vectors[0].shape[0]],
    )


def per_device(
    tokens, cotangent, doc_lengths, norm_gain1, w_qkv, w_out, b_out, norm_gain2, w_in, b_in,
    w_down, b_down, w_sort,
):
    grid = Grid()
    heads = grid.heads
    x = tokens[0]
    upstream = cotangent[0]
    tok = x.shape[0]
    own = tok // BLOCK
    context = HALO + own
    window = HALO + own + HALO
    second = HALO - own
    fast = heads == 4 and grid.cycles == 8
    at = jnp.stack([grid.head, grid.plane, grid.core]).astype(jnp.int32)
    vectors = (norm_gain1, b_out, norm_gain2, b_in, b_down)
    parameters = (w_qkv, w_sort, w_in, w_down, w_out)

    if fast:
        row = jnp.concatenate(vectors).reshape(1, LANES)
        one, two = pack(w_qkv, w_sort, row, w_in, w_down, w_out)
        ones = [one] + [grid.send(one, grid.swap_head(r)) for r in range(1, 4)]
        two = after(two, *ones)
        twos = [two] + [grid.send(two, grid.swap_head(r)) for r in range(1, 4)]
        ones = jnp.stack(ones)
        ones = [ones] + [grid.send(ones, grid.swap_plane(r)) for r in range(1, 4)]
        x_send = after(x, *twos)
    else:
        x_send = x
    halo_one = grid.send(x_send, grid.along(1))
    halo_two = grid.send(x_send[tok - second * BLOCK :], grid.along(2))
    if fast:
        ones = jnp.stack(ones)
        other = grid.send(ones, grid.swap_core())
        wt_q, wt_kv, w_pairs, *rows = assemble(at, ones, other)
        twos = after(jnp.stack(twos), other)
        twos = jnp.stack([twos] + [grid.send(twos, grid.swap_plane(r)) for r in range(1, 4)])
        feed_weights = (twos, grid.send(twos, grid.swap_core()))
    else:
        wt_q, wt_kv, w_pairs, rows, feed_weights = weights_slow(grid, vectors, parameters)
    gain_one, bias_out, gain_two, bias_in, bias_down = rows

    normed, q, kv, q_mean, k_mean = project(x, gain_one, wt_q, wt_kv)
    means = jnp.concatenate([q_mean, k_mean], axis=1)
    means_window = jnp.concatenate(
        [
            grid.send(means[own - second :], grid.along(2)),
            grid.send(means, grid.along(1)),
            means,
            grid.send(means, grid.along(-1)),
            grid.send(means[:second], grid.along(-2)),
        ]
    )
    x_context = jnp.concatenate([halo_two, halo_one, x]).reshape(context, BLOCK, D)

    begin = grid.place * own
    position = begin - HALO + jnp.arange(window, dtype=jnp.int32)
    doc_ends = jnp.cumsum(doc_lengths, dtype=jnp.int32)
    ended = jnp.sum(
        (doc_ends[None, :] <= position[:, None]).astype(jnp.int32), axis=1, dtype=jnp.int32
    )
    span_end = (grid.cycle + 1) * heads * own
    doc = jnp.where((position >= 0) & (position < span_end), ended, -1)
    fold = window - LANES
    docc = jnp.stack([doc[:LANES], jnp.concatenate([doc[LANES:], doc[fold:LANES]])])
    docn = doc[:, None]
    live = (doc[HALO:context] == doc[HALO - 1 : context - 1]) & (doc[HALO:context] >= 0)
    live = jnp.repeat(live.astype(F32), BLOCK).reshape(tok // LANES, LANES)

    q_window, k_window = means_window[:, :D], means_window[:, D:]
    plan = sink_forward(q_window, k_window, w_pairs, docn, docc, own, context)
    kvx, normed_halo = context_project(x_context, gain_one, wt_kv, HALO)
    attended, skv = attend(q, kv, kvx, plan, live)

    if fast:
        output, g_middle, g_att, keep, send = feed_fast(
            at, x, attended, upstream, bias_out, gain_two, bias_in, bias_down, *feed_weights
        )
        got = grid.send(send, grid.swap_core())
        twos = sum_planes(at, keep, got)
        twos = [twos[0]] + [grid.send(twos[r], grid.swap_plane(r)) for r in range(1, 4)]
    else:
        output, g_middle, g_att, *sums = feed_slow(
            x, attended, upstream, bias_out, gain_two, bias_in, bias_down, *feed_weights
        )
        g_in, g_down, g_out, g_b_out, g_gain_two, g_b_in, g_b_down = gradients_two_slow(
            grid, *sums, parameters, vectors
        )

    gq, gkv, gh, gplan = attend_back(q, kv, skv, g_att, kvx, plan, live)
    gn_halo, g_kv_halo = halo_back(gh, normed_halo, wt_kv)
    back_one = grid.send(gn_halo[:, second:], grid.along(-1))
    back_two = grid.send(gn_halo[:, :second], grid.along(-2))
    gq_window, gk_window, gsort = sink_backward(
        q_window, k_window, w_pairs, docn, docc, gplan, own, context
    )
    gmeans = jnp.concatenate([gq_window, gk_window], axis=1) / BLOCK
    gmeans_low = gmeans.astype(BF16)
    total = (
        gmeans[HALO:context]
        + grid.send(gmeans_low[second:HALO], grid.along(-1)).astype(F32)
        + grid.send(gmeans_low[context : context + own], grid.along(1)).astype(F32)
    )
    far_left = grid.send(gmeans_low[:second], grid.along(-2)).astype(F32)
    far_right = grid.send(gmeans_low[context + own :], grid.along(2)).astype(F32)
    total = total + jnp.pad(far_left, ((own - second, 0), (0, 0)))
    total = total + jnp.pad(far_right, ((0, own - second), (0, 0)))
    u, keep, send = weight_back(
        at, gq, gkv, normed, wt_q, wt_kv, total[:, :D], total[:, D:], g_kv_halo, gain_one, gsort,
        fast,
    )
    if fast:
        got = grid.send(send, grid.swap_core())
        ones = sum_planes(at, keep, got)
        ones = [ones[0]] + [grid.send(ones[r], grid.swap_plane(r)) for r in range(1, 4)]
        ones = sum_heads(at, ones)
        ones = [ones[0]] + [grid.send(ones[r], grid.swap_head(r)) for r in range(1, 4)]
        g_wqkv, g_sort, vec_one = last_one(ones)
        g_gain_one = vec_one[0, :16]
        twos = sum_heads(at, twos)
        twos = [twos[0]] + [grid.send(twos[r], grid.swap_head(r)) for r in range(1, 4)]
        g_in, g_down, g_out, vec_two = last_two(twos)
        g_b_out, g_gain_two = vec_two[0, 16:32], vec_two[0, 32:48]
        g_b_in, g_b_down = vec_two[0, 48:112], vec_two[0, 112:]
    else:
        g_wqkv, g_sort, g_gain_one = gradients_one_slow(
            grid, keep, send, gsort, parameters, vectors
        )
    input_grad = finish(x, u, back_one, back_two, g_middle, gain_one)
    return (
        output[None], input_grad[None], g_gain_one, g_wqkv, g_out, g_b_out, g_gain_two, g_in,
        g_b_in, g_down, g_b_down, g_sort,
    )


def solution(mesh):
    both = P(("head", "blk"))
    split = P("head", "blk")
    stream = P("blk", "head", None)
    return jax.shard_map(
        per_device,
        mesh=mesh,
        in_specs=(
            stream, stream, P(), both, split, split, both, both, split, both, split, both, split,
        ),
        out_specs=(
            stream, stream, both, split, split, both, both, split, both, split, both, split,
        ),
        check_vma=False,
    )
```

```python
import functools

import jax
import jax.numpy as jnp
from jax import lax
from jax.experimental import pallas as pl
from jax.experimental.pallas import tpu as pltpu
from jax.sharding import Mesh
from jax.sharding import PartitionSpec as P

D = 512
HEADS = 8
HEAD_DIM = 64
FF = 2048
BLOCK = 32
SINK_ITERS = 8
DOC_MOST = 62
LANES = 128
PAIRS = HEADS // 2
HALO = 64
UNROLL = 2
CHEAP = pl.CostEstimate(flops=0, transcendentals=0, bytes_accessed=0)
PRECISE = lax.Precision.HIGHEST
EPSILON = 1e-05
NEGATIVE = -1e30
F32 = jnp.float32
BF16 = jnp.bfloat16
NT = (((1,), (1,)), ((), ()))
NN = (((1,), (0,)), ((), ()))
TN = (((0,), (0,)), ((), ()))


def mm(a, b, dims=NN, precision=None):
    return lax.dot_general(a, b, dims, precision=precision, preferred_element_type=F32)


def vmem(limit=56):
    return pltpu.CompilerParams(vmem_limit_bytes=limit * 1024 * 1024)


def once(shape):
    return pl.BlockSpec(shape, lambda *i: (0,) * len(shape), pipeline_mode=pl.Buffered(1))


def sink_mask(docn_ref, docc_ref, window, context):
    first = context
    fold = window - LANES
    lane = lax.broadcasted_iota(jnp.int32, (1, LANES), 1)
    docn = docn_ref[...]
    row = lax.broadcasted_iota(jnp.int32, (window, 1), 0)
    col = jnp.where((row >= first) & (lane < fold), lane + LANES, lane)
    docc = jnp.where(row >= first, docc_ref[1:2, :], docc_ref[0:1, :])
    return (docn == docc) & (docn >= 0) & (col < row)


def fold_pair(top, low, fold, join):
    lane = lax.broadcasted_iota(jnp.int32, (1, LANES), 1)
    both = join(top, low)
    return jnp.where(lane < fold, top, both), jnp.where(lane < fold, low, both)


def sink_weight(w_ref, head):
    pair = w_ref[head // 2]
    lane = lax.broadcasted_iota(jnp.int32, pair.shape, 1)
    zero = jnp.zeros_like(pair)
    if head % 2 == 0:
        return jnp.concatenate([jnp.where(lane < HEAD_DIM, pair, zero), zero], axis=0)
    return jnp.concatenate([zero, jnp.where(lane >= HEAD_DIM, pair, zero)], axis=0)


def sink_logits(queries, keys, weight, context, fold):
    projected = mm(queries, weight, NT, PRECISE)
    keys_two = jnp.concatenate([keys[LANES:], keys[fold:LANES]], axis=0)
    top = mm(projected[:context], keys[:LANES], NT, PRECISE)
    low = mm(projected[context:], keys_two, NT, PRECISE)
    return projected, keys_two, jnp.concatenate([top, low], axis=0)


def row_step(values):
    highest = jnp.max(values, axis=1, keepdims=True)
    alive = highest > 0.5 * NEGATIVE
    highest = jnp.where(alive, highest, 0.0)
    shifted = jnp.exp(values - highest)
    total = jnp.where(alive, jnp.sum(shifted, axis=1, keepdims=True), 1.0)
    return values - (highest + jnp.log(total)), shifted, total


def column_step(values, context, fold):
    top, low = values[:context], values[context:]
    h1, h2 = fold_pair(
        jnp.max(top, axis=0, keepdims=True),
        jnp.max(low, axis=0, keepdims=True),
        fold,
        jnp.maximum,
    )
    a1, a2 = h1 > 0.5 * NEGATIVE, h2 > 0.5 * NEGATIVE
    h1, h2 = jnp.where(a1, h1, 0.0), jnp.where(a2, h2, 0.0)
    e1, e2 = jnp.exp(top - h1), jnp.exp(low - h2)
    t1, t2 = fold_pair(
        jnp.sum(e1, axis=0, keepdims=True), jnp.sum(e2, axis=0, keepdims=True), fold, jnp.add
    )
    t1, t2 = jnp.where(a1, t1, 1.0), jnp.where(a2, t2, 1.0)
    moved = jnp.concatenate([top - (h1 + jnp.log(t1)), low - (h2 + jnp.log(t2))], axis=0)
    return moved, (e1, e2), (t1, t2)


def sink_start(pieces, q_ref, k_ref, w_ref, docn_ref, docc_ref, vals, proj, context):
    window = q_ref.shape[0]
    at = 0
    for piece in pieces:
        rows = piece.shape[0]
        q_ref[at : at + rows, :] = piece[:, :D]
        k_ref[at : at + rows, :] = piece[:, D : 2 * D]
        at += rows
    fold = window - LANES
    permitted = sink_mask(docn_ref, docc_ref, window, context)
    for head in range(HEADS):
        lanes = slice(head // 2 * LANES, (head // 2 + 1) * LANES)
        projected, _, logits = sink_logits(
            q_ref[:, lanes], k_ref[:, lanes], sink_weight(w_ref, head), context, fold
        )
        vals[head] = jnp.where(permitted, logits, NEGATIVE)
        if proj is not None:
            proj[head] = projected


def sink_forward_kernel(
    own, context, a, b, c, d, e, w_ref, docn_ref, docc_ref, plan_ref, q_ref, k_ref, vals
):
    fold = q_ref.shape[0] - LANES
    sink_start((a, b, c, d, e), q_ref, k_ref, w_ref, docn_ref, docc_ref, vals, None, context)

    def step(_, carry):
        for head in range(HEADS):
            moved, _, _ = row_step(vals[head])
            moved, _, _ = column_step(moved, context, fold)
            vals[head] = moved
        return carry

    lax.fori_loop(0, SINK_ITERS, step, 0)
    for head in range(HEADS):
        plan_ref[head] = jnp.exp(vals[head, context - own : context, :]).astype(BF16)


def sink_backward_kernel(
    own, context, a, b, c, d, e, w_ref, docn_ref, docc_ref, gp_ref, gm_ref, gw_ref,
    sa, sb, sd, se, q_ref, k_ref, vals, proj, kept,
):
    window = q_ref.shape[0]
    fold = window - LANES
    sink_start((a, b, c, d, e), q_ref, k_ref, w_ref, docn_ref, docc_ref, vals, proj, context)

    def step(at, carry):
        for head in range(HEADS):
            moved, shifted, total = row_step(vals[head])
            kept[2 * at, head] = shifted * (1.0 / total)
            moved, (e1, e2), (t1, t2) = column_step(moved, context, fold)
            kept[2 * at + 1, head, :context, :] = e1 * (1.0 / t1)
            kept[2 * at + 1, head, context:, :] = e2 * (1.0 / t2)
            vals[head] = moved
        return carry

    lax.fori_loop(0, SINK_ITERS, step, 0)
    for head in range(HEADS):
        vals[head] = jnp.concatenate(
            [
                jnp.zeros((context - own, LANES), F32),
                gp_ref[head] * kept[2 * SINK_ITERS - 1, head, context - own : context, :],
                jnp.zeros((window - context, LANES), F32),
            ],
            axis=0,
        )

    def back(turn, carry):
        at = SINK_ITERS - 1 - turn
        for head in range(HEADS):
            g1, g2 = vals[head, :context, :], vals[head, context:, :]
            s1, s2 = fold_pair(
                jnp.sum(g1, axis=0, keepdims=True),
                jnp.sum(g2, axis=0, keepdims=True),
                fold,
                jnp.add,
            )
            grad = jnp.concatenate(
                [
                    g1 - kept[2 * at + 1, head, :context, :] * s1,
                    g2 - kept[2 * at + 1, head, context:, :] * s2,
                ],
                axis=0,
            )
            vals[head] = grad - kept[2 * at, head] * jnp.sum(grad, axis=1, keepdims=True)
        return carry

    lax.fori_loop(0, SINK_ITERS, back, 0)
    for pair in range(PAIRS):
        lanes = slice(pair * LANES, (pair + 1) * LANES)
        queries, keys = q_ref[:, lanes], k_ref[:, lanes]
        keys_two = jnp.concatenate([keys[LANES:], keys[fold:LANES]], axis=0)
        gq_total = jnp.zeros((window, LANES), F32)
        gk_total = jnp.zeros((window, LANES), F32)
        turned = []
        for head in (2 * pair, 2 * pair + 1):
            g1, g2 = vals[head, :context, :], vals[head, context:, :]
            against = jnp.concatenate(
                [mm(g1, keys[:LANES], NN, PRECISE), mm(g2, keys_two, NN, PRECISE)], axis=0
            )
            gq_total = gq_total + mm(against, sink_weight(w_ref, head), NN, PRECISE)
            u1 = mm(g1, proj[head, :context, :], TN, PRECISE)
            u2 = mm(g2, proj[head, context:, :], TN, PRECISE)
            gk_total = gk_total + jnp.concatenate(
                [u1[:fold], u1[fold:] + u2[fold:], u2[:fold]], axis=0
            )
            turned.append(mm(against, queries, TN, PRECISE))
        half = lax.broadcasted_iota(jnp.int32, (HEAD_DIM, LANES), 1) < HEAD_DIM
        gw_ref[pair] = jnp.where(half, turned[0][:HEAD_DIM], turned[1][HEAD_DIM:])
        gm_ref[:, lanes] = gq_total * (1.0 / BLOCK)
        gm_ref[:, D + pair * LANES : D + (pair + 1) * LANES] = gk_total * (1.0 / BLOCK)
    at = 0
    for piece, ref in ((a, sa), (b, sb), (c, None), (d, sd), (e, se)):
        if ref is not None:
            ref[...] = gm_ref[at : at + piece.shape[0], :].astype(BF16)
        at += piece.shape[0]


def sink_forward(pieces, weight, docn, docc, own, context):
    window = sum(piece.shape[0] for piece in pieces)
    return pl.pallas_call(
        functools.partial(sink_forward_kernel, own, context),
        out_shape=jax.ShapeDtypeStruct((HEADS, own, LANES), BF16),
        scratch_shapes=[
            pltpu.VMEM((window, D), F32),
            pltpu.VMEM((window, D), F32),
            pltpu.VMEM((HEADS, window, LANES), F32),
        ],
        cost_estimate=CHEAP,
        compiler_params=vmem(),
        name="sink_forward",
    )(*pieces, weight, docn, docc)


def sink_backward(pieces, weight, docn, docc, gplan, own, context):
    window = sum(piece.shape[0] for piece in pieces)
    return pl.pallas_call(
        functools.partial(sink_backward_kernel, own, context),
        out_shape=[
            jax.ShapeDtypeStruct((window, 2 * D), F32),
            jax.ShapeDtypeStruct((PAIRS, HEAD_DIM, LANES), F32),
            *(
                jax.ShapeDtypeStruct((pieces[i].shape[0], 2 * D), BF16)
                for i in (0, 1, 3, 4)
            ),
        ],
        scratch_shapes=[
            pltpu.VMEM((window, D), F32),
            pltpu.VMEM((window, D), F32),
            pltpu.VMEM((HEADS, window, LANES), F32),
            pltpu.VMEM((HEADS, window, LANES), F32),
            pltpu.VMEM((2 * SINK_ITERS, HEADS, window, LANES), F32),
        ],
        cost_estimate=CHEAP,
        compiler_params=vmem(),
        name="sink_backward",
    )(*pieces, weight, docn, docc, gplan)


def normalise(values):
    centre = values - jnp.mean(values, axis=-1, keepdims=True)
    spread = jnp.mean(centre * centre, axis=-1, keepdims=True)
    return centre * lax.rsqrt(spread + EPSILON)


def context_kernel(halo_blocks, far_ref, near_ref, x_ref, gain_ref, w_ref, kvx_ref, nh_ref):
    x = jnp.concatenate([far_ref[...], near_ref[...], x_ref[...]], axis=0)
    blocks = x.shape[0]
    normed = normalise(x.astype(F32)) * gain_ref[...].reshape(1, 1, D)
    normed = normed.astype(BF16).reshape(blocks * 8, D)
    row = lax.broadcasted_iota(jnp.int32, (LANES, LANES), 0)
    lane = lax.broadcasted_iota(jnp.int32, (LANES, LANES), 1)
    turn = (lane == (row % 16) * 8 + row // 16).astype(F32).astype(BF16)
    turned = [
        mm(turn, normed[i * LANES : (i + 1) * LANES]).astype(BF16) for i in range(blocks // 16)
    ]
    for b in range(8):
        rows = jnp.concatenate([part[b * 16 : (b + 1) * 16] for part in turned], axis=0)
        nh_ref[b] = rows[:halo_blocks]
        out = mm(rows, w_ref[...], NT).astype(BF16)
        for head in range(HEADS):
            kvx_ref[head, :, b * LANES : (b + 1) * LANES] = out[
                :, head * LANES : (head + 1) * LANES
            ]


def context_project(far, near, x, gain, w_kv):
    halo_blocks = far.shape[0] + near.shape[0]
    blocks = halo_blocks + x.shape[0]
    return pl.pallas_call(
        functools.partial(context_kernel, halo_blocks),
        grid=(BLOCK // 8,),
        in_specs=[
            *(pl.BlockSpec((v.shape[0], 8, D), lambda i: (0, i, 0)) for v in (far, near, x)),
            pl.BlockSpec((1, D), lambda i: (0, 0)),
            pl.BlockSpec((2 * D, D), lambda i: (0, 0)),
        ],
        out_specs=[
            pl.BlockSpec((HEADS, blocks, 8 * LANES), lambda i: (0, 0, i)),
            pl.BlockSpec((8, halo_blocks, D), lambda i: (i, 0, 0)),
        ],
        out_shape=[
            jax.ShapeDtypeStruct((HEADS, blocks, BLOCK * LANES), BF16),
            jax.ShapeDtypeStruct((BLOCK, halo_blocks, D), BF16),
        ],
        cost_estimate=CHEAP,
        compiler_params=vmem(),
        name="context_project",
    )(far, near, x, gain, w_kv)


def compact(values, lane_block):
    out = values[:BLOCK]
    for j in range(1, 4):
        out = jnp.where(lane_block == j, values[j * BLOCK : (j + 1) * BLOCK], out)
    return out


def spread(values, lane_block):
    zero = jnp.zeros_like(values)
    return jnp.concatenate([jnp.where(lane_block == j, values, zero) for j in range(4)], axis=0)


def softmax_pair(local, chosen, live):
    lane = lax.broadcasted_iota(jnp.int32, (BLOCK, LANES), 1)
    row = lax.broadcasted_iota(jnp.int32, (BLOCK, LANES), 0)
    local = jnp.where(row <= lax.rem(lane, BLOCK), local, NEGATIVE)
    chosen = jnp.where(live, chosen, NEGATIVE)
    highest = jnp.maximum(
        jnp.max(local, axis=0, keepdims=True), jnp.max(chosen, axis=0, keepdims=True)
    )
    el, es = jnp.exp(local - highest), jnp.exp(chosen - highest)
    total = jnp.sum(el, axis=0, keepdims=True) + jnp.sum(es, axis=0, keepdims=True)
    inverse = 1.0 / total
    return el * inverse, es * inverse


def half_mask(first):
    lane = lax.broadcasted_iota(jnp.int32, (LANES, LANES), 1)
    return (lane < HEAD_DIM) if first else (lane >= HEAD_DIM)


def attend_kernel(q_ref, kv_ref, kvx_ref, plan_ref, live_ref, att_ref, skv_ref, even_ref, odd_ref):
    own = plan_ref.shape[1]
    blocks = kvx_ref.shape[1]
    held = (even_ref, odd_ref)
    for e in range(2):
        plan = plan_ref[e][:, :blocks]
        for chunk in range(4):
            out = mm(plan, kvx_ref[e, :, chunk * 8 * LANES : (chunk + 1) * 8 * LANES])
            for b in range(8):
                at = (chunk * 8 + b) * (own + 1)
                held[e][at : at + own, :] = out[:, b * LANES : (b + 1) * LANES]
    lane_block = lax.broadcasted_iota(jnp.int32, (BLOCK, LANES), 1) // BLOCK
    lane_half = [half_mask(True), half_mask(False)]

    def group(g, carry):
        start = pl.multiple_of(g * LANES, LANES)
        live = live_ref[pl.ds(g, 1), :] > 0.0
        q = q_ref[pl.ds(start, LANES), :] * 0.125
        outs = []
        for e in range(2):
            local = kv_ref[pl.ds(start, LANES), e * LANES : (e + 1) * LANES]
            chosen = jnp.concatenate(
                [held[e][pl.ds(4 * g + i, BLOCK, stride=own + 1), :] for i in range(4)], axis=0
            ).astype(BF16)
            skv_ref[pl.ds(start, LANES), e * LANES : (e + 1) * LANES] = chosen
            both = jnp.concatenate([local, chosen], axis=0)
            qm = jnp.where(lane_half[e], q, jnp.zeros_like(q))
            scores = mm(both, qm, NT)
            wl, ws = softmax_pair(
                compact(scores[:LANES], lane_block), compact(scores[LANES:], lane_block), live
            )
            weights = jnp.concatenate(
                [spread(wl, lane_block), spread(ws, lane_block)], axis=0
            ).astype(BF16)
            turned = both.T
            values = turned[HEAD_DIM:] if e == 0 else turned[:HEAD_DIM]
            outs.append(mm(values, weights))
        att_ref[pl.ds(start, LANES), :] = jnp.concatenate(outs, axis=0).T.astype(BF16)
        return carry

    lax.fori_loop(0, own // 4, group, 0, unroll=UNROLL)


def attend(q, kv, kvx, plan, live):
    tok, own, blocks = q.shape[0], plan.shape[1], kvx.shape[1]
    return pl.pallas_call(
        attend_kernel,
        grid=(PAIRS,),
        in_specs=[
            pl.BlockSpec((tok, LANES), lambda j: (0, j)),
            pl.BlockSpec((tok, 2 * LANES), lambda j: (0, j)),
            pl.BlockSpec((2, blocks, BLOCK * LANES), lambda j: (j, 0, 0)),
            pl.BlockSpec((2, own, LANES), lambda j: (j, 0, 0)),
            pl.BlockSpec((tok // LANES, LANES), lambda j: (0, 0)),
        ],
        out_specs=[
            pl.BlockSpec((tok, LANES), lambda j: (0, j)),
            pl.BlockSpec((tok, 2 * LANES), lambda j: (0, j)),
        ],
        out_shape=[
            jax.ShapeDtypeStruct((tok, D), BF16),
            jax.ShapeDtypeStruct((tok, 2 * D), BF16),
        ],
        scratch_shapes=[pltpu.VMEM((BLOCK * (own + 1), LANES), F32)] * 2,
        cost_estimate=CHEAP,
        compiler_params=vmem(),
        name="attend",
    )(q, kv, kvx, plan, live)


def attend_back_kernel(
    q_ref, kv_ref, skv_ref, go_ref, kvx_ref, plan_ref, live_ref,
    gq_ref, gkv_ref, gh_ref, gp_ref, even_ref, odd_ref, leven_ref, lodd_ref,
):
    own = plan_ref.shape[1]
    blocks = kvx_ref.shape[1]
    halo = blocks - own
    held = (even_ref, odd_ref)
    lheld = (leven_ref, lodd_ref)
    lane_block = lax.broadcasted_iota(jnp.int32, (BLOCK, LANES), 1) // BLOCK
    lane_half = [half_mask(True), half_mask(False)]

    def group(g, carry):
        start = pl.multiple_of(g * LANES, LANES)
        live = live_ref[pl.ds(g, 1), :] > 0.0
        q = q_ref[pl.ds(start, LANES), :] * 0.125
        go = go_ref[pl.ds(start, LANES), :]
        go = jnp.concatenate([go[:, HEAD_DIM:], go[:, :HEAD_DIM]], axis=1)
        outs = []
        for e in range(2):
            local = kv_ref[pl.ds(start, LANES), e * LANES : (e + 1) * LANES]
            chosen = skv_ref[pl.ds(start, LANES), e * LANES : (e + 1) * LANES]
            both = jnp.concatenate([local, chosen], axis=0)
            qm = jnp.where(lane_half[e], q, jnp.zeros_like(q))
            gm = jnp.where(lane_half[1 - e], go, jnp.zeros_like(go))
            right = jnp.concatenate([qm, gm], axis=0)
            scores = mm(both, right, NT)
            wl, ws = softmax_pair(
                compact(scores[:LANES, :LANES], lane_block),
                compact(scores[LANES:, :LANES], lane_block),
                live,
            )
            dl = compact(scores[:LANES, LANES:], lane_block)
            ds = compact(scores[LANES:, LANES:], lane_block)
            inner = jnp.sum(wl * dl, axis=0, keepdims=True) + jnp.sum(
                ws * ds, axis=0, keepdims=True
            )
            gl, gs = wl * (dl - inner), ws * (ds - inner)
            weights = jnp.concatenate(
                [spread(wl, lane_block), spread(ws, lane_block)], axis=0
            ).astype(BF16)
            gscore = jnp.concatenate(
                [spread(gl, lane_block), spread(gs, lane_block)], axis=0
            ).astype(BF16)
            gboth = mm(jnp.concatenate([gscore, weights], axis=1), right)
            lheld[e][pl.ds(start, LANES), :] = gboth[:LANES]
            gchosen = gboth[LANES:]
            for i in range(4):
                held[e][pl.ds(4 * g + i, BLOCK, stride=own + 1), :] = gchosen[
                    i * BLOCK : (i + 1) * BLOCK
                ]
            turned = both.T
            keys = turned[:HEAD_DIM] if e == 0 else turned[HEAD_DIM:]
            outs.append(mm(keys, gscore))
        gq_ref[pl.ds(start, LANES), :] = (jnp.concatenate(outs, axis=0).T * 0.125).astype(BF16)
        return carry

    lax.fori_loop(0, own // 4, group, 0, unroll=UNROLL)
    for e in range(2):
        plan = plan_ref[e][:, :blocks]
        gplan = jnp.zeros((own, blocks), F32)
        for chunk in range(4):
            lanes = slice(chunk * 8 * LANES, (chunk + 1) * 8 * LANES)
            grads = jnp.concatenate(
                [
                    held[e][(chunk * 8 + b) * (own + 1) : (chunk * 8 + b) * (own + 1) + own, :]
                    for b in range(8)
                ],
                axis=1,
            ).astype(BF16)
            gplan = gplan + mm(grads, kvx_ref[e, :, lanes], NT)
            gcontext = mm(plan, grads, TN)
            gh_ref[e, :, lanes] = gcontext[:halo].astype(BF16)
            for b in range(8):
                at = (chunk * 8 + b) * (own + 1)
                held[e][at : at + own, :] = gcontext[halo:, b * LANES : (b + 1) * LANES]
        gp_ref[e] = jnp.concatenate([gplan, jnp.zeros((own, LANES - blocks), F32)], axis=1)

    def finish(g, carry):
        start = pl.multiple_of(g * LANES, LANES)
        for e in range(2):
            rest = jnp.concatenate(
                [held[e][pl.ds(4 * g + i, BLOCK, stride=own + 1), :] for i in range(4)], axis=0
            )
            gkv_ref[pl.ds(start, LANES), e * LANES : (e + 1) * LANES] = (
                rest + lheld[e][pl.ds(start, LANES), :]
            ).astype(BF16)
        return carry

    lax.fori_loop(0, own // 4, finish, 0)


def attend_back(q, kv, skv, go, kvx, plan, live, first, pairs):
    tok, own, blocks = q.shape[0], plan.shape[1], kvx.shape[1]
    halo = blocks - own
    return pl.pallas_call(
        attend_back_kernel,
        grid=(pairs,),
        in_specs=[
            pl.BlockSpec((tok, LANES), lambda j: (0, j + first)),
            pl.BlockSpec((tok, 2 * LANES), lambda j: (0, j + first)),
            pl.BlockSpec((tok, 2 * LANES), lambda j: (0, j + first)),
            pl.BlockSpec((tok, LANES), lambda j: (0, j + first)),
            pl.BlockSpec((2, blocks, BLOCK * LANES), lambda j: (j + first, 0, 0)),
            pl.BlockSpec((2, own, LANES), lambda j: (j + first, 0, 0)),
            pl.BlockSpec((tok // LANES, LANES), lambda j: (0, 0)),
        ],
        out_specs=[
            pl.BlockSpec((tok, LANES), lambda j: (0, j)),
            pl.BlockSpec((tok, 2 * LANES), lambda j: (0, j)),
            pl.BlockSpec((2, halo, BLOCK * LANES), lambda j: (j, 0, 0)),
            pl.BlockSpec((2, own, LANES), lambda j: (j, 0, 0)),
        ],
        out_shape=[
            jax.ShapeDtypeStruct((tok, pairs * LANES), BF16),
            jax.ShapeDtypeStruct((tok, 2 * pairs * LANES), BF16),
            jax.ShapeDtypeStruct((2 * pairs, halo, BLOCK * LANES), BF16),
            jax.ShapeDtypeStruct((2 * pairs, own, LANES), F32),
        ],
        scratch_shapes=[pltpu.VMEM((BLOCK * (own + 1), LANES), F32)] * 4,
        cost_estimate=CHEAP,
        compiler_params=vmem(),
        name="attend_back",
    )(q, kv, skv, go, kvx, plan, live)


def halo_kernel(low_ref, high_ref, nh_ref, w_ref, far_ref, near_ref, gw_ref):
    halo = low_ref.shape[1]
    far = far_ref.shape[1]

    @pl.when(pl.program_id(0) == 0)
    def _():
        gw_ref[...] = jnp.zeros_like(gw_ref)

    rows = jnp.concatenate(
        [
            jnp.concatenate(
                [
                    ref[head, :, b * LANES : (b + 1) * LANES]
                    for ref in (low_ref, high_ref)
                    for head in range(ref.shape[0])
                ],
                axis=1,
            )
            for b in range(8)
        ],
        axis=0,
    )
    out = mm(rows, w_ref[...]).astype(BF16).reshape(8, halo, D)
    far_ref[...] = out[:, :far]
    near_ref[...] = out[:, far:]
    gw_ref[...] += mm(rows, nh_ref[...].reshape(8 * halo, D), TN)


def halo_back(low, high, nh, w_kv, far):
    halo = low.shape[1]
    half = pl.BlockSpec((HEADS // 2, halo, 8 * LANES), lambda i: (0, 0, i))
    return pl.pallas_call(
        halo_kernel,
        grid=(BLOCK // 8,),
        in_specs=[
            half,
            half,
            pl.BlockSpec((8, halo, D), lambda i: (i, 0, 0)),
            pl.BlockSpec((2 * D, D), lambda i: (0, 0)),
        ],
        out_specs=[
            pl.BlockSpec((8, far, D), lambda i: (i, 0, 0)),
            pl.BlockSpec((8, halo - far, D), lambda i: (i, 0, 0)),
            pl.BlockSpec((2 * D, D), lambda i: (0, 0)),
        ],
        out_shape=[
            jax.ShapeDtypeStruct((BLOCK, far, D), BF16),
            jax.ShapeDtypeStruct((BLOCK, halo - far, D), BF16),
            jax.ShapeDtypeStruct((2 * D, D), F32),
        ],
        cost_estimate=CHEAP,
        compiler_params=vmem(),
        name="halo_back",
    )(low, high, nh, w_kv)


def project_kernel(x_ref, gain_ref, wq_ref, wkv_ref, n_ref, q_ref, kv_ref, m_ref, head_ref, tail_ref):
    rows = x_ref.shape[0]
    blocks = rows // BLOCK
    normed = (normalise(x_ref[...].astype(F32)) * gain_ref[...]).astype(BF16)
    n_ref[...] = normed
    q = mm(normed, wq_ref[...], NT).astype(BF16)
    q_ref[...] = q
    kv = mm(normed, wkv_ref[...], NT).astype(BF16)
    kv_ref[...] = kv
    half = lax.broadcasted_iota(jnp.int32, (1, LANES), 1) < HEAD_DIM
    m_ref[:, :D] = jnp.mean(q.astype(F32).reshape(blocks, BLOCK, D), axis=1)
    for pair in range(PAIRS):
        even = kv[:, 2 * pair * LANES : (2 * pair + 1) * LANES]
        odd = kv[:, (2 * pair + 1) * LANES : (2 * pair + 2) * LANES]
        keys = jnp.where(half, even.astype(F32), odd.astype(F32))
        m_ref[:, D + pair * LANES : D + (pair + 1) * LANES] = jnp.mean(
            keys.reshape(blocks, BLOCK, LANES), axis=1
        )
    m_ref[:, 2 * D :] = jnp.mean(normed.astype(F32).reshape(blocks, BLOCK, D), axis=1)
    at = pl.program_id(0)
    ends = head_ref.shape[0] // blocks
    for ref, first in ((head_ref, 0), (tail_ref, pl.num_programs(0) - ends)):

        @pl.when((at >= first) & (at < first + ends))
        def _():
            ref[pl.ds(pl.multiple_of((at - first) * blocks, 8), blocks), :] = m_ref[...]


def project(x, gain, wt_q, wt_kv, ends):
    tok = x.shape[0]
    tile = 8 * BLOCK
    return pl.pallas_call(
        project_kernel,
        grid=(tok // tile,),
        in_specs=[
            pl.BlockSpec((tile, D), lambda i: (i, 0)),
            pl.BlockSpec((1, D), lambda i: (0, 0)),
            pl.BlockSpec((D, D), lambda i: (0, 0)),
            pl.BlockSpec((2 * D, D), lambda i: (0, 0)),
        ],
        out_specs=[
            pl.BlockSpec((tile, D), lambda i: (i, 0)),
            pl.BlockSpec((tile, D), lambda i: (i, 0)),
            pl.BlockSpec((tile, 2 * D), lambda i: (i, 0)),
            pl.BlockSpec((8, 3 * D), lambda i: (i, 0)),
            once((ends, 3 * D)),
            once((ends, 3 * D)),
        ],
        out_shape=[
            jax.ShapeDtypeStruct((tok, D), BF16),
            jax.ShapeDtypeStruct((tok, D), BF16),
            jax.ShapeDtypeStruct((tok, 2 * D), BF16),
            jax.ShapeDtypeStruct((tok // BLOCK, 3 * D), F32),
            jax.ShapeDtypeStruct((ends, 3 * D), F32),
            jax.ShapeDtypeStruct((ends, 3 * D), F32),
        ],
        cost_estimate=CHEAP,
        compiler_params=vmem(),
        name="project",
    )(x, gain, wt_q, wt_kv)


PIECE_ONE = 208
PIECE_TWO = 576
PARTS_TWO = 592


def place(vector, start):
    size = vector.shape[1]
    row = lax.broadcasted_iota(jnp.int32, (size, LANES), 0)
    lane = lax.broadcasted_iota(jnp.int32, (size, LANES), 1)
    pick = (lane == row + start).astype(F32).astype(BF16)
    return mm(jnp.broadcast_to(vector.astype(F32), (16, size)).astype(BF16), pick)


def pack_kernel(wqkv_ref, wsort_ref, g1, bo, g2, bi, bd, win_ref, wdown_ref, wout_ref, one_ref, two_ref):
    one_ref[:192, :] = wqkv_ref[...]
    row = place(g1[...], 0) + place(bo[...], 16) + place(g2[...], 32)
    row = row + place(bi[...], 48) + place(bd[...], 112)
    one_ref[192:, :] = jnp.concatenate([wsort_ref[...].astype(F32), row[:8]], axis=0).astype(BF16)
    two_ref[:256, :] = win_ref[...].astype(F32).T.astype(BF16)
    for k in range(4):
        two_ref[256 + k * 64 : 256 + (k + 1) * 64, :] = wdown_ref[:, k * LANES : (k + 1) * LANES]
    two_ref[512:, :] = wout_ref[...]


def pack(w_qkv, w_sort, vectors, w_in, w_down, w_out):
    return pl.pallas_call(
        pack_kernel,
        out_shape=[
            jax.ShapeDtypeStruct((PIECE_ONE, LANES), BF16),
            jax.ShapeDtypeStruct((PIECE_TWO, LANES), BF16),
        ],
        cost_estimate=CHEAP,
        compiler_params=vmem(),
        name="pack",
    )(w_qkv.T, w_sort.T, *(v.reshape(1, -1) for v in vectors), w_in, w_down.T, w_out.T)


def each_piece(at_ref, mine_ref, other_ref, visit):
    for core in range(2):

        @pl.when(at_ref[2] == core)
        def _():
            for h in range(4):
                for z in range(4):
                    for c in range(2):
                        source = mine_ref if c == core else other_ref
                        visit(h, z, c, source.at[at_ref[1] ^ z, at_ref[0] ^ h])


def widen(vecs, start, size):
    total = 32 * size
    lane = lax.broadcasted_iota(jnp.int32, (LANES, total), 1)
    row = lax.broadcasted_iota(jnp.int32, (LANES, total), 0)
    pick = (row == start + lax.rem(lane, size)).astype(F32).astype(BF16)
    every = mm(vecs, pick)
    owner = lax.broadcasted_iota(jnp.int32, (32, total), 0)
    lane = lax.broadcasted_iota(jnp.int32, (32, total), 1)
    return jnp.sum(jnp.where(owner == lane // size, every, 0.0), axis=0, keepdims=True)


def assemble_kernel(
    at_ref, mine_ref, other_ref, wq_ref, wkv_ref, ws_ref, g1_ref, bo_ref, g2_ref, bi_ref, bd_ref,
    vecs_ref,
):
    def visit(h, z, c, piece):
        b = 2 * z + c
        lanes = slice(h * LANES, (h + 1) * LANES)
        wq_ref[b * 64 : (b + 1) * 64, lanes] = piece[:64, :]
        base = b * LANES
        wkv_ref[base : base + 64, lanes] = piece[64:128, :] if c == 0 else piece[128:192, :]
        wkv_ref[base + 64 : base + 128, lanes] = piece[128:192, :] if c == 0 else piece[64:128, :]
        tail = piece[192:208, :].astype(F32)
        ws_ref[h, b * 8 : (b + 1) * 8, :] = tail[:8]
        vecs_ref[h * 8 + b : h * 8 + b + 1, :] = tail[8:9]

    each_piece(at_ref, mine_ref, other_ref, visit)
    vecs = vecs_ref[...].astype(BF16)
    g1_ref[...] = widen(vecs, 0, 16)
    bo_ref[...] = widen(vecs, 16, 16)
    g2_ref[...] = widen(vecs, 32, 16)
    bi_ref[...] = widen(vecs, 48, 64)
    bd_ref[...] = widen(vecs, 112, 16)


SMEM = pl.BlockSpec(memory_space=pltpu.SMEM)
VMEM = pl.BlockSpec(memory_space=pltpu.VMEM)


def assemble(at, mine, other):
    row = jax.ShapeDtypeStruct((1, D), F32)
    return pl.pallas_call(
        assemble_kernel,
        in_specs=[SMEM, VMEM, VMEM],
        out_shape=[
            jax.ShapeDtypeStruct((D, D), BF16),
            jax.ShapeDtypeStruct((2 * D, D), BF16),
            jax.ShapeDtypeStruct((PAIRS, HEAD_DIM, LANES), F32),
            row, row, row, jax.ShapeDtypeStruct((1, FF), F32), row,
        ],
        scratch_shapes=[pltpu.VMEM((32, LANES), F32)],
        cost_estimate=CHEAP,
        compiler_params=vmem(),
        name="assemble",
    )(at, mine, other)


GELU_A = 0.7978845608028654
GELU_B = 0.044715


def feed_tile(x, att, g, bo, g2, bi, bd, win, wdown, wout, acc_in, acc_down, acc_out, sums):
    middle = x.astype(F32) + mm(att, wout[...], NT) + bo
    centre = middle - jnp.mean(middle, axis=-1, keepdims=True)
    spread_ = jnp.mean(centre * centre, axis=-1, keepdims=True)
    inverse = lax.rsqrt(spread_ + EPSILON)
    hat = centre * inverse
    normed = (hat * g2).astype(BF16)
    normed_t = normed.T
    g_t = g.T
    out = jnp.zeros(middle.shape, F32)
    u = jnp.zeros(middle.shape, F32)
    cut = 512
    for k in range(FF // cut):
        cols = slice(k * cut, (k + 1) * cut)
        pre = mm(normed, win[cols, :], NT) + bi[:, cols]
        square = pre * pre
        t = jnp.tanh(GELU_A * pre * (1.0 + GELU_B * square))
        half = 0.5 * (1.0 + t)
        hidden = (pre * half).astype(BF16)
        slope = half + (0.5 * GELU_A) * pre * (1.0 - t * t) * (1.0 + (3.0 * GELU_B) * square)
        g_pre = (mm(g, wdown[:, cols], NN) * slope).astype(BF16)
        out = out + mm(hidden, wdown[:, cols], NT)
        u = u + mm(g_pre, win[cols, :], NN)
        acc_in[:, cols] += mm(normed_t, g_pre)
        acc_down[:, cols] += mm(g_t, hidden)
        sums[4:5, cols] += jnp.sum(g_pre.astype(F32), axis=0, keepdims=True)
    gf = g.astype(F32)
    sums[1:2, :D] += jnp.sum(u * hat, axis=0, keepdims=True)
    sums[3:4, :D] += jnp.sum(gf, axis=0, keepdims=True)
    du = u * g2
    inner = jnp.mean(du * hat, axis=-1, keepdims=True)
    g_middle = gf + inverse * (du - jnp.mean(du, axis=-1, keepdims=True) - hat * inner)
    branch = g_middle.astype(BF16)
    sums[0:1, :D] += jnp.sum(branch.astype(F32), axis=0, keepdims=True)
    acc_out[...] += mm(branch.T, att)
    return (middle + out + bd).astype(BF16), g_middle, mm(branch, wout[...], NN).astype(BF16)


def clear(*refs):
    for ref in refs:
        ref[...] = jnp.zeros_like(ref)


def narrow(sums, h, b):
    lane = lax.broadcasted_iota(jnp.int32, (1, LANES), 1)
    owner = h * 8 + b
    row = jnp.zeros((1, LANES), F32)
    for index, start, size in ((0, 16, 16), (1, 32, 16), (4, 48, 64), (3, 112, 16)):
        at = owner * size
        tile = sums[index : index + 1, at // LANES * LANES : at // LANES * LANES + LANES]
        tile = pltpu.roll(jnp.broadcast_to(tile, (8, LANES)), (start - at) % LANES, 1)[:1]
        row = jnp.where((lane >= start) & (lane < start + size), tile, row)
    return row


def feed_fast_kernel(
    at_ref, x_ref, att_ref, g_ref, bo_ref, g2_ref, bi_ref, bd_ref, mine_ref, other_ref,
    out_ref, gm_ref, ga_ref, keep_ref, send_ref,
    win, wdown, wout, acc_in, acc_down, acc_out, sums,
):
    @pl.when(pl.program_id(0) == 0)
    def _():
        def visit(h, z, c, piece):
            b = 2 * z + c
            win[b * 256 : (b + 1) * 256, h * LANES : (h + 1) * LANES] = piece[:256, :]
            for k in range(4):
                lanes = slice(h * 512 + k * LANES, h * 512 + (k + 1) * LANES)
                wdown[b * 64 : (b + 1) * 64, lanes] = piece[256 + k * 64 : 320 + k * 64, :]
            wout[b * 64 : (b + 1) * 64, h * LANES : (h + 1) * LANES] = piece[512:576, :]

        each_piece(at_ref, mine_ref, other_ref, visit)
        clear(acc_in, acc_down, acc_out, sums)

    out_ref[...], gm_ref[...], ga_ref[...] = feed_tile(
        x_ref[...], att_ref[...], g_ref[...], bo_ref[...], g2_ref[...], bi_ref[...], bd_ref[...],
        win, wdown, wout, acc_in, acc_down, acc_out, sums,
    )

    @pl.when(pl.program_id(0) == pl.num_programs(0) - 1)
    def _():
        for core in range(2):

            @pl.when(at_ref[2] == core)
            def _():
                for h in range(4):
                    for z in range(4):
                        for c in range(2):
                            ref = keep_ref if c == core else send_ref
                            b = 2 * z + c
                            for k in range(2):
                                ref[z, h, k * LANES : (k + 1) * LANES, :] = acc_in[
                                    h * LANES : (h + 1) * LANES,
                                    b * 256 + k * LANES : b * 256 + (k + 1) * LANES,
                                ].astype(BF16)
                            for k in range(4):
                                ref[z, h, 256 + k * 64 : 320 + k * 64, :] = acc_down[
                                    b * 64 : (b + 1) * 64,
                                    h * 512 + k * LANES : h * 512 + (k + 1) * LANES,
                                ].astype(BF16)
                            ref[z, h, 512:576, :] = acc_out[
                                b * 64 : (b + 1) * 64, h * LANES : (h + 1) * LANES
                            ].astype(BF16)
                            ref[z, h, 576:592, :] = jnp.broadcast_to(
                                narrow(sums, h, b), (16, LANES)
                            ).astype(BF16)


def feed_fast(at, x, att, g, bo, g2, bi, bd, mine, other):
    tok = x.shape[0]
    tile = 512
    tiled = pl.BlockSpec((tile, D), lambda i: (i, 0))
    parts = (4, 4, PARTS_TWO, LANES)
    return pl.pallas_call(
        feed_fast_kernel,
        grid=(tok // tile,),
        in_specs=[
            SMEM, tiled, tiled, tiled, once((1, D)), once((1, D)), once((1, FF)), once((1, D)),
            once(mine.shape), once(other.shape),
        ],
        out_specs=[tiled, tiled, tiled, once(parts), once(parts)],
        out_shape=[
            jax.ShapeDtypeStruct((tok, D), BF16),
            jax.ShapeDtypeStruct((tok, D), F32),
            jax.ShapeDtypeStruct((tok, D), BF16),
            jax.ShapeDtypeStruct(parts, BF16),
            jax.ShapeDtypeStruct(parts, BF16),
        ],
        scratch_shapes=[
            pltpu.VMEM((FF, D), BF16), pltpu.VMEM((D, FF), BF16), pltpu.VMEM((D, D), BF16),
            pltpu.VMEM((D, FF), F32), pltpu.VMEM((D, FF), F32), pltpu.VMEM((D, D), F32),
            pltpu.VMEM((8, FF), F32),
        ],
        cost_estimate=CHEAP,
        compiler_params=vmem(60),
        name="feed",
    )(at, x, att, g, bo, g2, bi, bd, mine, other)


def feed_slow_kernel(
    x_ref, att_ref, g_ref, bo_ref, g2_ref, bi_ref, bd_ref, win, wdown, wout,
    out_ref, gm_ref, ga_ref, acc_in, acc_down, acc_out, sums,
):
    @pl.when(pl.program_id(0) == 0)
    def _():
        clear(acc_in, acc_down, acc_out, sums)

    out_ref[...], gm_ref[...], ga_ref[...] = feed_tile(
        x_ref[...], att_ref[...], g_ref[...], bo_ref[...], g2_ref[...], bi_ref[...], bd_ref[...],
        win, wdown, wout, acc_in, acc_down, acc_out, sums,
    )


def feed_slow(x, att, g, bo, g2, bi, bd, win, wdown, wout):
    tok = x.shape[0]
    tile = 512
    tiled = pl.BlockSpec((tile, D), lambda i: (i, 0))
    wide, square, rows = (D, FF), (D, D), (8, FF)
    return pl.pallas_call(
        feed_slow_kernel,
        grid=(tok // tile,),
        in_specs=[
            tiled, tiled, tiled, once((1, D)), once((1, D)), once((1, FF)), once((1, D)),
            once((FF, D)), once(wide), once(square),
        ],
        out_specs=[tiled, tiled, tiled, once(wide), once(wide), once(square), once(rows)],
        out_shape=[
            jax.ShapeDtypeStruct((tok, D), BF16),
            jax.ShapeDtypeStruct((tok, D), F32),
            jax.ShapeDtypeStruct((tok, D), BF16),
            jax.ShapeDtypeStruct(wide, F32),
            jax.ShapeDtypeStruct(wide, F32),
            jax.ShapeDtypeStruct(square, F32),
            jax.ShapeDtypeStruct(rows, F32),
        ],
        cost_estimate=CHEAP,
        compiler_params=vmem(60),
        name="feed_whole",
    )(x, att, g, bo, g2, bi, bd, win, wdown, wout)


def split_kernel(which, at_ref, keep_ref, got_ref, *outs):
    for r, out in enumerate(outs):
        i = at_ref[which] ^ r
        out[0] = (keep_ref[i, 0].astype(F32) + got_ref[i, 0].astype(F32)).astype(BF16)


def split_sum(at, which, keep, got):
    one, two, rows, lanes = keep.shape
    block = pl.BlockSpec((one, 1, rows, lanes), lambda i: (0, i, 0, 0))
    return pl.pallas_call(
        functools.partial(split_kernel, which),
        grid=(two,),
        in_specs=[SMEM, block, block],
        out_specs=[pl.BlockSpec((1, rows, lanes), lambda i: (i, 0, 0))] * one,
        out_shape=[jax.ShapeDtypeStruct((two, rows, lanes), BF16)] * one,
        cost_estimate=CHEAP,
        compiler_params=vmem(),
        name="split_sum",
    )(at, keep, got)


def merge_kernel(which, at_ref, a_ref, b_ref, c_ref, d_ref, *outs):
    for r, out in enumerate(outs):
        i = at_ref[which] ^ r
        total = a_ref[i].astype(F32) + b_ref[i].astype(F32)
        out[...] = (total + c_ref[i].astype(F32) + d_ref[i].astype(F32)).astype(BF16)


def merge_sum(at, which, pieces):
    count, rows, lanes = pieces[0].shape
    return pl.pallas_call(
        functools.partial(merge_kernel, which),
        in_specs=[SMEM] + [VMEM] * 4,
        out_shape=[jax.ShapeDtypeStruct((rows, lanes), BF16)] * count,
        cost_estimate=CHEAP,
        compiler_params=vmem(),
        name="merge_sum",
    )(at, *pieces)


def last_two_kernel(a_ref, b_ref, c_ref, d_ref, gin_ref, gdown_ref, gout_ref, bo, g2, bi, bd):
    total = a_ref[...].astype(F32) + b_ref[...].astype(F32)
    total = total + c_ref[...].astype(F32) + d_ref[...].astype(F32)
    for k in range(2):
        gin_ref[:, k * LANES : (k + 1) * LANES] = total[k * LANES : (k + 1) * LANES]
    for k in range(4):
        gdown_ref[:, k * LANES : (k + 1) * LANES] = total[256 + k * 64 : 320 + k * 64]
    gout_ref[...] = total[512:576]
    row = total[576:577]
    bo[...], g2[...], bi[...], bd[...] = row[:, 16:32], row[:, 32:48], row[:, 48:112], row[:, 112:]


def last_two(pieces):
    return pl.pallas_call(
        last_two_kernel,
        out_shape=[
            jax.ShapeDtypeStruct((LANES, 256), F32),
            jax.ShapeDtypeStruct((64, 512), F32),
            jax.ShapeDtypeStruct((64, LANES), F32),
            *(jax.ShapeDtypeStruct((1, n), F32) for n in (16, 16, 64, 16)),
        ],
        cost_estimate=CHEAP,
        compiler_params=vmem(),
        name="last_two",
    )(*pieces)


def last_one_kernel(a_ref, b_ref, c_ref, d_ref, gw_ref, gs_ref, g1_ref):
    total = a_ref[...].astype(F32) + b_ref[...].astype(F32)
    total = total + c_ref[...].astype(F32) + d_ref[...].astype(F32)
    gw_ref[...] = total[:192]
    gs_ref[...] = total[192:200]
    g1_ref[...] = total[200:201, :16]


def last_one(pieces):
    return pl.pallas_call(
        last_one_kernel,
        out_shape=[
            jax.ShapeDtypeStruct((192, LANES), F32),
            jax.ShapeDtypeStruct((8, LANES), F32),
            jax.ShapeDtypeStruct((1, 16), F32),
        ],
        cost_estimate=CHEAP,
        compiler_params=vmem(),
        name="last_one",
    )(*pieces)


def widen_keys(gmk):
    half = lax.broadcasted_iota(jnp.int32, (gmk.shape[0], LANES), 1) < HEAD_DIM
    zero = jnp.zeros((gmk.shape[0], LANES), gmk.dtype)
    wide = []
    for pair in range(PAIRS):
        tile = gmk[:, pair * LANES : (pair + 1) * LANES]
        wide += [jnp.where(half, tile, zero), jnp.where(half, zero, tile)]
    return jnp.concatenate(wide, axis=1)


def weight_kernel(
    fast, at_ref, ql_ref, qh_ref, kvl_ref, kvh_ref, n_ref, wq_ref, wkv_ref, gm_ref,
    pa, pb, pc, pd, pe, halo_ref, gain_ref, gs_ref, keep_ref, send_ref, acc_q, acc_kv,
):
    @pl.when(pl.program_id(0) == 0)
    def _():
        means = jnp.concatenate([ref[:, 2 * D :] for ref in (pa, pb, pc, pd, pe)], axis=0)
        means = means.astype(BF16)
        grads = (gm_ref[...] * float(BLOCK)).astype(BF16)
        acc_q[...] = mm(grads[:, :D], means, TN)
        acc_kv[...] = halo_ref[...] + mm(widen_keys(grads[:, D:]), means, TN)

    normed = n_ref[...]
    for i, (q_ref, kv_ref) in enumerate(((ql_ref, kvl_ref), (qh_ref, kvh_ref))):
        acc_q[i * 256 : (i + 1) * 256, :] += mm(q_ref[...].T, normed)
        acc_kv[i * 512 : (i + 1) * 512, :] += mm(kv_ref[...].T, normed)

    @pl.when(pl.program_id(0) == pl.num_programs(0) - 1)
    def _():
        gain = jnp.sum(acc_q[...] * wq_ref[...].astype(F32), axis=0, keepdims=True)
        gain = gain + jnp.sum(acc_kv[...] * wkv_ref[...].astype(F32), axis=0, keepdims=True)
        gain = gain / gain_ref[...]
        if not fast:
            keep_ref[:D, :] = acc_q[...]
            keep_ref[D:, :] = acc_kv[...]
            send_ref[...] = jnp.broadcast_to(gain, (8, D))
            return
        for core in range(2):

            @pl.when(at_ref[2] == core)
            def _():
                for h in range(4):
                    lanes = slice(h * LANES, (h + 1) * LANES)
                    for z in range(4):
                        for c in range(2):
                            ref = keep_ref if c == core else send_ref
                            b = 2 * z + c
                            base = b * LANES
                            ref[h, z, :64, :] = acc_q[b * 64 : (b + 1) * 64, lanes].astype(BF16)
                            low = acc_kv[base : base + 64, lanes].astype(BF16)
                            high = acc_kv[base + 64 : base + 128, lanes].astype(BF16)
                            ref[h, z, 64:128, :] = low if c == 0 else high
                            ref[h, z, 128:192, :] = high if c == 0 else low
                            own = pltpu.roll(
                                jnp.broadcast_to(gain[:, lanes], (8, LANES)), -16 * b % LANES, 1
                            )
                            ref[h, z, 192:208, :] = jnp.concatenate(
                                [gs_ref[h, b * 8 : (b + 1) * 8, :], own], axis=0
                            ).astype(BF16)


def weight_back(at, gq, gkv, normed, wt_q, wt_kv, gm, pieces, halo, gain, gsort, fast):
    tok = normed.shape[0]
    tile = 512
    parts = (4, 4, PIECE_ONE, LANES)
    shapes = (parts, parts) if fast else ((3 * D, D), (8, D))
    kind = BF16 if fast else F32
    rows = lambda width: pl.BlockSpec((tile, width), lambda i: (i, 0))
    return pl.pallas_call(
        functools.partial(weight_kernel, fast),
        grid=(tok // tile,),
        in_specs=[
            SMEM, rows(D // 2), rows(D // 2), rows(D), rows(D), rows(D), once((D, D)),
            once((2 * D, D)), once(gm.shape), *(once(p.shape) for p in pieces),
            once((2 * D, D)), once((1, D)), once(gsort.shape),
        ],
        out_specs=[once(shapes[0]), once(shapes[1])],
        out_shape=[
            jax.ShapeDtypeStruct(shapes[0], kind),
            jax.ShapeDtypeStruct(shapes[1], kind),
        ],
        scratch_shapes=[pltpu.VMEM((D, D), F32), pltpu.VMEM((2 * D, D), F32)],
        cost_estimate=CHEAP,
        compiler_params=vmem(),
        name="weight_back",
    )(at, *gq, *gkv, normed, wt_q, wt_kv, gm, *pieces, halo, gain, gsort)


def finish_kernel(
    skip, x_ref, ql_ref, qh_ref, kvl_ref, kvh_ref, wq_ref, wkv_ref, gm_ref, fa, fb, fd, fe,
    one_ref, two_ref, g_ref, gain_ref, out_ref, total, blocks_ref,
):
    rows = x_ref.shape[0]
    per = rows // BLOCK

    @pl.when(pl.program_id(0) == 0)
    def _():
        own, ends = fb.shape[0], fa.shape[0]
        halo = own + ends
        blocks_ref[...] = gm_ref[halo : halo + own, :] + fb[...].astype(F32) + fd[...].astype(F32)
        blocks_ref[own - ends :, :] += fa[...].astype(F32)
        blocks_ref[:ends, :] += fe[...].astype(F32)

    at = lax.broadcasted_iota(jnp.int32, (rows, rows), 0)
    lane = lax.broadcasted_iota(jnp.int32, (rows, rows), 1)
    order = (lane == lax.rem(at, BLOCK) * 8 + at // BLOCK).astype(F32).astype(BF16)
    value = mm(order, one_ref[...].reshape(rows, D))
    value = value + mm(ql_ref[...], wq_ref[: D // 2, :]) + mm(qh_ref[...], wq_ref[D // 2 :, :])
    value = value + mm(kvl_ref[...], wkv_ref[:D, :]) + mm(kvh_ref[...], wkv_ref[D:, :])
    grads = blocks_ref[pl.ds(pl.multiple_of(pl.program_id(0) * per, per), per), :].astype(BF16)
    block = mm(grads[:, :D], wq_ref[...]) + mm(widen_keys(grads[:, D:]), wkv_ref[...])
    value = value + jnp.broadcast_to(block[:, None, :], (per, BLOCK, D)).reshape(rows, D)
    total[...] = value

    @pl.when(pl.program_id(0) >= skip)
    def _():
        total[...] += mm(order, two_ref[...].reshape(rows, D))

    x = x_ref[...].astype(F32)
    centre = x - jnp.mean(x, axis=-1, keepdims=True)
    inverse = lax.rsqrt(jnp.mean(centre * centre, axis=-1, keepdims=True) + EPSILON)
    hat = centre * inverse
    du = total[...] * gain_ref[...]
    inner = jnp.mean(du * hat, axis=-1, keepdims=True)
    out_ref[...] = g_ref[...] + inverse * (
        du - jnp.mean(du, axis=-1, keepdims=True) - hat * inner
    )


def finish(x, gq, gkv, wt_q, wt_kv, gm, far, one, two, g_middle, gain):
    tok = x.shape[0]
    tile = 8 * BLOCK
    skip = (tok // BLOCK - two.shape[1]) // 8
    rows = lambda width: pl.BlockSpec((tile, width), lambda i: (i, 0))
    return pl.pallas_call(
        functools.partial(finish_kernel, skip),
        grid=(tok // tile,),
        in_specs=[
            rows(D), rows(D // 2), rows(D // 2), rows(D), rows(D), once((D, D)), once((2 * D, D)),
            once(gm.shape), *(once(f.shape) for f in far),
            pl.BlockSpec((BLOCK, 8, D), lambda i: (0, i, 0)),
            pl.BlockSpec((BLOCK, 8, D), lambda i: (0, jnp.maximum(i - skip, 0), 0)),
            rows(D), once((1, D)),
        ],
        out_specs=rows(D),
        out_shape=jax.ShapeDtypeStruct((tok, D), F32),
        scratch_shapes=[
            pltpu.VMEM((tile, D), F32),
            pltpu.VMEM((tok // BLOCK, 2 * D), F32),
        ],
        cost_estimate=CHEAP,
        compiler_params=vmem(),
        name="finish",
    )(x, *gq, *gkv, wt_q, wt_kv, gm, *far, one, two, g_middle, gain)


class Grid:
    def __init__(self):
        self.heads = lax.axis_size("head")
        self.planes = lax.axis_size("plane")
        self.cycles = 2 * self.planes
        self.head = lax.axis_index("head")
        self.plane = lax.axis_index("plane")
        self.core = lax.axis_index("core")
        self.cycle = 2 * self.plane + self.core
        self.place = self.cycle * self.heads + self.head

    def send(self, value, pairs):
        return lax.ppermute(value, ("head", "plane", "core"), pairs)

    def number(self, head, cycle):
        return head * self.cycles + cycle

    def along(self, steps):
        count = self.heads * self.cycles
        at = lambda place: self.number(place % self.heads, place // self.heads)
        return [(at(i), at(i + steps)) for i in range(count) if 0 <= i + steps < count]

    def swap_head(self, flip):
        return [
            (self.number(h, b), self.number(h ^ flip, b))
            for h in range(self.heads)
            for b in range(self.cycles)
        ]

    def swap_plane(self, flip):
        return [
            (self.number(h, b), self.number(h, b ^ (2 * flip)))
            for h in range(self.heads)
            for b in range(self.cycles)
        ]

    def swap_core(self):
        return [
            (self.number(h, b), self.number(h, b ^ 1))
            for h in range(self.heads)
            for b in range(self.cycles)
        ]


def in_order(pieces, index):
    stacked = jnp.stack(pieces)
    count = len(pieces)
    bit = 1
    while bit < count:
        swapped = jnp.stack([stacked[i ^ bit] for i in range(count)])
        stacked = jnp.where((index & bit) != 0, swapped, stacked)
        bit *= 2
    return stacked


def gather_all(grid, piece):
    got = [piece] + [grid.send(piece, grid.swap_plane(r)) for r in range(1, grid.planes)]
    got = in_order(got, grid.plane)
    got = [got] + [grid.send(got, grid.swap_head(r)) for r in range(1, grid.heads)]
    got = in_order(got, grid.head)
    got = in_order([got, grid.send(got, grid.swap_core())], grid.core)
    got = got.transpose(1, 2, 0, *range(3, got.ndim))
    return got.reshape(grid.heads, grid.cycles, *piece.shape)


def across_planes(parts):
    return lax.all_to_all(parts, "plane", 0, 0, tiled=True)


def across_heads(parts):
    return lax.all_to_all(parts, "head", 0, 0, tiled=True)


def scatter_sum(grid, parts):
    mine = lax.dynamic_index_in_dim(parts, grid.core, 0, keepdims=False)
    other = lax.dynamic_index_in_dim(parts, 1 - grid.core, 0, keepdims=False)
    got = grid.send(other, grid.swap_core())
    total = (mine.astype(F32) + got.astype(F32)).astype(BF16)
    total = jnp.sum(across_heads(total).astype(F32), axis=0).astype(BF16)
    return jnp.sum(across_planes(total).astype(F32), axis=0)


def as_rows(value):
    flat = value.reshape(-1)
    short = -flat.shape[0] % LANES
    return jnp.pad(flat, (0, short)).reshape(-1, LANES)


def by_owner(grid, value):
    columns, rows = value.shape
    cut = value.reshape(grid.planes, 2, columns // grid.cycles, grid.heads, rows // grid.heads)
    return cut.transpose(1, 3, 0, 2, 4)


def vector_by_owner(grid, value):
    cut = value.reshape(grid.heads, grid.planes, 2, -1)
    return cut.transpose(2, 0, 1, 3)


def rows_of(value):
    lead = value.shape[:3]
    flat = value.reshape(*lead, -1)
    short = -flat.shape[-1] % LANES
    flat = jnp.pad(flat, ((0, 0),) * 3 + ((0, short),))
    return flat.reshape(*lead, -1, LANES)


def after(value, *others):
    return lax.optimization_barrier((value, *others))[0]


def weights_slow(grid, vectors, parameters):
    w_qkv, w_sort, w_in, w_down, w_out = parameters
    heads, cycles = grid.heads, grid.cycles
    first = jnp.concatenate([as_rows(w_qkv.T), as_rows(w_sort), as_rows(jnp.concatenate(vectors))])
    wide, sort_rows = as_rows(w_qkv.T).shape[0], as_rows(w_sort).shape[0]
    got = gather_all(grid, first)
    span = w_qkv.shape[1]
    wt_qkv = (
        got[:, :, :wide]
        .reshape(heads, cycles, span, D // heads)
        .transpose(1, 2, 0, 3)
        .reshape(HEADS, 3, HEAD_DIM, D)
    )
    wt_q = wt_qkv[:, 0].reshape(D, D)
    paired = wt_qkv.reshape(PAIRS, 2, 3, HEAD_DIM, D)
    wt_kv = jnp.stack(
        [paired[:, 0, 1], paired[:, 0, 2], paired[:, 1, 2], paired[:, 1, 1]], axis=1
    ).reshape(2 * D, D)
    size = w_sort.shape[0] * w_sort.shape[1]
    w_pairs = (
        got[:, :, wide : wide + sort_rows]
        .reshape(heads, cycles, -1)[:, :, :size]
        .reshape(heads, cycles, *w_sort.shape)
        .transpose(1, 3, 0, 2)
        .reshape(HEAD_DIM, PAIRS, LANES)
        .transpose(1, 0, 2)
        .astype(F32)
    )
    flat = got[:, :, wide + sort_rows :].reshape(heads, cycles, -1)
    sizes = [v.shape[0] for v in vectors]
    cuts = [sum(sizes[:i]) for i in range(len(sizes) + 1)]
    rows = [
        flat[:, :, cuts[i] : cuts[i + 1]].reshape(1, -1).astype(F32) for i in range(len(sizes))
    ]
    second = jnp.concatenate([as_rows(w_in.T), as_rows(w_down.T), as_rows(w_out.T)])
    in_rows, down_rows = as_rows(w_in.T).shape[0], as_rows(w_down.T).shape[0]
    got = gather_all(grid, second)

    def whole(depth, columns, part):
        return (
            part.reshape(heads, cycles, -1)[:, :, : columns // cycles * (depth // heads)]
            .reshape(heads, cycles, columns // cycles, depth // heads)
            .transpose(1, 2, 0, 3)
            .reshape(columns, depth)
        )

    feed = (
        whole(D, FF, got[:, :, :in_rows]),
        whole(FF, D, got[:, :, in_rows : in_rows + down_rows]),
        whole(D, D, got[:, :, in_rows + down_rows :]),
    )
    return wt_q, wt_kv, w_pairs, rows, feed


def matrix(rows, shape):
    flat = rows.reshape(-1)[: shape[0] * shape[1]]
    return flat.reshape(shape[1], shape[0]).T


def gradients_two_slow(grid, acc_in, acc_down, acc_out, sums, parameters, vectors):
    w_qkv, w_sort, w_in, w_down, w_out = parameters
    low = [
        rows_of(by_owner(grid, v.astype(BF16))) for v in (acc_in.T, acc_down, acc_out)
    ]
    order = ((0, D), (1, D), (4, FF), (3, D))
    small = [vector_by_owner(grid, sums[i, :n]) for i, n in order]
    low.append(rows_of(jnp.concatenate(small, axis=-1).astype(BF16)))
    total = scatter_sum(grid, jnp.concatenate(low, axis=3))
    cuts = [0]
    for item in low:
        cuts.append(cuts[-1] + item.shape[3])
    g_in, g_down, g_out = (
        matrix(total[cuts[i] : cuts[i + 1]], w.shape) for i, w in enumerate((w_in, w_down, w_out))
    )
    flat = total[cuts[3] :].reshape(-1)
    sizes = [v.shape[0] for v in vectors[1:]]
    at = [sum(sizes[:i]) for i in range(5)]
    return g_in, g_down, g_out, *(flat[at[i] : at[i + 1]] for i in range(4))


def gradients_one_slow(grid, both, gain, gsort, parameters, vectors):
    w_qkv, w_sort = parameters[:2]
    q = both[:D].reshape(HEADS, HEAD_DIM, D)
    kv = both[D:].reshape(PAIRS, 4, HEAD_DIM, D)
    k = jnp.stack([kv[:, 0], kv[:, 3]], axis=1).reshape(HEADS, HEAD_DIM, D)
    v = jnp.stack([kv[:, 1], kv[:, 2]], axis=1).reshape(HEADS, HEAD_DIM, D)
    wide = jnp.stack([q, k, v], axis=1).reshape(3 * D, D)
    sort = gsort.transpose(0, 2, 1).reshape(grid.heads, D // grid.heads, grid.planes, 2, -1)
    low = [
        rows_of(by_owner(grid, wide.astype(BF16))),
        rows_of(sort.transpose(3, 0, 2, 1, 4).astype(BF16)),
        rows_of(vector_by_owner(grid, gain[0]).astype(BF16)),
    ]
    total = scatter_sum(grid, jnp.concatenate(low, axis=3))
    one, two = low[0].shape[3], low[0].shape[3] + low[1].shape[3]
    size = w_sort.shape[0] * w_sort.shape[1]
    return (
        matrix(total[:one], w_qkv.shape),
        total[one:two].reshape(-1)[:size].reshape(w_sort.shape),
        total[two:].reshape(-1)[: vectors[0].shape[0]],
    )


def per_device(
    tokens, cotangent, doc_lengths, norm_gain1, w_qkv, w_out, b_out, norm_gain2, w_in, b_in,
    w_down, b_down, w_sort,
):
    grid = Grid()
    heads = grid.heads
    x = tokens[0]
    upstream = cotangent[0]
    tok = x.shape[0]
    own = tok // BLOCK
    context = HALO + own
    window = HALO + own + HALO
    second = HALO - own
    fast = heads == 4 and grid.cycles == 8
    at = jnp.stack([grid.head, grid.plane, grid.core]).astype(jnp.int32)
    vectors = (norm_gain1, b_out, norm_gain2, b_in, b_down)
    parameters = (w_qkv, w_sort, w_in, w_down, w_out)

    three = range(1, 4)
    if fast:
        one, two = pack(w_qkv, w_sort, vectors, w_in, w_down, w_out)
        ones = [one] + [grid.send(one, grid.swap_head(r)) for r in three]
        x_send = after(x, *ones)
        ones = jnp.stack(ones)
        ones = [ones] + [grid.send(ones, grid.swap_plane(r)) for r in three]
    else:
        x_send = x
    halo_one = grid.send(x_send, grid.along(1))
    halo_two = grid.send(x_send[tok - second * BLOCK :], grid.along(2))
    if fast:
        two = after(two, *ones)
        ones = jnp.stack(ones)
        other = grid.send(ones, grid.swap_core())
        twos = [two] + [grid.send(two, grid.swap_plane(r)) for r in three]
        wt_q, wt_kv, w_pairs, *rows = assemble(at, ones, other)
    else:
        wt_q, wt_kv, w_pairs, rows, feed_weights = weights_slow(grid, vectors, parameters)
    gain_one, bias_out, gain_two, bias_in, bias_down = rows

    normed, q, kv, means, means_head, means_tail = project(x, gain_one, wt_q, wt_kv, second)
    means_send, means_head, means_tail = lax.optimization_barrier(
        (means, means_head, means_tail, halo_one, halo_two)
    )[:3]
    pieces = (
        grid.send(means_tail, grid.along(2)),
        grid.send(means_send, grid.along(1)),
        means,
        grid.send(means_send, grid.along(-1)),
        grid.send(means_head, grid.along(-2)),
    )
    blocked = lambda value: value.reshape(-1, BLOCK, D)
    kvx, normed_halo = context_project(
        blocked(halo_two), blocked(halo_one), blocked(x), gain_one, wt_kv
    )
    if fast:
        twos = jnp.stack(lax.optimization_barrier((*twos, *pieces))[:4])
        twos = [twos] + [grid.send(twos, grid.swap_head(r)) for r in three]

    begin = grid.place * own
    position = begin - HALO + jnp.arange(window, dtype=jnp.int32)
    doc_ends = jnp.cumsum(doc_lengths, dtype=jnp.int32)
    ended = jnp.sum(
        (doc_ends[None, :] <= position[:, None]).astype(jnp.int32), axis=1, dtype=jnp.int32
    )
    span_end = (grid.cycle + 1) * heads * own
    doc = jnp.where((position >= 0) & (position < span_end), ended, -1)
    fold = window - LANES
    docc = jnp.stack([doc[:LANES], jnp.concatenate([doc[LANES:], doc[fold:LANES]])])
    docn = doc[:, None]
    live = (doc[HALO:context] == doc[HALO - 1 : context - 1]) & (doc[HALO:context] >= 0)
    live = jnp.repeat(live.astype(F32), BLOCK).reshape(tok // LANES, LANES)

    plan = sink_forward(pieces, after(w_pairs, kvx), docn, docc, own, context)
    if fast:
        twos = jnp.stack(lax.optimization_barrier((*twos, plan))[:4], axis=1)
        feed_weights = (twos, grid.send(twos, grid.swap_core()))
    attended, skv = attend(q, kv, kvx, plan, live)

    if fast:
        output, g_middle, g_att, keep, send = feed_fast(
            at, x, attended, upstream, bias_out, gain_two, bias_in, bias_down, *feed_weights
        )
        got = grid.send(send, grid.swap_core())
    else:
        output, g_middle, g_att, *sums = feed_slow(
            x, attended, upstream, bias_out, gain_two, bias_in, bias_down, *feed_weights
        )
        g_in, g_down, g_out, g_b_out, g_gain_two, g_b_in, g_b_down = gradients_two_slow(
            grid, *sums, parameters, vectors
        )

    gq_low, gkv_low, gh_low, gplan_low = attend_back(
        q, kv, skv, g_att, kvx, plan, live, 0, PAIRS // 2
    )
    if fast:
        twos = split_sum(at, 1, after(keep, gh_low), got)
        g_att = after(g_att, *twos)
        twos = [twos[0]] + [grid.send(twos[r], grid.swap_plane(r)) for r in three]
    gq_high, gkv_high, gh_high, gplan_high = attend_back(
        q, kv, skv, g_att, kvx, plan, live, PAIRS // 2, PAIRS // 2
    )
    gq, gkv = (gq_low, gq_high), (gkv_low, gkv_high)
    gn_far, gn_near, g_kv_halo = halo_back(gh_low, gh_high, normed_halo, wt_kv, second)
    back_one = grid.send(gn_near, grid.along(-1))
    back_two = grid.send(gn_far, grid.along(-2))
    gplan = after(jnp.concatenate([gplan_low, gplan_high]), gn_near)
    gmeans, gsort, *sends = sink_backward(pieces, w_pairs, docn, docc, gplan, own, context)
    gmeans_here = after(gmeans, *twos) if fast else gmeans
    keep, send = weight_back(
        at, gq, gkv, normed, wt_q, wt_kv, gmeans_here, pieces, g_kv_halo, gain_one, gsort, fast
    )
    if fast:
        got = grid.send(send, grid.swap_core())
        ones = split_sum(at, 0, keep, got)
        ones = [ones[0]] + [grid.send(ones[r], grid.swap_head(r)) for r in three]
        sends = lax.optimization_barrier((*sends, ones[0]))[:4]
        twos = merge_sum(at, 0, lax.optimization_barrier((*twos, ones[0]))[:4])
        twos = [twos[0]] + [grid.send(twos[r], grid.swap_head(r)) for r in three]
    steps = (-2, -1, 1, 2)
    far = [grid.send(value, grid.along(step)) for value, step in zip(sends, steps)]
    if fast:
        ones = merge_sum(at, 1, ones)
        ones = [ones[0]] + [grid.send(ones[r], grid.swap_plane(r)) for r in three]
    input_grad = finish(
        x, gq, gkv, wt_q, wt_kv, gmeans, far, back_one, back_two, g_middle, gain_one
    )
    if fast:
        g_wqkv, g_sort, g_gain_one = last_one(ones)
        g_in, g_down, g_out, *small = last_two(twos)
        g_wqkv, g_sort, g_down, g_out = g_wqkv.T, g_sort.T, g_down.T, g_out.T
        g_gain_one = g_gain_one[0]
        g_b_out, g_gain_two, g_b_in, g_b_down = (value[0] for value in small)
    else:
        g_wqkv, g_sort, g_gain_one = gradients_one_slow(
            grid, keep, send, gsort, parameters, vectors
        )
    return (
        output[None], input_grad[None], g_gain_one, g_wqkv, g_out, g_b_out, g_gain_two, g_in,
        g_b_in, g_down, g_b_down, g_sort,
    )


def solution(mesh):
    heads, cycles = mesh.shape["head"], mesh.shape["blk"]
    fine = Mesh(mesh.devices.reshape(heads, cycles // 2, 2), ("head", "plane", "core"))
    both = P(("head", "plane", "core"))
    split = P("head", ("plane", "core"))
    stream = P(("plane", "core"), "head", None)
    return jax.shard_map(
        per_device,
        mesh=fine,
        in_specs=(
            stream, stream, P(), both, split, split, both, both, split, both, split, both, split,
        ),
        out_specs=(
            stream, stream, both, split, split, both, both, split, both, split, both, split,
        ),
        check_vma=False,
    )
```

```python
import functools

import jax
import jax.numpy as jnp
from jax import lax
from jax.experimental import pallas as pl
from jax.experimental.pallas import tpu as pltpu
from jax.sharding import Mesh
from jax.sharding import PartitionSpec as P

D = 512
HEADS = 8
HEAD_DIM = 64
FF = 2048
BLOCK = 32
SINK_ITERS = 8
DOC_MOST = 62
LANES = 128
PAIRS = HEADS // 2
HALO = 64
GROUPS = 4
CHEAP = pl.CostEstimate(flops=0, transcendentals=0, bytes_accessed=0)
EPSILON = 1e-05
NEGATIVE = -1e30
FLOOR = -1e20
LOG2E = 1.4426950408889634
TINY = 1e-37
F32 = jnp.float32
BF16 = jnp.bfloat16
NT = (((1,), (1,)), ((), ()))
NN = (((1,), (0,)), ((), ()))
TN = (((0,), (0,)), ((), ()))


def mm(a, b, dims=NN):
    return lax.dot_general(a, b, dims, preferred_element_type=F32)


def vmem(limit=56):
    return pltpu.CompilerParams(vmem_limit_bytes=limit * 1024 * 1024)


def once(shape):
    return pl.BlockSpec(shape, lambda *i: (0,) * len(shape), pipeline_mode=pl.Buffered(1))


def halves(value):
    high = value.astype(BF16)
    return high, (value - high.astype(F32)).astype(BF16)


def mm3(a, b, dims):
    (da,), (db,) = dims[0]
    ah, al = halves(a)
    bh, bl = halves(b)
    return mm(
        jnp.concatenate([ah, al, ah], axis=da), jnp.concatenate([bh, bh, bl], axis=db), dims
    )


def sink_mask(docn_ref, docc_ref, window, context):
    first = context
    fold = window - LANES
    lane = lax.broadcasted_iota(jnp.int32, (1, LANES), 1)
    docn = docn_ref[...]
    row = lax.broadcasted_iota(jnp.int32, (window, 1), 0)
    col = jnp.where((row >= first) & (lane < fold), lane + LANES, lane)
    docc = jnp.where(row >= first, docc_ref[1:2, :], docc_ref[0:1, :])
    return (docn == docc) & (docn >= 0) & (col < row)


def fold_pair(top, low, fold, join):
    lane = lax.broadcasted_iota(jnp.int32, (1, LANES), 1)
    both = join(top, low)
    return jnp.where(lane < fold, top, both), jnp.where(lane < fold, low, both)


def sink_weight(pair, odd):
    lane = lax.broadcasted_iota(jnp.int32, pair.shape, 1)
    zero = jnp.zeros_like(pair)
    if odd:
        return jnp.concatenate([zero, jnp.where(lane >= HEAD_DIM, pair, zero)], axis=0)
    return jnp.concatenate([jnp.where(lane < HEAD_DIM, pair, zero), zero], axis=0)


def refold(keys, fold):
    return jnp.concatenate([keys[LANES:], keys[fold:LANES]], axis=0)


def row_step(values):
    highest = jnp.maximum(jnp.max(values, axis=1, keepdims=True), FLOOR)
    total = jnp.sum(jnp.exp2(values - highest), axis=1, keepdims=True)
    return values - (highest + LOG2E * jnp.log(jnp.maximum(total, TINY)))


def column_step(values, context, fold):
    top, low = values[:context], values[context:]
    h1, h2 = fold_pair(
        jnp.max(top, axis=0, keepdims=True),
        jnp.max(low, axis=0, keepdims=True),
        fold,
        jnp.maximum,
    )
    h1, h2 = jnp.maximum(h1, FLOOR), jnp.maximum(h2, FLOOR)
    e1, e2 = jnp.exp2(top - h1), jnp.exp2(low - h2)
    t1, t2 = fold_pair(
        jnp.sum(e1, axis=0, keepdims=True), jnp.sum(e2, axis=0, keepdims=True), fold, jnp.add
    )
    t1, t2 = jnp.maximum(t1, TINY), jnp.maximum(t2, TINY)
    moved = jnp.concatenate(
        [top - (h1 + LOG2E * jnp.log(t1)), low - (h2 + LOG2E * jnp.log(t2))], axis=0
    )
    scales = jnp.concatenate([jnp.exp2(h1), jnp.exp2(h2), 1.0 / t1, 1.0 / t2], axis=0)
    return moved, e1, e2, scales


def sink_forward_kernel(
    own, context, a, b, c, d, e, w_ref, docn_ref, docc_ref, plan_ref, kept_ref, scale_ref, proj_ref,
    q_ref, k_ref, vals, kept, sems,
):
    window = q_ref.shape[1]
    fold = window - LANES
    at = 0
    for piece in (a, b, c, d, e):
        rows = piece.shape[0]
        for pair in range(PAIRS):
            q_ref[pair, at : at + rows, :] = piece[:, pair * LANES : (pair + 1) * LANES]
            k_ref[pair, at : at + rows, :] = piece[:, D + pair * LANES : D + (pair + 1) * LANES]
        at += rows

    def logits(pair, carry):
        permitted = sink_mask(docn_ref, docc_ref, window, context)
        queries, keys = q_ref[pair], k_ref[pair]
        keys_two = refold(keys, fold)
        for odd in range(2):
            projected = mm3(queries, sink_weight(w_ref[pair], odd), NT)
            proj_ref[2 * pair + odd] = projected
            top = mm3(projected[:context], keys[:LANES], NT)
            low = mm3(projected[context:], keys_two, NT)
            vals[2 * pair + odd] = jnp.where(
                permitted, LOG2E * jnp.concatenate([top, low], axis=0), NEGATIVE
            )
        return carry

    lax.fori_loop(0, PAIRS, logits, 0)

    def send(step):
        return pltpu.make_async_copy(kept.at[step], kept_ref.at[step], sems.at[step])

    def step(turn, carry):
        for head in range(HEADS):
            moved, top, low, scales = column_step(row_step(vals[head]), context, fold)
            kept[turn, head, :context, :] = top
            kept[turn, head, context:, :] = low
            scale_ref[turn, head] = scales
            vals[head] = moved
        send(turn).start()
        return carry

    lax.fori_loop(0, SINK_ITERS, step, 0)
    for head in range(HEADS):
        plan_ref[head] = (
            kept[SINK_ITERS - 1, head, context - own : context, :]
            * scale_ref[SINK_ITERS - 1, head, 2:3, :]
        ).astype(BF16)
    lax.fori_loop(0, SINK_ITERS, lambda turn, carry: (send(turn).wait(), carry)[1], 0)


def sink_backward_kernel(
    own, context, a, b, c, d, e, w_ref, kept_ref, scale_ref, proj, gl_ref, gh_ref,
    gm_ref, gw_ref, sa, sb, sd, se, q_ref, k_ref, vals, gq, gk, kept, sems,
):
    window = q_ref.shape[1]
    fold = window - LANES

    def fetch(step):
        return pltpu.make_async_copy(kept_ref.at[step], kept.at[step], sems.at[step])

    def begin(turn, carry):
        fetch(SINK_ITERS - 1 - turn).start()
        return carry

    lax.fori_loop(0, SINK_ITERS, begin, 0)
    at = 0
    for piece in (a, b, c, d, e):
        rows = piece.shape[0]
        for pair in range(PAIRS):
            q_ref[pair, at : at + rows, :] = piece[:, pair * LANES : (pair + 1) * LANES]
            k_ref[pair, at : at + rows, :] = piece[:, D + pair * LANES : D + (pair + 1) * LANES]
        at += rows

    def back(turn, carry):
        at = SINK_ITERS - 1 - turn
        fetch(at).wait()

        @pl.when(turn == 0)
        def _():
            for head in range(HEADS):
                ref = gl_ref if head < HEADS // 2 else gh_ref
                vals[head, : context - own, :] = jnp.zeros((context - own, LANES), F32)
                vals[head, context - own : context, :] = (
                    ref[head % (HEADS // 2)]
                    * kept[SINK_ITERS - 1, head, context - own : context, :]
                    * scale_ref[SINK_ITERS - 1, head, 2:3, :]
                )
                vals[head, context:, :] = jnp.zeros((window - context, LANES), F32)

        for head in range(HEADS):
            g1, g2 = vals[head, :context, :], vals[head, context:, :]
            s1, s2 = fold_pair(
                jnp.sum(g1, axis=0, keepdims=True),
                jnp.sum(g2, axis=0, keepdims=True),
                fold,
                jnp.add,
            )
            scales = scale_ref[at, head]
            e1, e2 = kept[at, head, :context, :], kept[at, head, context:, :]
            g1, g2 = g1 - e1 * (s1 * scales[2:3]), g2 - e2 * (s2 * scales[3:4])
            r1, r2 = jnp.sum(g1, axis=1, keepdims=True), jnp.sum(g2, axis=1, keepdims=True)
            vals[head, :context, :] = g1 - (e1 * scales[0:1]) * r1
            vals[head, context:, :] = g2 - (e2 * scales[1:2]) * r2
        return carry

    lax.fori_loop(0, SINK_ITERS, back, 0)

    def products(pair, carry):
        queries, keys = q_ref[pair], k_ref[pair]
        keys_two = refold(keys, fold)
        turned = []
        gq_total = jnp.zeros((window, LANES), F32)
        gk_total = jnp.zeros((window, LANES), F32)
        for odd in range(2):
            head = 2 * pair + odd
            g1, g2 = vals[head, :context, :], vals[head, context:, :]
            against = jnp.concatenate(
                [mm3(g1, keys[:LANES], NN), mm3(g2, keys_two, NN)], axis=0
            )
            gq_total = gq_total + mm3(against, sink_weight(w_ref[pair], odd), NN)
            u1 = mm3(g1, proj[head, :context, :], TN)
            u2 = mm3(g2, proj[head, context:, :], TN)
            gk_total = gk_total + jnp.concatenate(
                [u1[:fold], u1[fold:] + u2[fold:], u2[:fold]], axis=0
            )
            turned.append(mm3(against, queries, TN))
        half = lax.broadcasted_iota(jnp.int32, (HEAD_DIM, LANES), 1) < HEAD_DIM
        gw_ref[pair] = jnp.where(half, turned[0][:HEAD_DIM], turned[1][HEAD_DIM:])
        gq[pair] = gq_total * (1.0 / BLOCK)
        gk[pair] = gk_total * (1.0 / BLOCK)
        return carry

    lax.fori_loop(0, PAIRS, products, 0)
    for pair in range(PAIRS):
        gm_ref[:, pair * LANES : (pair + 1) * LANES] = gq[pair]
        gm_ref[:, D + pair * LANES : D + (pair + 1) * LANES] = gk[pair]
    at = 0
    for piece, ref in ((a, sa), (b, sb), (c, None), (d, sd), (e, se)):
        if ref is not None:
            ref[...] = gm_ref[at : at + piece.shape[0], :].astype(BF16)
        at += piece.shape[0]


HBM = pl.BlockSpec(memory_space=pl.ANY)
VMEM = pl.BlockSpec(memory_space=pltpu.VMEM)
SMEM = pl.BlockSpec(memory_space=pltpu.SMEM)


def sink_forward(pieces, weight, docn, docc, own, context):
    window = sum(piece.shape[0] for piece in pieces)
    kept = (SINK_ITERS, HEADS, window, LANES)
    return pl.pallas_call(
        functools.partial(sink_forward_kernel, own, context),
        in_specs=[VMEM] * 8,
        out_specs=[VMEM, HBM, VMEM, VMEM],
        out_shape=[
            jax.ShapeDtypeStruct((HEADS, own, LANES), BF16),
            jax.ShapeDtypeStruct(kept, F32),
            jax.ShapeDtypeStruct((SINK_ITERS, HEADS, 4, LANES), F32),
            jax.ShapeDtypeStruct((HEADS, window, LANES), F32),
        ],
        scratch_shapes=[
            pltpu.VMEM((PAIRS, window, LANES), F32),
            pltpu.VMEM((PAIRS, window, LANES), F32),
            pltpu.VMEM((HEADS, window, LANES), F32),
            pltpu.VMEM(kept, F32),
            pltpu.SemaphoreType.DMA((SINK_ITERS,)),
        ],
        cost_estimate=CHEAP,
        compiler_params=vmem(),
        name="sink_forward",
    )(*pieces, weight, docn, docc)


def sink_backward(pieces, weight, kept, scales, projected, low, high, own, context):
    window = sum(piece.shape[0] for piece in pieces)
    return pl.pallas_call(
        functools.partial(sink_backward_kernel, own, context),
        in_specs=[VMEM] * 6 + [HBM] + [VMEM] * 4,
        out_shape=[
            jax.ShapeDtypeStruct((window, 2 * D), F32),
            jax.ShapeDtypeStruct((PAIRS, HEAD_DIM, LANES), F32),
            *(
                jax.ShapeDtypeStruct((pieces[i].shape[0], 2 * D), BF16)
                for i in (0, 1, 3, 4)
            ),
        ],
        scratch_shapes=[
            *[pltpu.VMEM((PAIRS, window, LANES), F32)] * 2,
            pltpu.VMEM((HEADS, window, LANES), F32),
            *[pltpu.VMEM((PAIRS, window, LANES), F32)] * 2,
            pltpu.VMEM(kept.shape, F32),
            pltpu.SemaphoreType.DMA((SINK_ITERS,)),
        ],
        cost_estimate=CHEAP,
        compiler_params=vmem(),
        name="sink_backward",
    )(*pieces, weight, kept, scales, projected, low, high)


def normalise(values):
    centre = values - jnp.mean(values, axis=-1, keepdims=True)
    spread = jnp.mean(centre * centre, axis=-1, keepdims=True)
    return centre * lax.rsqrt(spread + EPSILON)


def context_kernel(halo_blocks, far_ref, near_ref, x_ref, gain_ref, w_ref, kvx_ref, nh_ref):
    x = jnp.concatenate([far_ref[...], near_ref[...], x_ref[...]], axis=0)
    blocks = x.shape[0]
    normed = normalise(x.astype(F32)) * gain_ref[...].reshape(1, 1, D)
    normed = normed.astype(BF16).reshape(blocks * 8, D)
    row = lax.broadcasted_iota(jnp.int32, (LANES, LANES), 0)
    lane = lax.broadcasted_iota(jnp.int32, (LANES, LANES), 1)
    turn = (lane == (row % 16) * 8 + row // 16).astype(F32).astype(BF16)
    turned = [
        mm(turn, normed[i * LANES : (i + 1) * LANES]).astype(BF16) for i in range(blocks // 16)
    ]
    rows = []
    for b in range(8):
        part = jnp.concatenate([part[b * 16 : (b + 1) * 16] for part in turned], axis=0)
        nh_ref[b] = part[:halo_blocks]
        rows.append(part)
    rows = jnp.concatenate(rows, axis=0)
    for head in range(0, HEADS, 2):
        out = mm(rows, w_ref[head * LANES : (head + 2) * LANES, :], NT).astype(BF16)
        for b in range(8):
            for e in range(2):
                kvx_ref[head + e, :, b * LANES : (b + 1) * LANES] = out[
                    b * blocks : (b + 1) * blocks, e * LANES : (e + 1) * LANES
                ]


def context_project(far, near, x, gain, w_kv):
    halo_blocks = far.shape[0] + near.shape[0]
    blocks = halo_blocks + x.shape[0]
    return pl.pallas_call(
        functools.partial(context_kernel, halo_blocks),
        grid=(BLOCK // 8,),
        in_specs=[
            *(pl.BlockSpec((v.shape[0], 8, D), lambda i: (0, i, 0)) for v in (far, near, x)),
            pl.BlockSpec((1, D), lambda i: (0, 0)),
            pl.BlockSpec((2 * D, D), lambda i: (0, 0)),
        ],
        out_specs=[
            pl.BlockSpec((HEADS, blocks, 8 * LANES), lambda i: (0, 0, i)),
            pl.BlockSpec((8, halo_blocks, D), lambda i: (i, 0, 0)),
        ],
        out_shape=[
            jax.ShapeDtypeStruct((HEADS, blocks, BLOCK * LANES), BF16),
            jax.ShapeDtypeStruct((BLOCK, halo_blocks, D), BF16),
        ],
        cost_estimate=CHEAP,
        compiler_params=vmem(),
        name="context_project",
    )(far, near, x, gain, w_kv)


def compact(values, lane_block):
    out = values[:BLOCK]
    for j in range(1, 4):
        out = jnp.where(lane_block == j, values[j * BLOCK : (j + 1) * BLOCK], out)
    return out


def spread(values, lane_block):
    zero = jnp.zeros_like(values)
    return jnp.concatenate([jnp.where(lane_block == j, values, zero) for j in range(4)], axis=0)


def softmax_pair(local, chosen, live):
    lane = lax.broadcasted_iota(jnp.int32, (BLOCK, LANES), 1)
    row = lax.broadcasted_iota(jnp.int32, (BLOCK, LANES), 0)
    local = jnp.where(row <= lax.rem(lane, BLOCK), local, NEGATIVE)
    chosen = jnp.where(live, chosen, NEGATIVE)
    highest = jnp.maximum(
        jnp.max(local, axis=0, keepdims=True), jnp.max(chosen, axis=0, keepdims=True)
    )
    el, es = jnp.exp(local - highest), jnp.exp(chosen - highest)
    total = jnp.sum(el, axis=0, keepdims=True) + jnp.sum(es, axis=0, keepdims=True)
    inverse = 1.0 / total
    return el * inverse, es * inverse


def half_mask(first):
    lane = lax.broadcasted_iota(jnp.int32, (LANES, LANES), 1)
    return (lane < HEAD_DIM) if first else (lane >= HEAD_DIM)


def attend_kernel(q_ref, kv_ref, kvx_ref, plan_ref, live_ref, att_ref, skv_ref, even_ref, odd_ref):
    own = plan_ref.shape[1]
    blocks = kvx_ref.shape[1]
    held = (even_ref, odd_ref)
    for e in range(2):
        plan = plan_ref[e][:, :blocks]
        for chunk in range(4):
            out = mm(plan, kvx_ref[e, :, chunk * 8 * LANES : (chunk + 1) * 8 * LANES])
            for b in range(8):
                at = (chunk * 8 + b) * (own + 1)
                held[e][at : at + own, :] = out[:, b * LANES : (b + 1) * LANES]
    lane_block = lax.broadcasted_iota(jnp.int32, (BLOCK, LANES), 1) // BLOCK
    lane_half = [half_mask(True), half_mask(False)]

    def group(turn, carry):
        chains = [(turn * GROUPS + i, e) for i in range(GROUPS) for e in range(2)]
        starts = [pl.multiple_of(g * LANES, LANES) for g, _ in chains]
        both, scores = [], []
        for (g, e), start in zip(chains, starts):
            local = kv_ref[pl.ds(start, LANES), e * LANES : (e + 1) * LANES]
            chosen = jnp.concatenate(
                [held[e][pl.ds(4 * g + i, BLOCK, stride=own + 1), :] for i in range(4)], axis=0
            ).astype(BF16)
            skv_ref[pl.ds(start, LANES), e * LANES : (e + 1) * LANES] = chosen
            both.append(jnp.concatenate([local, chosen], axis=0))
        for (g, e), start, kv in zip(chains, starts, both):
            q = q_ref[pl.ds(start, LANES), :] * 0.125
            qm = jnp.where(lane_half[e], q, jnp.zeros_like(q))
            out = mm(kv, qm, NT)
            scores.append((compact(out[:LANES], lane_block), compact(out[LANES:], lane_block)))
        weights = []
        for (g, e), (local, chosen) in zip(chains, scores):
            weights.append(softmax_pair(local, chosen, live_ref[pl.ds(g, 1), :] > 0.0))
        outs = []
        for (g, e), kv, (wl, ws) in zip(chains, both, weights):
            wide = jnp.concatenate(
                [spread(wl.astype(BF16), lane_block), spread(ws.astype(BF16), lane_block)], axis=0
            )
            turned = kv.T
            outs.append(mm(turned[HEAD_DIM:] if e == 0 else turned[:HEAD_DIM], wide))
        for i in range(GROUPS):
            att_ref[pl.ds(starts[2 * i], LANES), :] = jnp.concatenate(
                outs[2 * i : 2 * i + 2], axis=0
            ).T.astype(BF16)
        return carry

    lax.fori_loop(0, own // 4 // GROUPS, group, 0)


def attend(q, kv, kvx, plan, live):
    tok, own, blocks = q.shape[0], plan.shape[1], kvx.shape[1]
    return pl.pallas_call(
        attend_kernel,
        grid=(PAIRS,),
        in_specs=[
            pl.BlockSpec((tok, LANES), lambda j: (0, j)),
            pl.BlockSpec((tok, 2 * LANES), lambda j: (0, j)),
            pl.BlockSpec((2, blocks, BLOCK * LANES), lambda j: (j, 0, 0)),
            pl.BlockSpec((2, own, LANES), lambda j: (j, 0, 0)),
            pl.BlockSpec((tok // LANES, LANES), lambda j: (0, 0)),
        ],
        out_specs=[
            pl.BlockSpec((tok, LANES), lambda j: (0, j)),
            pl.BlockSpec((tok, 2 * LANES), lambda j: (0, j)),
        ],
        out_shape=[
            jax.ShapeDtypeStruct((tok, D), BF16),
            jax.ShapeDtypeStruct((tok, 2 * D), BF16),
        ],
        scratch_shapes=[pltpu.VMEM((BLOCK * (own + 1), LANES), F32)] * 2,
        cost_estimate=CHEAP,
        compiler_params=vmem(),
        name="attend",
    )(q, kv, kvx, plan, live)


def attend_back_kernel(
    q_ref, kv_ref, skv_ref, go_ref, kvx_ref, plan_ref, live_ref,
    gq_ref, gkv_ref, gh_ref, gp_ref, even_ref, odd_ref, leven_ref, lodd_ref,
):
    own = plan_ref.shape[1]
    blocks = kvx_ref.shape[1]
    halo = blocks - own
    held = (even_ref, odd_ref)
    lheld = (leven_ref, lodd_ref)
    lane_block = lax.broadcasted_iota(jnp.int32, (BLOCK, LANES), 1) // BLOCK
    lane_half = [half_mask(True), half_mask(False)]

    def group(turn, carry):
        chains = [(turn * GROUPS + i, e) for i in range(GROUPS) for e in range(2)]
        starts = [pl.multiple_of(g * LANES, LANES) for g, _ in chains]
        both, right, scores = [], [], []
        for (g, e), start in zip(chains, starts):
            lanes = slice(e * LANES, (e + 1) * LANES)
            rows = pl.ds(start, LANES)
            both.append(jnp.concatenate([kv_ref[rows, lanes], skv_ref[rows, lanes]], axis=0))
            q = q_ref[rows, :] * 0.125
            go = go_ref[rows, :]
            go = jnp.concatenate([go[:, HEAD_DIM:], go[:, :HEAD_DIM]], axis=1)
            qm = jnp.where(lane_half[e], q, jnp.zeros_like(q))
            gm = jnp.where(lane_half[1 - e], go, jnp.zeros_like(go))
            right.append(jnp.concatenate([qm, gm], axis=0))
        for kv, other in zip(both, right):
            out = mm(kv, other, NT)
            scores.append(
                [
                    compact(out[rows, lanes], lane_block)
                    for lanes in (slice(0, LANES), slice(LANES, 2 * LANES))
                    for rows in (slice(0, LANES), slice(LANES, 2 * LANES))
                ]
            )
        wides = []
        for (g, e), (sl, ss, dl, ds) in zip(chains, scores):
            wl, ws = softmax_pair(sl, ss, live_ref[pl.ds(g, 1), :] > 0.0)
            inner = jnp.sum(wl * dl + ws * ds, axis=0, keepdims=True)
            low = [v.astype(BF16) for v in (wl, ws, wl * (dl - inner), ws * (ds - inner))]
            wides.append(low)
        outs = []
        for (g, e), start, kv, other, (wl, ws, gl, gs) in zip(chains, starts, both, right, wides):
            weights = jnp.concatenate([spread(wl, lane_block), spread(ws, lane_block)], axis=0)
            gscore = jnp.concatenate([spread(gl, lane_block), spread(gs, lane_block)], axis=0)
            gboth = mm(jnp.concatenate([gscore, weights], axis=1), other)
            lheld[e][pl.ds(start, LANES), :] = gboth[:LANES]
            for i in range(4):
                held[e][pl.ds(4 * g + i, BLOCK, stride=own + 1), :] = gboth[
                    LANES + i * BLOCK : LANES + (i + 1) * BLOCK
                ]
            turned = kv.T
            outs.append(mm(turned[:HEAD_DIM] if e == 0 else turned[HEAD_DIM:], gscore))
        for i in range(GROUPS):
            gq_ref[pl.ds(starts[2 * i], LANES), :] = (
                jnp.concatenate(outs[2 * i : 2 * i + 2], axis=0).T * 0.125
            ).astype(BF16)
        return carry

    lax.fori_loop(0, own // 4 // GROUPS, group, 0)
    for e in range(2):
        plan = plan_ref[e][:, :blocks]
        gplan = jnp.zeros((own, blocks), F32)
        for chunk in range(4):
            lanes = slice(chunk * 8 * LANES, (chunk + 1) * 8 * LANES)
            grads = jnp.concatenate(
                [
                    held[e][(chunk * 8 + b) * (own + 1) : (chunk * 8 + b) * (own + 1) + own, :]
                    for b in range(8)
                ],
                axis=1,
            ).astype(BF16)
            gplan = gplan + mm(grads, kvx_ref[e, :, lanes], NT)
            gcontext = mm(plan, grads, TN)
            gh_ref[e, :, lanes] = gcontext[:halo].astype(BF16)
            for b in range(8):
                at = (chunk * 8 + b) * (own + 1)
                held[e][at : at + own, :] = gcontext[halo:, b * LANES : (b + 1) * LANES]
        gp_ref[e] = jnp.concatenate([gplan, jnp.zeros((own, LANES - blocks), F32)], axis=1)

    def finish(g, carry):
        start = pl.multiple_of(g * LANES, LANES)
        for e in range(2):
            rest = jnp.concatenate(
                [held[e][pl.ds(4 * g + i, BLOCK, stride=own + 1), :] for i in range(4)], axis=0
            )
            gkv_ref[pl.ds(start, LANES), e * LANES : (e + 1) * LANES] = (
                rest + lheld[e][pl.ds(start, LANES), :]
            ).astype(BF16)
        return carry

    lax.fori_loop(0, own // 4, finish, 0)


def attend_back(q, kv, skv, go, kvx, plan, live, first, pairs):
    tok, own, blocks = q.shape[0], plan.shape[1], kvx.shape[1]
    halo = blocks - own
    return pl.pallas_call(
        attend_back_kernel,
        grid=(pairs,),
        in_specs=[
            pl.BlockSpec((tok, LANES), lambda j: (0, j + first)),
            pl.BlockSpec((tok, 2 * LANES), lambda j: (0, j + first)),
            pl.BlockSpec((tok, 2 * LANES), lambda j: (0, j + first)),
            pl.BlockSpec((tok, LANES), lambda j: (0, j + first)),
            pl.BlockSpec((2, blocks, BLOCK * LANES), lambda j: (j + first, 0, 0)),
            pl.BlockSpec((2, own, LANES), lambda j: (j + first, 0, 0)),
            pl.BlockSpec((tok // LANES, LANES), lambda j: (0, 0)),
        ],
        out_specs=[
            pl.BlockSpec((tok, LANES), lambda j: (0, j)),
            pl.BlockSpec((tok, 2 * LANES), lambda j: (0, j)),
            pl.BlockSpec((2, halo, BLOCK * LANES), lambda j: (j, 0, 0)),
            pl.BlockSpec((2, own, LANES), lambda j: (j, 0, 0)),
        ],
        out_shape=[
            jax.ShapeDtypeStruct((tok, pairs * LANES), BF16),
            jax.ShapeDtypeStruct((tok, 2 * pairs * LANES), BF16),
            jax.ShapeDtypeStruct((2 * pairs, halo, BLOCK * LANES), BF16),
            jax.ShapeDtypeStruct((2 * pairs, own, LANES), F32),
        ],
        scratch_shapes=[pltpu.VMEM((BLOCK * (own + 1), LANES), F32)] * 4,
        cost_estimate=CHEAP,
        compiler_params=vmem(),
        name="attend_back",
    )(q, kv, skv, go, kvx, plan, live)


def halo_kernel(low_ref, high_ref, nh_ref, w_ref, far_ref, near_ref, gw_ref):
    halo = low_ref.shape[1]
    far = far_ref.shape[1]

    @pl.when(pl.program_id(0) == 0)
    def _():
        gw_ref[...] = jnp.zeros_like(gw_ref)

    rows = jnp.concatenate(
        [
            jnp.concatenate(
                [
                    ref[head, :, b * LANES : (b + 1) * LANES]
                    for ref in (low_ref, high_ref)
                    for head in range(ref.shape[0])
                ],
                axis=1,
            )
            for b in range(8)
        ],
        axis=0,
    )
    out = mm(rows, w_ref[...]).astype(BF16).reshape(8, halo, D)
    far_ref[...] = out[:, :far]
    near_ref[...] = out[:, far:]
    gw_ref[...] += mm(rows, nh_ref[...].reshape(8 * halo, D), TN)


def halo_back(low, high, nh, w_kv, far):
    halo = low.shape[1]
    half = pl.BlockSpec((HEADS // 2, halo, 8 * LANES), lambda i: (0, 0, i))
    return pl.pallas_call(
        halo_kernel,
        grid=(BLOCK // 8,),
        in_specs=[
            half,
            half,
            pl.BlockSpec((8, halo, D), lambda i: (i, 0, 0)),
            pl.BlockSpec((2 * D, D), lambda i: (0, 0)),
        ],
        out_specs=[
            pl.BlockSpec((8, far, D), lambda i: (i, 0, 0)),
            pl.BlockSpec((8, halo - far, D), lambda i: (i, 0, 0)),
            pl.BlockSpec((2 * D, D), lambda i: (0, 0)),
        ],
        out_shape=[
            jax.ShapeDtypeStruct((BLOCK, far, D), BF16),
            jax.ShapeDtypeStruct((BLOCK, halo - far, D), BF16),
            jax.ShapeDtypeStruct((2 * D, D), F32),
        ],
        cost_estimate=CHEAP,
        compiler_params=vmem(),
        name="halo_back",
    )(low, high, nh, w_kv)


def project_kernel(x_ref, gain_ref, wq_ref, wkv_ref, n_ref, q_ref, kv_ref, m_ref, head_ref, tail_ref):
    rows = x_ref.shape[0]
    blocks = rows // BLOCK
    normed = (normalise(x_ref[...].astype(F32)) * gain_ref[...]).astype(BF16)
    n_ref[...] = normed
    q = mm(normed, wq_ref[...], NT).astype(BF16)
    q_ref[...] = q
    kv = mm(normed, wkv_ref[...], NT).astype(BF16)
    kv_ref[...] = kv
    half = lax.broadcasted_iota(jnp.int32, (1, LANES), 1) < HEAD_DIM
    m_ref[:, :D] = jnp.mean(q.astype(F32).reshape(blocks, BLOCK, D), axis=1)
    for pair in range(PAIRS):
        even = kv[:, 2 * pair * LANES : (2 * pair + 1) * LANES]
        odd = kv[:, (2 * pair + 1) * LANES : (2 * pair + 2) * LANES]
        keys = jnp.where(half, even.astype(F32), odd.astype(F32))
        m_ref[:, D + pair * LANES : D + (pair + 1) * LANES] = jnp.mean(
            keys.reshape(blocks, BLOCK, LANES), axis=1
        )
    m_ref[:, 2 * D :] = jnp.mean(normed.astype(F32).reshape(blocks, BLOCK, D), axis=1)
    at = pl.program_id(0)
    ends = head_ref.shape[0] // blocks
    for ref, first in ((head_ref, 0), (tail_ref, pl.num_programs(0) - ends)):

        @pl.when((at >= first) & (at < first + ends))
        def _():
            ref[pl.ds(pl.multiple_of((at - first) * blocks, 8), blocks), :] = m_ref[...]


def project(x, gain, wt_q, wt_kv, ends):
    tok = x.shape[0]
    tile = 8 * BLOCK
    return pl.pallas_call(
        project_kernel,
        grid=(tok // tile,),
        in_specs=[
            pl.BlockSpec((tile, D), lambda i: (i, 0)),
            pl.BlockSpec((1, D), lambda i: (0, 0)),
            pl.BlockSpec((D, D), lambda i: (0, 0)),
            pl.BlockSpec((2 * D, D), lambda i: (0, 0)),
        ],
        out_specs=[
            pl.BlockSpec((tile, D), lambda i: (i, 0)),
            pl.BlockSpec((tile, D), lambda i: (i, 0)),
            pl.BlockSpec((tile, 2 * D), lambda i: (i, 0)),
            pl.BlockSpec((8, 3 * D), lambda i: (i, 0)),
            once((ends, 3 * D)),
            once((ends, 3 * D)),
        ],
        out_shape=[
            jax.ShapeDtypeStruct((tok, D), BF16),
            jax.ShapeDtypeStruct((tok, D), BF16),
            jax.ShapeDtypeStruct((tok, 2 * D), BF16),
            jax.ShapeDtypeStruct((tok // BLOCK, 3 * D), F32),
            jax.ShapeDtypeStruct((ends, 3 * D), F32),
            jax.ShapeDtypeStruct((ends, 3 * D), F32),
        ],
        cost_estimate=CHEAP,
        compiler_params=vmem(),
        name="project",
    )(x, gain, wt_q, wt_kv)


PIECE_ONE = 208
PIECE_TWO = 576
PARTS_TWO = 592


def place(vector, start):
    size = vector.shape[1]
    row = lax.broadcasted_iota(jnp.int32, (size, LANES), 0)
    lane = lax.broadcasted_iota(jnp.int32, (size, LANES), 1)
    pick = (lane == row + start).astype(F32).astype(BF16)
    return mm(jnp.broadcast_to(vector.astype(F32), (16, size)).astype(BF16), pick)


def pack_kernel(wqkv_ref, wsort_ref, g1, bo, g2, bi, bd, win_ref, wdown_ref, wout_ref, one_ref, two_ref):
    one_ref[:192, :] = wqkv_ref[...]
    row = place(g1[...], 0) + place(bo[...], 16) + place(g2[...], 32)
    row = row + place(bi[...], 48) + place(bd[...], 112)
    one_ref[192:, :] = jnp.concatenate([wsort_ref[...].astype(F32), row[:8]], axis=0).astype(BF16)
    two_ref[:256, :] = win_ref[...].astype(F32).T.astype(BF16)
    for k in range(4):
        two_ref[256 + k * 64 : 256 + (k + 1) * 64, :] = wdown_ref[:, k * LANES : (k + 1) * LANES]
    two_ref[512:, :] = wout_ref[...]


def pack(w_qkv, w_sort, vectors, w_in, w_down, w_out):
    return pl.pallas_call(
        pack_kernel,
        out_shape=[
            jax.ShapeDtypeStruct((PIECE_ONE, LANES), BF16),
            jax.ShapeDtypeStruct((PIECE_TWO, LANES), BF16),
        ],
        cost_estimate=CHEAP,
        compiler_params=vmem(),
        name="pack",
    )(w_qkv.T, w_sort.T, *(v.reshape(1, -1) for v in vectors), w_in, w_down.T, w_out.T)


def rows_at(start, size):
    return pl.ds(pl.multiple_of(start * size, size), size)


def each_owner(at_ref, visit):
    def planes(z, carry):
        for other in range(2):
            c = at_ref[2] ^ other
            for h in range(4):
                visit(other == 0, h, z, 2 * z + c, c)
        return carry

    lax.fori_loop(0, 4, planes, 0)


def each_piece(at_ref, mine_ref, other_ref, visit):
    def owner(own, h, z, b, c):
        source = mine_ref if own else other_ref
        visit(h, b, c, source.at[at_ref[1] ^ z, at_ref[0] ^ h])

    each_owner(at_ref, owner)


def widen(vecs, start, size):
    total = 32 * size
    lane = lax.broadcasted_iota(jnp.int32, (LANES, total), 1)
    row = lax.broadcasted_iota(jnp.int32, (LANES, total), 0)
    pick = (row == start + lax.rem(lane, size)).astype(F32).astype(BF16)
    every = mm(vecs, pick)
    owner = lax.broadcasted_iota(jnp.int32, (32, total), 0)
    lane = lax.broadcasted_iota(jnp.int32, (32, total), 1)
    return jnp.sum(jnp.where(owner == lane // size, every, 0.0), axis=0, keepdims=True)


def assemble_kernel(
    at_ref, mine_ref, other_ref, wq_ref, wkv_ref, ws_ref, g1_ref, bo_ref, g2_ref, bi_ref, bd_ref,
    vecs_ref,
):
    def visit(h, b, c, piece):
        lanes = slice(h * LANES, (h + 1) * LANES)
        wq_ref[rows_at(b, 64), lanes] = piece[:64, :]
        wkv_ref[rows_at(2 * b + c, 64), lanes] = piece[64:128, :]
        wkv_ref[rows_at(2 * b + 1 - c, 64), lanes] = piece[128:192, :]
        tail = piece[192:208, :].astype(F32)
        ws_ref[h, rows_at(b, 8), :] = tail[:8]
        vecs_ref[pl.ds(h * 8 + b, 1), :] = tail[8:9]

    each_piece(at_ref, mine_ref, other_ref, visit)
    vecs = vecs_ref[...].astype(BF16)
    g1_ref[...] = widen(vecs, 0, 16)
    bo_ref[...] = widen(vecs, 16, 16)
    g2_ref[...] = widen(vecs, 32, 16)
    bi_ref[...] = widen(vecs, 48, 64)
    bd_ref[...] = widen(vecs, 112, 16)


def assemble(at, mine, other):
    row = jax.ShapeDtypeStruct((1, D), F32)
    return pl.pallas_call(
        assemble_kernel,
        in_specs=[SMEM, VMEM, VMEM],
        out_shape=[
            jax.ShapeDtypeStruct((D, D), BF16),
            jax.ShapeDtypeStruct((2 * D, D), BF16),
            jax.ShapeDtypeStruct((PAIRS, HEAD_DIM, LANES), F32),
            row, row, row, jax.ShapeDtypeStruct((1, FF), F32), row,
        ],
        scratch_shapes=[pltpu.VMEM((32, LANES), F32)],
        cost_estimate=CHEAP,
        compiler_params=vmem(),
        name="assemble",
    )(at, mine, other)


GELU_A = 0.7978845608028654
GELU_B = 0.044715


def feed_tile(x, att, g, bo, g2, bi, bd, win, wdown, wout, acc_in, acc_down, acc_out, sums):
    middle = x.astype(F32) + mm(att, wout[...], NT) + bo
    centre = middle - jnp.mean(middle, axis=-1, keepdims=True)
    spread_ = jnp.mean(centre * centre, axis=-1, keepdims=True)
    inverse = lax.rsqrt(spread_ + EPSILON)
    hat = centre * inverse
    normed = (hat * g2).astype(BF16)
    normed_t = normed.T
    g_t = g.T
    out = jnp.zeros(middle.shape, F32)
    u = jnp.zeros(middle.shape, F32)
    cut = 512
    for k in range(FF // cut):
        cols = slice(k * cut, (k + 1) * cut)
        pre = mm(normed, win[cols, :], NT) + bi[:, cols]
        square = pre * pre
        t = jnp.tanh(GELU_A * pre * (1.0 + GELU_B * square))
        half = 0.5 * (1.0 + t)
        hidden = (pre * half).astype(BF16)
        slope = half + (0.5 * GELU_A) * pre * (1.0 - t * t) * (1.0 + (3.0 * GELU_B) * square)
        g_pre = (mm(g, wdown[:, cols], NN) * slope).astype(BF16)
        out = out + mm(hidden, wdown[:, cols], NT)
        u = u + mm(g_pre, win[cols, :], NN)
        part = mm(normed_t, g_pre)
        for i in range(2):
            acc_in[2 * k + i] += part[:, i * 256 : (i + 1) * 256]
        acc_down[:, cols] += mm(g_t, hidden)
        sums[4:5, cols] += jnp.sum(g_pre.astype(F32), axis=0, keepdims=True)
    gf = g.astype(F32)
    sums[1:2, :D] += jnp.sum(u * hat, axis=0, keepdims=True)
    sums[3:4, :D] += jnp.sum(gf, axis=0, keepdims=True)
    du = u * g2
    inner = jnp.mean(du * hat, axis=-1, keepdims=True)
    g_middle = gf + inverse * (du - jnp.mean(du, axis=-1, keepdims=True) - hat * inner)
    branch = g_middle.astype(BF16)
    sums[0:1, :D] += jnp.sum(branch.astype(F32), axis=0, keepdims=True)
    acc_out[...] += mm(branch.T, att)
    return (middle + out + bd).astype(BF16), g_middle, mm(branch, wout[...], NN).astype(BF16)


def clear(*refs):
    for ref in refs:
        ref[...] = jnp.zeros_like(ref)


def narrow(sums):
    total = jnp.zeros((32, LANES), F32)
    for index, start, size in ((0, 16, 16), (1, 32, 16), (4, 48, 64), (3, 112, 16)):
        width = 32 * size
        owner = lax.broadcasted_iota(jnp.int32, (32, width), 0)
        lane = lax.broadcasted_iota(jnp.int32, (32, width), 1)
        kept = jnp.where(owner == lane // size, sums[index : index + 1, :width], 0.0)
        row = lax.broadcasted_iota(jnp.int32, (width, LANES), 0)
        lane = lax.broadcasted_iota(jnp.int32, (width, LANES), 1)
        pick = (lane == start + lax.rem(row, size)).astype(F32).astype(BF16)
        total = total + mm(kept.astype(BF16), pick)
    return total


def feed_fast_kernel(
    at_ref, x_ref, att_ref, g_ref, bo_ref, g2_ref, bi_ref, bd_ref, mine_ref, other_ref,
    out_ref, gm_ref, ga_ref, keep_ref, send_ref,
    win, wdown, wout, acc_in, acc_down, acc_out, sums, vecs,
):
    @pl.when(pl.program_id(0) == 0)
    def _():
        def visit(h, b, c, piece):
            win[rows_at(b, 256), h * LANES : (h + 1) * LANES] = piece[:256, :]
            for k in range(4):
                lanes = slice(h * 512 + k * LANES, h * 512 + (k + 1) * LANES)
                wdown[rows_at(b, 64), lanes] = piece[256 + k * 64 : 320 + k * 64, :]
            wout[rows_at(b, 64), h * LANES : (h + 1) * LANES] = piece[512:576, :]

        each_piece(at_ref, mine_ref, other_ref, visit)
        clear(acc_in, acc_down, acc_out, sums)

    out_ref[...], gm_ref[...], ga_ref[...] = feed_tile(
        x_ref[...], att_ref[...], g_ref[...], bo_ref[...], g2_ref[...], bi_ref[...], bd_ref[...],
        win, wdown, wout, acc_in, acc_down, acc_out, sums,
    )

    @pl.when(pl.program_id(0) == pl.num_programs(0) - 1)
    def _():
        vecs[...] = narrow(sums)

        def owner(own, h, z, b, c):
            ref = keep_ref if own else send_ref
            for k in range(2):
                ref[z, h, k * LANES : (k + 1) * LANES, :] = acc_in[
                    b, h * LANES : (h + 1) * LANES, k * LANES : (k + 1) * LANES
                ].astype(BF16)
            for k in range(4):
                ref[z, h, 256 + k * 64 : 320 + k * 64, :] = acc_down[
                    rows_at(b, 64), h * 512 + k * LANES : h * 512 + (k + 1) * LANES
                ].astype(BF16)
            ref[z, h, 512:576, :] = acc_out[
                rows_at(b, 64), h * LANES : (h + 1) * LANES
            ].astype(BF16)
            ref[z, h, 576:592, :] = jnp.broadcast_to(
                vecs[pl.ds(h * 8 + b, 1), :], (16, LANES)
            ).astype(BF16)

        each_owner(at_ref, owner)


def feed_fast(at, x, att, g, bo, g2, bi, bd, mine, other):
    tok = x.shape[0]
    tile = 512
    tiled = pl.BlockSpec((tile, D), lambda i: (i, 0))
    parts = (4, 4, PARTS_TWO, LANES)
    return pl.pallas_call(
        feed_fast_kernel,
        grid=(tok // tile,),
        in_specs=[
            SMEM, tiled, tiled, tiled, once((1, D)), once((1, D)), once((1, FF)), once((1, D)),
            once(mine.shape), once(other.shape),
        ],
        out_specs=[tiled, tiled, tiled, once(parts), once(parts)],
        out_shape=[
            jax.ShapeDtypeStruct((tok, D), BF16),
            jax.ShapeDtypeStruct((tok, D), F32),
            jax.ShapeDtypeStruct((tok, D), BF16),
            jax.ShapeDtypeStruct(parts, BF16),
            jax.ShapeDtypeStruct(parts, BF16),
        ],
        scratch_shapes=[
            pltpu.VMEM((FF, D), BF16), pltpu.VMEM((D, FF), BF16), pltpu.VMEM((D, D), BF16),
            pltpu.VMEM((8, D, FF // 8), F32), pltpu.VMEM((D, FF), F32), pltpu.VMEM((D, D), F32),
            pltpu.VMEM((8, FF), F32), pltpu.VMEM((32, LANES), F32),
        ],
        cost_estimate=CHEAP,
        compiler_params=vmem(60),
        name="feed",
    )(at, x, att, g, bo, g2, bi, bd, mine, other)


def feed_slow_kernel(
    x_ref, att_ref, g_ref, bo_ref, g2_ref, bi_ref, bd_ref, win, wdown, wout,
    out_ref, gm_ref, ga_ref, acc_in, acc_down, acc_out, sums,
):
    @pl.when(pl.program_id(0) == 0)
    def _():
        clear(acc_in, acc_down, acc_out, sums)

    out_ref[...], gm_ref[...], ga_ref[...] = feed_tile(
        x_ref[...], att_ref[...], g_ref[...], bo_ref[...], g2_ref[...], bi_ref[...], bd_ref[...],
        win, wdown, wout, acc_in, acc_down, acc_out, sums,
    )


def feed_slow(x, att, g, bo, g2, bi, bd, win, wdown, wout):
    tok = x.shape[0]
    tile = 512
    tiled = pl.BlockSpec((tile, D), lambda i: (i, 0))
    wide, square, rows, cut = (D, FF), (D, D), (8, FF), (8, D, FF // 8)
    return pl.pallas_call(
        feed_slow_kernel,
        grid=(tok // tile,),
        in_specs=[
            tiled, tiled, tiled, once((1, D)), once((1, D)), once((1, FF)), once((1, D)),
            once((FF, D)), once(wide), once(square),
        ],
        out_specs=[tiled, tiled, tiled, once(cut), once(wide), once(square), once(rows)],
        out_shape=[
            jax.ShapeDtypeStruct((tok, D), BF16),
            jax.ShapeDtypeStruct((tok, D), F32),
            jax.ShapeDtypeStruct((tok, D), BF16),
            jax.ShapeDtypeStruct(cut, F32),
            jax.ShapeDtypeStruct(wide, F32),
            jax.ShapeDtypeStruct(square, F32),
            jax.ShapeDtypeStruct(rows, F32),
        ],
        cost_estimate=CHEAP,
        compiler_params=vmem(60),
        name="feed_whole",
    )(x, att, g, bo, g2, bi, bd, win, wdown, wout)


def split_kernel(which, at_ref, keep_ref, got_ref, *outs):
    for r, out in enumerate(outs):
        i = at_ref[which] ^ r
        out[0] = (keep_ref[i, 0].astype(F32) + got_ref[i, 0].astype(F32)).astype(BF16)


def split_sum(at, which, keep, got):
    one, two, rows, lanes = keep.shape
    block = pl.BlockSpec((one, 1, rows, lanes), lambda i: (0, i, 0, 0))
    return pl.pallas_call(
        functools.partial(split_kernel, which),
        grid=(two,),
        in_specs=[SMEM, block, block],
        out_specs=[pl.BlockSpec((1, rows, lanes), lambda i: (i, 0, 0))] * one,
        out_shape=[jax.ShapeDtypeStruct((two, rows, lanes), BF16)] * one,
        cost_estimate=CHEAP,
        compiler_params=vmem(),
        name="split_sum",
    )(at, keep, got)


def merge_kernel(which, at_ref, a_ref, b_ref, c_ref, d_ref, *outs):
    for r, out in enumerate(outs):
        i = at_ref[which] ^ r
        total = a_ref[i].astype(F32) + b_ref[i].astype(F32)
        out[...] = (total + c_ref[i].astype(F32) + d_ref[i].astype(F32)).astype(BF16)


def merge_sum(at, which, pieces):
    count, rows, lanes = pieces[0].shape
    return pl.pallas_call(
        functools.partial(merge_kernel, which),
        in_specs=[SMEM] + [VMEM] * 4,
        out_shape=[jax.ShapeDtypeStruct((rows, lanes), BF16)] * count,
        cost_estimate=CHEAP,
        compiler_params=vmem(),
        name="merge_sum",
    )(at, *pieces)


def last_two_kernel(a_ref, b_ref, c_ref, d_ref, gin_ref, gdown_ref, gout_ref, bo, g2, bi, bd):
    total = a_ref[...].astype(F32) + b_ref[...].astype(F32)
    total = total + c_ref[...].astype(F32) + d_ref[...].astype(F32)
    for k in range(2):
        gin_ref[:, k * LANES : (k + 1) * LANES] = total[k * LANES : (k + 1) * LANES]
    for k in range(4):
        gdown_ref[:, k * LANES : (k + 1) * LANES] = total[256 + k * 64 : 320 + k * 64]
    gout_ref[...] = total[512:576]
    row = total[576:577]
    bo[...], g2[...], bi[...], bd[...] = row[:, 16:32], row[:, 32:48], row[:, 48:112], row[:, 112:]


def last_two(pieces):
    return pl.pallas_call(
        last_two_kernel,
        out_shape=[
            jax.ShapeDtypeStruct((LANES, 256), F32),
            jax.ShapeDtypeStruct((64, 512), F32),
            jax.ShapeDtypeStruct((64, LANES), F32),
            *(jax.ShapeDtypeStruct((1, n), F32) for n in (16, 16, 64, 16)),
        ],
        cost_estimate=CHEAP,
        compiler_params=vmem(),
        name="last_two",
    )(*pieces)


def last_one_kernel(a_ref, b_ref, c_ref, d_ref, gw_ref, gs_ref, g1_ref):
    total = a_ref[...].astype(F32) + b_ref[...].astype(F32)
    total = total + c_ref[...].astype(F32) + d_ref[...].astype(F32)
    gw_ref[...] = total[:192]
    gs_ref[...] = total[192:200]
    g1_ref[...] = total[200:201, :16]


def last_one(pieces):
    return pl.pallas_call(
        last_one_kernel,
        out_shape=[
            jax.ShapeDtypeStruct((192, LANES), F32),
            jax.ShapeDtypeStruct((8, LANES), F32),
            jax.ShapeDtypeStruct((1, 16), F32),
        ],
        cost_estimate=CHEAP,
        compiler_params=vmem(),
        name="last_one",
    )(*pieces)


def widen_keys(gmk):
    half = lax.broadcasted_iota(jnp.int32, (gmk.shape[0], LANES), 1) < HEAD_DIM
    zero = jnp.zeros((gmk.shape[0], LANES), gmk.dtype)
    wide = []
    for pair in range(PAIRS):
        tile = gmk[:, pair * LANES : (pair + 1) * LANES]
        wide += [jnp.where(half, tile, zero), jnp.where(half, zero, tile)]
    return jnp.concatenate(wide, axis=1)


def weight_kernel(
    fast, at_ref, ql_ref, qh_ref, kvl_ref, kvh_ref, n_ref, wq_ref, wkv_ref, gm_ref,
    pa, pb, pc, pd, pe, halo_ref, gain_ref, gs_ref, keep_ref, send_ref, acc_q, acc_kv,
):
    @pl.when(pl.program_id(0) == 0)
    def _():
        means = jnp.concatenate([ref[:, 2 * D :] for ref in (pa, pb, pc, pd, pe)], axis=0)
        means = means.astype(BF16)
        grads = (gm_ref[...] * float(BLOCK)).astype(BF16)
        acc_q[...] = mm(grads[:, :D], means, TN)
        acc_kv[...] = halo_ref[...] + mm(widen_keys(grads[:, D:]), means, TN)

    normed = n_ref[...]
    for i, (q_ref, kv_ref) in enumerate(((ql_ref, kvl_ref), (qh_ref, kvh_ref))):
        acc_q[i * 256 : (i + 1) * 256, :] += mm(q_ref[...].T, normed)
        acc_kv[i * 512 : (i + 1) * 512, :] += mm(kv_ref[...].T, normed)

    @pl.when(pl.program_id(0) == pl.num_programs(0) - 1)
    def _():
        gain = jnp.sum(acc_q[...] * wq_ref[...].astype(F32), axis=0, keepdims=True)
        gain = gain + jnp.sum(acc_kv[...] * wkv_ref[...].astype(F32), axis=0, keepdims=True)
        gain = gain / gain_ref[...]
        if not fast:
            keep_ref[:D, :] = acc_q[...]
            keep_ref[D:, :] = acc_kv[...]
            send_ref[...] = jnp.broadcast_to(gain, (8, D))
            return
        def owner(own, h, z, b, c):
            ref = keep_ref if own else send_ref
            lanes = slice(h * LANES, (h + 1) * LANES)
            ref[h, z, :64, :] = acc_q[rows_at(b, 64), lanes].astype(BF16)
            ref[h, z, 64:128, :] = acc_kv[rows_at(2 * b + c, 64), lanes].astype(BF16)
            ref[h, z, 128:192, :] = acc_kv[rows_at(2 * b + 1 - c, 64), lanes].astype(BF16)
            share = pltpu.roll(
                jnp.broadcast_to(gain[:, lanes], (8, LANES)), lax.rem(LANES - 16 * b, LANES), 1
            )
            ref[h, z, 192:208, :] = jnp.concatenate(
                [gs_ref[h, rows_at(b, 8), :], share], axis=0
            ).astype(BF16)

        each_owner(at_ref, owner)


def weight_back(at, gq, gkv, normed, wt_q, wt_kv, gm, pieces, halo, gain, gsort, fast):
    tok = normed.shape[0]
    tile = 512
    parts = (4, 4, PIECE_ONE, LANES)
    shapes = (parts, parts) if fast else ((3 * D, D), (8, D))
    kind = BF16 if fast else F32
    rows = lambda width: pl.BlockSpec((tile, width), lambda i: (i, 0))
    return pl.pallas_call(
        functools.partial(weight_kernel, fast),
        grid=(tok // tile,),
        in_specs=[
            SMEM, rows(D // 2), rows(D // 2), rows(D), rows(D), rows(D), once((D, D)),
            once((2 * D, D)), once(gm.shape), *(once(p.shape) for p in pieces),
            once((2 * D, D)), once((1, D)), once(gsort.shape),
        ],
        out_specs=[once(shapes[0]), once(shapes[1])],
        out_shape=[
            jax.ShapeDtypeStruct(shapes[0], kind),
            jax.ShapeDtypeStruct(shapes[1], kind),
        ],
        scratch_shapes=[pltpu.VMEM((D, D), F32), pltpu.VMEM((2 * D, D), F32)],
        cost_estimate=CHEAP,
        compiler_params=vmem(),
        name="weight_back",
    )(at, *gq, *gkv, normed, wt_q, wt_kv, gm, *pieces, halo, gain, gsort)


def finish_kernel(
    skip, x_ref, ql_ref, qh_ref, kvl_ref, kvh_ref, wq_ref, wkv_ref, gm_ref, fa, fb, fd, fe,
    one_ref, two_ref, g_ref, gain_ref, out_ref, total, blocks_ref,
):
    rows = x_ref.shape[0]
    per = rows // BLOCK

    @pl.when(pl.program_id(0) == 0)
    def _():
        own, ends = fb.shape[0], fa.shape[0]
        halo = own + ends
        blocks_ref[...] = gm_ref[halo : halo + own, :] + fb[...].astype(F32) + fd[...].astype(F32)
        blocks_ref[own - ends :, :] += fa[...].astype(F32)
        blocks_ref[:ends, :] += fe[...].astype(F32)

    at = lax.broadcasted_iota(jnp.int32, (rows, rows), 0)
    lane = lax.broadcasted_iota(jnp.int32, (rows, rows), 1)
    order = (lane == lax.rem(at, BLOCK) * 8 + at // BLOCK).astype(F32).astype(BF16)
    value = mm(order, one_ref[...].reshape(rows, D))
    value = value + mm(ql_ref[...], wq_ref[: D // 2, :]) + mm(qh_ref[...], wq_ref[D // 2 :, :])
    value = value + mm(kvl_ref[...], wkv_ref[:D, :]) + mm(kvh_ref[...], wkv_ref[D:, :])
    grads = blocks_ref[pl.ds(pl.multiple_of(pl.program_id(0) * per, per), per), :].astype(BF16)
    block = mm(grads[:, :D], wq_ref[...]) + mm(widen_keys(grads[:, D:]), wkv_ref[...])
    value = value + jnp.broadcast_to(block[:, None, :], (per, BLOCK, D)).reshape(rows, D)
    total[...] = value

    @pl.when(pl.program_id(0) >= skip)
    def _():
        total[...] += mm(order, two_ref[...].reshape(rows, D))

    x = x_ref[...].astype(F32)
    centre = x - jnp.mean(x, axis=-1, keepdims=True)
    inverse = lax.rsqrt(jnp.mean(centre * centre, axis=-1, keepdims=True) + EPSILON)
    hat = centre * inverse
    du = total[...] * gain_ref[...]
    inner = jnp.mean(du * hat, axis=-1, keepdims=True)
    out_ref[...] = g_ref[...] + inverse * (
        du - jnp.mean(du, axis=-1, keepdims=True) - hat * inner
    )


def finish(x, gq, gkv, wt_q, wt_kv, gm, far, one, two, g_middle, gain):
    tok = x.shape[0]
    tile = 8 * BLOCK
    skip = (tok // BLOCK - two.shape[1]) // 8
    rows = lambda width: pl.BlockSpec((tile, width), lambda i: (i, 0))
    return pl.pallas_call(
        functools.partial(finish_kernel, skip),
        grid=(tok // tile,),
        in_specs=[
            rows(D), rows(D // 2), rows(D // 2), rows(D), rows(D), once((D, D)), once((2 * D, D)),
            once(gm.shape), *(once(f.shape) for f in far),
            pl.BlockSpec((BLOCK, 8, D), lambda i: (0, i, 0)),
            pl.BlockSpec((BLOCK, 8, D), lambda i: (0, jnp.maximum(i - skip, 0), 0)),
            rows(D), once((1, D)),
        ],
        out_specs=rows(D),
        out_shape=jax.ShapeDtypeStruct((tok, D), F32),
        scratch_shapes=[
            pltpu.VMEM((tile, D), F32),
            pltpu.VMEM((tok // BLOCK, 2 * D), F32),
        ],
        cost_estimate=CHEAP,
        compiler_params=vmem(),
        name="finish",
    )(x, *gq, *gkv, wt_q, wt_kv, gm, *far, one, two, g_middle, gain)


class Grid:
    def __init__(self):
        self.heads = lax.axis_size("head")
        self.planes = lax.axis_size("plane")
        self.cycles = 2 * self.planes
        self.head = lax.axis_index("head")
        self.plane = lax.axis_index("plane")
        self.core = lax.axis_index("core")
        self.cycle = 2 * self.plane + self.core
        self.place = self.cycle * self.heads + self.head

    def send(self, value, pairs):
        return lax.ppermute(value, ("head", "plane", "core"), pairs)

    def number(self, head, cycle):
        return head * self.cycles + cycle

    def along(self, steps):
        count = self.heads * self.cycles
        at = lambda place: self.number(place % self.heads, place // self.heads)
        return [(at(i), at(i + steps)) for i in range(count) if 0 <= i + steps < count]

    def swap_head(self, flip):
        return [
            (self.number(h, b), self.number(h ^ flip, b))
            for h in range(self.heads)
            for b in range(self.cycles)
        ]

    def swap_plane(self, flip):
        return [
            (self.number(h, b), self.number(h, b ^ (2 * flip)))
            for h in range(self.heads)
            for b in range(self.cycles)
        ]

    def swap_core(self):
        return [
            (self.number(h, b), self.number(h, b ^ 1))
            for h in range(self.heads)
            for b in range(self.cycles)
        ]


def in_order(pieces, index):
    stacked = jnp.stack(pieces)
    count = len(pieces)
    bit = 1
    while bit < count:
        swapped = jnp.stack([stacked[i ^ bit] for i in range(count)])
        stacked = jnp.where((index & bit) != 0, swapped, stacked)
        bit *= 2
    return stacked


def gather_all(grid, piece):
    got = [piece] + [grid.send(piece, grid.swap_plane(r)) for r in range(1, grid.planes)]
    got = in_order(got, grid.plane)
    got = [got] + [grid.send(got, grid.swap_head(r)) for r in range(1, grid.heads)]
    got = in_order(got, grid.head)
    got = in_order([got, grid.send(got, grid.swap_core())], grid.core)
    got = got.transpose(1, 2, 0, *range(3, got.ndim))
    return got.reshape(grid.heads, grid.cycles, *piece.shape)


def across_planes(parts):
    return lax.all_to_all(parts, "plane", 0, 0, tiled=True)


def across_heads(parts):
    return lax.all_to_all(parts, "head", 0, 0, tiled=True)


def scatter_sum(grid, parts):
    mine = lax.dynamic_index_in_dim(parts, grid.core, 0, keepdims=False)
    other = lax.dynamic_index_in_dim(parts, 1 - grid.core, 0, keepdims=False)
    got = grid.send(other, grid.swap_core())
    total = (mine.astype(F32) + got.astype(F32)).astype(BF16)
    total = jnp.sum(across_heads(total).astype(F32), axis=0).astype(BF16)
    return jnp.sum(across_planes(total).astype(F32), axis=0)


def as_rows(value):
    flat = value.reshape(-1)
    short = -flat.shape[0] % LANES
    return jnp.pad(flat, (0, short)).reshape(-1, LANES)


def by_owner(grid, value):
    columns, rows = value.shape
    cut = value.reshape(grid.planes, 2, columns // grid.cycles, grid.heads, rows // grid.heads)
    return cut.transpose(1, 3, 0, 2, 4)


def vector_by_owner(grid, value):
    cut = value.reshape(grid.heads, grid.planes, 2, -1)
    return cut.transpose(2, 0, 1, 3)


def rows_of(value):
    lead = value.shape[:3]
    flat = value.reshape(*lead, -1)
    short = -flat.shape[-1] % LANES
    flat = jnp.pad(flat, ((0, 0),) * 3 + ((0, short),))
    return flat.reshape(*lead, -1, LANES)


def after(value, *others):
    return lax.optimization_barrier((value, *others))[0]


def weights_slow(grid, vectors, parameters):
    w_qkv, w_sort, w_in, w_down, w_out = parameters
    heads, cycles = grid.heads, grid.cycles
    first = jnp.concatenate([as_rows(w_qkv.T), as_rows(w_sort), as_rows(jnp.concatenate(vectors))])
    wide, sort_rows = as_rows(w_qkv.T).shape[0], as_rows(w_sort).shape[0]
    got = gather_all(grid, first)
    span = w_qkv.shape[1]
    wt_qkv = (
        got[:, :, :wide]
        .reshape(heads, cycles, span, D // heads)
        .transpose(1, 2, 0, 3)
        .reshape(HEADS, 3, HEAD_DIM, D)
    )
    wt_q = wt_qkv[:, 0].reshape(D, D)
    paired = wt_qkv.reshape(PAIRS, 2, 3, HEAD_DIM, D)
    wt_kv = jnp.stack(
        [paired[:, 0, 1], paired[:, 0, 2], paired[:, 1, 2], paired[:, 1, 1]], axis=1
    ).reshape(2 * D, D)
    size = w_sort.shape[0] * w_sort.shape[1]
    w_pairs = (
        got[:, :, wide : wide + sort_rows]
        .reshape(heads, cycles, -1)[:, :, :size]
        .reshape(heads, cycles, *w_sort.shape)
        .transpose(1, 3, 0, 2)
        .reshape(HEAD_DIM, PAIRS, LANES)
        .transpose(1, 0, 2)
        .astype(F32)
    )
    flat = got[:, :, wide + sort_rows :].reshape(heads, cycles, -1)
    sizes = [v.shape[0] for v in vectors]
    cuts = [sum(sizes[:i]) for i in range(len(sizes) + 1)]
    rows = [
        flat[:, :, cuts[i] : cuts[i + 1]].reshape(1, -1).astype(F32) for i in range(len(sizes))
    ]
    second = jnp.concatenate([as_rows(w_in.T), as_rows(w_down.T), as_rows(w_out.T)])
    in_rows, down_rows = as_rows(w_in.T).shape[0], as_rows(w_down.T).shape[0]
    got = gather_all(grid, second)

    def whole(depth, columns, part):
        return (
            part.reshape(heads, cycles, -1)[:, :, : columns // cycles * (depth // heads)]
            .reshape(heads, cycles, columns // cycles, depth // heads)
            .transpose(1, 2, 0, 3)
            .reshape(columns, depth)
        )

    feed = (
        whole(D, FF, got[:, :, :in_rows]),
        whole(FF, D, got[:, :, in_rows : in_rows + down_rows]),
        whole(D, D, got[:, :, in_rows + down_rows :]),
    )
    return wt_q, wt_kv, w_pairs, rows, feed


def matrix(rows, shape):
    flat = rows.reshape(-1)[: shape[0] * shape[1]]
    return flat.reshape(shape[1], shape[0]).T


def gradients_two_slow(grid, acc_in, acc_down, acc_out, sums, parameters, vectors):
    w_qkv, w_sort, w_in, w_down, w_out = parameters
    low = [
        rows_of(by_owner(grid, v.astype(BF16))) for v in (acc_in.transpose(0, 2, 1).reshape(FF, D), acc_down, acc_out)
    ]
    order = ((0, D), (1, D), (4, FF), (3, D))
    small = [vector_by_owner(grid, sums[i, :n]) for i, n in order]
    low.append(rows_of(jnp.concatenate(small, axis=-1).astype(BF16)))
    total = scatter_sum(grid, jnp.concatenate(low, axis=3))
    cuts = [0]
    for item in low:
        cuts.append(cuts[-1] + item.shape[3])
    g_in, g_down, g_out = (
        matrix(total[cuts[i] : cuts[i + 1]], w.shape) for i, w in enumerate((w_in, w_down, w_out))
    )
    flat = total[cuts[3] :].reshape(-1)
    sizes = [v.shape[0] for v in vectors[1:]]
    at = [sum(sizes[:i]) for i in range(5)]
    return g_in, g_down, g_out, *(flat[at[i] : at[i + 1]] for i in range(4))


def gradients_one_slow(grid, both, gain, gsort, parameters, vectors):
    w_qkv, w_sort = parameters[:2]
    q = both[:D].reshape(HEADS, HEAD_DIM, D)
    kv = both[D:].reshape(PAIRS, 4, HEAD_DIM, D)
    k = jnp.stack([kv[:, 0], kv[:, 3]], axis=1).reshape(HEADS, HEAD_DIM, D)
    v = jnp.stack([kv[:, 1], kv[:, 2]], axis=1).reshape(HEADS, HEAD_DIM, D)
    wide = jnp.stack([q, k, v], axis=1).reshape(3 * D, D)
    sort = gsort.transpose(0, 2, 1).reshape(grid.heads, D // grid.heads, grid.planes, 2, -1)
    low = [
        rows_of(by_owner(grid, wide.astype(BF16))),
        rows_of(sort.transpose(3, 0, 2, 1, 4).astype(BF16)),
        rows_of(vector_by_owner(grid, gain[0]).astype(BF16)),
    ]
    total = scatter_sum(grid, jnp.concatenate(low, axis=3))
    one, two = low[0].shape[3], low[0].shape[3] + low[1].shape[3]
    size = w_sort.shape[0] * w_sort.shape[1]
    return (
        matrix(total[:one], w_qkv.shape),
        total[one:two].reshape(-1)[:size].reshape(w_sort.shape),
        total[two:].reshape(-1)[: vectors[0].shape[0]],
    )


def per_device(
    tokens, cotangent, doc_lengths, norm_gain1, w_qkv, w_out, b_out, norm_gain2, w_in, b_in,
    w_down, b_down, w_sort,
):
    grid = Grid()
    heads = grid.heads
    x = tokens[0]
    upstream = cotangent[0]
    tok = x.shape[0]
    own = tok // BLOCK
    context = HALO + own
    window = HALO + own + HALO
    second = HALO - own
    fast = heads == 4 and grid.cycles == 8
    at = jnp.stack([grid.head, grid.plane, grid.core]).astype(jnp.int32)
    vectors = (norm_gain1, b_out, norm_gain2, b_in, b_down)
    parameters = (w_qkv, w_sort, w_in, w_down, w_out)

    three = range(1, 4)
    if fast:
        one, two = pack(w_qkv, w_sort, vectors, w_in, w_down, w_out)
        ones = [one] + [grid.send(one, grid.swap_head(r)) for r in three]
        x_send = after(x, *ones)
        ones = jnp.stack(ones)
        ones = [ones] + [grid.send(ones, grid.swap_plane(r)) for r in three]
    else:
        x_send = x
    halo_one = grid.send(x_send, grid.along(1))
    halo_two = grid.send(x_send[tok - second * BLOCK :], grid.along(2))
    if fast:
        two = after(two, *ones)
        ones = jnp.stack(ones)
        other = grid.send(ones, grid.swap_core())
        twos = [two] + [grid.send(two, grid.swap_plane(r)) for r in three]
        wt_q, wt_kv, w_pairs, *rows = assemble(at, ones, other)
    else:
        wt_q, wt_kv, w_pairs, rows, feed_weights = weights_slow(grid, vectors, parameters)
    gain_one, bias_out, gain_two, bias_in, bias_down = rows

    normed, q, kv, means, means_head, means_tail = project(x, gain_one, wt_q, wt_kv, second)
    means_send, means_head, means_tail = lax.optimization_barrier(
        (means, means_head, means_tail, halo_one, halo_two)
    )[:3]
    pieces = (
        grid.send(means_tail, grid.along(2)),
        grid.send(means_send, grid.along(1)),
        means,
        grid.send(means_send, grid.along(-1)),
        grid.send(means_head, grid.along(-2)),
    )
    blocked = lambda value: value.reshape(-1, BLOCK, D)
    kvx, normed_halo = context_project(
        blocked(halo_two), blocked(halo_one), blocked(x), gain_one, wt_kv
    )
    if fast:
        twos = jnp.stack(lax.optimization_barrier((*twos, *pieces))[:4])
        twos = [twos] + [grid.send(twos, grid.swap_head(r)) for r in three]

    begin = grid.place * own
    position = begin - HALO + jnp.arange(window, dtype=jnp.int32)
    doc_ends = jnp.cumsum(doc_lengths, dtype=jnp.int32)
    ended = jnp.sum(
        (doc_ends[None, :] <= position[:, None]).astype(jnp.int32), axis=1, dtype=jnp.int32
    )
    span_end = (grid.cycle + 1) * heads * own
    doc = jnp.where((position >= 0) & (position < span_end), ended, -1)
    fold = window - LANES
    docc = jnp.stack([doc[:LANES], jnp.concatenate([doc[LANES:], doc[fold:LANES]])])
    docn = doc[:, None]
    live = (doc[HALO:context] == doc[HALO - 1 : context - 1]) & (doc[HALO:context] >= 0)
    live = jnp.repeat(live.astype(F32), BLOCK).reshape(tok // LANES, LANES)

    plan, *kept = sink_forward(pieces, after(w_pairs, kvx), docn, docc, own, context)
    if fast:
        twos = jnp.stack(lax.optimization_barrier((*twos, plan))[:4], axis=1)
        feed_weights = (twos, grid.send(twos, grid.swap_core()))
    attended, skv = attend(q, kv, kvx, plan, live)

    if fast:
        output, g_middle, g_att, keep, send = feed_fast(
            at, x, attended, upstream, bias_out, gain_two, bias_in, bias_down, *feed_weights
        )
        got = grid.send(send, grid.swap_core())
    else:
        output, g_middle, g_att, *sums = feed_slow(
            x, attended, upstream, bias_out, gain_two, bias_in, bias_down, *feed_weights
        )
        g_in, g_down, g_out, g_b_out, g_gain_two, g_b_in, g_b_down = gradients_two_slow(
            grid, *sums, parameters, vectors
        )

    gq_low, gkv_low, gh_low, gplan_low = attend_back(
        q, kv, skv, g_att, kvx, plan, live, 0, PAIRS // 2
    )
    if fast:
        twos = split_sum(at, 1, after(keep, gh_low), got)
        g_att = after(g_att, *twos)
        twos = [twos[0]] + [grid.send(twos[r], grid.swap_plane(r)) for r in three]
    gq_high, gkv_high, gh_high, gplan_high = attend_back(
        q, kv, skv, g_att, kvx, plan, live, PAIRS // 2, PAIRS // 2
    )
    gq, gkv = (gq_low, gq_high), (gkv_low, gkv_high)
    gn_far, gn_near, g_kv_halo = halo_back(gh_low, gh_high, normed_halo, wt_kv, second)
    back_one = grid.send(gn_near, grid.along(-1))
    back_two = grid.send(gn_far, grid.along(-2))
    gmeans, gsort, *sends = sink_backward(
        pieces, w_pairs, *kept, gplan_low, after(gplan_high, gn_near), own, context
    )
    gmeans_here = after(gmeans, *twos) if fast else gmeans
    keep, send = weight_back(
        at, gq, gkv, normed, wt_q, wt_kv, gmeans_here, pieces, g_kv_halo, gain_one, gsort, fast
    )
    if fast:
        got = grid.send(send, grid.swap_core())
        ones = split_sum(at, 0, keep, got)
        ones = [ones[0]] + [grid.send(ones[r], grid.swap_head(r)) for r in three]
        sends = lax.optimization_barrier((*sends, ones[0]))[:4]
        twos = merge_sum(at, 0, lax.optimization_barrier((*twos, ones[0]))[:4])
        twos = [twos[0]] + [grid.send(twos[r], grid.swap_head(r)) for r in three]
    steps = (-2, -1, 1, 2)
    far = [grid.send(value, grid.along(step)) for value, step in zip(sends, steps)]
    if fast:
        ones = merge_sum(at, 1, ones)
        ones = [ones[0]] + [grid.send(ones[r], grid.swap_plane(r)) for r in three]
    input_grad = finish(
        x, gq, gkv, wt_q, wt_kv, gmeans, far, back_one, back_two, g_middle, gain_one
    )
    if fast:
        g_wqkv, g_sort, g_gain_one = last_one(ones)
        g_in, g_down, g_out, *small = last_two(twos)
        g_wqkv, g_sort, g_down, g_out = g_wqkv.T, g_sort.T, g_down.T, g_out.T
        g_gain_one = g_gain_one[0]
        g_b_out, g_gain_two, g_b_in, g_b_down = (value[0] for value in small)
    else:
        g_wqkv, g_sort, g_gain_one = gradients_one_slow(
            grid, keep, send, gsort, parameters, vectors
        )
    return (
        output[None], input_grad[None], g_gain_one, g_wqkv, g_out, g_b_out, g_gain_two, g_in,
        g_b_in, g_down, g_b_down, g_sort,
    )


def solution(mesh):
    heads, cycles = mesh.shape["head"], mesh.shape["blk"]
    fine = Mesh(mesh.devices.reshape(heads, cycles // 2, 2), ("head", "plane", "core"))
    both = P(("head", "plane", "core"))
    split = P("head", ("plane", "core"))
    stream = P(("plane", "core"), "head", None)
    return jax.shard_map(
        per_device,
        mesh=fine,
        in_specs=(
            stream, stream, P(), both, split, split, both, both, split, both, split, both, split,
        ),
        out_specs=(
            stream, stream, both, split, split, both, both, split, both, split, both, split,
        ),
        check_vma=False,
    )
```

```python
import functools

import jax
import jax.numpy as jnp
from jax import lax
from jax.experimental import pallas as pl
from jax.experimental.pallas import tpu as pltpu
from jax.sharding import Mesh
from jax.sharding import PartitionSpec as P

D = 512
HEADS = 8
HEAD_DIM = 64
FF = 2048
BLOCK = 32
SINK_ITERS = 8
DOC_MOST = 62
LANES = 128
PAIRS = HEADS // 2
HALO = 64
GROUPS = 4
CHEAP = pl.CostEstimate(flops=0, transcendentals=0, bytes_accessed=0)
EPSILON = 1e-05
NEGATIVE = -1e30
FLOOR = -1e20
LOG2E = 1.4426950408889634
TINY = 1e-37
F32 = jnp.float32
BF16 = jnp.bfloat16
NT = (((1,), (1,)), ((), ()))
NN = (((1,), (0,)), ((), ()))
TN = (((0,), (0,)), ((), ()))


def mm(a, b, dims=NN):
    return lax.dot_general(a, b, dims, preferred_element_type=F32)


def vmem(limit=56):
    return pltpu.CompilerParams(vmem_limit_bytes=limit * 1024 * 1024)


def once(shape):
    return pl.BlockSpec(shape, lambda *i: (0,) * len(shape), pipeline_mode=pl.Buffered(1))


def halves(value):
    high = value.astype(BF16)
    return high, (value - high.astype(F32)).astype(BF16)


def mm3(a, b, dims):
    (da,), (db,) = dims[0]
    ah, al = halves(a)
    bh, bl = halves(b)
    return mm(
        jnp.concatenate([ah, al, ah], axis=da), jnp.concatenate([bh, bh, bl], axis=db), dims
    )


def sink_mask(docn_ref, docc_ref, window, context):
    first = context
    fold = window - LANES
    lane = lax.broadcasted_iota(jnp.int32, (1, LANES), 1)
    docn = docn_ref[...]
    row = lax.broadcasted_iota(jnp.int32, (window, 1), 0)
    col = jnp.where((row >= first) & (lane < fold), lane + LANES, lane)
    docc = jnp.where(row >= first, docc_ref[1:2, :], docc_ref[0:1, :])
    return (docn == docc) & (docn >= 0) & (col < row)


def fold_pair(top, low, fold, join):
    lane = lax.broadcasted_iota(jnp.int32, (1, LANES), 1)
    both = join(top, low)
    return jnp.where(lane < fold, top, both), jnp.where(lane < fold, low, both)


def sink_weight(pair, odd):
    lane = lax.broadcasted_iota(jnp.int32, pair.shape, 1)
    zero = jnp.zeros_like(pair)
    if odd:
        return jnp.concatenate([zero, jnp.where(lane >= HEAD_DIM, pair, zero)], axis=0)
    return jnp.concatenate([jnp.where(lane < HEAD_DIM, pair, zero), zero], axis=0)


def refold(keys, fold):
    return jnp.concatenate([keys[LANES:], keys[fold:LANES]], axis=0)


def row_step(values):
    highest = jnp.maximum(jnp.max(values, axis=1, keepdims=True), FLOOR)
    total = jnp.sum(jnp.exp2(values - highest), axis=1, keepdims=True)
    return values - (highest + LOG2E * jnp.log(jnp.maximum(total, TINY)))


def column_step(values, context, fold):
    top, low = values[:context], values[context:]
    h1, h2 = fold_pair(
        jnp.max(top, axis=0, keepdims=True),
        jnp.max(low, axis=0, keepdims=True),
        fold,
        jnp.maximum,
    )
    h1, h2 = jnp.maximum(h1, FLOOR), jnp.maximum(h2, FLOOR)
    e1, e2 = jnp.exp2(top - h1), jnp.exp2(low - h2)
    t1, t2 = fold_pair(
        jnp.sum(e1, axis=0, keepdims=True), jnp.sum(e2, axis=0, keepdims=True), fold, jnp.add
    )
    t1, t2 = jnp.maximum(t1, TINY), jnp.maximum(t2, TINY)
    moved = jnp.concatenate(
        [top - (h1 + LOG2E * jnp.log(t1)), low - (h2 + LOG2E * jnp.log(t2))], axis=0
    )
    scales = jnp.concatenate([jnp.exp2(h1), jnp.exp2(h2), 1.0 / t1, 1.0 / t2], axis=0)
    return moved, e1, e2, scales


def sink_forward_kernel(
    own, context, a, b, c, d, e, w_ref, docn_ref, docc_ref, plan_ref, kept_ref, scale_ref, proj_ref,
    q_ref, k_ref, vals, kept, sems,
):
    window = q_ref.shape[1]
    fold = window - LANES
    at = 0
    for piece in (a, b, c, d, e):
        rows = piece.shape[0]
        for pair in range(PAIRS):
            q_ref[pair, at : at + rows, :] = piece[:, pair * LANES : (pair + 1) * LANES]
            k_ref[pair, at : at + rows, :] = piece[:, D + pair * LANES : D + (pair + 1) * LANES]
        at += rows

    def logits(pair, carry):
        permitted = sink_mask(docn_ref, docc_ref, window, context)
        queries, keys = q_ref[pair], k_ref[pair]
        keys_two = refold(keys, fold)
        for odd in range(2):
            projected = mm3(queries, sink_weight(w_ref[pair], odd), NT)
            proj_ref[2 * pair + odd] = projected
            top = mm3(projected[:context], keys[:LANES], NT)
            low = mm3(projected[context:], keys_two, NT)
            vals[2 * pair + odd] = jnp.where(
                permitted, LOG2E * jnp.concatenate([top, low], axis=0), NEGATIVE
            )
        return carry

    lax.fori_loop(0, PAIRS, logits, 0)

    def send(step):
        return pltpu.make_async_copy(kept.at[step], kept_ref.at[step], sems.at[step])

    def step(turn, carry):
        for head in range(HEADS):
            moved, top, low, scales = column_step(row_step(vals[head]), context, fold)
            kept[turn, head, :context, :] = top
            kept[turn, head, context:, :] = low
            scale_ref[turn, head] = scales
            vals[head] = moved
        send(turn).start()
        return carry

    lax.fori_loop(0, SINK_ITERS, step, 0)
    for head in range(HEADS):
        plan_ref[head] = (
            kept[SINK_ITERS - 1, head, context - own : context, :]
            * scale_ref[SINK_ITERS - 1, head, 2:3, :]
        ).astype(BF16)
    lax.fori_loop(0, SINK_ITERS, lambda turn, carry: (send(turn).wait(), carry)[1], 0)


def sink_backward_kernel(
    own, context, a, b, c, d, e, w_ref, kept_ref, scale_ref, proj, gl_ref, gh_ref,
    gm_ref, gw_ref, sd, se, q_ref, k_ref, vals, gq, gk, kept, sems,
):
    window = q_ref.shape[1]
    fold = window - LANES

    def fetch(step):
        return pltpu.make_async_copy(kept_ref.at[step], kept.at[step], sems.at[step])

    def begin(turn, carry):
        fetch(SINK_ITERS - 1 - turn).start()
        return carry

    lax.fori_loop(0, SINK_ITERS, begin, 0)
    at = 0
    for piece in (a, b, c, d, e):
        rows = piece.shape[0]
        for pair in range(PAIRS):
            q_ref[pair, at : at + rows, :] = piece[:, pair * LANES : (pair + 1) * LANES]
            k_ref[pair, at : at + rows, :] = piece[:, D + pair * LANES : D + (pair + 1) * LANES]
        at += rows

    def back(turn, carry):
        at = SINK_ITERS - 1 - turn
        fetch(at).wait()

        @pl.when(turn == 0)
        def _():
            for head in range(HEADS):
                low = gl_ref.shape[0]
                ref, index = (gl_ref, head) if head < low else (gh_ref, head - low)
                vals[head, : context - own, :] = jnp.zeros((context - own, LANES), F32)
                vals[head, context - own : context, :] = (
                    ref[index]
                    * kept[SINK_ITERS - 1, head, context - own : context, :]
                    * scale_ref[SINK_ITERS - 1, head, 2:3, :]
                )
                vals[head, context:, :] = jnp.zeros((window - context, LANES), F32)

        for head in range(HEADS):
            g1, g2 = vals[head, :context, :], vals[head, context:, :]
            s1, s2 = fold_pair(
                jnp.sum(g1, axis=0, keepdims=True),
                jnp.sum(g2, axis=0, keepdims=True),
                fold,
                jnp.add,
            )
            scales = scale_ref[at, head]
            e1, e2 = kept[at, head, :context, :], kept[at, head, context:, :]
            g1, g2 = g1 - e1 * (s1 * scales[2:3]), g2 - e2 * (s2 * scales[3:4])
            r1, r2 = jnp.sum(g1, axis=1, keepdims=True), jnp.sum(g2, axis=1, keepdims=True)
            vals[head, :context, :] = g1 - (e1 * scales[0:1]) * r1
            vals[head, context:, :] = g2 - (e2 * scales[1:2]) * r2
        return carry

    lax.fori_loop(0, SINK_ITERS, back, 0)

    def products(pair, carry):
        queries, keys = q_ref[pair], k_ref[pair]
        keys_two = refold(keys, fold)
        turned = []
        gq_total = jnp.zeros((window, LANES), F32)
        gk_total = jnp.zeros((window, LANES), F32)
        for odd in range(2):
            head = 2 * pair + odd
            g1, g2 = vals[head, :context, :], vals[head, context:, :]
            against = jnp.concatenate(
                [mm3(g1, keys[:LANES], NN), mm3(g2, keys_two, NN)], axis=0
            )
            gq_total = gq_total + mm3(against, sink_weight(w_ref[pair], odd), NN)
            u1 = mm3(g1, proj[head, :context, :], TN)
            u2 = mm3(g2, proj[head, context:, :], TN)
            gk_total = gk_total + jnp.concatenate(
                [u1[:fold], u1[fold:] + u2[fold:], u2[:fold]], axis=0
            )
            turned.append(mm3(against, queries, TN))
        half = lax.broadcasted_iota(jnp.int32, (HEAD_DIM, LANES), 1) < HEAD_DIM
        gw_ref[pair] = jnp.where(half, turned[0][:HEAD_DIM], turned[1][HEAD_DIM:])
        gq[pair] = gq_total * (1.0 / BLOCK)
        gk[pair] = gk_total * (1.0 / BLOCK)
        return carry

    lax.fori_loop(0, PAIRS, products, 0)
    for pair in range(PAIRS):
        gm_ref[:, pair * LANES : (pair + 1) * LANES] = gq[pair]
        gm_ref[:, D + pair * LANES : D + (pair + 1) * LANES] = gk[pair]
    sd[...] = gm_ref[context : context + d.shape[0], :].astype(BF16)
    se[...] = gm_ref[context + d.shape[0] :, :].astype(BF16)


HBM = pl.BlockSpec(memory_space=pl.ANY)
VMEM = pl.BlockSpec(memory_space=pltpu.VMEM)
SMEM = pl.BlockSpec(memory_space=pltpu.SMEM)


def sink_forward(pieces, weight, docn, docc, own, context):
    window = sum(piece.shape[0] for piece in pieces)
    kept = (SINK_ITERS, HEADS, window, LANES)
    return pl.pallas_call(
        functools.partial(sink_forward_kernel, own, context),
        in_specs=[VMEM] * 8,
        out_specs=[VMEM, HBM, VMEM, VMEM],
        out_shape=[
            jax.ShapeDtypeStruct((HEADS, own, LANES), BF16),
            jax.ShapeDtypeStruct(kept, F32),
            jax.ShapeDtypeStruct((SINK_ITERS, HEADS, 4, LANES), F32),
            jax.ShapeDtypeStruct((HEADS, window, LANES), F32),
        ],
        scratch_shapes=[
            pltpu.VMEM((PAIRS, window, LANES), F32),
            pltpu.VMEM((PAIRS, window, LANES), F32),
            pltpu.VMEM((HEADS, window, LANES), F32),
            pltpu.VMEM(kept, F32),
            pltpu.SemaphoreType.DMA((SINK_ITERS,)),
        ],
        cost_estimate=CHEAP,
        compiler_params=vmem(),
        name="sink_forward",
    )(*pieces, weight, docn, docc)


def sink_backward(pieces, weight, kept, scales, projected, low, high, own, context):
    window = sum(piece.shape[0] for piece in pieces)
    return pl.pallas_call(
        functools.partial(sink_backward_kernel, own, context),
        in_specs=[VMEM] * 6 + [HBM] + [VMEM] * 4,
        out_shape=[
            jax.ShapeDtypeStruct((window, 2 * D), F32),
            jax.ShapeDtypeStruct((PAIRS, HEAD_DIM, LANES), F32),
            *(
                jax.ShapeDtypeStruct((pieces[i].shape[0], 2 * D), BF16)
                for i in (3, 4)
            ),
        ],
        scratch_shapes=[
            *[pltpu.VMEM((PAIRS, window, LANES), F32)] * 2,
            pltpu.VMEM((HEADS, window, LANES), F32),
            *[pltpu.VMEM((PAIRS, window, LANES), F32)] * 2,
            pltpu.VMEM(kept.shape, F32),
            pltpu.SemaphoreType.DMA((SINK_ITERS,)),
        ],
        cost_estimate=CHEAP,
        compiler_params=vmem(),
        name="sink_backward",
    )(*pieces, weight, kept, scales, projected, low, high)


def normalise(values):
    centre = values - jnp.mean(values, axis=-1, keepdims=True)
    spread = jnp.mean(centre * centre, axis=-1, keepdims=True)
    return centre * lax.rsqrt(spread + EPSILON)


def context_kernel(count, keep, *refs):
    gain_ref, w_ref, kvx_ref = refs[count : count + 3]
    x = jnp.concatenate([ref[...] for ref in refs[:count]], axis=0)
    blocks = x.shape[0]
    normed = normalise(x.astype(F32)) * gain_ref[...].reshape(1, 1, D)
    normed = normed.astype(BF16).reshape(blocks * 8, D)
    row = lax.broadcasted_iota(jnp.int32, (LANES, LANES), 0)
    lane = lax.broadcasted_iota(jnp.int32, (LANES, LANES), 1)
    turn = (lane == (row % 16) * 8 + row // 16).astype(F32).astype(BF16)
    turned = [
        mm(turn, normed[i * LANES : (i + 1) * LANES]).astype(BF16) for i in range(blocks // 16)
    ]
    rows = []
    for b in range(8):
        part = jnp.concatenate([part[b * 16 : (b + 1) * 16] for part in turned], axis=0)
        if keep:
            refs[count + 3][b] = part
        rows.append(part)
    rows = jnp.concatenate(rows, axis=0)
    for head in range(0, HEADS, 2):
        out = mm(rows, w_ref[head * LANES : (head + 2) * LANES, :], NT).astype(BF16)
        for b in range(8):
            for e in range(2):
                kvx_ref[head + e, :, b * LANES : (b + 1) * LANES] = out[
                    b * blocks : (b + 1) * blocks, e * LANES : (e + 1) * LANES
                ]


def context_project(values, gain, w_kv, keep):
    blocks = sum(v.shape[0] for v in values)
    outs = 2 if keep else 1
    return pl.pallas_call(
        functools.partial(context_kernel, len(values), keep),
        grid=(BLOCK // 8,),
        in_specs=[
            *(pl.BlockSpec((v.shape[0], 8, D), lambda i: (0, i, 0)) for v in values),
            pl.BlockSpec((1, D), lambda i: (0, 0)),
            pl.BlockSpec((2 * D, D), lambda i: (0, 0)),
        ],
        out_specs=[
            pl.BlockSpec((HEADS, blocks, 8 * LANES), lambda i: (0, 0, i)),
            pl.BlockSpec((8, blocks, D), lambda i: (i, 0, 0)),
        ][:outs],
        out_shape=[
            jax.ShapeDtypeStruct((HEADS, blocks, BLOCK * LANES), BF16),
            jax.ShapeDtypeStruct((BLOCK, blocks, D), BF16),
        ][:outs],
        cost_estimate=CHEAP,
        compiler_params=vmem(),
        name="context_halo" if keep else "context_own",
    )(*values, gain, w_kv)


def compact(values, lane_block):
    out = values[:BLOCK]
    for j in range(1, 4):
        out = jnp.where(lane_block == j, values[j * BLOCK : (j + 1) * BLOCK], out)
    return out


def spread(values, lane_block):
    zero = jnp.zeros_like(values)
    return jnp.concatenate([jnp.where(lane_block == j, values, zero) for j in range(4)], axis=0)


def softmax_pair(local, chosen, live):
    lane = lax.broadcasted_iota(jnp.int32, (BLOCK, LANES), 1)
    row = lax.broadcasted_iota(jnp.int32, (BLOCK, LANES), 0)
    local = jnp.where(row <= lax.rem(lane, BLOCK), local, NEGATIVE)
    chosen = jnp.where(live, chosen, NEGATIVE)
    highest = jnp.maximum(
        jnp.max(local, axis=0, keepdims=True), jnp.max(chosen, axis=0, keepdims=True)
    )
    el, es = jnp.exp(local - highest), jnp.exp(chosen - highest)
    total = jnp.sum(el, axis=0, keepdims=True) + jnp.sum(es, axis=0, keepdims=True)
    inverse = 1.0 / total
    return el * inverse, es * inverse


def half_mask(first):
    lane = lax.broadcasted_iota(jnp.int32, (LANES, LANES), 1)
    return (lane < HEAD_DIM) if first else (lane >= HEAD_DIM)


def attend_kernel(
    q_ref, kv_ref, kvh_ref, kvo_ref, plan_ref, live_ref, att_ref, skv_ref, even_ref, odd_ref
):
    own = plan_ref.shape[1]
    blocks = kvh_ref.shape[1] + own
    held = (even_ref, odd_ref)
    for e in range(2):
        plan = plan_ref[e][:, :blocks]
        for chunk in range(4):
            lanes = slice(chunk * 8 * LANES, (chunk + 1) * 8 * LANES)
            out = mm(plan, jnp.concatenate([kvh_ref[e, :, lanes], kvo_ref[e, :, lanes]], axis=0))
            for b in range(8):
                at = (chunk * 8 + b) * (own + 1)
                held[e][at : at + own, :] = out[:, b * LANES : (b + 1) * LANES]
    lane_block = lax.broadcasted_iota(jnp.int32, (BLOCK, LANES), 1) // BLOCK
    lane_half = [half_mask(True), half_mask(False)]

    def group(turn, carry):
        chains = [(turn * GROUPS + i, e) for i in range(GROUPS) for e in range(2)]
        starts = [pl.multiple_of(g * LANES, LANES) for g, _ in chains]
        both, scores = [], []
        for (g, e), start in zip(chains, starts):
            local = kv_ref[pl.ds(start, LANES), e * LANES : (e + 1) * LANES]
            chosen = jnp.concatenate(
                [held[e][pl.ds(4 * g + i, BLOCK, stride=own + 1), :] for i in range(4)], axis=0
            ).astype(BF16)
            skv_ref[pl.ds(start, LANES), e * LANES : (e + 1) * LANES] = chosen
            both.append(jnp.concatenate([local, chosen], axis=0))
        for (g, e), start, kv in zip(chains, starts, both):
            q = q_ref[pl.ds(start, LANES), :] * 0.125
            qm = jnp.where(lane_half[e], q, jnp.zeros_like(q))
            out = mm(kv, qm, NT)
            scores.append((compact(out[:LANES], lane_block), compact(out[LANES:], lane_block)))
        weights = []
        for (g, e), (local, chosen) in zip(chains, scores):
            weights.append(softmax_pair(local, chosen, live_ref[pl.ds(g, 1), :] > 0.0))
        outs = []
        for (g, e), kv, (wl, ws) in zip(chains, both, weights):
            wide = jnp.concatenate(
                [spread(wl.astype(BF16), lane_block), spread(ws.astype(BF16), lane_block)], axis=0
            )
            turned = kv.T
            outs.append(mm(turned[HEAD_DIM:] if e == 0 else turned[:HEAD_DIM], wide))
        for i in range(GROUPS):
            att_ref[pl.ds(starts[2 * i], LANES), :] = jnp.concatenate(
                outs[2 * i : 2 * i + 2], axis=0
            ).T.astype(BF16)
        return carry

    lax.fori_loop(0, own // 4 // GROUPS, group, 0)


def attend(q, kv, kvh, kvo, plan, live):
    tok, own, halo = q.shape[0], plan.shape[1], kvh.shape[1]
    return pl.pallas_call(
        attend_kernel,
        grid=(PAIRS,),
        in_specs=[
            pl.BlockSpec((tok, LANES), lambda j: (0, j)),
            pl.BlockSpec((tok, 2 * LANES), lambda j: (0, j)),
            pl.BlockSpec((2, halo, BLOCK * LANES), lambda j: (j, 0, 0)),
            pl.BlockSpec((2, own, BLOCK * LANES), lambda j: (j, 0, 0)),
            pl.BlockSpec((2, own, LANES), lambda j: (j, 0, 0)),
            pl.BlockSpec((tok // LANES, LANES), lambda j: (0, 0)),
        ],
        out_specs=[
            pl.BlockSpec((tok, LANES), lambda j: (0, j)),
            pl.BlockSpec((tok, 2 * LANES), lambda j: (0, j)),
        ],
        out_shape=[
            jax.ShapeDtypeStruct((tok, D), BF16),
            jax.ShapeDtypeStruct((tok, 2 * D), BF16),
        ],
        scratch_shapes=[pltpu.VMEM((BLOCK * (own + 1), LANES), F32)] * 2,
        cost_estimate=CHEAP,
        compiler_params=vmem(),
        name="attend",
    )(q, kv, kvh, kvo, plan, live)


def attend_back_kernel(
    q_ref, kv_ref, skv_ref, go_ref, kvh_ref, kvo_ref, plan_ref, live_ref,
    gq_ref, gkv_ref, gh_ref, gp_ref, even_ref, odd_ref, leven_ref, lodd_ref,
):
    own = plan_ref.shape[1]
    halo = kvh_ref.shape[1]
    blocks = halo + own
    held = (even_ref, odd_ref)
    lheld = (leven_ref, lodd_ref)
    lane_block = lax.broadcasted_iota(jnp.int32, (BLOCK, LANES), 1) // BLOCK
    lane_half = [half_mask(True), half_mask(False)]

    def group(turn, carry):
        chains = [(turn * GROUPS + i, e) for i in range(GROUPS) for e in range(2)]
        starts = [pl.multiple_of(g * LANES, LANES) for g, _ in chains]
        both, right, scores = [], [], []
        for (g, e), start in zip(chains, starts):
            lanes = slice(e * LANES, (e + 1) * LANES)
            rows = pl.ds(start, LANES)
            both.append(jnp.concatenate([kv_ref[rows, lanes], skv_ref[rows, lanes]], axis=0))
            q = q_ref[rows, :] * 0.125
            go = go_ref[rows, :]
            go = jnp.concatenate([go[:, HEAD_DIM:], go[:, :HEAD_DIM]], axis=1)
            qm = jnp.where(lane_half[e], q, jnp.zeros_like(q))
            gm = jnp.where(lane_half[1 - e], go, jnp.zeros_like(go))
            right.append(jnp.concatenate([qm, gm], axis=0))
        for kv, other in zip(both, right):
            out = mm(kv, other, NT)
            scores.append(
                [
                    compact(out[rows, lanes], lane_block)
                    for lanes in (slice(0, LANES), slice(LANES, 2 * LANES))
                    for rows in (slice(0, LANES), slice(LANES, 2 * LANES))
                ]
            )
        wides = []
        for (g, e), (sl, ss, dl, ds) in zip(chains, scores):
            wl, ws = softmax_pair(sl, ss, live_ref[pl.ds(g, 1), :] > 0.0)
            inner = jnp.sum(wl * dl + ws * ds, axis=0, keepdims=True)
            low = [v.astype(BF16) for v in (wl, ws, wl * (dl - inner), ws * (ds - inner))]
            wides.append(low)
        outs = []
        for (g, e), start, kv, other, (wl, ws, gl, gs) in zip(chains, starts, both, right, wides):
            weights = jnp.concatenate([spread(wl, lane_block), spread(ws, lane_block)], axis=0)
            gscore = jnp.concatenate([spread(gl, lane_block), spread(gs, lane_block)], axis=0)
            gboth = mm(jnp.concatenate([gscore, weights], axis=1), other)
            lheld[e][pl.ds(start, LANES), :] = gboth[:LANES]
            for i in range(4):
                held[e][pl.ds(4 * g + i, BLOCK, stride=own + 1), :] = gboth[
                    LANES + i * BLOCK : LANES + (i + 1) * BLOCK
                ]
            turned = kv.T
            outs.append(mm(turned[:HEAD_DIM] if e == 0 else turned[HEAD_DIM:], gscore))
        for i in range(GROUPS):
            gq_ref[pl.ds(starts[2 * i], LANES), :] = (
                jnp.concatenate(outs[2 * i : 2 * i + 2], axis=0).T * 0.125
            ).astype(BF16)
        return carry

    lax.fori_loop(0, own // 4 // GROUPS, group, 0)
    for e in range(2):
        plan = plan_ref[e][:, :blocks]
        gplan = jnp.zeros((own, blocks), F32)
        for chunk in range(4):
            lanes = slice(chunk * 8 * LANES, (chunk + 1) * 8 * LANES)
            grads = jnp.concatenate(
                [
                    held[e][(chunk * 8 + b) * (own + 1) : (chunk * 8 + b) * (own + 1) + own, :]
                    for b in range(8)
                ],
                axis=1,
            ).astype(BF16)
            here = jnp.concatenate([kvh_ref[e, :, lanes], kvo_ref[e, :, lanes]], axis=0)
            gplan = gplan + mm(grads, here, NT)
            gcontext = mm(plan, grads, TN)
            gh_ref[e, :, lanes] = gcontext[:halo].astype(BF16)
            for b in range(8):
                at = (chunk * 8 + b) * (own + 1)
                held[e][at : at + own, :] = gcontext[halo:, b * LANES : (b + 1) * LANES]
        gp_ref[e] = jnp.concatenate([gplan, jnp.zeros((own, LANES - blocks), F32)], axis=1)

    def finish(g, carry):
        start = pl.multiple_of(g * LANES, LANES)
        for e in range(2):
            rest = jnp.concatenate(
                [held[e][pl.ds(4 * g + i, BLOCK, stride=own + 1), :] for i in range(4)], axis=0
            )
            gkv_ref[pl.ds(start, LANES), e * LANES : (e + 1) * LANES] = (
                rest + lheld[e][pl.ds(start, LANES), :]
            ).astype(BF16)
        return carry

    lax.fori_loop(0, own // 4, finish, 0)


def attend_back(q, kv, skv, go, kvh, kvo, plan, live, first, pairs):
    tok, own, halo = q.shape[0], plan.shape[1], kvh.shape[1]
    return pl.pallas_call(
        attend_back_kernel,
        grid=(pairs,),
        in_specs=[
            pl.BlockSpec((tok, LANES), lambda j: (0, j + first)),
            pl.BlockSpec((tok, 2 * LANES), lambda j: (0, j + first)),
            pl.BlockSpec((tok, 2 * LANES), lambda j: (0, j + first)),
            pl.BlockSpec((tok, LANES), lambda j: (0, j + first)),
            pl.BlockSpec((2, halo, BLOCK * LANES), lambda j: (j + first, 0, 0)),
            pl.BlockSpec((2, own, BLOCK * LANES), lambda j: (j + first, 0, 0)),
            pl.BlockSpec((2, own, LANES), lambda j: (j + first, 0, 0)),
            pl.BlockSpec((tok // LANES, LANES), lambda j: (0, 0)),
        ],
        out_specs=[
            pl.BlockSpec((tok, LANES), lambda j: (0, j)),
            pl.BlockSpec((tok, 2 * LANES), lambda j: (0, j)),
            pl.BlockSpec((2, halo, BLOCK * LANES), lambda j: (j, 0, 0)),
            pl.BlockSpec((2, own, LANES), lambda j: (j, 0, 0)),
        ],
        out_shape=[
            jax.ShapeDtypeStruct((tok, pairs * LANES), BF16),
            jax.ShapeDtypeStruct((tok, 2 * pairs * LANES), BF16),
            jax.ShapeDtypeStruct((2 * pairs, halo, BLOCK * LANES), BF16),
            jax.ShapeDtypeStruct((2 * pairs, own, LANES), F32),
        ],
        scratch_shapes=[pltpu.VMEM((BLOCK * (own + 1), LANES), F32)] * 4,
        cost_estimate=CHEAP,
        compiler_params=vmem(),
        name="attend_back",
    )(q, kv, skv, go, kvh, kvo, plan, live)


def halo_kernel(
    low_ref, high_ref, nh_ref, wq_ref, w_ref, gm_ref, far_ref, near_ref, gw_ref, block_ref
):
    halo = low_ref.shape[1]
    far = far_ref.shape[1]

    @pl.when(pl.program_id(0) == 0)
    def _():
        gw_ref[...] = jnp.zeros_like(gw_ref)
        grads = gm_ref[...].astype(BF16)
        block_ref[...] = mm(grads[:, :D], wq_ref[...]) + mm(widen_keys(grads[:, D:]), w_ref[...])

    rows = jnp.concatenate(
        [
            jnp.concatenate(
                [
                    ref[head, :, b * LANES : (b + 1) * LANES]
                    for ref in (low_ref, high_ref)
                    for head in range(ref.shape[0])
                ],
                axis=1,
            )
            for b in range(8)
        ],
        axis=0,
    )
    out = (mm(rows, w_ref[...]).reshape(8, halo, D) + block_ref[...][None]).astype(BF16)
    far_ref[...] = out[:, :far]
    near_ref[...] = out[:, far:]
    gw_ref[...] += mm(rows, nh_ref[...].reshape(8 * halo, D), TN)


def halo_back(low, high, nh, w_q, w_kv, gm, far):
    halo = low.shape[1]
    part = lambda v: pl.BlockSpec((v.shape[0], halo, 8 * LANES), lambda i: (0, 0, i))
    return pl.pallas_call(
        halo_kernel,
        grid=(BLOCK // 8,),
        in_specs=[
            part(low),
            part(high),
            pl.BlockSpec((8, halo, D), lambda i: (i, 0, 0)),
            once((D, D)),
            once((2 * D, D)),
            once((halo, 2 * D)),
        ],
        out_specs=[
            pl.BlockSpec((8, far, D), lambda i: (i, 0, 0)),
            pl.BlockSpec((8, halo - far, D), lambda i: (i, 0, 0)),
            pl.BlockSpec((2 * D, D), lambda i: (0, 0)),
        ],
        out_shape=[
            jax.ShapeDtypeStruct((BLOCK, far, D), BF16),
            jax.ShapeDtypeStruct((BLOCK, halo - far, D), BF16),
            jax.ShapeDtypeStruct((2 * D, D), F32),
        ],
        scratch_shapes=[pltpu.VMEM((halo, D), F32)],
        cost_estimate=CHEAP,
        compiler_params=vmem(),
        name="halo_back",
    )(low, high, nh, w_q, w_kv, gm)


def project_kernel(x_ref, gain_ref, wq_ref, wkv_ref, n_ref, q_ref, kv_ref, m_ref, head_ref, tail_ref):
    rows = x_ref.shape[0]
    blocks = rows // BLOCK
    normed = (normalise(x_ref[...].astype(F32)) * gain_ref[...]).astype(BF16)
    n_ref[...] = normed
    q = mm(normed, wq_ref[...], NT).astype(BF16)
    q_ref[...] = q
    kv = mm(normed, wkv_ref[...], NT).astype(BF16)
    kv_ref[...] = kv
    half = lax.broadcasted_iota(jnp.int32, (1, LANES), 1) < HEAD_DIM
    m_ref[:, :D] = jnp.mean(q.astype(F32).reshape(blocks, BLOCK, D), axis=1)
    for pair in range(PAIRS):
        even = kv[:, 2 * pair * LANES : (2 * pair + 1) * LANES]
        odd = kv[:, (2 * pair + 1) * LANES : (2 * pair + 2) * LANES]
        keys = jnp.where(half, even.astype(F32), odd.astype(F32))
        m_ref[:, D + pair * LANES : D + (pair + 1) * LANES] = jnp.mean(
            keys.reshape(blocks, BLOCK, LANES), axis=1
        )
    m_ref[:, 2 * D :] = jnp.mean(normed.astype(F32).reshape(blocks, BLOCK, D), axis=1)
    at = pl.program_id(0)
    ends = head_ref.shape[0] // blocks
    for ref, first in ((head_ref, 0), (tail_ref, pl.num_programs(0) - ends)):

        @pl.when((at >= first) & (at < first + ends))
        def _():
            ref[pl.ds(pl.multiple_of((at - first) * blocks, 8), blocks), :] = m_ref[...]


def project(x, gain, wt_q, wt_kv, ends):
    tok = x.shape[0]
    tile = 8 * BLOCK
    return pl.pallas_call(
        project_kernel,
        grid=(tok // tile,),
        in_specs=[
            pl.BlockSpec((tile, D), lambda i: (i, 0)),
            pl.BlockSpec((1, D), lambda i: (0, 0)),
            pl.BlockSpec((D, D), lambda i: (0, 0)),
            pl.BlockSpec((2 * D, D), lambda i: (0, 0)),
        ],
        out_specs=[
            pl.BlockSpec((tile, D), lambda i: (i, 0)),
            pl.BlockSpec((tile, D), lambda i: (i, 0)),
            pl.BlockSpec((tile, 2 * D), lambda i: (i, 0)),
            pl.BlockSpec((8, 3 * D), lambda i: (i, 0)),
            once((ends, 3 * D)),
            once((ends, 3 * D)),
        ],
        out_shape=[
            jax.ShapeDtypeStruct((tok, D), BF16),
            jax.ShapeDtypeStruct((tok, D), BF16),
            jax.ShapeDtypeStruct((tok, 2 * D), BF16),
            jax.ShapeDtypeStruct((tok // BLOCK, 3 * D), F32),
            jax.ShapeDtypeStruct((ends, 3 * D), F32),
            jax.ShapeDtypeStruct((ends, 3 * D), F32),
        ],
        cost_estimate=CHEAP,
        compiler_params=vmem(),
        name="project",
    )(x, gain, wt_q, wt_kv)


PIECE_ONE = 208
PIECE_TWO = 576
PARTS_TWO = 592


def place(vector, start):
    size = vector.shape[1]
    row = lax.broadcasted_iota(jnp.int32, (size, LANES), 0)
    lane = lax.broadcasted_iota(jnp.int32, (size, LANES), 1)
    pick = (lane == row + start).astype(F32).astype(BF16)
    return mm(jnp.broadcast_to(vector.astype(F32), (16, size)).astype(BF16), pick)


def pack_kernel(
    wqkv_ref, wsort_ref, g1, bo, g2, bi, bd, win_ref, wdown_ref, wout_ref, x_ref,
    one_ref, two_ref, tail_ref,
):
    tail_ref[...] = x_ref[...]
    one_ref[:192, :] = wqkv_ref[...]
    row = place(g1[...], 0) + place(bo[...], 16) + place(g2[...], 32)
    row = row + place(bi[...], 48) + place(bd[...], 112)
    one_ref[192:, :] = jnp.concatenate([wsort_ref[...].astype(F32), row[:8]], axis=0).astype(BF16)
    two_ref[:256, :] = win_ref[...].astype(F32).T.astype(BF16)
    for k in range(4):
        two_ref[256 + k * 64 : 256 + (k + 1) * 64, :] = wdown_ref[:, k * LANES : (k + 1) * LANES]
    two_ref[512:, :] = wout_ref[...]


def pack(w_qkv, w_sort, vectors, w_in, w_down, w_out, x, tail):
    last = x.shape[0] // tail - 1
    return pl.pallas_call(
        pack_kernel,
        grid=(1,),
        in_specs=[VMEM] * 10 + [pl.BlockSpec((tail, D), lambda i: (last, 0))],
        out_shape=[
            jax.ShapeDtypeStruct((PIECE_ONE, LANES), BF16),
            jax.ShapeDtypeStruct((PIECE_TWO, LANES), BF16),
            jax.ShapeDtypeStruct((tail, D), BF16),
        ],
        cost_estimate=CHEAP,
        compiler_params=vmem(),
        name="pack",
    )(w_qkv.T, w_sort.T, *(v.reshape(1, -1) for v in vectors), w_in, w_down.T, w_out.T, x)


def rows_at(start, size):
    return pl.ds(pl.multiple_of(start * size, size), size)


def each_owner(at_ref, visit):
    def planes(z, carry):
        for other in range(2):
            c = at_ref[2] ^ other
            for h in range(4):
                visit(other == 0, h, z, 2 * z + c, c)
        return carry

    lax.fori_loop(0, 4, planes, 0)


def each_piece(at_ref, mine_ref, other_ref, visit):
    def owner(own, h, z, b, c):
        source = mine_ref if own else other_ref
        visit(h, b, c, source.at[at_ref[0] ^ h, at_ref[1] ^ z])

    each_owner(at_ref, owner)


def widen(vecs, start, size):
    total = 32 * size
    lane = lax.broadcasted_iota(jnp.int32, (LANES, total), 1)
    row = lax.broadcasted_iota(jnp.int32, (LANES, total), 0)
    pick = (row == start + lax.rem(lane, size)).astype(F32).astype(BF16)
    every = mm(vecs, pick)
    owner = lax.broadcasted_iota(jnp.int32, (32, total), 0)
    lane = lax.broadcasted_iota(jnp.int32, (32, total), 1)
    return jnp.sum(jnp.where(owner == lane // size, every, 0.0), axis=0, keepdims=True)


def assemble_kernel(
    at_ref, mine_ref, other_ref, wq_ref, wkv_ref, ws_ref, g1_ref, bo_ref, g2_ref, bi_ref, bd_ref,
    vecs_ref,
):
    def visit(h, b, c, piece):
        lanes = slice(h * LANES, (h + 1) * LANES)
        wq_ref[rows_at(b, 64), lanes] = piece[:64, :]
        wkv_ref[rows_at(2 * b + c, 64), lanes] = piece[64:128, :]
        wkv_ref[rows_at(2 * b + 1 - c, 64), lanes] = piece[128:192, :]
        tail = piece[192:208, :].astype(F32)
        ws_ref[h, rows_at(b, 8), :] = tail[:8]
        vecs_ref[pl.ds(h * 8 + b, 1), :] = tail[8:9]

    each_piece(at_ref, mine_ref, other_ref, visit)
    vecs = vecs_ref[...].astype(BF16)
    g1_ref[...] = widen(vecs, 0, 16)
    bo_ref[...] = widen(vecs, 16, 16)
    g2_ref[...] = widen(vecs, 32, 16)
    bi_ref[...] = widen(vecs, 48, 64)
    bd_ref[...] = widen(vecs, 112, 16)


def assemble(at, mine, other):
    row = jax.ShapeDtypeStruct((1, D), F32)
    return pl.pallas_call(
        assemble_kernel,
        in_specs=[SMEM, VMEM, VMEM],
        out_shape=[
            jax.ShapeDtypeStruct((D, D), BF16),
            jax.ShapeDtypeStruct((2 * D, D), BF16),
            jax.ShapeDtypeStruct((PAIRS, HEAD_DIM, LANES), F32),
            row, row, row, jax.ShapeDtypeStruct((1, FF), F32), row,
        ],
        scratch_shapes=[pltpu.VMEM((32, LANES), F32)],
        cost_estimate=CHEAP,
        compiler_params=vmem(),
        name="assemble",
    )(at, mine, other)


GELU_A = 0.7978845608028654
GELU_B = 0.044715


def feed_tile(x, att, g, bo, g2, bi, bd, win, wdown, wout, acc_in, acc_down, acc_out, sums):
    middle = x.astype(F32) + mm(att, wout[...], NT) + bo
    centre = middle - jnp.mean(middle, axis=-1, keepdims=True)
    spread_ = jnp.mean(centre * centre, axis=-1, keepdims=True)
    inverse = lax.rsqrt(spread_ + EPSILON)
    hat = centre * inverse
    normed = (hat * g2).astype(BF16)
    normed_t = normed.T
    g_t = g.T
    out = jnp.zeros(middle.shape, F32)
    u = jnp.zeros(middle.shape, F32)
    cut = 512
    for k in range(FF // cut):
        cols = slice(k * cut, (k + 1) * cut)
        pre = mm(normed, win[cols, :], NT) + bi[:, cols]
        square = pre * pre
        t = jnp.tanh(GELU_A * pre * (1.0 + GELU_B * square))
        half = 0.5 * (1.0 + t)
        hidden = (pre * half).astype(BF16)
        slope = half + (0.5 * GELU_A) * pre * (1.0 - t * t) * (1.0 + (3.0 * GELU_B) * square)
        g_pre = (mm(g, wdown[:, cols], NN) * slope).astype(BF16)
        out = out + mm(hidden, wdown[:, cols], NT)
        u = u + mm(g_pre, win[cols, :], NN)
        part = mm(normed_t, g_pre)
        for i in range(2):
            acc_in[2 * k + i] += part[:, i * 256 : (i + 1) * 256]
        acc_down[:, cols] += mm(g_t, hidden)
        sums[4:5, cols] += jnp.sum(g_pre.astype(F32), axis=0, keepdims=True)
    gf = g.astype(F32)
    sums[1:2, :D] += jnp.sum(u * hat, axis=0, keepdims=True)
    sums[3:4, :D] += jnp.sum(gf, axis=0, keepdims=True)
    du = u * g2
    inner = jnp.mean(du * hat, axis=-1, keepdims=True)
    g_middle = gf + inverse * (du - jnp.mean(du, axis=-1, keepdims=True) - hat * inner)
    branch = g_middle.astype(BF16)
    sums[0:1, :D] += jnp.sum(branch.astype(F32), axis=0, keepdims=True)
    acc_out[...] += mm(branch.T, att)
    return (middle + out + bd).astype(BF16), g_middle, mm(branch, wout[...], NN).astype(BF16)


def clear(*refs):
    for ref in refs:
        ref[...] = jnp.zeros_like(ref)


def narrow(sums):
    total = jnp.zeros((32, LANES), F32)
    for index, start, size in ((0, 16, 16), (1, 32, 16), (4, 48, 64), (3, 112, 16)):
        width = 32 * size
        owner = lax.broadcasted_iota(jnp.int32, (32, width), 0)
        lane = lax.broadcasted_iota(jnp.int32, (32, width), 1)
        kept = jnp.where(owner == lane // size, sums[index : index + 1, :width], 0.0)
        row = lax.broadcasted_iota(jnp.int32, (width, LANES), 0)
        lane = lax.broadcasted_iota(jnp.int32, (width, LANES), 1)
        pick = (lane == start + lax.rem(row, size)).astype(F32).astype(BF16)
        total = total + mm(kept.astype(BF16), pick)
    return total


def feed_fast_kernel(
    at_ref, x_ref, att_ref, g_ref, bo_ref, g2_ref, bi_ref, bd_ref, mine_ref, other_ref,
    out_ref, gm_ref, ga_ref, keep_ref, send_ref,
    win, wdown, wout, acc_in, acc_down, acc_out, sums, vecs,
):
    @pl.when(pl.program_id(0) == 0)
    def _():
        def visit(h, b, c, piece):
            win[rows_at(b, 256), h * LANES : (h + 1) * LANES] = piece[:256, :]
            for k in range(4):
                lanes = slice(h * 512 + k * LANES, h * 512 + (k + 1) * LANES)
                wdown[rows_at(b, 64), lanes] = piece[256 + k * 64 : 320 + k * 64, :]
            wout[rows_at(b, 64), h * LANES : (h + 1) * LANES] = piece[512:576, :]

        each_piece(at_ref, mine_ref, other_ref, visit)
        clear(acc_in, acc_down, acc_out, sums)

    out_ref[...], gm_ref[...], ga_ref[...] = feed_tile(
        x_ref[...], att_ref[...], g_ref[...], bo_ref[...], g2_ref[...], bi_ref[...], bd_ref[...],
        win, wdown, wout, acc_in, acc_down, acc_out, sums,
    )

    @pl.when(pl.program_id(0) == pl.num_programs(0) - 1)
    def _():
        vecs[...] = narrow(sums)

        def owner(own, h, z, b, c):
            ref = keep_ref if own else send_ref
            for k in range(2):
                ref[h, z, k * LANES : (k + 1) * LANES, :] = acc_in[
                    b, h * LANES : (h + 1) * LANES, k * LANES : (k + 1) * LANES
                ].astype(BF16)
            for k in range(4):
                ref[h, z, 256 + k * 64 : 320 + k * 64, :] = acc_down[
                    rows_at(b, 64), h * 512 + k * LANES : h * 512 + (k + 1) * LANES
                ].astype(BF16)
            ref[h, z, 512:576, :] = acc_out[
                rows_at(b, 64), h * LANES : (h + 1) * LANES
            ].astype(BF16)
            ref[h, z, 576:592, :] = jnp.broadcast_to(
                vecs[pl.ds(h * 8 + b, 1), :], (16, LANES)
            ).astype(BF16)

        each_owner(at_ref, owner)


def feed_fast(at, x, att, g, bo, g2, bi, bd, mine, other):
    tok = x.shape[0]
    tile = 512
    tiled = pl.BlockSpec((tile, D), lambda i: (i, 0))
    parts = (4, 4, PARTS_TWO, LANES)
    return pl.pallas_call(
        feed_fast_kernel,
        grid=(tok // tile,),
        in_specs=[
            SMEM, tiled, tiled, tiled, once((1, D)), once((1, D)), once((1, FF)), once((1, D)),
            once(mine.shape), once(other.shape),
        ],
        out_specs=[tiled, tiled, tiled, once(parts), once(parts)],
        out_shape=[
            jax.ShapeDtypeStruct((tok, D), BF16),
            jax.ShapeDtypeStruct((tok, D), F32),
            jax.ShapeDtypeStruct((tok, D), BF16),
            jax.ShapeDtypeStruct(parts, BF16),
            jax.ShapeDtypeStruct(parts, BF16),
        ],
        scratch_shapes=[
            pltpu.VMEM((FF, D), BF16), pltpu.VMEM((D, FF), BF16), pltpu.VMEM((D, D), BF16),
            pltpu.VMEM((8, D, FF // 8), F32), pltpu.VMEM((D, FF), F32), pltpu.VMEM((D, D), F32),
            pltpu.VMEM((8, FF), F32), pltpu.VMEM((32, LANES), F32),
        ],
        cost_estimate=CHEAP,
        compiler_params=vmem(60),
        name="feed",
    )(at, x, att, g, bo, g2, bi, bd, mine, other)


def feed_slow_kernel(
    x_ref, att_ref, g_ref, bo_ref, g2_ref, bi_ref, bd_ref, win, wdown, wout,
    out_ref, gm_ref, ga_ref, acc_in, acc_down, acc_out, sums,
):
    @pl.when(pl.program_id(0) == 0)
    def _():
        clear(acc_in, acc_down, acc_out, sums)

    out_ref[...], gm_ref[...], ga_ref[...] = feed_tile(
        x_ref[...], att_ref[...], g_ref[...], bo_ref[...], g2_ref[...], bi_ref[...], bd_ref[...],
        win, wdown, wout, acc_in, acc_down, acc_out, sums,
    )


def feed_slow(x, att, g, bo, g2, bi, bd, win, wdown, wout):
    tok = x.shape[0]
    tile = 512
    tiled = pl.BlockSpec((tile, D), lambda i: (i, 0))
    wide, square, rows, cut = (D, FF), (D, D), (8, FF), (8, D, FF // 8)
    return pl.pallas_call(
        feed_slow_kernel,
        grid=(tok // tile,),
        in_specs=[
            tiled, tiled, tiled, once((1, D)), once((1, D)), once((1, FF)), once((1, D)),
            once((FF, D)), once(wide), once(square),
        ],
        out_specs=[tiled, tiled, tiled, once(cut), once(wide), once(square), once(rows)],
        out_shape=[
            jax.ShapeDtypeStruct((tok, D), BF16),
            jax.ShapeDtypeStruct((tok, D), F32),
            jax.ShapeDtypeStruct((tok, D), BF16),
            jax.ShapeDtypeStruct(cut, F32),
            jax.ShapeDtypeStruct(wide, F32),
            jax.ShapeDtypeStruct(square, F32),
            jax.ShapeDtypeStruct(rows, F32),
        ],
        cost_estimate=CHEAP,
        compiler_params=vmem(60),
        name="feed_whole",
    )(x, att, g, bo, g2, bi, bd, win, wdown, wout)


def split_kernel(which, at_ref, keep_ref, got_ref, *outs):
    for r, out in enumerate(outs):
        i = at_ref[which] ^ r
        out[0] = (keep_ref[i, 0].astype(F32) + got_ref[i, 0].astype(F32)).astype(BF16)


def split_sum(at, which, keep, got):
    one, two, rows, lanes = keep.shape
    block = pl.BlockSpec((one, 1, rows, lanes), lambda i: (0, i, 0, 0))
    return pl.pallas_call(
        functools.partial(split_kernel, which),
        grid=(two,),
        in_specs=[SMEM, block, block],
        out_specs=[pl.BlockSpec((1, rows, lanes), lambda i: (i, 0, 0))] * one,
        out_shape=[jax.ShapeDtypeStruct((two, rows, lanes), BF16)] * one,
        cost_estimate=CHEAP,
        compiler_params=vmem(),
        name="split_sum",
    )(at, keep, got)


def merge_kernel(which, at_ref, a_ref, b_ref, c_ref, d_ref, *outs):
    for r, out in enumerate(outs):
        i = at_ref[which] ^ r
        total = a_ref[i].astype(F32) + b_ref[i].astype(F32)
        out[...] = (total + c_ref[i].astype(F32) + d_ref[i].astype(F32)).astype(BF16)


def merge_sum(at, which, pieces):
    count, rows, lanes = pieces[0].shape
    return pl.pallas_call(
        functools.partial(merge_kernel, which),
        in_specs=[SMEM] + [VMEM] * 4,
        out_shape=[jax.ShapeDtypeStruct((rows, lanes), BF16)] * count,
        cost_estimate=CHEAP,
        compiler_params=vmem(),
        name="merge_sum",
    )(at, *pieces)


def last_two_kernel(a_ref, b_ref, c_ref, d_ref, gin_ref, gdown_ref, gout_ref, bo, g2, bi, bd):
    total = a_ref[...].astype(F32) + b_ref[...].astype(F32)
    total = total + c_ref[...].astype(F32) + d_ref[...].astype(F32)
    for k in range(2):
        gin_ref[:, k * LANES : (k + 1) * LANES] = total[k * LANES : (k + 1) * LANES]
    for k in range(4):
        gdown_ref[:, k * LANES : (k + 1) * LANES] = total[256 + k * 64 : 320 + k * 64]
    gout_ref[...] = total[512:576]
    row = total[576:577]
    bo[...], g2[...], bi[...], bd[...] = row[:, 16:32], row[:, 32:48], row[:, 48:112], row[:, 112:]


def last_two(pieces):
    return pl.pallas_call(
        last_two_kernel,
        out_shape=[
            jax.ShapeDtypeStruct((LANES, 256), F32),
            jax.ShapeDtypeStruct((64, 512), F32),
            jax.ShapeDtypeStruct((64, LANES), F32),
            *(jax.ShapeDtypeStruct((1, n), F32) for n in (16, 16, 64, 16)),
        ],
        cost_estimate=CHEAP,
        compiler_params=vmem(),
        name="last_two",
    )(*pieces)


def last_one_kernel(a_ref, b_ref, c_ref, d_ref, gw_ref, gs_ref, g1_ref):
    total = a_ref[...].astype(F32) + b_ref[...].astype(F32)
    total = total + c_ref[...].astype(F32) + d_ref[...].astype(F32)
    gw_ref[...] = total[:192]
    gs_ref[...] = total[192:200]
    g1_ref[...] = total[200:201, :16]


def last_one(pieces):
    return pl.pallas_call(
        last_one_kernel,
        out_shape=[
            jax.ShapeDtypeStruct((192, LANES), F32),
            jax.ShapeDtypeStruct((8, LANES), F32),
            jax.ShapeDtypeStruct((1, 16), F32),
        ],
        cost_estimate=CHEAP,
        compiler_params=vmem(),
        name="last_one",
    )(*pieces)


def widen_keys(gmk):
    half = lax.broadcasted_iota(jnp.int32, (gmk.shape[0], LANES), 1) < HEAD_DIM
    zero = jnp.zeros((gmk.shape[0], LANES), gmk.dtype)
    wide = []
    for pair in range(PAIRS):
        tile = gmk[:, pair * LANES : (pair + 1) * LANES]
        wide += [jnp.where(half, tile, zero), jnp.where(half, zero, tile)]
    return jnp.concatenate(wide, axis=1)


def weight_kernel(
    fast, at_ref, ql_ref, qh_ref, kvl_ref, kvh_ref, n_ref, wq_ref, wkv_ref, gm_ref,
    pa, pb, pc, pd, pe, halo_ref, gain_ref, gs_ref, keep_ref, send_ref, acc_q, acc_kv,
):
    @pl.when(pl.program_id(0) == 0)
    def _():
        means = jnp.concatenate([ref[:, 2 * D :] for ref in (pa, pb, pc, pd, pe)], axis=0)
        means = means.astype(BF16)
        grads = (gm_ref[...] * float(BLOCK)).astype(BF16)
        acc_q[...] = mm(grads[:, :D], means, TN)
        acc_kv[...] = halo_ref[...] + mm(widen_keys(grads[:, D:]), means, TN)

    normed = n_ref[...]
    cut = ql_ref.shape[1]
    for lo, q_ref, kv_ref in ((0, ql_ref, kvl_ref), (cut, qh_ref, kvh_ref)):
        hi = lo + q_ref.shape[1]
        acc_q[lo:hi, :] += mm(q_ref[...].T, normed)
        acc_kv[2 * lo : 2 * hi, :] += mm(kv_ref[...].T, normed)

    @pl.when(pl.program_id(0) == pl.num_programs(0) - 1)
    def _():
        gain = jnp.sum(acc_q[...] * wq_ref[...].astype(F32), axis=0, keepdims=True)
        gain = gain + jnp.sum(acc_kv[...] * wkv_ref[...].astype(F32), axis=0, keepdims=True)
        gain = gain / gain_ref[...]
        if not fast:
            keep_ref[:D, :] = acc_q[...]
            keep_ref[D:, :] = acc_kv[...]
            send_ref[...] = jnp.broadcast_to(gain, (8, D))
            return
        def owner(own, h, z, b, c):
            ref = keep_ref if own else send_ref
            lanes = slice(h * LANES, (h + 1) * LANES)
            ref[z, h, :64, :] = acc_q[rows_at(b, 64), lanes].astype(BF16)
            ref[z, h, 64:128, :] = acc_kv[rows_at(2 * b + c, 64), lanes].astype(BF16)
            ref[z, h, 128:192, :] = acc_kv[rows_at(2 * b + 1 - c, 64), lanes].astype(BF16)
            share = pltpu.roll(
                jnp.broadcast_to(gain[:, lanes], (8, LANES)), lax.rem(LANES - 16 * b, LANES), 1
            )
            ref[z, h, 192:208, :] = jnp.concatenate(
                [gs_ref[h, rows_at(b, 8), :], share], axis=0
            ).astype(BF16)

        each_owner(at_ref, owner)


def weight_back(at, gq, gkv, normed, wt_q, wt_kv, gm, pieces, halo, gain, gsort, fast):
    tok = normed.shape[0]
    tile = 512
    parts = (4, 4, PIECE_ONE, LANES)
    shapes = (parts, parts) if fast else ((3 * D, D), (8, D))
    kind = BF16 if fast else F32
    rows = lambda width: pl.BlockSpec((tile, width), lambda i: (i, 0))
    return pl.pallas_call(
        functools.partial(weight_kernel, fast),
        grid=(tok // tile,),
        in_specs=[
            SMEM, *(rows(v.shape[1]) for v in (*gq, *gkv)), rows(D), once((D, D)),
            once((2 * D, D)), once(gm.shape), *(once(p.shape) for p in pieces),
            once((2 * D, D)), once((1, D)), once(gsort.shape),
        ],
        out_specs=[once(shapes[0]), once(shapes[1])],
        out_shape=[
            jax.ShapeDtypeStruct(shapes[0], kind),
            jax.ShapeDtypeStruct(shapes[1], kind),
        ],
        scratch_shapes=[pltpu.VMEM((D, D), F32), pltpu.VMEM((2 * D, D), F32)],
        cost_estimate=CHEAP,
        compiler_params=vmem(),
        name="weight_back",
    )(at, *gq, *gkv, normed, wt_q, wt_kv, gm, *pieces, halo, gain, gsort)


def finish_kernel(
    skip, x_ref, ql_ref, qh_ref, kvl_ref, kvh_ref, wq_ref, wkv_ref, gm_ref, fd, fe,
    one_ref, two_ref, g_ref, gain_ref, out_ref, total, blocks_ref,
):
    rows = x_ref.shape[0]
    per = rows // BLOCK

    @pl.when(pl.program_id(0) == 0)
    def _():
        own, ends = fd.shape[0], fe.shape[0]
        halo = own + ends
        blocks_ref[...] = gm_ref[halo : halo + own, :] + fd[...].astype(F32)
        blocks_ref[:ends, :] += fe[...].astype(F32)

    at = lax.broadcasted_iota(jnp.int32, (rows, rows), 0)
    lane = lax.broadcasted_iota(jnp.int32, (rows, rows), 1)
    order = (lane == lax.rem(at, BLOCK) * 8 + at // BLOCK).astype(F32).astype(BF16)
    value = mm(order, one_ref[...].reshape(rows, D))
    cut = ql_ref.shape[1]
    value = value + mm(ql_ref[...], wq_ref[:cut, :]) + mm(qh_ref[...], wq_ref[cut:, :])
    value = value + mm(kvl_ref[...], wkv_ref[: 2 * cut, :])
    value = value + mm(kvh_ref[...], wkv_ref[2 * cut :, :])
    grads = blocks_ref[pl.ds(pl.multiple_of(pl.program_id(0) * per, per), per), :].astype(BF16)
    block = mm(grads[:, :D], wq_ref[...]) + mm(widen_keys(grads[:, D:]), wkv_ref[...])
    value = value + jnp.broadcast_to(block[:, None, :], (per, BLOCK, D)).reshape(rows, D)
    total[...] = value

    @pl.when(pl.program_id(0) >= skip)
    def _():
        total[...] += mm(order, two_ref[...].reshape(rows, D))

    x = x_ref[...].astype(F32)
    centre = x - jnp.mean(x, axis=-1, keepdims=True)
    inverse = lax.rsqrt(jnp.mean(centre * centre, axis=-1, keepdims=True) + EPSILON)
    hat = centre * inverse
    du = total[...] * gain_ref[...]
    inner = jnp.mean(du * hat, axis=-1, keepdims=True)
    out_ref[...] = g_ref[...] + inverse * (
        du - jnp.mean(du, axis=-1, keepdims=True) - hat * inner
    )


def finish(x, gq, gkv, wt_q, wt_kv, gm, far, one, two, g_middle, gain):
    tok = x.shape[0]
    tile = 8 * BLOCK
    skip = (tok // BLOCK - two.shape[1]) // 8
    rows = lambda width: pl.BlockSpec((tile, width), lambda i: (i, 0))
    return pl.pallas_call(
        functools.partial(finish_kernel, skip),
        grid=(tok // tile,),
        in_specs=[
            rows(D), *(rows(v.shape[1]) for v in (*gq, *gkv)), once((D, D)), once((2 * D, D)),
            once(gm.shape), *(once(f.shape) for f in far),
            pl.BlockSpec((BLOCK, 8, D), lambda i: (0, i, 0)),
            pl.BlockSpec((BLOCK, 8, D), lambda i: (0, jnp.maximum(i - skip, 0), 0)),
            rows(D), once((1, D)),
        ],
        out_specs=rows(D),
        out_shape=jax.ShapeDtypeStruct((tok, D), F32),
        scratch_shapes=[
            pltpu.VMEM((tile, D), F32),
            pltpu.VMEM((tok // BLOCK, 2 * D), F32),
        ],
        cost_estimate=CHEAP,
        compiler_params=vmem(),
        name="finish",
    )(x, *gq, *gkv, wt_q, wt_kv, gm, *far, one, two, g_middle, gain)


class Grid:
    def __init__(self):
        self.heads = lax.axis_size("head")
        self.planes = lax.axis_size("plane")
        self.cycles = 2 * self.planes
        self.head = lax.axis_index("head")
        self.plane = lax.axis_index("plane")
        self.core = lax.axis_index("core")
        self.cycle = 2 * self.plane + self.core
        self.place = self.cycle * self.heads + self.head

    def send(self, value, pairs):
        return lax.ppermute(value, ("head", "plane", "core"), pairs)

    def number(self, head, cycle):
        return head * self.cycles + cycle

    def along(self, steps):
        count = self.heads * self.cycles
        at = lambda place: self.number(place % self.heads, place // self.heads)
        return [(at(i), at(i + steps)) for i in range(count) if 0 <= i + steps < count]

    def swap_head(self, flip):
        return [
            (self.number(h, b), self.number(h ^ flip, b))
            for h in range(self.heads)
            for b in range(self.cycles)
        ]

    def swap_plane(self, flip):
        return [
            (self.number(h, b), self.number(h, b ^ (2 * flip)))
            for h in range(self.heads)
            for b in range(self.cycles)
        ]

    def swap_core(self):
        return [
            (self.number(h, b), self.number(h, b ^ 1))
            for h in range(self.heads)
            for b in range(self.cycles)
        ]


def in_order(pieces, index):
    stacked = jnp.stack(pieces)
    count = len(pieces)
    bit = 1
    while bit < count:
        swapped = jnp.stack([stacked[i ^ bit] for i in range(count)])
        stacked = jnp.where((index & bit) != 0, swapped, stacked)
        bit *= 2
    return stacked


def gather_all(grid, piece):
    got = [piece] + [grid.send(piece, grid.swap_plane(r)) for r in range(1, grid.planes)]
    got = in_order(got, grid.plane)
    got = [got] + [grid.send(got, grid.swap_head(r)) for r in range(1, grid.heads)]
    got = in_order(got, grid.head)
    got = in_order([got, grid.send(got, grid.swap_core())], grid.core)
    got = got.transpose(1, 2, 0, *range(3, got.ndim))
    return got.reshape(grid.heads, grid.cycles, *piece.shape)


def across_planes(parts):
    return lax.all_to_all(parts, "plane", 0, 0, tiled=True)


def across_heads(parts):
    return lax.all_to_all(parts, "head", 0, 0, tiled=True)


def scatter_sum(grid, parts):
    mine = lax.dynamic_index_in_dim(parts, grid.core, 0, keepdims=False)
    other = lax.dynamic_index_in_dim(parts, 1 - grid.core, 0, keepdims=False)
    got = grid.send(other, grid.swap_core())
    total = (mine.astype(F32) + got.astype(F32)).astype(BF16)
    total = jnp.sum(across_heads(total).astype(F32), axis=0).astype(BF16)
    return jnp.sum(across_planes(total).astype(F32), axis=0)


def as_rows(value):
    flat = value.reshape(-1)
    short = -flat.shape[0] % LANES
    return jnp.pad(flat, (0, short)).reshape(-1, LANES)


def by_owner(grid, value):
    columns, rows = value.shape
    cut = value.reshape(grid.planes, 2, columns // grid.cycles, grid.heads, rows // grid.heads)
    return cut.transpose(1, 3, 0, 2, 4)


def vector_by_owner(grid, value):
    cut = value.reshape(grid.heads, grid.planes, 2, -1)
    return cut.transpose(2, 0, 1, 3)


def rows_of(value):
    lead = value.shape[:3]
    flat = value.reshape(*lead, -1)
    short = -flat.shape[-1] % LANES
    flat = jnp.pad(flat, ((0, 0),) * 3 + ((0, short),))
    return flat.reshape(*lead, -1, LANES)


def after(value, *others):
    return lax.optimization_barrier((value, *others))[0]


def weights_slow(grid, vectors, parameters):
    w_qkv, w_sort, w_in, w_down, w_out = parameters
    heads, cycles = grid.heads, grid.cycles
    first = jnp.concatenate([as_rows(w_qkv.T), as_rows(w_sort), as_rows(jnp.concatenate(vectors))])
    wide, sort_rows = as_rows(w_qkv.T).shape[0], as_rows(w_sort).shape[0]
    got = gather_all(grid, first)
    span = w_qkv.shape[1]
    wt_qkv = (
        got[:, :, :wide]
        .reshape(heads, cycles, span, D // heads)
        .transpose(1, 2, 0, 3)
        .reshape(HEADS, 3, HEAD_DIM, D)
    )
    wt_q = wt_qkv[:, 0].reshape(D, D)
    paired = wt_qkv.reshape(PAIRS, 2, 3, HEAD_DIM, D)
    wt_kv = jnp.stack(
        [paired[:, 0, 1], paired[:, 0, 2], paired[:, 1, 2], paired[:, 1, 1]], axis=1
    ).reshape(2 * D, D)
    size = w_sort.shape[0] * w_sort.shape[1]
    w_pairs = (
        got[:, :, wide : wide + sort_rows]
        .reshape(heads, cycles, -1)[:, :, :size]
        .reshape(heads, cycles, *w_sort.shape)
        .transpose(1, 3, 0, 2)
        .reshape(HEAD_DIM, PAIRS, LANES)
        .transpose(1, 0, 2)
        .astype(F32)
    )
    flat = got[:, :, wide + sort_rows :].reshape(heads, cycles, -1)
    sizes = [v.shape[0] for v in vectors]
    cuts = [sum(sizes[:i]) for i in range(len(sizes) + 1)]
    rows = [
        flat[:, :, cuts[i] : cuts[i + 1]].reshape(1, -1).astype(F32) for i in range(len(sizes))
    ]
    second = jnp.concatenate([as_rows(w_in.T), as_rows(w_down.T), as_rows(w_out.T)])
    in_rows, down_rows = as_rows(w_in.T).shape[0], as_rows(w_down.T).shape[0]
    got = gather_all(grid, second)

    def whole(depth, columns, part):
        return (
            part.reshape(heads, cycles, -1)[:, :, : columns // cycles * (depth // heads)]
            .reshape(heads, cycles, columns // cycles, depth // heads)
            .transpose(1, 2, 0, 3)
            .reshape(columns, depth)
        )

    feed = (
        whole(D, FF, got[:, :, :in_rows]),
        whole(FF, D, got[:, :, in_rows : in_rows + down_rows]),
        whole(D, D, got[:, :, in_rows + down_rows :]),
    )
    return wt_q, wt_kv, w_pairs, rows, feed


def matrix(rows, shape):
    flat = rows.reshape(-1)[: shape[0] * shape[1]]
    return flat.reshape(shape[1], shape[0]).T


def gradients_two_slow(grid, acc_in, acc_down, acc_out, sums, parameters, vectors):
    w_qkv, w_sort, w_in, w_down, w_out = parameters
    low = [
        rows_of(by_owner(grid, v.astype(BF16))) for v in (acc_in.transpose(0, 2, 1).reshape(FF, D), acc_down, acc_out)
    ]
    order = ((0, D), (1, D), (4, FF), (3, D))
    small = [vector_by_owner(grid, sums[i, :n]) for i, n in order]
    low.append(rows_of(jnp.concatenate(small, axis=-1).astype(BF16)))
    total = scatter_sum(grid, jnp.concatenate(low, axis=3))
    cuts = [0]
    for item in low:
        cuts.append(cuts[-1] + item.shape[3])
    g_in, g_down, g_out = (
        matrix(total[cuts[i] : cuts[i + 1]], w.shape) for i, w in enumerate((w_in, w_down, w_out))
    )
    flat = total[cuts[3] :].reshape(-1)
    sizes = [v.shape[0] for v in vectors[1:]]
    at = [sum(sizes[:i]) for i in range(5)]
    return g_in, g_down, g_out, *(flat[at[i] : at[i + 1]] for i in range(4))


def gradients_one_slow(grid, both, gain, gsort, parameters, vectors):
    w_qkv, w_sort = parameters[:2]
    q = both[:D].reshape(HEADS, HEAD_DIM, D)
    kv = both[D:].reshape(PAIRS, 4, HEAD_DIM, D)
    k = jnp.stack([kv[:, 0], kv[:, 3]], axis=1).reshape(HEADS, HEAD_DIM, D)
    v = jnp.stack([kv[:, 1], kv[:, 2]], axis=1).reshape(HEADS, HEAD_DIM, D)
    wide = jnp.stack([q, k, v], axis=1).reshape(3 * D, D)
    sort = gsort.transpose(0, 2, 1).reshape(grid.heads, D // grid.heads, grid.planes, 2, -1)
    low = [
        rows_of(by_owner(grid, wide.astype(BF16))),
        rows_of(sort.transpose(3, 0, 2, 1, 4).astype(BF16)),
        rows_of(vector_by_owner(grid, gain[0]).astype(BF16)),
    ]
    total = scatter_sum(grid, jnp.concatenate(low, axis=3))
    one, two = low[0].shape[3], low[0].shape[3] + low[1].shape[3]
    size = w_sort.shape[0] * w_sort.shape[1]
    return (
        matrix(total[:one], w_qkv.shape),
        total[one:two].reshape(-1)[:size].reshape(w_sort.shape),
        total[two:].reshape(-1)[: vectors[0].shape[0]],
    )


def per_device(
    tokens, cotangent, doc_lengths, norm_gain1, w_qkv, w_out, b_out, norm_gain2, w_in, b_in,
    w_down, b_down, w_sort,
):
    grid = Grid()
    heads = grid.heads
    x = tokens[0]
    upstream = cotangent[0]
    tok = x.shape[0]
    own = tok // BLOCK
    context = HALO + own
    window = HALO + own + HALO
    second = HALO - own
    fast = heads == 4 and grid.cycles == 8
    at = jnp.stack([grid.head, grid.plane, grid.core]).astype(jnp.int32)
    vectors = (norm_gain1, b_out, norm_gain2, b_in, b_down)
    parameters = (w_qkv, w_sort, w_in, w_down, w_out)

    three = range(1, 4)
    tail = second * BLOCK
    if fast:
        one, two, x_tail = pack(w_qkv, w_sort, vectors, w_in, w_down, w_out, x, tail)
        ones = [one] + [grid.send(one, grid.swap_plane(r)) for r in three]
        ones = jnp.stack(ones)
        ones = [ones] + [grid.send(ones, grid.swap_head(r)) for r in three]
        x_send, x_tail = lax.optimization_barrier((x, x_tail, *ones))[:2]
    else:
        x_send, x_tail = x, x[tok - tail :]
    halo_one = grid.send(x_send, grid.along(1))
    halo_two = grid.send(x_tail, grid.along(2))
    if fast:
        ones = jnp.stack(ones)
        other = grid.send(ones, grid.swap_core())
        two = after(two, other)
        twos = [two] + [grid.send(two, grid.swap_plane(r)) for r in three]
        wt_q, wt_kv, w_pairs, *rows = assemble(at, ones, other)
    else:
        wt_q, wt_kv, w_pairs, rows, feed_weights = weights_slow(grid, vectors, parameters)
        twos = []
    gain_one, bias_out, gain_two, bias_in, bias_down = rows

    normed, q, kv, means, means_head, means_tail = project(x, gain_one, wt_q, wt_kv, second)
    blocked = lambda value: value.reshape(-1, BLOCK, D)
    (kv_own,) = context_project((blocked(x),), after(gain_one, means), wt_kv, False)
    means_send, means_head, means_tail = lax.optimization_barrier(
        (means, means_head, means_tail, halo_one, halo_two, kv_own, *twos)
    )[:3]
    pieces = (
        grid.send(means_tail, grid.along(2)),
        grid.send(means_send, grid.along(1)),
        means,
        grid.send(means_send, grid.along(-1)),
        grid.send(means_head, grid.along(-2)),
    )
    kv_halo, normed_halo = context_project(
        (blocked(halo_two), blocked(halo_one)), after(gain_one, kv_own), wt_kv, True
    )
    if fast:
        twos = jnp.stack(lax.optimization_barrier((*twos, *pieces, kv_halo))[:4])
        twos = [twos] + [grid.send(twos, grid.swap_head(r)) for r in three]

    begin = grid.place * own
    position = begin - HALO + jnp.arange(window, dtype=jnp.int32)
    doc_ends = jnp.cumsum(doc_lengths, dtype=jnp.int32)
    ended = jnp.sum(
        (doc_ends[None, :] <= position[:, None]).astype(jnp.int32), axis=1, dtype=jnp.int32
    )
    span_end = (grid.cycle + 1) * heads * own
    doc = jnp.where((position >= 0) & (position < span_end), ended, -1)
    fold = window - LANES
    docc = jnp.stack([doc[:LANES], jnp.concatenate([doc[LANES:], doc[fold:LANES]])])
    docn = doc[:, None]
    live = (doc[HALO:context] == doc[HALO - 1 : context - 1]) & (doc[HALO:context] >= 0)
    live = jnp.repeat(live.astype(F32), BLOCK).reshape(tok // LANES, LANES)

    plan, *kept = sink_forward(pieces, after(w_pairs, kv_halo), docn, docc, own, context)
    attended, skv = attend(q, kv, kv_halo, kv_own, plan, live)
    if fast:
        twos = jnp.stack(lax.optimization_barrier((*twos, attended))[:4])
        feed_weights = (twos, grid.send(twos, grid.swap_core()))

    if fast:
        output, g_middle, g_att, keep, send = feed_fast(
            at, x, attended, upstream, bias_out, gain_two, bias_in, bias_down, *feed_weights
        )
        got = grid.send(send, grid.swap_core())
    else:
        output, g_middle, g_att, *sums = feed_slow(
            x, attended, upstream, bias_out, gain_two, bias_in, bias_down, *feed_weights
        )
        g_in, g_down, g_out, g_b_out, g_gain_two, g_b_in, g_b_down = gradients_two_slow(
            grid, *sums, parameters, vectors
        )
        twos = []

    gq_low, gkv_low, gh_low, gplan_low = attend_back(
        q, kv, skv, g_att, kv_halo, kv_own, plan, live, 0, 1
    )
    if fast:
        twos = split_sum(at, 0, after(keep, gh_low), got)
        g_att = after(g_att, *twos)
        twos = [twos[0]] + [grid.send(twos[r], grid.swap_head(r)) for r in three]
    gq_high, gkv_high, gh_high, gplan_high = attend_back(
        q, kv, skv, g_att, kv_halo, kv_own, plan, live, 1, PAIRS - 1
    )
    gq, gkv = (gq_low, gq_high), (gkv_low, gkv_high)
    gmeans, gsort, *sends = sink_backward(
        pieces, w_pairs, *kept, gplan_low, gplan_high, own, context
    )
    if fast:
        twos = merge_sum(at, 1, lax.optimization_barrier((*twos, gmeans))[:4])
        gh_high = after(gh_high, *twos)
        twos = [twos[0]] + [grid.send(twos[r], grid.swap_plane(r)) for r in three]
    gn_far, gn_near, g_kv_halo = halo_back(
        gh_low, gh_high, normed_halo, wt_q, wt_kv, gmeans, second
    )
    sends = lax.optimization_barrier((*sends, gn_near))[:2]
    far = [grid.send(value, grid.along(step)) for value, step in zip(sends, (1, 2))]
    gn_far, gn_near = lax.optimization_barrier((gn_far, gn_near, *far, *twos))[:2]
    back_one = grid.send(gn_near, grid.along(-1))
    back_two = grid.send(gn_far, grid.along(-2))
    gmeans = after(gmeans, gn_near)
    keep, send = weight_back(
        at, gq, gkv, normed, wt_q, wt_kv, gmeans, pieces, g_kv_halo, gain_one, gsort, fast
    )
    if fast:
        got = grid.send(send, grid.swap_core())
        ones = split_sum(at, 1, keep, got)
        ones = [ones[0]] + [grid.send(ones[r], grid.swap_plane(r)) for r in three]
        ones = merge_sum(at, 0, ones)
        ones = [ones[0]] + [grid.send(ones[r], grid.swap_head(r)) for r in three]
    input_grad = finish(
        x, gq, gkv, wt_q, wt_kv, gmeans, far, back_one, back_two, g_middle, gain_one
    )
    if fast:
        g_wqkv, g_sort, g_gain_one = last_one(lax.optimization_barrier((*ones, input_grad))[:4])
        g_in, g_down, g_out, *small = last_two(twos)
        g_wqkv, g_sort, g_down, g_out = g_wqkv.T, g_sort.T, g_down.T, g_out.T
        g_gain_one = g_gain_one[0]
        g_b_out, g_gain_two, g_b_in, g_b_down = (value[0] for value in small)
    else:
        g_wqkv, g_sort, g_gain_one = gradients_one_slow(
            grid, keep, send, gsort, parameters, vectors
        )
    return (
        output[None], input_grad[None], g_gain_one, g_wqkv, g_out, g_b_out, g_gain_two, g_in,
        g_b_in, g_down, g_b_down, g_sort,
    )


def solution(mesh):
    heads, cycles = mesh.shape["head"], mesh.shape["blk"]
    fine = Mesh(mesh.devices.reshape(heads, cycles // 2, 2), ("head", "plane", "core"))
    both = P(("head", "plane", "core"))
    split = P("head", ("plane", "core"))
    stream = P(("plane", "core"), "head", None)
    return jax.shard_map(
        per_device,
        mesh=fine,
        in_specs=(
            stream, stream, P(), both, split, split, both, both, split, both, split, both, split,
        ),
        out_specs=(
            stream, stream, both, split, split, both, both, split, both, split, both, split,
        ),
        check_vma=False,
    )
```

```python
import functools

import jax
import jax.numpy as jnp
from jax import lax
from jax.experimental import pallas as pl
from jax.experimental.pallas import tpu as pltpu
from jax.sharding import Mesh
from jax.sharding import PartitionSpec as P

D = 512
HEADS = 8
HEAD_DIM = 64
FF = 2048
BLOCK = 32
SINK_ITERS = 8
DOC_MOST = 62
LANES = 128
PAIRS = HEADS // 2
HALO = 64
GROUPS = 4
CHEAP = pl.CostEstimate(flops=0, transcendentals=0, bytes_accessed=0)
EPSILON = 1e-05
NEGATIVE = -1e30
FLOOR = -1e20
LOG2E = 1.4426950408889634
TINY = 1e-37
F32 = jnp.float32
BF16 = jnp.bfloat16
NT = (((1,), (1,)), ((), ()))
NN = (((1,), (0,)), ((), ()))
TN = (((0,), (0,)), ((), ()))


def mm(a, b, dims=NN):
    return lax.dot_general(a, b, dims, preferred_element_type=F32)


def vmem(limit=56):
    return pltpu.CompilerParams(vmem_limit_bytes=limit * 1024 * 1024)


def once(shape):
    return pl.BlockSpec(shape, lambda *i: (0,) * len(shape), pipeline_mode=pl.Buffered(1))


def halves(value):
    high = value.astype(BF16)
    return high, (value - high.astype(F32)).astype(BF16)


def mm3(a, b, dims):
    (da,), (db,) = dims[0]
    ah, al = halves(a)
    bh, bl = halves(b)
    return mm(
        jnp.concatenate([ah, al, ah], axis=da), jnp.concatenate([bh, bh, bl], axis=db), dims
    )


def sink_mask(docn_ref, docc_ref, window, context):
    first = context
    fold = window - LANES
    lane = lax.broadcasted_iota(jnp.int32, (1, LANES), 1)
    docn = docn_ref[...]
    row = lax.broadcasted_iota(jnp.int32, (window, 1), 0)
    col = jnp.where((row >= first) & (lane < fold), lane + LANES, lane)
    docc = jnp.where(row >= first, docc_ref[1:2, :], docc_ref[0:1, :])
    return (docn == docc) & (docn >= 0) & (col < row)


def fold_pair(top, low, fold, join):
    lane = lax.broadcasted_iota(jnp.int32, (1, LANES), 1)
    both = join(top, low)
    return jnp.where(lane < fold, top, both), jnp.where(lane < fold, low, both)


def sink_weight(pair, odd):
    lane = lax.broadcasted_iota(jnp.int32, pair.shape, 1)
    zero = jnp.zeros_like(pair)
    if odd:
        return jnp.concatenate([zero, jnp.where(lane >= HEAD_DIM, pair, zero)], axis=0)
    return jnp.concatenate([jnp.where(lane < HEAD_DIM, pair, zero), zero], axis=0)


def refold(keys, fold):
    return jnp.concatenate([keys[LANES:], keys[fold:LANES]], axis=0)


def row_step(values):
    highest = jnp.maximum(jnp.max(values, axis=1, keepdims=True), FLOOR)
    total = jnp.sum(jnp.exp2(values - highest), axis=1, keepdims=True)
    return values - (highest + LOG2E * jnp.log(jnp.maximum(total, TINY)))


def column_step(values, context, fold):
    top, low = values[:context], values[context:]
    h1, h2 = fold_pair(
        jnp.max(top, axis=0, keepdims=True),
        jnp.max(low, axis=0, keepdims=True),
        fold,
        jnp.maximum,
    )
    h1, h2 = jnp.maximum(h1, FLOOR), jnp.maximum(h2, FLOOR)
    e1, e2 = jnp.exp2(top - h1), jnp.exp2(low - h2)
    t1, t2 = fold_pair(
        jnp.sum(e1, axis=0, keepdims=True), jnp.sum(e2, axis=0, keepdims=True), fold, jnp.add
    )
    t1, t2 = jnp.maximum(t1, TINY), jnp.maximum(t2, TINY)
    moved = jnp.concatenate(
        [top - (h1 + LOG2E * jnp.log(t1)), low - (h2 + LOG2E * jnp.log(t2))], axis=0
    )
    scales = jnp.concatenate([jnp.exp2(h1), jnp.exp2(h2), 1.0 / t1, 1.0 / t2], axis=0)
    return moved, e1, e2, scales


def sink_forward_kernel(
    own, context, a, b, c, d, e, w_ref, docn_ref, docc_ref, plan_ref, kept_ref, scale_ref, proj_ref,
    q_ref, k_ref, vals, kept, sems,
):
    window = q_ref.shape[1]
    fold = window - LANES
    at = 0
    for piece in (a, b, c, d, e):
        rows = piece.shape[0]
        for pair in range(PAIRS):
            q_ref[pair, at : at + rows, :] = piece[:, pair * LANES : (pair + 1) * LANES]
            k_ref[pair, at : at + rows, :] = piece[:, D + pair * LANES : D + (pair + 1) * LANES]
        at += rows

    def logits(pair, carry):
        permitted = sink_mask(docn_ref, docc_ref, window, context)
        queries, keys = q_ref[pair], k_ref[pair]
        keys_two = refold(keys, fold)
        for odd in range(2):
            projected = mm3(queries, sink_weight(w_ref[pair], odd), NT)
            proj_ref[2 * pair + odd] = projected
            top = mm3(projected[:context], keys[:LANES], NT)
            low = mm3(projected[context:], keys_two, NT)
            vals[2 * pair + odd] = jnp.where(
                permitted, LOG2E * jnp.concatenate([top, low], axis=0), NEGATIVE
            )
        return carry

    lax.fori_loop(0, PAIRS, logits, 0)

    def send(step):
        return pltpu.make_async_copy(kept.at[step], kept_ref.at[step], sems.at[step])

    def step(turn, carry):
        for head in range(HEADS):
            moved, top, low, scales = column_step(row_step(vals[head]), context, fold)
            kept[turn, head, :context, :] = top
            kept[turn, head, context:, :] = low
            scale_ref[turn, head] = scales
            vals[head] = moved
        send(turn).start()
        return carry

    lax.fori_loop(0, SINK_ITERS, step, 0)
    for head in range(HEADS):
        plan_ref[head] = (
            kept[SINK_ITERS - 1, head, context - own : context, :]
            * scale_ref[SINK_ITERS - 1, head, 2:3, :]
        ).astype(BF16)
    lax.fori_loop(0, SINK_ITERS, lambda turn, carry: (send(turn).wait(), carry)[1], 0)


def sink_backward_kernel(
    own, context, a, b, c, d, e, w_ref, kept_ref, scale_ref, proj, gl_ref, gh_ref,
    gm_ref, gw_ref, sd, se, q_ref, k_ref, vals, gq, gk, kept, sems,
):
    window = q_ref.shape[1]
    fold = window - LANES

    def fetch(step):
        return pltpu.make_async_copy(kept_ref.at[step], kept.at[step], sems.at[step])

    def begin(turn, carry):
        fetch(SINK_ITERS - 1 - turn).start()
        return carry

    lax.fori_loop(0, SINK_ITERS, begin, 0)
    at = 0
    for piece in (a, b, c, d, e):
        rows = piece.shape[0]
        for pair in range(PAIRS):
            q_ref[pair, at : at + rows, :] = piece[:, pair * LANES : (pair + 1) * LANES]
            k_ref[pair, at : at + rows, :] = piece[:, D + pair * LANES : D + (pair + 1) * LANES]
        at += rows

    def back(turn, carry):
        at = SINK_ITERS - 1 - turn
        fetch(at).wait()

        @pl.when(turn == 0)
        def _():
            for head in range(HEADS):
                low = gl_ref.shape[0]
                ref, index = (gl_ref, head) if head < low else (gh_ref, head - low)
                vals[head, : context - own, :] = jnp.zeros((context - own, LANES), F32)
                vals[head, context - own : context, :] = (
                    ref[index]
                    * kept[SINK_ITERS - 1, head, context - own : context, :]
                    * scale_ref[SINK_ITERS - 1, head, 2:3, :]
                )
                vals[head, context:, :] = jnp.zeros((window - context, LANES), F32)

        for head in range(HEADS):
            g1, g2 = vals[head, :context, :], vals[head, context:, :]
            s1, s2 = fold_pair(
                jnp.sum(g1, axis=0, keepdims=True),
                jnp.sum(g2, axis=0, keepdims=True),
                fold,
                jnp.add,
            )
            scales = scale_ref[at, head]
            e1, e2 = kept[at, head, :context, :], kept[at, head, context:, :]
            g1, g2 = g1 - e1 * (s1 * scales[2:3]), g2 - e2 * (s2 * scales[3:4])
            r1, r2 = jnp.sum(g1, axis=1, keepdims=True), jnp.sum(g2, axis=1, keepdims=True)
            vals[head, :context, :] = g1 - (e1 * scales[0:1]) * r1
            vals[head, context:, :] = g2 - (e2 * scales[1:2]) * r2
        return carry

    lax.fori_loop(0, SINK_ITERS, back, 0)

    def products(pair, carry):
        queries, keys = q_ref[pair], k_ref[pair]
        keys_two = refold(keys, fold)
        turned = []
        gq_total = jnp.zeros((window, LANES), F32)
        gk_total = jnp.zeros((window, LANES), F32)
        for odd in range(2):
            head = 2 * pair + odd
            g1, g2 = vals[head, :context, :], vals[head, context:, :]
            against = jnp.concatenate(
                [mm3(g1, keys[:LANES], NN), mm3(g2, keys_two, NN)], axis=0
            )
            gq_total = gq_total + mm3(against, sink_weight(w_ref[pair], odd), NN)
            u1 = mm3(g1, proj[head, :context, :], TN)
            u2 = mm3(g2, proj[head, context:, :], TN)
            gk_total = gk_total + jnp.concatenate(
                [u1[:fold], u1[fold:] + u2[fold:], u2[:fold]], axis=0
            )
            turned.append(mm3(against, queries, TN))
        half = lax.broadcasted_iota(jnp.int32, (HEAD_DIM, LANES), 1) < HEAD_DIM
        gw_ref[pair] = jnp.where(half, turned[0][:HEAD_DIM], turned[1][HEAD_DIM:])
        gq[pair] = gq_total * (1.0 / BLOCK)
        gk[pair] = gk_total * (1.0 / BLOCK)
        return carry

    lax.fori_loop(0, PAIRS, products, 0)
    for pair in range(PAIRS):
        gm_ref[:, pair * LANES : (pair + 1) * LANES] = gq[pair]
        gm_ref[:, D + pair * LANES : D + (pair + 1) * LANES] = gk[pair]
    sd[...] = gm_ref[context : context + d.shape[0], :].astype(BF16)
    se[...] = gm_ref[context + d.shape[0] :, :].astype(BF16)


HBM = pl.BlockSpec(memory_space=pl.ANY)
VMEM = pl.BlockSpec(memory_space=pltpu.VMEM)
SMEM = pl.BlockSpec(memory_space=pltpu.SMEM)


def sink_forward(pieces, weight, docn, docc, own, context):
    window = sum(piece.shape[0] for piece in pieces)
    kept = (SINK_ITERS, HEADS, window, LANES)
    return pl.pallas_call(
        functools.partial(sink_forward_kernel, own, context),
        in_specs=[VMEM] * 8,
        out_specs=[VMEM, HBM, VMEM, VMEM],
        out_shape=[
            jax.ShapeDtypeStruct((HEADS, own, LANES), BF16),
            jax.ShapeDtypeStruct(kept, F32),
            jax.ShapeDtypeStruct((SINK_ITERS, HEADS, 4, LANES), F32),
            jax.ShapeDtypeStruct((HEADS, window, LANES), F32),
        ],
        scratch_shapes=[
            pltpu.VMEM((PAIRS, window, LANES), F32),
            pltpu.VMEM((PAIRS, window, LANES), F32),
            pltpu.VMEM((HEADS, window, LANES), F32),
            pltpu.VMEM(kept, F32),
            pltpu.SemaphoreType.DMA((SINK_ITERS,)),
        ],
        cost_estimate=CHEAP,
        compiler_params=vmem(),
        name="sink_forward",
    )(*pieces, weight, docn, docc)


def sink_backward(pieces, weight, kept, scales, projected, low, high, own, context):
    window = sum(piece.shape[0] for piece in pieces)
    return pl.pallas_call(
        functools.partial(sink_backward_kernel, own, context),
        in_specs=[VMEM] * 6 + [HBM] + [VMEM] * 4,
        out_shape=[
            jax.ShapeDtypeStruct((window, 2 * D), F32),
            jax.ShapeDtypeStruct((PAIRS, HEAD_DIM, LANES), F32),
            *(
                jax.ShapeDtypeStruct((pieces[i].shape[0], 2 * D), BF16)
                for i in (3, 4)
            ),
        ],
        scratch_shapes=[
            *[pltpu.VMEM((PAIRS, window, LANES), F32)] * 2,
            pltpu.VMEM((HEADS, window, LANES), F32),
            *[pltpu.VMEM((PAIRS, window, LANES), F32)] * 2,
            pltpu.VMEM(kept.shape, F32),
            pltpu.SemaphoreType.DMA((SINK_ITERS,)),
        ],
        cost_estimate=CHEAP,
        compiler_params=vmem(),
        name="sink_backward",
    )(*pieces, weight, kept, scales, projected, low, high)


def normalise(values):
    centre = values - jnp.mean(values, axis=-1, keepdims=True)
    spread = jnp.mean(centre * centre, axis=-1, keepdims=True)
    return centre * lax.rsqrt(spread + EPSILON)


def context_kernel(count, keep, *refs):
    gain_ref, w_ref, kvx_ref = refs[count : count + 3]
    x = jnp.concatenate([ref[...] for ref in refs[:count]], axis=0)
    blocks = x.shape[0]
    normed = normalise(x.astype(F32)) * gain_ref[...].reshape(1, 1, D)
    normed = normed.astype(BF16).reshape(blocks * 8, D)
    row = lax.broadcasted_iota(jnp.int32, (LANES, LANES), 0)
    lane = lax.broadcasted_iota(jnp.int32, (LANES, LANES), 1)
    turn = (lane == (row % 16) * 8 + row // 16).astype(F32).astype(BF16)
    turned = [
        mm(turn, normed[i * LANES : (i + 1) * LANES]).astype(BF16) for i in range(blocks // 16)
    ]
    rows = []
    for b in range(8):
        part = jnp.concatenate([part[b * 16 : (b + 1) * 16] for part in turned], axis=0)
        if keep:
            refs[count + 3][b] = part
        rows.append(part)
    rows = jnp.concatenate(rows, axis=0)
    for head in range(0, HEADS, 2):
        out = mm(rows, w_ref[head * LANES : (head + 2) * LANES, :], NT).astype(BF16)
        for b in range(8):
            for e in range(2):
                kvx_ref[head + e, :, b * LANES : (b + 1) * LANES] = out[
                    b * blocks : (b + 1) * blocks, e * LANES : (e + 1) * LANES
                ]


def context_project(values, gain, w_kv, keep):
    blocks = sum(v.shape[0] for v in values)
    outs = 2 if keep else 1
    return pl.pallas_call(
        functools.partial(context_kernel, len(values), keep),
        grid=(BLOCK // 8,),
        in_specs=[
            *(pl.BlockSpec((v.shape[0], 8, D), lambda i: (0, i, 0)) for v in values),
            pl.BlockSpec((1, D), lambda i: (0, 0)),
            pl.BlockSpec((2 * D, D), lambda i: (0, 0)),
        ],
        out_specs=[
            pl.BlockSpec((HEADS, blocks, 8 * LANES), lambda i: (0, 0, i)),
            pl.BlockSpec((8, blocks, D), lambda i: (i, 0, 0)),
        ][:outs],
        out_shape=[
            jax.ShapeDtypeStruct((HEADS, blocks, BLOCK * LANES), BF16),
            jax.ShapeDtypeStruct((BLOCK, blocks, D), BF16),
        ][:outs],
        cost_estimate=CHEAP,
        compiler_params=vmem(),
        name="context_halo" if keep else "context_own",
    )(*values, gain, w_kv)


def compact(values, lane_block):
    out = values[:BLOCK]
    for j in range(1, 4):
        out = jnp.where(lane_block == j, values[j * BLOCK : (j + 1) * BLOCK], out)
    return out


def spread(values, lane_block):
    zero = jnp.zeros_like(values)
    return jnp.concatenate([jnp.where(lane_block == j, values, zero) for j in range(4)], axis=0)


def softmax_pair(local, chosen, live):
    lane = lax.broadcasted_iota(jnp.int32, (BLOCK, LANES), 1)
    row = lax.broadcasted_iota(jnp.int32, (BLOCK, LANES), 0)
    local = jnp.where(row <= lax.rem(lane, BLOCK), local, NEGATIVE)
    chosen = jnp.where(live, chosen, NEGATIVE)
    highest = jnp.maximum(
        jnp.max(local, axis=0, keepdims=True), jnp.max(chosen, axis=0, keepdims=True)
    )
    el, es = jnp.exp(local - highest), jnp.exp(chosen - highest)
    total = jnp.sum(el, axis=0, keepdims=True) + jnp.sum(es, axis=0, keepdims=True)
    inverse = 1.0 / total
    return el * inverse, es * inverse


def half_mask(first):
    lane = lax.broadcasted_iota(jnp.int32, (LANES, LANES), 1)
    return (lane < HEAD_DIM) if first else (lane >= HEAD_DIM)


def attend_kernel(
    q_ref, kv_ref, kvh_ref, kvo_ref, plan_ref, live_ref, att_ref, skv_ref, even_ref, odd_ref
):
    own = plan_ref.shape[1]
    blocks = kvh_ref.shape[1] + own
    held = (even_ref, odd_ref)
    for e in range(2):
        plan = plan_ref[e][:, :blocks]
        for chunk in range(4):
            lanes = slice(chunk * 8 * LANES, (chunk + 1) * 8 * LANES)
            out = mm(plan, jnp.concatenate([kvh_ref[e, :, lanes], kvo_ref[e, :, lanes]], axis=0))
            for b in range(8):
                at = (chunk * 8 + b) * (own + 1)
                held[e][at : at + own, :] = out[:, b * LANES : (b + 1) * LANES]
    lane_block = lax.broadcasted_iota(jnp.int32, (BLOCK, LANES), 1) // BLOCK
    lane_half = [half_mask(True), half_mask(False)]

    def group(turn, carry):
        chains = [(turn * GROUPS + i, e) for i in range(GROUPS) for e in range(2)]
        starts = [pl.multiple_of(g * LANES, LANES) for g, _ in chains]
        both, scores = [], []
        for (g, e), start in zip(chains, starts):
            local = kv_ref[pl.ds(start, LANES), e * LANES : (e + 1) * LANES]
            chosen = jnp.concatenate(
                [held[e][pl.ds(4 * g + i, BLOCK, stride=own + 1), :] for i in range(4)], axis=0
            ).astype(BF16)
            skv_ref[pl.ds(start, LANES), e * LANES : (e + 1) * LANES] = chosen
            both.append(jnp.concatenate([local, chosen], axis=0))
        for (g, e), start, kv in zip(chains, starts, both):
            q = q_ref[pl.ds(start, LANES), :] * 0.125
            qm = jnp.where(lane_half[e], q, jnp.zeros_like(q))
            out = mm(kv, qm, NT)
            scores.append((compact(out[:LANES], lane_block), compact(out[LANES:], lane_block)))
        weights = []
        for (g, e), (local, chosen) in zip(chains, scores):
            weights.append(softmax_pair(local, chosen, live_ref[pl.ds(g, 1), :] > 0.0))
        outs = []
        for (g, e), kv, (wl, ws) in zip(chains, both, weights):
            wide = jnp.concatenate(
                [spread(wl.astype(BF16), lane_block), spread(ws.astype(BF16), lane_block)], axis=0
            )
            turned = kv.T
            outs.append(mm(turned[HEAD_DIM:] if e == 0 else turned[:HEAD_DIM], wide))
        for i in range(GROUPS):
            att_ref[pl.ds(starts[2 * i], LANES), :] = jnp.concatenate(
                outs[2 * i : 2 * i + 2], axis=0
            ).T.astype(BF16)
        return carry

    lax.fori_loop(0, own // 4 // GROUPS, group, 0)


def attend(q, kv, kvh, kvo, plan, live):
    tok, own, halo = q.shape[0], plan.shape[1], kvh.shape[1]
    return pl.pallas_call(
        attend_kernel,
        grid=(PAIRS,),
        in_specs=[
            pl.BlockSpec((tok, LANES), lambda j: (0, j)),
            pl.BlockSpec((tok, 2 * LANES), lambda j: (0, j)),
            pl.BlockSpec((2, halo, BLOCK * LANES), lambda j: (j, 0, 0)),
            pl.BlockSpec((2, own, BLOCK * LANES), lambda j: (j, 0, 0)),
            pl.BlockSpec((2, own, LANES), lambda j: (j, 0, 0)),
            pl.BlockSpec((tok // LANES, LANES), lambda j: (0, 0)),
        ],
        out_specs=[
            pl.BlockSpec((tok, LANES), lambda j: (0, j)),
            pl.BlockSpec((tok, 2 * LANES), lambda j: (0, j)),
        ],
        out_shape=[
            jax.ShapeDtypeStruct((tok, D), BF16),
            jax.ShapeDtypeStruct((tok, 2 * D), BF16),
        ],
        scratch_shapes=[pltpu.VMEM((BLOCK * (own + 1), LANES), F32)] * 2,
        cost_estimate=CHEAP,
        compiler_params=vmem(),
        name="attend",
    )(q, kv, kvh, kvo, plan, live)


def attend_back_kernel(
    q_ref, kv_ref, skv_ref, go_ref, kvh_ref, kvo_ref, plan_ref, live_ref,
    gq_ref, gkv_ref, gh_ref, gp_ref, even_ref, odd_ref, leven_ref, lodd_ref,
):
    own = plan_ref.shape[1]
    halo = kvh_ref.shape[1]
    blocks = halo + own
    held = (even_ref, odd_ref)
    lheld = (leven_ref, lodd_ref)
    lane_block = lax.broadcasted_iota(jnp.int32, (BLOCK, LANES), 1) // BLOCK
    lane_half = [half_mask(True), half_mask(False)]

    def group(turn, carry):
        chains = [(turn * GROUPS + i, e) for i in range(GROUPS) for e in range(2)]
        starts = [pl.multiple_of(g * LANES, LANES) for g, _ in chains]
        both, right, scores = [], [], []
        for (g, e), start in zip(chains, starts):
            lanes = slice(e * LANES, (e + 1) * LANES)
            rows = pl.ds(start, LANES)
            both.append(jnp.concatenate([kv_ref[rows, lanes], skv_ref[rows, lanes]], axis=0))
            q = q_ref[rows, :] * 0.125
            go = go_ref[rows, :]
            go = jnp.concatenate([go[:, HEAD_DIM:], go[:, :HEAD_DIM]], axis=1)
            qm = jnp.where(lane_half[e], q, jnp.zeros_like(q))
            gm = jnp.where(lane_half[1 - e], go, jnp.zeros_like(go))
            right.append(jnp.concatenate([qm, gm], axis=0))
        for kv, other in zip(both, right):
            out = mm(kv, other, NT)
            scores.append(
                [
                    compact(out[rows, lanes], lane_block)
                    for lanes in (slice(0, LANES), slice(LANES, 2 * LANES))
                    for rows in (slice(0, LANES), slice(LANES, 2 * LANES))
                ]
            )
        wides = []
        for (g, e), (sl, ss, dl, ds) in zip(chains, scores):
            wl, ws = softmax_pair(sl, ss, live_ref[pl.ds(g, 1), :] > 0.0)
            inner = jnp.sum(wl * dl + ws * ds, axis=0, keepdims=True)
            low = [v.astype(BF16) for v in (wl, ws, wl * (dl - inner), ws * (ds - inner))]
            wides.append(low)
        outs = []
        for (g, e), start, kv, other, (wl, ws, gl, gs) in zip(chains, starts, both, right, wides):
            weights = jnp.concatenate([spread(wl, lane_block), spread(ws, lane_block)], axis=0)
            gscore = jnp.concatenate([spread(gl, lane_block), spread(gs, lane_block)], axis=0)
            gboth = mm(jnp.concatenate([gscore, weights], axis=1), other)
            lheld[e][pl.ds(start, LANES), :] = gboth[:LANES]
            for i in range(4):
                held[e][pl.ds(4 * g + i, BLOCK, stride=own + 1), :] = gboth[
                    LANES + i * BLOCK : LANES + (i + 1) * BLOCK
                ]
            turned = kv.T
            outs.append(mm(turned[:HEAD_DIM] if e == 0 else turned[HEAD_DIM:], gscore))
        for i in range(GROUPS):
            gq_ref[pl.ds(starts[2 * i], LANES), :] = (
                jnp.concatenate(outs[2 * i : 2 * i + 2], axis=0).T * 0.125
            ).astype(BF16)
        return carry

    lax.fori_loop(0, own // 4 // GROUPS, group, 0)
    for e in range(2):
        plan = plan_ref[e][:, :blocks]
        gplan = jnp.zeros((own, blocks), F32)
        for chunk in range(4):
            lanes = slice(chunk * 8 * LANES, (chunk + 1) * 8 * LANES)
            grads = jnp.concatenate(
                [
                    held[e][(chunk * 8 + b) * (own + 1) : (chunk * 8 + b) * (own + 1) + own, :]
                    for b in range(8)
                ],
                axis=1,
            ).astype(BF16)
            here = jnp.concatenate([kvh_ref[e, :, lanes], kvo_ref[e, :, lanes]], axis=0)
            gplan = gplan + mm(grads, here, NT)
            gcontext = mm(plan, grads, TN)
            gh_ref[e, :, lanes] = gcontext[:halo].astype(BF16)
            for b in range(8):
                at = (chunk * 8 + b) * (own + 1)
                held[e][at : at + own, :] = gcontext[halo:, b * LANES : (b + 1) * LANES]
        gp_ref[e] = jnp.concatenate([gplan, jnp.zeros((own, LANES - blocks), F32)], axis=1)

    def finish(g, carry):
        start = pl.multiple_of(g * LANES, LANES)
        for e in range(2):
            rest = jnp.concatenate(
                [held[e][pl.ds(4 * g + i, BLOCK, stride=own + 1), :] for i in range(4)], axis=0
            )
            gkv_ref[pl.ds(start, LANES), e * LANES : (e + 1) * LANES] = (
                rest + lheld[e][pl.ds(start, LANES), :]
            ).astype(BF16)
        return carry

    lax.fori_loop(0, own // 4, finish, 0)


def attend_back(q, kv, skv, go, kvh, kvo, plan, live, first, pairs):
    tok, own, halo = q.shape[0], plan.shape[1], kvh.shape[1]
    return pl.pallas_call(
        attend_back_kernel,
        grid=(pairs,),
        in_specs=[
            pl.BlockSpec((tok, LANES), lambda j: (0, j + first)),
            pl.BlockSpec((tok, 2 * LANES), lambda j: (0, j + first)),
            pl.BlockSpec((tok, 2 * LANES), lambda j: (0, j + first)),
            pl.BlockSpec((tok, LANES), lambda j: (0, j + first)),
            pl.BlockSpec((2, halo, BLOCK * LANES), lambda j: (j + first, 0, 0)),
            pl.BlockSpec((2, own, BLOCK * LANES), lambda j: (j + first, 0, 0)),
            pl.BlockSpec((2, own, LANES), lambda j: (j + first, 0, 0)),
            pl.BlockSpec((tok // LANES, LANES), lambda j: (0, 0)),
        ],
        out_specs=[
            pl.BlockSpec((tok, LANES), lambda j: (0, j)),
            pl.BlockSpec((tok, 2 * LANES), lambda j: (0, j)),
            pl.BlockSpec((2, halo, BLOCK * LANES), lambda j: (j, 0, 0)),
            pl.BlockSpec((2, own, LANES), lambda j: (j, 0, 0)),
        ],
        out_shape=[
            jax.ShapeDtypeStruct((tok, pairs * LANES), BF16),
            jax.ShapeDtypeStruct((tok, 2 * pairs * LANES), BF16),
            jax.ShapeDtypeStruct((2 * pairs, halo, BLOCK * LANES), BF16),
            jax.ShapeDtypeStruct((2 * pairs, own, LANES), F32),
        ],
        scratch_shapes=[pltpu.VMEM((BLOCK * (own + 1), LANES), F32)] * 4,
        cost_estimate=CHEAP,
        compiler_params=vmem(),
        name="attend_back",
    )(q, kv, skv, go, kvh, kvo, plan, live)


def halo_kernel(
    low_ref, high_ref, nh_ref, wq_ref, w_ref, gm_ref, far_ref, near_ref, gw_ref, block_ref
):
    halo = low_ref.shape[1]
    far = far_ref.shape[1]

    @pl.when(pl.program_id(0) == 0)
    def _():
        gw_ref[...] = jnp.zeros_like(gw_ref)
        grads = gm_ref[...].astype(BF16)
        block_ref[...] = mm(grads[:, :D], wq_ref[...]) + mm(widen_keys(grads[:, D:]), w_ref[...])

    rows = jnp.concatenate(
        [
            jnp.concatenate(
                [
                    ref[head, :, b * LANES : (b + 1) * LANES]
                    for ref in (low_ref, high_ref)
                    for head in range(ref.shape[0])
                ],
                axis=1,
            )
            for b in range(8)
        ],
        axis=0,
    )
    out = (mm(rows, w_ref[...]).reshape(8, halo, D) + block_ref[...][None]).astype(BF16)
    far_ref[...] = out[:, :far]
    near_ref[...] = out[:, far:]
    gw_ref[...] += mm(rows, nh_ref[...].reshape(8 * halo, D), TN)


def halo_back(low, high, nh, w_q, w_kv, gm, far):
    halo = low.shape[1]
    part = lambda v: pl.BlockSpec((v.shape[0], halo, 8 * LANES), lambda i: (0, 0, i))
    return pl.pallas_call(
        halo_kernel,
        grid=(BLOCK // 8,),
        in_specs=[
            part(low),
            part(high),
            pl.BlockSpec((8, halo, D), lambda i: (i, 0, 0)),
            once((D, D)),
            once((2 * D, D)),
            once((halo, 2 * D)),
        ],
        out_specs=[
            pl.BlockSpec((8, far, D), lambda i: (i, 0, 0)),
            pl.BlockSpec((8, halo - far, D), lambda i: (i, 0, 0)),
            pl.BlockSpec((2 * D, D), lambda i: (0, 0)),
        ],
        out_shape=[
            jax.ShapeDtypeStruct((BLOCK, far, D), BF16),
            jax.ShapeDtypeStruct((BLOCK, halo - far, D), BF16),
            jax.ShapeDtypeStruct((2 * D, D), F32),
        ],
        scratch_shapes=[pltpu.VMEM((halo, D), F32)],
        cost_estimate=CHEAP,
        compiler_params=vmem(),
        name="halo_back",
    )(low, high, nh, w_q, w_kv, gm)


def project_kernel(x_ref, gain_ref, wq_ref, wkv_ref, n_ref, q_ref, kv_ref, m_ref, head_ref, tail_ref):
    rows = x_ref.shape[0]
    blocks = rows // BLOCK
    normed = (normalise(x_ref[...].astype(F32)) * gain_ref[...]).astype(BF16)
    n_ref[...] = normed
    q = mm(normed, wq_ref[...], NT).astype(BF16)
    q_ref[...] = q
    kv = mm(normed, wkv_ref[...], NT).astype(BF16)
    kv_ref[...] = kv
    half = lax.broadcasted_iota(jnp.int32, (1, LANES), 1) < HEAD_DIM
    m_ref[:, :D] = jnp.mean(q.astype(F32).reshape(blocks, BLOCK, D), axis=1)
    for pair in range(PAIRS):
        even = kv[:, 2 * pair * LANES : (2 * pair + 1) * LANES]
        odd = kv[:, (2 * pair + 1) * LANES : (2 * pair + 2) * LANES]
        keys = jnp.where(half, even.astype(F32), odd.astype(F32))
        m_ref[:, D + pair * LANES : D + (pair + 1) * LANES] = jnp.mean(
            keys.reshape(blocks, BLOCK, LANES), axis=1
        )
    m_ref[:, 2 * D :] = jnp.mean(normed.astype(F32).reshape(blocks, BLOCK, D), axis=1)
    at = pl.program_id(0)
    ends = head_ref.shape[0] // blocks
    for ref, first in ((head_ref, 0), (tail_ref, pl.num_programs(0) - ends)):

        @pl.when((at >= first) & (at < first + ends))
        def _():
            ref[pl.ds(pl.multiple_of((at - first) * blocks, 8), blocks), :] = m_ref[...]


def project(x, gain, wt_q, wt_kv, ends):
    tok = x.shape[0]
    tile = 8 * BLOCK
    return pl.pallas_call(
        project_kernel,
        grid=(tok // tile,),
        in_specs=[
            pl.BlockSpec((tile, D), lambda i: (i, 0)),
            pl.BlockSpec((1, D), lambda i: (0, 0)),
            pl.BlockSpec((D, D), lambda i: (0, 0)),
            pl.BlockSpec((2 * D, D), lambda i: (0, 0)),
        ],
        out_specs=[
            pl.BlockSpec((tile, D), lambda i: (i, 0)),
            pl.BlockSpec((tile, D), lambda i: (i, 0)),
            pl.BlockSpec((tile, 2 * D), lambda i: (i, 0)),
            pl.BlockSpec((8, 3 * D), lambda i: (i, 0)),
            once((ends, 3 * D)),
            once((ends, 3 * D)),
        ],
        out_shape=[
            jax.ShapeDtypeStruct((tok, D), BF16),
            jax.ShapeDtypeStruct((tok, D), BF16),
            jax.ShapeDtypeStruct((tok, 2 * D), BF16),
            jax.ShapeDtypeStruct((tok // BLOCK, 3 * D), F32),
            jax.ShapeDtypeStruct((ends, 3 * D), F32),
            jax.ShapeDtypeStruct((ends, 3 * D), F32),
        ],
        cost_estimate=CHEAP,
        compiler_params=vmem(),
        name="project",
    )(x, gain, wt_q, wt_kv)


PIECE_ONE = 208
PIECE_TWO = 576
PARTS_TWO = 592


def place(vector, start):
    size = vector.shape[1]
    row = lax.broadcasted_iota(jnp.int32, (size, LANES), 0)
    lane = lax.broadcasted_iota(jnp.int32, (size, LANES), 1)
    pick = (lane == row + start).astype(F32).astype(BF16)
    return mm(jnp.broadcast_to(vector.astype(F32), (16, size)).astype(BF16), pick)


def pack_kernel(
    wqkv_ref, wsort_ref, g1, bo, g2, bi, bd, win_ref, wdown_ref, wout_ref, x_ref,
    one_ref, two_ref, tail_ref,
):
    tail_ref[...] = x_ref[...]
    one_ref[:192, :] = wqkv_ref[...]
    row = place(g1[...], 0) + place(bo[...], 16) + place(g2[...], 32)
    row = row + place(bi[...], 48) + place(bd[...], 112)
    one_ref[192:, :] = jnp.concatenate([wsort_ref[...].astype(F32), row[:8]], axis=0).astype(BF16)
    two_ref[:256, :] = win_ref[...].astype(F32).T.astype(BF16)
    for k in range(4):
        two_ref[256 + k * 64 : 256 + (k + 1) * 64, :] = wdown_ref[:, k * LANES : (k + 1) * LANES]
    two_ref[512:, :] = wout_ref[...]


def pack(w_qkv, w_sort, vectors, w_in, w_down, w_out, x, tail):
    last = x.shape[0] // tail - 1
    return pl.pallas_call(
        pack_kernel,
        grid=(1,),
        in_specs=[VMEM] * 10 + [pl.BlockSpec((tail, D), lambda i: (last, 0))],
        out_shape=[
            jax.ShapeDtypeStruct((PIECE_ONE, LANES), BF16),
            jax.ShapeDtypeStruct((PIECE_TWO, LANES), BF16),
            jax.ShapeDtypeStruct((tail, D), BF16),
        ],
        cost_estimate=CHEAP,
        compiler_params=vmem(),
        name="pack",
    )(w_qkv.T, w_sort.T, *(v.reshape(1, -1) for v in vectors), w_in, w_down.T, w_out.T, x)


def rows_at(start, size):
    return pl.ds(pl.multiple_of(start * size, size), size)


def each_owner(at_ref, visit):
    def planes(z, carry):
        for other in range(2):
            c = at_ref[2] ^ other
            for h in range(4):
                visit(other == 0, h, z, 2 * z + c, c)
        return carry

    lax.fori_loop(0, 4, planes, 0)


def each_piece(at_ref, mine_ref, other_ref, visit):
    def owner(own, h, z, b, c):
        source = mine_ref if own else other_ref
        visit(h, b, c, source.at[at_ref[0] ^ h, at_ref[1] ^ z])

    each_owner(at_ref, owner)


def widen(vecs, start, size):
    total = 32 * size
    lane = lax.broadcasted_iota(jnp.int32, (LANES, total), 1)
    row = lax.broadcasted_iota(jnp.int32, (LANES, total), 0)
    pick = (row == start + lax.rem(lane, size)).astype(F32).astype(BF16)
    every = mm(vecs, pick)
    owner = lax.broadcasted_iota(jnp.int32, (32, total), 0)
    lane = lax.broadcasted_iota(jnp.int32, (32, total), 1)
    return jnp.sum(jnp.where(owner == lane // size, every, 0.0), axis=0, keepdims=True)


def assemble_kernel(
    at_ref, mine_ref, other_ref, wq_ref, wkv_ref, ws_ref, g1_ref, bo_ref, g2_ref, bi_ref, bd_ref,
    vecs_ref,
):
    def visit(h, b, c, piece):
        lanes = slice(h * LANES, (h + 1) * LANES)
        wq_ref[rows_at(b, 64), lanes] = piece[:64, :]
        wkv_ref[rows_at(2 * b + c, 64), lanes] = piece[64:128, :]
        wkv_ref[rows_at(2 * b + 1 - c, 64), lanes] = piece[128:192, :]
        tail = piece[192:208, :].astype(F32)
        ws_ref[h, rows_at(b, 8), :] = tail[:8]
        vecs_ref[pl.ds(h * 8 + b, 1), :] = tail[8:9]

    each_piece(at_ref, mine_ref, other_ref, visit)
    vecs = vecs_ref[...].astype(BF16)
    g1_ref[...] = widen(vecs, 0, 16)
    bo_ref[...] = widen(vecs, 16, 16)
    g2_ref[...] = widen(vecs, 32, 16)
    bi_ref[...] = widen(vecs, 48, 64)
    bd_ref[...] = widen(vecs, 112, 16)


def assemble(at, mine, other):
    row = jax.ShapeDtypeStruct((1, D), F32)
    return pl.pallas_call(
        assemble_kernel,
        in_specs=[SMEM, VMEM, VMEM],
        out_shape=[
            jax.ShapeDtypeStruct((D, D), BF16),
            jax.ShapeDtypeStruct((2 * D, D), BF16),
            jax.ShapeDtypeStruct((PAIRS, HEAD_DIM, LANES), F32),
            row, row, row, jax.ShapeDtypeStruct((1, FF), F32), row,
        ],
        scratch_shapes=[pltpu.VMEM((32, LANES), F32)],
        cost_estimate=CHEAP,
        compiler_params=vmem(),
        name="assemble",
    )(at, mine, other)


GELU_A = 0.7978845608028654
GELU_B = 0.044715


def feed_tile(x, att, g, bo, g2, bi, bd, win, wdown, wout, acc_in, acc_down, acc_out, sums):
    middle = x.astype(F32) + mm(att, wout[...], NT) + bo
    centre = middle - jnp.mean(middle, axis=-1, keepdims=True)
    spread_ = jnp.mean(centre * centre, axis=-1, keepdims=True)
    inverse = lax.rsqrt(spread_ + EPSILON)
    hat = centre * inverse
    normed = (hat * g2).astype(BF16)
    normed_t = normed.T
    g_t = g.T
    out = jnp.zeros(middle.shape, F32)
    u = jnp.zeros(middle.shape, F32)
    cut = 512
    for k in range(FF // cut):
        cols = slice(k * cut, (k + 1) * cut)
        pre = mm(normed, win[cols, :], NT) + bi[:, cols]
        square = pre * pre
        t = jnp.tanh(GELU_A * pre * (1.0 + GELU_B * square))
        half = 0.5 * (1.0 + t)
        hidden = (pre * half).astype(BF16)
        slope = half + (0.5 * GELU_A) * pre * (1.0 - t * t) * (1.0 + (3.0 * GELU_B) * square)
        g_pre = (mm(g, wdown[:, cols], NN) * slope).astype(BF16)
        out = out + mm(hidden, wdown[:, cols], NT)
        u = u + mm(g_pre, win[cols, :], NN)
        part = mm(normed_t, g_pre)
        for i in range(2):
            acc_in[2 * k + i] += part[:, i * 256 : (i + 1) * 256]
        acc_down[:, cols] += mm(g_t, hidden)
        sums[4:5, cols] += jnp.sum(g_pre.astype(F32), axis=0, keepdims=True)
    gf = g.astype(F32)
    sums[1:2, :D] += jnp.sum(u * hat, axis=0, keepdims=True)
    sums[3:4, :D] += jnp.sum(gf, axis=0, keepdims=True)
    du = u * g2
    inner = jnp.mean(du * hat, axis=-1, keepdims=True)
    g_middle = gf + inverse * (du - jnp.mean(du, axis=-1, keepdims=True) - hat * inner)
    branch = g_middle.astype(BF16)
    sums[0:1, :D] += jnp.sum(branch.astype(F32), axis=0, keepdims=True)
    acc_out[...] += mm(branch.T, att)
    return (middle + out + bd).astype(BF16), g_middle, mm(branch, wout[...], NN).astype(BF16)


def clear(*refs):
    for ref in refs:
        ref[...] = jnp.zeros_like(ref)


def narrow(sums):
    total = jnp.zeros((32, LANES), F32)
    for index, start, size in ((0, 16, 16), (1, 32, 16), (4, 48, 64), (3, 112, 16)):
        width = 32 * size
        owner = lax.broadcasted_iota(jnp.int32, (32, width), 0)
        lane = lax.broadcasted_iota(jnp.int32, (32, width), 1)
        kept = jnp.where(owner == lane // size, sums[index : index + 1, :width], 0.0)
        row = lax.broadcasted_iota(jnp.int32, (width, LANES), 0)
        lane = lax.broadcasted_iota(jnp.int32, (width, LANES), 1)
        pick = (lane == start + lax.rem(row, size)).astype(F32).astype(BF16)
        total = total + mm(kept.astype(BF16), pick)
    return total


def feed_fast_kernel(
    at_ref, x_ref, att_ref, g_ref, bo_ref, g2_ref, bi_ref, bd_ref, mine_ref, other_ref,
    out_ref, gm_ref, ga_ref, keep_ref, send_ref,
    win, wdown, wout, acc_in, acc_down, acc_out, sums, vecs,
):
    @pl.when(pl.program_id(0) == 0)
    def _():
        def visit(h, b, c, piece):
            win[rows_at(b, 256), h * LANES : (h + 1) * LANES] = piece[:256, :]
            for k in range(4):
                lanes = slice(h * 512 + k * LANES, h * 512 + (k + 1) * LANES)
                wdown[rows_at(b, 64), lanes] = piece[256 + k * 64 : 320 + k * 64, :]
            wout[rows_at(b, 64), h * LANES : (h + 1) * LANES] = piece[512:576, :]

        each_piece(at_ref, mine_ref, other_ref, visit)
        clear(acc_in, acc_down, acc_out, sums)

    out_ref[...], gm_ref[...], ga_ref[...] = feed_tile(
        x_ref[...], att_ref[...], g_ref[...], bo_ref[...], g2_ref[...], bi_ref[...], bd_ref[...],
        win, wdown, wout, acc_in, acc_down, acc_out, sums,
    )

    @pl.when(pl.program_id(0) == pl.num_programs(0) - 1)
    def _():
        vecs[...] = narrow(sums)

        def owner(own, h, z, b, c):
            ref = keep_ref if own else send_ref
            for k in range(2):
                ref[h, z, k * LANES : (k + 1) * LANES, :] = acc_in[
                    b, h * LANES : (h + 1) * LANES, k * LANES : (k + 1) * LANES
                ].astype(BF16)
            for k in range(4):
                ref[h, z, 256 + k * 64 : 320 + k * 64, :] = acc_down[
                    rows_at(b, 64), h * 512 + k * LANES : h * 512 + (k + 1) * LANES
                ].astype(BF16)
            ref[h, z, 512:576, :] = acc_out[
                rows_at(b, 64), h * LANES : (h + 1) * LANES
            ].astype(BF16)
            ref[h, z, 576:592, :] = jnp.broadcast_to(
                vecs[pl.ds(h * 8 + b, 1), :], (16, LANES)
            ).astype(BF16)

        each_owner(at_ref, owner)


def feed_fast(at, x, att, g, bo, g2, bi, bd, mine, other):
    tok = x.shape[0]
    tile = 512
    tiled = pl.BlockSpec((tile, D), lambda i: (i, 0))
    parts = (4, 4, PARTS_TWO, LANES)
    return pl.pallas_call(
        feed_fast_kernel,
        grid=(tok // tile,),
        in_specs=[
            SMEM, tiled, tiled, tiled, once((1, D)), once((1, D)), once((1, FF)), once((1, D)),
            once(mine.shape), once(other.shape),
        ],
        out_specs=[tiled, tiled, tiled, once(parts), once(parts)],
        out_shape=[
            jax.ShapeDtypeStruct((tok, D), BF16),
            jax.ShapeDtypeStruct((tok, D), F32),
            jax.ShapeDtypeStruct((tok, D), BF16),
            jax.ShapeDtypeStruct(parts, BF16),
            jax.ShapeDtypeStruct(parts, BF16),
        ],
        scratch_shapes=[
            pltpu.VMEM((FF, D), BF16), pltpu.VMEM((D, FF), BF16), pltpu.VMEM((D, D), BF16),
            pltpu.VMEM((8, D, FF // 8), F32), pltpu.VMEM((D, FF), F32), pltpu.VMEM((D, D), F32),
            pltpu.VMEM((8, FF), F32), pltpu.VMEM((32, LANES), F32),
        ],
        cost_estimate=CHEAP,
        compiler_params=vmem(60),
        name="feed",
    )(at, x, att, g, bo, g2, bi, bd, mine, other)


def feed_slow_kernel(
    x_ref, att_ref, g_ref, bo_ref, g2_ref, bi_ref, bd_ref, win, wdown, wout,
    out_ref, gm_ref, ga_ref, acc_in, acc_down, acc_out, sums,
):
    @pl.when(pl.program_id(0) == 0)
    def _():
        clear(acc_in, acc_down, acc_out, sums)

    out_ref[...], gm_ref[...], ga_ref[...] = feed_tile(
        x_ref[...], att_ref[...], g_ref[...], bo_ref[...], g2_ref[...], bi_ref[...], bd_ref[...],
        win, wdown, wout, acc_in, acc_down, acc_out, sums,
    )


def feed_slow(x, att, g, bo, g2, bi, bd, win, wdown, wout):
    tok = x.shape[0]
    tile = 512
    tiled = pl.BlockSpec((tile, D), lambda i: (i, 0))
    wide, square, rows, cut = (D, FF), (D, D), (8, FF), (8, D, FF // 8)
    return pl.pallas_call(
        feed_slow_kernel,
        grid=(tok // tile,),
        in_specs=[
            tiled, tiled, tiled, once((1, D)), once((1, D)), once((1, FF)), once((1, D)),
            once((FF, D)), once(wide), once(square),
        ],
        out_specs=[tiled, tiled, tiled, once(cut), once(wide), once(square), once(rows)],
        out_shape=[
            jax.ShapeDtypeStruct((tok, D), BF16),
            jax.ShapeDtypeStruct((tok, D), F32),
            jax.ShapeDtypeStruct((tok, D), BF16),
            jax.ShapeDtypeStruct(cut, F32),
            jax.ShapeDtypeStruct(wide, F32),
            jax.ShapeDtypeStruct(square, F32),
            jax.ShapeDtypeStruct(rows, F32),
        ],
        cost_estimate=CHEAP,
        compiler_params=vmem(60),
        name="feed_whole",
    )(x, att, g, bo, g2, bi, bd, win, wdown, wout)


def split_kernel(which, at_ref, keep_ref, got_ref, *outs):
    for r, out in enumerate(outs):
        i = at_ref[which] ^ r
        out[0] = (keep_ref[i, 0].astype(F32) + got_ref[i, 0].astype(F32)).astype(BF16)


def split_sum(at, which, keep, got):
    one, two, rows, lanes = keep.shape
    block = pl.BlockSpec((one, 1, rows, lanes), lambda i: (0, i, 0, 0))
    return pl.pallas_call(
        functools.partial(split_kernel, which),
        grid=(two,),
        in_specs=[SMEM, block, block],
        out_specs=[pl.BlockSpec((1, rows, lanes), lambda i: (i, 0, 0))] * one,
        out_shape=[jax.ShapeDtypeStruct((two, rows, lanes), BF16)] * one,
        cost_estimate=CHEAP,
        compiler_params=vmem(),
        name="split_sum",
    )(at, keep, got)


def merge_kernel(which, at_ref, a_ref, b_ref, c_ref, d_ref, *outs):
    for r, out in enumerate(outs):
        i = at_ref[which] ^ r
        total = a_ref[i].astype(F32) + b_ref[i].astype(F32)
        out[...] = (total + c_ref[i].astype(F32) + d_ref[i].astype(F32)).astype(BF16)


def merge_sum(at, which, pieces):
    count, rows, lanes = pieces[0].shape
    return pl.pallas_call(
        functools.partial(merge_kernel, which),
        in_specs=[SMEM] + [VMEM] * 4,
        out_shape=[jax.ShapeDtypeStruct((rows, lanes), BF16)] * count,
        cost_estimate=CHEAP,
        compiler_params=vmem(),
        name="merge_sum",
    )(at, *pieces)


def last_two_kernel(a_ref, b_ref, c_ref, d_ref, gin_ref, gdown_ref, gout_ref, bo, g2, bi, bd):
    total = a_ref[...].astype(F32) + b_ref[...].astype(F32)
    total = total + c_ref[...].astype(F32) + d_ref[...].astype(F32)
    for k in range(2):
        gin_ref[:, k * LANES : (k + 1) * LANES] = total[k * LANES : (k + 1) * LANES]
    for k in range(4):
        gdown_ref[:, k * LANES : (k + 1) * LANES] = total[256 + k * 64 : 320 + k * 64]
    gout_ref[...] = total[512:576]
    row = total[576:577]
    bo[...], g2[...], bi[...], bd[...] = row[:, 16:32], row[:, 32:48], row[:, 48:112], row[:, 112:]


def last_two(pieces):
    return pl.pallas_call(
        last_two_kernel,
        out_shape=[
            jax.ShapeDtypeStruct((LANES, 256), F32),
            jax.ShapeDtypeStruct((64, 512), F32),
            jax.ShapeDtypeStruct((64, LANES), F32),
            *(jax.ShapeDtypeStruct((1, n), F32) for n in (16, 16, 64, 16)),
        ],
        cost_estimate=CHEAP,
        compiler_params=vmem(),
        name="last_two",
    )(*pieces)


def last_one_kernel(a_ref, b_ref, c_ref, d_ref, gw_ref, gs_ref, g1_ref):
    total = a_ref[...].astype(F32) + b_ref[...].astype(F32)
    total = total + c_ref[...].astype(F32) + d_ref[...].astype(F32)
    gw_ref[...] = total[:192]
    gs_ref[...] = total[192:200]
    g1_ref[...] = total[200:201, :16]


def last_one(pieces):
    return pl.pallas_call(
        last_one_kernel,
        out_shape=[
            jax.ShapeDtypeStruct((192, LANES), F32),
            jax.ShapeDtypeStruct((8, LANES), F32),
            jax.ShapeDtypeStruct((1, 16), F32),
        ],
        cost_estimate=CHEAP,
        compiler_params=vmem(),
        name="last_one",
    )(*pieces)


def widen_keys(gmk):
    half = lax.broadcasted_iota(jnp.int32, (gmk.shape[0], LANES), 1) < HEAD_DIM
    zero = jnp.zeros((gmk.shape[0], LANES), gmk.dtype)
    wide = []
    for pair in range(PAIRS):
        tile = gmk[:, pair * LANES : (pair + 1) * LANES]
        wide += [jnp.where(half, tile, zero), jnp.where(half, zero, tile)]
    return jnp.concatenate(wide, axis=1)


def weight_kernel(
    fast, at_ref, ql_ref, qh_ref, kvl_ref, kvh_ref, n_ref, wq_ref, wkv_ref, gm_ref,
    pa, pb, pc, pd, pe, halo_ref, gain_ref, gs_ref, keep_ref, send_ref, acc_q, acc_kv,
):
    @pl.when(pl.program_id(0) == 0)
    def _():
        means = jnp.concatenate([ref[:, 2 * D :] for ref in (pa, pb, pc, pd, pe)], axis=0)
        means = means.astype(BF16)
        grads = (gm_ref[...] * float(BLOCK)).astype(BF16)
        acc_q[...] = mm(grads[:, :D], means, TN)
        acc_kv[...] = halo_ref[...] + mm(widen_keys(grads[:, D:]), means, TN)

    normed = n_ref[...]
    cut = ql_ref.shape[1]
    for lo, q_ref, kv_ref in ((0, ql_ref, kvl_ref), (cut, qh_ref, kvh_ref)):
        hi = lo + q_ref.shape[1]
        acc_q[lo:hi, :] += mm(q_ref[...].T, normed)
        acc_kv[2 * lo : 2 * hi, :] += mm(kv_ref[...].T, normed)

    @pl.when(pl.program_id(0) == pl.num_programs(0) - 1)
    def _():
        gain = jnp.sum(acc_q[...] * wq_ref[...].astype(F32), axis=0, keepdims=True)
        gain = gain + jnp.sum(acc_kv[...] * wkv_ref[...].astype(F32), axis=0, keepdims=True)
        gain = gain / gain_ref[...]
        if not fast:
            keep_ref[:D, :] = acc_q[...]
            keep_ref[D:, :] = acc_kv[...]
            send_ref[...] = jnp.broadcast_to(gain, (8, D))
            return
        def owner(own, h, z, b, c):
            ref = keep_ref if own else send_ref
            lanes = slice(h * LANES, (h + 1) * LANES)
            ref[z, h, :64, :] = acc_q[rows_at(b, 64), lanes].astype(BF16)
            ref[z, h, 64:128, :] = acc_kv[rows_at(2 * b + c, 64), lanes].astype(BF16)
            ref[z, h, 128:192, :] = acc_kv[rows_at(2 * b + 1 - c, 64), lanes].astype(BF16)
            share = pltpu.roll(
                jnp.broadcast_to(gain[:, lanes], (8, LANES)), lax.rem(LANES - 16 * b, LANES), 1
            )
            ref[z, h, 192:208, :] = jnp.concatenate(
                [gs_ref[h, rows_at(b, 8), :], share], axis=0
            ).astype(BF16)

        each_owner(at_ref, owner)


def weight_back(at, gq, gkv, normed, wt_q, wt_kv, gm, pieces, halo, gain, gsort, fast):
    tok = normed.shape[0]
    tile = 512
    parts = (4, 4, PIECE_ONE, LANES)
    shapes = (parts, parts) if fast else ((3 * D, D), (8, D))
    kind = BF16 if fast else F32
    rows = lambda width: pl.BlockSpec((tile, width), lambda i: (i, 0))
    return pl.pallas_call(
        functools.partial(weight_kernel, fast),
        grid=(tok // tile,),
        in_specs=[
            SMEM, *(rows(v.shape[1]) for v in (*gq, *gkv)), rows(D), once((D, D)),
            once((2 * D, D)), once(gm.shape), *(once(p.shape) for p in pieces),
            once((2 * D, D)), once((1, D)), once(gsort.shape),
        ],
        out_specs=[once(shapes[0]), once(shapes[1])],
        out_shape=[
            jax.ShapeDtypeStruct(shapes[0], kind),
            jax.ShapeDtypeStruct(shapes[1], kind),
        ],
        scratch_shapes=[pltpu.VMEM((D, D), F32), pltpu.VMEM((2 * D, D), F32)],
        cost_estimate=CHEAP,
        compiler_params=vmem(),
        name="weight_back",
    )(at, *gq, *gkv, normed, wt_q, wt_kv, gm, *pieces, halo, gain, gsort)


def inner_kernel(
    ql_ref, qh_ref, kvl_ref, kvh_ref, wq_ref, wkv_ref, gm_ref, fd, fe, out_ref, blocks_ref
):
    rows = ql_ref.shape[0]
    per = rows // BLOCK

    @pl.when(pl.program_id(0) == 0)
    def _():
        own, ends = fd.shape[0], fe.shape[0]
        halo = own + ends
        blocks_ref[...] = gm_ref[halo : halo + own, :] + fd[...].astype(F32)
        blocks_ref[:ends, :] += fe[...].astype(F32)

    cut = ql_ref.shape[1]
    value = mm(ql_ref[...], wq_ref[:cut, :]) + mm(qh_ref[...], wq_ref[cut:, :])
    value = value + mm(kvl_ref[...], wkv_ref[: 2 * cut, :])
    value = value + mm(kvh_ref[...], wkv_ref[2 * cut :, :])
    grads = blocks_ref[pl.ds(pl.multiple_of(pl.program_id(0) * per, per), per), :].astype(BF16)
    block = mm(grads[:, :D], wq_ref[...]) + mm(widen_keys(grads[:, D:]), wkv_ref[...])
    out_ref[...] = value + jnp.broadcast_to(block[:, None, :], (per, BLOCK, D)).reshape(rows, D)


def inner_gradient(gq, gkv, wt_q, wt_kv, gm, far):
    tok = gq[0].shape[0]
    tile = 8 * BLOCK
    rows = lambda width: pl.BlockSpec((tile, width), lambda i: (i, 0))
    return pl.pallas_call(
        inner_kernel,
        grid=(tok // tile,),
        in_specs=[
            *(rows(v.shape[1]) for v in (*gq, *gkv)), once((D, D)), once((2 * D, D)),
            once(gm.shape), *(once(f.shape) for f in far),
        ],
        out_specs=rows(D),
        out_shape=jax.ShapeDtypeStruct((tok, D), F32),
        scratch_shapes=[pltpu.VMEM((tok // BLOCK, 2 * D), F32)],
        cost_estimate=CHEAP,
        compiler_params=vmem(),
        name="inner_gradient",
    )(*gq, *gkv, wt_q, wt_kv, gm, *far)


def finish_kernel(skip, x_ref, u_ref, one_ref, two_ref, g_ref, gain_ref, out_ref, total):
    rows = x_ref.shape[0]
    at = lax.broadcasted_iota(jnp.int32, (rows, rows), 0)
    lane = lax.broadcasted_iota(jnp.int32, (rows, rows), 1)
    order = (lane == lax.rem(at, BLOCK) * 8 + at // BLOCK).astype(F32).astype(BF16)
    total[...] = u_ref[...] + mm(order, one_ref[...].reshape(rows, D))

    @pl.when(pl.program_id(0) >= skip)
    def _():
        total[...] += mm(order, two_ref[...].reshape(rows, D))

    x = x_ref[...].astype(F32)
    centre = x - jnp.mean(x, axis=-1, keepdims=True)
    inverse = lax.rsqrt(jnp.mean(centre * centre, axis=-1, keepdims=True) + EPSILON)
    hat = centre * inverse
    du = total[...] * gain_ref[...]
    inner = jnp.mean(du * hat, axis=-1, keepdims=True)
    out_ref[...] = g_ref[...] + inverse * (
        du - jnp.mean(du, axis=-1, keepdims=True) - hat * inner
    )


def finish(x, u, one, two, g_middle, gain):
    tok = x.shape[0]
    tile = 8 * BLOCK
    skip = (tok // BLOCK - two.shape[1]) // 8
    rows = lambda width: pl.BlockSpec((tile, width), lambda i: (i, 0))
    return pl.pallas_call(
        functools.partial(finish_kernel, skip),
        grid=(tok // tile,),
        in_specs=[
            rows(D), rows(D),
            pl.BlockSpec((BLOCK, 8, D), lambda i: (0, i, 0)),
            pl.BlockSpec((BLOCK, 8, D), lambda i: (0, jnp.maximum(i - skip, 0), 0)),
            rows(D), once((1, D)),
        ],
        out_specs=rows(D),
        out_shape=jax.ShapeDtypeStruct((tok, D), F32),
        scratch_shapes=[pltpu.VMEM((tile, D), F32)],
        cost_estimate=CHEAP,
        compiler_params=vmem(),
        name="finish",
    )(x, u, one, two, g_middle, gain)


class Grid:
    def __init__(self):
        self.heads = lax.axis_size("head")
        self.planes = lax.axis_size("plane")
        self.cycles = 2 * self.planes
        self.head = lax.axis_index("head")
        self.plane = lax.axis_index("plane")
        self.core = lax.axis_index("core")
        self.cycle = 2 * self.plane + self.core
        self.place = self.cycle * self.heads + self.head

    def send(self, value, pairs):
        return lax.ppermute(value, ("head", "plane", "core"), pairs)

    def number(self, head, cycle):
        return head * self.cycles + cycle

    def along(self, steps):
        count = self.heads * self.cycles
        at = lambda place: self.number(place % self.heads, place // self.heads)
        return [(at(i), at(i + steps)) for i in range(count) if 0 <= i + steps < count]

    def swap_head(self, flip):
        return [
            (self.number(h, b), self.number(h ^ flip, b))
            for h in range(self.heads)
            for b in range(self.cycles)
        ]

    def swap_plane(self, flip):
        return [
            (self.number(h, b), self.number(h, b ^ (2 * flip)))
            for h in range(self.heads)
            for b in range(self.cycles)
        ]

    def swap_core(self):
        return [
            (self.number(h, b), self.number(h, b ^ 1))
            for h in range(self.heads)
            for b in range(self.cycles)
        ]


def in_order(pieces, index):
    stacked = jnp.stack(pieces)
    count = len(pieces)
    bit = 1
    while bit < count:
        swapped = jnp.stack([stacked[i ^ bit] for i in range(count)])
        stacked = jnp.where((index & bit) != 0, swapped, stacked)
        bit *= 2
    return stacked


def gather_all(grid, piece):
    got = [piece] + [grid.send(piece, grid.swap_plane(r)) for r in range(1, grid.planes)]
    got = in_order(got, grid.plane)
    got = [got] + [grid.send(got, grid.swap_head(r)) for r in range(1, grid.heads)]
    got = in_order(got, grid.head)
    got = in_order([got, grid.send(got, grid.swap_core())], grid.core)
    got = got.transpose(1, 2, 0, *range(3, got.ndim))
    return got.reshape(grid.heads, grid.cycles, *piece.shape)


def across_planes(parts):
    return lax.all_to_all(parts, "plane", 0, 0, tiled=True)


def across_heads(parts):
    return lax.all_to_all(parts, "head", 0, 0, tiled=True)


def scatter_sum(grid, parts):
    mine = lax.dynamic_index_in_dim(parts, grid.core, 0, keepdims=False)
    other = lax.dynamic_index_in_dim(parts, 1 - grid.core, 0, keepdims=False)
    got = grid.send(other, grid.swap_core())
    total = (mine.astype(F32) + got.astype(F32)).astype(BF16)
    total = jnp.sum(across_heads(total).astype(F32), axis=0).astype(BF16)
    return jnp.sum(across_planes(total).astype(F32), axis=0)


def as_rows(value):
    flat = value.reshape(-1)
    short = -flat.shape[0] % LANES
    return jnp.pad(flat, (0, short)).reshape(-1, LANES)


def by_owner(grid, value):
    columns, rows = value.shape
    cut = value.reshape(grid.planes, 2, columns // grid.cycles, grid.heads, rows // grid.heads)
    return cut.transpose(1, 3, 0, 2, 4)


def vector_by_owner(grid, value):
    cut = value.reshape(grid.heads, grid.planes, 2, -1)
    return cut.transpose(2, 0, 1, 3)


def rows_of(value):
    lead = value.shape[:3]
    flat = value.reshape(*lead, -1)
    short = -flat.shape[-1] % LANES
    flat = jnp.pad(flat, ((0, 0),) * 3 + ((0, short),))
    return flat.reshape(*lead, -1, LANES)


def after(value, *others):
    return lax.optimization_barrier((value, *others))[0]


def weights_slow(grid, vectors, parameters):
    w_qkv, w_sort, w_in, w_down, w_out = parameters
    heads, cycles = grid.heads, grid.cycles
    first = jnp.concatenate([as_rows(w_qkv.T), as_rows(w_sort), as_rows(jnp.concatenate(vectors))])
    wide, sort_rows = as_rows(w_qkv.T).shape[0], as_rows(w_sort).shape[0]
    got = gather_all(grid, first)
    span = w_qkv.shape[1]
    wt_qkv = (
        got[:, :, :wide]
        .reshape(heads, cycles, span, D // heads)
        .transpose(1, 2, 0, 3)
        .reshape(HEADS, 3, HEAD_DIM, D)
    )
    wt_q = wt_qkv[:, 0].reshape(D, D)
    paired = wt_qkv.reshape(PAIRS, 2, 3, HEAD_DIM, D)
    wt_kv = jnp.stack(
        [paired[:, 0, 1], paired[:, 0, 2], paired[:, 1, 2], paired[:, 1, 1]], axis=1
    ).reshape(2 * D, D)
    size = w_sort.shape[0] * w_sort.shape[1]
    w_pairs = (
        got[:, :, wide : wide + sort_rows]
        .reshape(heads, cycles, -1)[:, :, :size]
        .reshape(heads, cycles, *w_sort.shape)
        .transpose(1, 3, 0, 2)
        .reshape(HEAD_DIM, PAIRS, LANES)
        .transpose(1, 0, 2)
        .astype(F32)
    )
    flat = got[:, :, wide + sort_rows :].reshape(heads, cycles, -1)
    sizes = [v.shape[0] for v in vectors]
    cuts = [sum(sizes[:i]) for i in range(len(sizes) + 1)]
    rows = [
        flat[:, :, cuts[i] : cuts[i + 1]].reshape(1, -1).astype(F32) for i in range(len(sizes))
    ]
    second = jnp.concatenate([as_rows(w_in.T), as_rows(w_down.T), as_rows(w_out.T)])
    in_rows, down_rows = as_rows(w_in.T).shape[0], as_rows(w_down.T).shape[0]
    got = gather_all(grid, second)

    def whole(depth, columns, part):
        return (
            part.reshape(heads, cycles, -1)[:, :, : columns // cycles * (depth // heads)]
            .reshape(heads, cycles, columns // cycles, depth // heads)
            .transpose(1, 2, 0, 3)
            .reshape(columns, depth)
        )

    feed = (
        whole(D, FF, got[:, :, :in_rows]),
        whole(FF, D, got[:, :, in_rows : in_rows + down_rows]),
        whole(D, D, got[:, :, in_rows + down_rows :]),
    )
    return wt_q, wt_kv, w_pairs, rows, feed


def matrix(rows, shape):
    flat = rows.reshape(-1)[: shape[0] * shape[1]]
    return flat.reshape(shape[1], shape[0]).T


def gradients_two_slow(grid, acc_in, acc_down, acc_out, sums, parameters, vectors):
    w_qkv, w_sort, w_in, w_down, w_out = parameters
    low = [
        rows_of(by_owner(grid, v.astype(BF16))) for v in (acc_in.transpose(0, 2, 1).reshape(FF, D), acc_down, acc_out)
    ]
    order = ((0, D), (1, D), (4, FF), (3, D))
    small = [vector_by_owner(grid, sums[i, :n]) for i, n in order]
    low.append(rows_of(jnp.concatenate(small, axis=-1).astype(BF16)))
    total = scatter_sum(grid, jnp.concatenate(low, axis=3))
    cuts = [0]
    for item in low:
        cuts.append(cuts[-1] + item.shape[3])
    g_in, g_down, g_out = (
        matrix(total[cuts[i] : cuts[i + 1]], w.shape) for i, w in enumerate((w_in, w_down, w_out))
    )
    flat = total[cuts[3] :].reshape(-1)
    sizes = [v.shape[0] for v in vectors[1:]]
    at = [sum(sizes[:i]) for i in range(5)]
    return g_in, g_down, g_out, *(flat[at[i] : at[i + 1]] for i in range(4))


def gradients_one_slow(grid, both, gain, gsort, parameters, vectors):
    w_qkv, w_sort = parameters[:2]
    q = both[:D].reshape(HEADS, HEAD_DIM, D)
    kv = both[D:].reshape(PAIRS, 4, HEAD_DIM, D)
    k = jnp.stack([kv[:, 0], kv[:, 3]], axis=1).reshape(HEADS, HEAD_DIM, D)
    v = jnp.stack([kv[:, 1], kv[:, 2]], axis=1).reshape(HEADS, HEAD_DIM, D)
    wide = jnp.stack([q, k, v], axis=1).reshape(3 * D, D)
    sort = gsort.transpose(0, 2, 1).reshape(grid.heads, D // grid.heads, grid.planes, 2, -1)
    low = [
        rows_of(by_owner(grid, wide.astype(BF16))),
        rows_of(sort.transpose(3, 0, 2, 1, 4).astype(BF16)),
        rows_of(vector_by_owner(grid, gain[0]).astype(BF16)),
    ]
    total = scatter_sum(grid, jnp.concatenate(low, axis=3))
    one, two = low[0].shape[3], low[0].shape[3] + low[1].shape[3]
    size = w_sort.shape[0] * w_sort.shape[1]
    return (
        matrix(total[:one], w_qkv.shape),
        total[one:two].reshape(-1)[:size].reshape(w_sort.shape),
        total[two:].reshape(-1)[: vectors[0].shape[0]],
    )


def per_device(
    tokens, cotangent, doc_lengths, norm_gain1, w_qkv, w_out, b_out, norm_gain2, w_in, b_in,
    w_down, b_down, w_sort,
):
    grid = Grid()
    heads = grid.heads
    x = tokens[0]
    upstream = cotangent[0]
    tok = x.shape[0]
    own = tok // BLOCK
    context = HALO + own
    window = HALO + own + HALO
    second = HALO - own
    fast = heads == 4 and grid.cycles == 8
    at = jnp.stack([grid.head, grid.plane, grid.core]).astype(jnp.int32)
    vectors = (norm_gain1, b_out, norm_gain2, b_in, b_down)
    parameters = (w_qkv, w_sort, w_in, w_down, w_out)

    three = range(1, 4)
    tail = second * BLOCK
    if fast:
        one, two, x_tail = pack(w_qkv, w_sort, vectors, w_in, w_down, w_out, x, tail)
        ones = [one] + [grid.send(one, grid.swap_plane(r)) for r in three]
        ones = jnp.stack(ones)
        ones = [ones] + [grid.send(ones, grid.swap_head(r)) for r in three]
        x_send, x_tail = lax.optimization_barrier((x, x_tail, *ones))[:2]
    else:
        x_send, x_tail = x, x[tok - tail :]
    halo_one = grid.send(x_send, grid.along(1))
    halo_two = grid.send(x_tail, grid.along(2))
    if fast:
        ones = jnp.stack(ones)
        other = grid.send(ones, grid.swap_core())
        two = after(two, other)
        twos = [two] + [grid.send(two, grid.swap_plane(r)) for r in three]
        wt_q, wt_kv, w_pairs, *rows = assemble(at, ones, other)
    else:
        wt_q, wt_kv, w_pairs, rows, feed_weights = weights_slow(grid, vectors, parameters)
        twos = []
    gain_one, bias_out, gain_two, bias_in, bias_down = rows

    begin = grid.place * own
    position = begin - HALO + jnp.arange(window, dtype=jnp.int32)
    doc_ends = jnp.cumsum(doc_lengths, dtype=jnp.int32)
    ended = jnp.sum(
        (doc_ends[None, :] <= position[:, None]).astype(jnp.int32), axis=1, dtype=jnp.int32
    )
    span_end = (grid.cycle + 1) * heads * own
    doc = jnp.where((position >= 0) & (position < span_end), ended, -1)
    fold = window - LANES
    docc = jnp.stack([doc[:LANES], jnp.concatenate([doc[LANES:], doc[fold:LANES]])])
    docn = doc[:, None]
    live = (doc[HALO:context] == doc[HALO - 1 : context - 1]) & (doc[HALO:context] >= 0)
    live = jnp.repeat(live.astype(F32), BLOCK).reshape(tok // LANES, LANES)

    normed, q, kv, means, means_head, means_tail = project(x, gain_one, wt_q, wt_kv, second)
    blocked = lambda value: value.reshape(-1, BLOCK, D)
    (kv_own,) = context_project((blocked(x),), after(gain_one, means), wt_kv, False)
    means_send, means_head, means_tail, docn, docc, live = lax.optimization_barrier(
        (means, means_head, means_tail, docn, docc, live, halo_one, halo_two, kv_own, *twos)
    )[:6]
    pieces = (
        grid.send(means_tail, grid.along(2)),
        grid.send(means_send, grid.along(1)),
        means,
        grid.send(means_send, grid.along(-1)),
        grid.send(means_head, grid.along(-2)),
    )
    kv_halo, normed_halo = context_project(
        (blocked(halo_two), blocked(halo_one)), after(gain_one, kv_own), wt_kv, True
    )
    if fast:
        twos = jnp.stack(lax.optimization_barrier((*twos, *pieces, kv_halo))[:4])
        twos = [twos] + [grid.send(twos, grid.swap_head(r)) for r in three]

    plan, *kept = sink_forward(pieces, after(w_pairs, kv_halo), docn, docc, own, context)
    attended, skv = attend(q, kv, kv_halo, kv_own, plan, live)
    if fast:
        twos = jnp.stack(lax.optimization_barrier((*twos, attended))[:4])
        feed_weights = (twos, grid.send(twos, grid.swap_core()))

    if fast:
        output, g_middle, g_att, keep, send = feed_fast(
            at, x, attended, upstream, bias_out, gain_two, bias_in, bias_down, *feed_weights
        )
        got = grid.send(send, grid.swap_core())
    else:
        output, g_middle, g_att, *sums = feed_slow(
            x, attended, upstream, bias_out, gain_two, bias_in, bias_down, *feed_weights
        )
        g_in, g_down, g_out, g_b_out, g_gain_two, g_b_in, g_b_down = gradients_two_slow(
            grid, *sums, parameters, vectors
        )
        twos = []

    gq_low, gkv_low, gh_low, gplan_low = attend_back(
        q, kv, skv, g_att, kv_halo, kv_own, plan, live, 0, 1
    )
    if fast:
        twos = split_sum(at, 0, after(keep, gh_low), got)
        g_att = after(g_att, *twos)
        twos = [twos[0]] + [grid.send(twos[r], grid.swap_head(r)) for r in three]
    gq_high, gkv_high, gh_high, gplan_high = attend_back(
        q, kv, skv, g_att, kv_halo, kv_own, plan, live, 1, PAIRS - 1
    )
    gq, gkv = (gq_low, gq_high), (gkv_low, gkv_high)
    gmeans, gsort, *sends = sink_backward(
        pieces, w_pairs, *kept, gplan_low, gplan_high, own, context
    )
    if fast:
        twos = merge_sum(at, 1, lax.optimization_barrier((*twos, gmeans))[:4])
        gh_high = after(gh_high, *twos)
        twos = [twos[0]] + [grid.send(twos[r], grid.swap_plane(r)) for r in three]
    gn_far, gn_near, g_kv_halo = halo_back(
        gh_low, gh_high, normed_halo, wt_q, wt_kv, gmeans, second
    )
    sends = lax.optimization_barrier((*sends, gn_near))[:2]
    far = [grid.send(value, grid.along(step)) for value, step in zip(sends, (1, 2))]
    gn_far, gn_near = lax.optimization_barrier((gn_far, gn_near, *far, *twos))[:2]
    back_one = grid.send(gn_near, grid.along(-1))
    back_two = grid.send(gn_far, grid.along(-2))
    gmeans = after(gmeans, gn_near)
    keep, send = weight_back(
        at, gq, gkv, normed, wt_q, wt_kv, gmeans, pieces, g_kv_halo, gain_one, gsort, fast
    )
    if fast:
        got = grid.send(send, grid.swap_core())
        ones = split_sum(at, 1, keep, got)
        waiting = [ones[0]] + [grid.send(ones[r], grid.swap_plane(r)) for r in three]
        inner = inner_gradient((gq[0], after(gq[1], *ones)), gkv, wt_q, wt_kv, gmeans, far)
        ones = merge_sum(at, 0, lax.optimization_barrier((*waiting, inner))[:4])
        ones = [ones[0]] + [grid.send(ones[r], grid.swap_head(r)) for r in three]
    else:
        inner = inner_gradient(gq, gkv, wt_q, wt_kv, gmeans, far)
    input_grad = finish(x, inner, back_one, back_two, g_middle, gain_one)
    if fast:
        g_wqkv, g_sort, g_gain_one = last_one(lax.optimization_barrier((*ones, input_grad))[:4])
        g_in, g_down, g_out, *small = last_two(twos)
        g_wqkv, g_sort, g_down, g_out = g_wqkv.T, g_sort.T, g_down.T, g_out.T
        g_gain_one = g_gain_one[0]
        g_b_out, g_gain_two, g_b_in, g_b_down = (value[0] for value in small)
    else:
        g_wqkv, g_sort, g_gain_one = gradients_one_slow(
            grid, keep, send, gsort, parameters, vectors
        )
    return (
        output[None], input_grad[None], g_gain_one, g_wqkv, g_out, g_b_out, g_gain_two, g_in,
        g_b_in, g_down, g_b_down, g_sort,
    )


def solution(mesh):
    heads, cycles = mesh.shape["head"], mesh.shape["blk"]
    fine = Mesh(mesh.devices.reshape(heads, cycles // 2, 2), ("head", "plane", "core"))
    both = P(("head", "plane", "core"))
    split = P("head", ("plane", "core"))
    stream = P(("plane", "core"), "head", None)
    return jax.shard_map(
        per_device,
        mesh=fine,
        in_specs=(
            stream, stream, P(), both, split, split, both, both, split, both, split, both, split,
        ),
        out_specs=(
            stream, stream, both, split, split, both, both, split, both, split, both, split,
        ),
        check_vma=False,
    )
```

```python
import functools

import jax
import jax.numpy as jnp
from jax import lax
from jax.experimental import pallas as pl
from jax.experimental.pallas import tpu as pltpu
from jax.sharding import Mesh
from jax.sharding import PartitionSpec as P

D = 512
HEADS = 8
HEAD_DIM = 64
FF = 2048
BLOCK = 32
SINK_ITERS = 8
DOC_MOST = 62
LANES = 128
PAIRS = HEADS // 2
HALO = 64
GROUPS = 4
CHEAP = pl.CostEstimate(flops=0, transcendentals=0, bytes_accessed=0)
EPSILON = 1e-05
NEGATIVE = -1e30
FLOOR = -1e20
LOG2E = 1.4426950408889634
TINY = 1e-37
F32 = jnp.float32
BF16 = jnp.bfloat16
NT = (((1,), (1,)), ((), ()))
NN = (((1,), (0,)), ((), ()))
TN = (((0,), (0,)), ((), ()))


def mm(a, b, dims=NN):
    return lax.dot_general(a, b, dims, preferred_element_type=F32)


def vmem(limit=56):
    return pltpu.CompilerParams(vmem_limit_bytes=limit * 1024 * 1024)


def once(shape):
    return pl.BlockSpec(shape, lambda *i: (0,) * len(shape), pipeline_mode=pl.Buffered(1))


def halves(value):
    high = value.astype(BF16)
    return high, (value - high.astype(F32)).astype(BF16)


def mm3(a, b, dims):
    (da,), (db,) = dims[0]
    ah, al = halves(a)
    bh, bl = halves(b)
    return mm(
        jnp.concatenate([ah, al, ah], axis=da), jnp.concatenate([bh, bh, bl], axis=db), dims
    )


def sink_mask(docn_ref, docc_ref, window, context):
    first = context
    fold = window - LANES
    lane = lax.broadcasted_iota(jnp.int32, (1, LANES), 1)
    docn = docn_ref[...]
    row = lax.broadcasted_iota(jnp.int32, (window, 1), 0)
    col = jnp.where((row >= first) & (lane < fold), lane + LANES, lane)
    docc = jnp.where(row >= first, docc_ref[1:2, :], docc_ref[0:1, :])
    return (docn == docc) & (docn >= 0) & (col < row)


def fold_pair(top, low, fold, join):
    lane = lax.broadcasted_iota(jnp.int32, (1, LANES), 1)
    both = join(top, low)
    return jnp.where(lane < fold, top, both), jnp.where(lane < fold, low, both)


def sink_weight(pair, odd):
    lane = lax.broadcasted_iota(jnp.int32, pair.shape, 1)
    zero = jnp.zeros_like(pair)
    if odd:
        return jnp.concatenate([zero, jnp.where(lane >= HEAD_DIM, pair, zero)], axis=0)
    return jnp.concatenate([jnp.where(lane < HEAD_DIM, pair, zero), zero], axis=0)


def refold(keys, fold):
    return jnp.concatenate([keys[LANES:], keys[fold:LANES]], axis=0)


def row_step(values):
    highest = jnp.maximum(jnp.max(values, axis=1, keepdims=True), FLOOR)
    total = jnp.sum(jnp.exp2(values - highest), axis=1, keepdims=True)
    return values - (highest + LOG2E * jnp.log(jnp.maximum(total, TINY)))


def column_step(values, context, fold):
    top, low = values[:context], values[context:]
    h1, h2 = fold_pair(
        jnp.max(top, axis=0, keepdims=True),
        jnp.max(low, axis=0, keepdims=True),
        fold,
        jnp.maximum,
    )
    h1, h2 = jnp.maximum(h1, FLOOR), jnp.maximum(h2, FLOOR)
    e1, e2 = jnp.exp2(top - h1), jnp.exp2(low - h2)
    t1, t2 = fold_pair(
        jnp.sum(e1, axis=0, keepdims=True), jnp.sum(e2, axis=0, keepdims=True), fold, jnp.add
    )
    t1, t2 = jnp.maximum(t1, TINY), jnp.maximum(t2, TINY)
    moved = jnp.concatenate(
        [top - (h1 + LOG2E * jnp.log(t1)), low - (h2 + LOG2E * jnp.log(t2))], axis=0
    )
    scales = jnp.concatenate([jnp.exp2(h1), jnp.exp2(h2), 1.0 / t1, 1.0 / t2], axis=0)
    return moved, e1, e2, scales


def sink_forward_kernel(
    own, context, a, b, c, d, e, w_ref, docn_ref, docc_ref, plan_ref, kept_ref, scale_ref, proj_ref,
    q_ref, k_ref, vals, kept, sems,
):
    window = q_ref.shape[1]
    fold = window - LANES
    at = 0
    for piece in (a, b, c, d, e):
        rows = piece.shape[0]
        for pair in range(PAIRS):
            q_ref[pair, at : at + rows, :] = piece[:, pair * LANES : (pair + 1) * LANES]
            k_ref[pair, at : at + rows, :] = piece[:, D + pair * LANES : D + (pair + 1) * LANES]
        at += rows

    def logits(pair, carry):
        permitted = sink_mask(docn_ref, docc_ref, window, context)
        queries, keys = q_ref[pair], k_ref[pair]
        keys_two = refold(keys, fold)
        for odd in range(2):
            projected = mm3(queries, sink_weight(w_ref[pair], odd), NT)
            proj_ref[2 * pair + odd] = projected
            top = mm3(projected[:context], keys[:LANES], NT)
            low = mm3(projected[context:], keys_two, NT)
            vals[2 * pair + odd] = jnp.where(
                permitted, LOG2E * jnp.concatenate([top, low], axis=0), NEGATIVE
            )
        return carry

    lax.fori_loop(0, PAIRS, logits, 0)

    def send(step):
        return pltpu.make_async_copy(kept.at[step], kept_ref.at[step], sems.at[step])

    def step(turn, carry):
        for head in range(HEADS):
            moved, top, low, scales = column_step(row_step(vals[head]), context, fold)
            kept[turn, head, :context, :] = top
            kept[turn, head, context:, :] = low
            scale_ref[turn, head] = scales
            vals[head] = moved
        send(turn).start()
        return carry

    lax.fori_loop(0, SINK_ITERS, step, 0)
    for head in range(HEADS):
        plan_ref[head] = (
            kept[SINK_ITERS - 1, head, context - own : context, :]
            * scale_ref[SINK_ITERS - 1, head, 2:3, :]
        ).astype(BF16)
    lax.fori_loop(0, SINK_ITERS, lambda turn, carry: (send(turn).wait(), carry)[1], 0)


def sink_backward_kernel(
    own, context, a, b, c, d, e, w_ref, kept_ref, scale_ref, proj, gl_ref, gh_ref,
    gm_ref, gw_ref, sd, se, q_ref, k_ref, vals, gq, gk, kept, sems,
):
    window = q_ref.shape[1]
    fold = window - LANES

    def fetch(step):
        return pltpu.make_async_copy(kept_ref.at[step], kept.at[step], sems.at[step])

    def begin(turn, carry):
        fetch(SINK_ITERS - 1 - turn).start()
        return carry

    lax.fori_loop(0, SINK_ITERS, begin, 0)
    at = 0
    for piece in (a, b, c, d, e):
        rows = piece.shape[0]
        for pair in range(PAIRS):
            q_ref[pair, at : at + rows, :] = piece[:, pair * LANES : (pair + 1) * LANES]
            k_ref[pair, at : at + rows, :] = piece[:, D + pair * LANES : D + (pair + 1) * LANES]
        at += rows

    def back(turn, carry):
        at = SINK_ITERS - 1 - turn
        fetch(at).wait()

        @pl.when(turn == 0)
        def _():
            for head in range(HEADS):
                low = gl_ref.shape[0]
                ref, index = (gl_ref, head) if head < low else (gh_ref, head - low)
                vals[head, : context - own, :] = jnp.zeros((context - own, LANES), F32)
                vals[head, context - own : context, :] = (
                    ref[index]
                    * kept[SINK_ITERS - 1, head, context - own : context, :]
                    * scale_ref[SINK_ITERS - 1, head, 2:3, :]
                )
                vals[head, context:, :] = jnp.zeros((window - context, LANES), F32)

        for head in range(HEADS):
            g1, g2 = vals[head, :context, :], vals[head, context:, :]
            s1, s2 = fold_pair(
                jnp.sum(g1, axis=0, keepdims=True),
                jnp.sum(g2, axis=0, keepdims=True),
                fold,
                jnp.add,
            )
            scales = scale_ref[at, head]
            e1, e2 = kept[at, head, :context, :], kept[at, head, context:, :]
            g1, g2 = g1 - e1 * (s1 * scales[2:3]), g2 - e2 * (s2 * scales[3:4])
            r1, r2 = jnp.sum(g1, axis=1, keepdims=True), jnp.sum(g2, axis=1, keepdims=True)
            vals[head, :context, :] = g1 - (e1 * scales[0:1]) * r1
            vals[head, context:, :] = g2 - (e2 * scales[1:2]) * r2
        return carry

    lax.fori_loop(0, SINK_ITERS, back, 0)

    def products(pair, carry):
        queries, keys = q_ref[pair], k_ref[pair]
        keys_two = refold(keys, fold)
        turned = []
        gq_total = jnp.zeros((window, LANES), F32)
        gk_total = jnp.zeros((window, LANES), F32)
        for odd in range(2):
            head = 2 * pair + odd
            g1, g2 = vals[head, :context, :], vals[head, context:, :]
            against = jnp.concatenate(
                [mm3(g1, keys[:LANES], NN), mm3(g2, keys_two, NN)], axis=0
            )
            gq_total = gq_total + mm3(against, sink_weight(w_ref[pair], odd), NN)
            u1 = mm3(g1, proj[head, :context, :], TN)
            u2 = mm3(g2, proj[head, context:, :], TN)
            gk_total = gk_total + jnp.concatenate(
                [u1[:fold], u1[fold:] + u2[fold:], u2[:fold]], axis=0
            )
            turned.append(mm3(against, queries, TN))
        half = lax.broadcasted_iota(jnp.int32, (HEAD_DIM, LANES), 1) < HEAD_DIM
        gw_ref[pair] = jnp.where(half, turned[0][:HEAD_DIM], turned[1][HEAD_DIM:])
        gq[pair] = gq_total * (1.0 / BLOCK)
        gk[pair] = gk_total * (1.0 / BLOCK)
        return carry

    lax.fori_loop(0, PAIRS, products, 0)
    for pair in range(PAIRS):
        gm_ref[:, pair * LANES : (pair + 1) * LANES] = gq[pair]
        gm_ref[:, D + pair * LANES : D + (pair + 1) * LANES] = gk[pair]
    sd[...] = gm_ref[context : context + d.shape[0], :].astype(BF16)
    se[...] = gm_ref[context + d.shape[0] :, :].astype(BF16)


HBM = pl.BlockSpec(memory_space=pl.ANY)
VMEM = pl.BlockSpec(memory_space=pltpu.VMEM)
SMEM = pl.BlockSpec(memory_space=pltpu.SMEM)


def sink_forward(pieces, weight, docn, docc, own, context):
    window = sum(piece.shape[0] for piece in pieces)
    kept = (SINK_ITERS, HEADS, window, LANES)
    return pl.pallas_call(
        functools.partial(sink_forward_kernel, own, context),
        in_specs=[VMEM] * 8,
        out_specs=[VMEM, HBM, VMEM, VMEM],
        out_shape=[
            jax.ShapeDtypeStruct((HEADS, own, LANES), BF16),
            jax.ShapeDtypeStruct(kept, F32),
            jax.ShapeDtypeStruct((SINK_ITERS, HEADS, 4, LANES), F32),
            jax.ShapeDtypeStruct((HEADS, window, LANES), F32),
        ],
        scratch_shapes=[
            pltpu.VMEM((PAIRS, window, LANES), F32),
            pltpu.VMEM((PAIRS, window, LANES), F32),
            pltpu.VMEM((HEADS, window, LANES), F32),
            pltpu.VMEM(kept, F32),
            pltpu.SemaphoreType.DMA((SINK_ITERS,)),
        ],
        cost_estimate=CHEAP,
        compiler_params=vmem(),
        name="sink_forward",
    )(*pieces, weight, docn, docc)


def sink_backward(pieces, weight, kept, scales, projected, low, high, own, context):
    window = sum(piece.shape[0] for piece in pieces)
    return pl.pallas_call(
        functools.partial(sink_backward_kernel, own, context),
        in_specs=[VMEM] * 6 + [HBM] + [VMEM] * 4,
        out_shape=[
            jax.ShapeDtypeStruct((window, 2 * D), F32),
            jax.ShapeDtypeStruct((PAIRS, HEAD_DIM, LANES), F32),
            *(
                jax.ShapeDtypeStruct((pieces[i].shape[0], 2 * D), BF16)
                for i in (3, 4)
            ),
        ],
        scratch_shapes=[
            *[pltpu.VMEM((PAIRS, window, LANES), F32)] * 2,
            pltpu.VMEM((HEADS, window, LANES), F32),
            *[pltpu.VMEM((PAIRS, window, LANES), F32)] * 2,
            pltpu.VMEM(kept.shape, F32),
            pltpu.SemaphoreType.DMA((SINK_ITERS,)),
        ],
        cost_estimate=CHEAP,
        compiler_params=vmem(),
        name="sink_backward",
    )(*pieces, weight, kept, scales, projected, low, high)


def normalise(values):
    centre = values - jnp.mean(values, axis=-1, keepdims=True)
    spread = jnp.mean(centre * centre, axis=-1, keepdims=True)
    return centre * lax.rsqrt(spread + EPSILON)


def context_kernel(count, keep, *refs):
    gain_ref, w_ref, kvx_ref = refs[count : count + 3]
    x = jnp.concatenate([ref[...].astype(F32) for ref in refs[:count]], axis=0)
    short = -x.shape[0] % 16
    if short:
        x = jnp.concatenate([jnp.zeros((short, 8, D), F32), x], axis=0)
    blocks = x.shape[0]
    normed = normalise(x) * gain_ref[...].reshape(1, 1, D)
    normed = normed.astype(BF16).reshape(blocks * 8, D)
    row = lax.broadcasted_iota(jnp.int32, (LANES, LANES), 0)
    lane = lax.broadcasted_iota(jnp.int32, (LANES, LANES), 1)
    turn = (lane == (row % 16) * 8 + row // 16).astype(F32).astype(BF16)
    turned = [
        mm(turn, normed[i * LANES : (i + 1) * LANES]).astype(BF16) for i in range(blocks // 16)
    ]
    rows = []
    for b in range(8):
        part = jnp.concatenate([part[b * 16 : (b + 1) * 16] for part in turned], axis=0)
        if keep:
            refs[count + 3][b] = part
        rows.append(part)
    rows = jnp.concatenate(rows, axis=0)
    for head in range(0, HEADS, 2):
        out = mm(rows, w_ref[head * LANES : (head + 2) * LANES, :], NT).astype(BF16)
        for b in range(8):
            for e in range(2):
                kvx_ref[head + e, :, b * LANES : (b + 1) * LANES] = out[
                    b * blocks : (b + 1) * blocks, e * LANES : (e + 1) * LANES
                ]


def context_project(values, gain, w_kv, keep):
    blocks = sum(v.shape[0] for v in values)
    blocks += -blocks % 16
    outs = 2 if keep else 1
    return pl.pallas_call(
        functools.partial(context_kernel, len(values), keep),
        grid=(BLOCK // 8,),
        in_specs=[
            *(pl.BlockSpec((v.shape[0], 8, D), lambda i: (0, i, 0)) for v in values),
            pl.BlockSpec((1, D), lambda i: (0, 0)),
            pl.BlockSpec((2 * D, D), lambda i: (0, 0)),
        ],
        out_specs=[
            pl.BlockSpec((HEADS, blocks, 8 * LANES), lambda i: (0, 0, i)),
            pl.BlockSpec((8, blocks, D), lambda i: (i, 0, 0)),
        ][:outs],
        out_shape=[
            jax.ShapeDtypeStruct((HEADS, blocks, BLOCK * LANES), BF16),
            jax.ShapeDtypeStruct((BLOCK, blocks, D), BF16),
        ][:outs],
        cost_estimate=CHEAP,
        compiler_params=vmem(),
        name="context_halo" if keep else "context_own",
    )(*values, gain, w_kv)


def compact(values, lane_block):
    out = values[:BLOCK]
    for j in range(1, 4):
        out = jnp.where(lane_block == j, values[j * BLOCK : (j + 1) * BLOCK], out)
    return out


def spread(values, lane_block):
    zero = jnp.zeros_like(values)
    return jnp.concatenate([jnp.where(lane_block == j, values, zero) for j in range(4)], axis=0)


def softmax_pair(local, chosen, live):
    lane = lax.broadcasted_iota(jnp.int32, (BLOCK, LANES), 1)
    row = lax.broadcasted_iota(jnp.int32, (BLOCK, LANES), 0)
    local = jnp.where(row <= lax.rem(lane, BLOCK), local, NEGATIVE)
    chosen = jnp.where(live, chosen, NEGATIVE)
    highest = jnp.maximum(
        jnp.max(local, axis=0, keepdims=True), jnp.max(chosen, axis=0, keepdims=True)
    )
    el, es = jnp.exp(local - highest), jnp.exp(chosen - highest)
    total = jnp.sum(el, axis=0, keepdims=True) + jnp.sum(es, axis=0, keepdims=True)
    inverse = 1.0 / total
    return el * inverse, es * inverse


def half_mask(first):
    lane = lax.broadcasted_iota(jnp.int32, (LANES, LANES), 1)
    return (lane < HEAD_DIM) if first else (lane >= HEAD_DIM)


def attend_kernel(
    q_ref, kv_ref, kvh_ref, kvo_ref, plan_ref, live_ref, att_ref, skv_ref, even_ref, odd_ref
):
    own = plan_ref.shape[1]
    blocks = kvh_ref.shape[1] + own
    held = (even_ref, odd_ref)
    for e in range(2):
        plan = plan_ref[e][:, :blocks]
        for chunk in range(4):
            lanes = slice(chunk * 8 * LANES, (chunk + 1) * 8 * LANES)
            out = mm(plan, jnp.concatenate([kvh_ref[e, :, lanes], kvo_ref[e, :, lanes]], axis=0))
            for b in range(8):
                at = (chunk * 8 + b) * (own + 1)
                held[e][at : at + own, :] = out[:, b * LANES : (b + 1) * LANES]
    lane_block = lax.broadcasted_iota(jnp.int32, (BLOCK, LANES), 1) // BLOCK
    lane_half = [half_mask(True), half_mask(False)]

    def group(turn, carry):
        chains = [(turn * GROUPS + i, e) for i in range(GROUPS) for e in range(2)]
        starts = [pl.multiple_of(g * LANES, LANES) for g, _ in chains]
        both, scores = [], []
        for (g, e), start in zip(chains, starts):
            local = kv_ref[pl.ds(start, LANES), e * LANES : (e + 1) * LANES]
            chosen = jnp.concatenate(
                [held[e][pl.ds(4 * g + i, BLOCK, stride=own + 1), :] for i in range(4)], axis=0
            ).astype(BF16)
            skv_ref[pl.ds(start, LANES), e * LANES : (e + 1) * LANES] = chosen
            both.append(jnp.concatenate([local, chosen], axis=0))
        for (g, e), start, kv in zip(chains, starts, both):
            q = q_ref[pl.ds(start, LANES), :] * 0.125
            qm = jnp.where(lane_half[e], q, jnp.zeros_like(q))
            out = mm(kv, qm, NT)
            scores.append((compact(out[:LANES], lane_block), compact(out[LANES:], lane_block)))
        weights = []
        for (g, e), (local, chosen) in zip(chains, scores):
            weights.append(softmax_pair(local, chosen, live_ref[pl.ds(g, 1), :] > 0.0))
        outs = []
        for (g, e), kv, (wl, ws) in zip(chains, both, weights):
            wide = jnp.concatenate(
                [spread(wl.astype(BF16), lane_block), spread(ws.astype(BF16), lane_block)], axis=0
            )
            turned = kv.T
            outs.append(mm(turned[HEAD_DIM:] if e == 0 else turned[:HEAD_DIM], wide))
        for i in range(GROUPS):
            att_ref[pl.ds(starts[2 * i], LANES), :] = jnp.concatenate(
                outs[2 * i : 2 * i + 2], axis=0
            ).T.astype(BF16)
        return carry

    lax.fori_loop(0, own // 4 // GROUPS, group, 0)


def attend(q, kv, kvh, kvo, plan, live):
    tok, own, halo = q.shape[0], plan.shape[1], kvh.shape[1]
    return pl.pallas_call(
        attend_kernel,
        grid=(PAIRS,),
        in_specs=[
            pl.BlockSpec((tok, LANES), lambda j: (0, j)),
            pl.BlockSpec((tok, 2 * LANES), lambda j: (0, j)),
            pl.BlockSpec((2, halo, BLOCK * LANES), lambda j: (j, 0, 0)),
            pl.BlockSpec((2, own, BLOCK * LANES), lambda j: (j, 0, 0)),
            pl.BlockSpec((2, own, LANES), lambda j: (j, 0, 0)),
            pl.BlockSpec((tok // LANES, LANES), lambda j: (0, 0)),
        ],
        out_specs=[
            pl.BlockSpec((tok, LANES), lambda j: (0, j)),
            pl.BlockSpec((tok, 2 * LANES), lambda j: (0, j)),
        ],
        out_shape=[
            jax.ShapeDtypeStruct((tok, D), BF16),
            jax.ShapeDtypeStruct((tok, 2 * D), BF16),
        ],
        scratch_shapes=[pltpu.VMEM((BLOCK * (own + 1), LANES), F32)] * 2,
        cost_estimate=CHEAP,
        compiler_params=vmem(),
        name="attend",
    )(q, kv, kvh, kvo, plan, live)


def attend_back_kernel(
    q_ref, kv_ref, skv_ref, go_ref, kvh_ref, kvo_ref, plan_ref, live_ref,
    gq_ref, gkv_ref, gh_ref, gp_ref, even_ref, odd_ref, leven_ref, lodd_ref,
):
    own = plan_ref.shape[1]
    halo = kvh_ref.shape[1]
    blocks = halo + own
    held = (even_ref, odd_ref)
    lheld = (leven_ref, lodd_ref)
    lane_block = lax.broadcasted_iota(jnp.int32, (BLOCK, LANES), 1) // BLOCK
    lane_half = [half_mask(True), half_mask(False)]

    def group(turn, carry):
        chains = [(turn * GROUPS + i, e) for i in range(GROUPS) for e in range(2)]
        starts = [pl.multiple_of(g * LANES, LANES) for g, _ in chains]
        both, right, scores = [], [], []
        for (g, e), start in zip(chains, starts):
            lanes = slice(e * LANES, (e + 1) * LANES)
            rows = pl.ds(start, LANES)
            both.append(jnp.concatenate([kv_ref[rows, lanes], skv_ref[rows, lanes]], axis=0))
            q = q_ref[rows, :] * 0.125
            go = go_ref[rows, :]
            go = jnp.concatenate([go[:, HEAD_DIM:], go[:, :HEAD_DIM]], axis=1)
            qm = jnp.where(lane_half[e], q, jnp.zeros_like(q))
            gm = jnp.where(lane_half[1 - e], go, jnp.zeros_like(go))
            right.append(jnp.concatenate([qm, gm], axis=0))
        for kv, other in zip(both, right):
            out = mm(kv, other, NT)
            scores.append(
                [
                    compact(out[rows, lanes], lane_block)
                    for lanes in (slice(0, LANES), slice(LANES, 2 * LANES))
                    for rows in (slice(0, LANES), slice(LANES, 2 * LANES))
                ]
            )
        wides = []
        for (g, e), (sl, ss, dl, ds) in zip(chains, scores):
            wl, ws = softmax_pair(sl, ss, live_ref[pl.ds(g, 1), :] > 0.0)
            inner = jnp.sum(wl * dl + ws * ds, axis=0, keepdims=True)
            low = [v.astype(BF16) for v in (wl, ws, wl * (dl - inner), ws * (ds - inner))]
            wides.append(low)
        outs = []
        for (g, e), start, kv, other, (wl, ws, gl, gs) in zip(chains, starts, both, right, wides):
            weights = jnp.concatenate([spread(wl, lane_block), spread(ws, lane_block)], axis=0)
            gscore = jnp.concatenate([spread(gl, lane_block), spread(gs, lane_block)], axis=0)
            gboth = mm(jnp.concatenate([gscore, weights], axis=1), other)
            lheld[e][pl.ds(start, LANES), :] = gboth[:LANES]
            for i in range(4):
                held[e][pl.ds(4 * g + i, BLOCK, stride=own + 1), :] = gboth[
                    LANES + i * BLOCK : LANES + (i + 1) * BLOCK
                ]
            turned = kv.T
            outs.append(mm(turned[:HEAD_DIM] if e == 0 else turned[HEAD_DIM:], gscore))
        for i in range(GROUPS):
            gq_ref[pl.ds(starts[2 * i], LANES), :] = (
                jnp.concatenate(outs[2 * i : 2 * i + 2], axis=0).T * 0.125
            ).astype(BF16)
        return carry

    lax.fori_loop(0, own // 4 // GROUPS, group, 0)
    for e in range(2):
        plan = plan_ref[e][:, :blocks]
        gplan = jnp.zeros((own, blocks), F32)
        for chunk in range(4):
            lanes = slice(chunk * 8 * LANES, (chunk + 1) * 8 * LANES)
            grads = jnp.concatenate(
                [
                    held[e][(chunk * 8 + b) * (own + 1) : (chunk * 8 + b) * (own + 1) + own, :]
                    for b in range(8)
                ],
                axis=1,
            ).astype(BF16)
            here = jnp.concatenate([kvh_ref[e, :, lanes], kvo_ref[e, :, lanes]], axis=0)
            gplan = gplan + mm(grads, here, NT)
            gcontext = mm(plan, grads, TN)
            gh_ref[e, :, lanes] = gcontext[:halo].astype(BF16)
            for b in range(8):
                at = (chunk * 8 + b) * (own + 1)
                held[e][at : at + own, :] = gcontext[halo:, b * LANES : (b + 1) * LANES]
        gp_ref[e] = jnp.concatenate([gplan, jnp.zeros((own, LANES - blocks), F32)], axis=1)

    def finish(g, carry):
        start = pl.multiple_of(g * LANES, LANES)
        for e in range(2):
            rest = jnp.concatenate(
                [held[e][pl.ds(4 * g + i, BLOCK, stride=own + 1), :] for i in range(4)], axis=0
            )
            gkv_ref[pl.ds(start, LANES), e * LANES : (e + 1) * LANES] = (
                rest + lheld[e][pl.ds(start, LANES), :]
            ).astype(BF16)
        return carry

    lax.fori_loop(0, own // 4, finish, 0)


def attend_back(q, kv, skv, go, kvh, kvo, plan, live, first, pairs):
    tok, own, halo = q.shape[0], plan.shape[1], kvh.shape[1]
    return pl.pallas_call(
        attend_back_kernel,
        grid=(pairs,),
        in_specs=[
            pl.BlockSpec((tok, LANES), lambda j: (0, j + first)),
            pl.BlockSpec((tok, 2 * LANES), lambda j: (0, j + first)),
            pl.BlockSpec((tok, 2 * LANES), lambda j: (0, j + first)),
            pl.BlockSpec((tok, LANES), lambda j: (0, j + first)),
            pl.BlockSpec((2, halo, BLOCK * LANES), lambda j: (j + first, 0, 0)),
            pl.BlockSpec((2, own, BLOCK * LANES), lambda j: (j + first, 0, 0)),
            pl.BlockSpec((2, own, LANES), lambda j: (j + first, 0, 0)),
            pl.BlockSpec((tok // LANES, LANES), lambda j: (0, 0)),
        ],
        out_specs=[
            pl.BlockSpec((tok, LANES), lambda j: (0, j)),
            pl.BlockSpec((tok, 2 * LANES), lambda j: (0, j)),
            pl.BlockSpec((2, halo, BLOCK * LANES), lambda j: (j, 0, 0)),
            pl.BlockSpec((2, own, LANES), lambda j: (j, 0, 0)),
        ],
        out_shape=[
            jax.ShapeDtypeStruct((tok, pairs * LANES), BF16),
            jax.ShapeDtypeStruct((tok, 2 * pairs * LANES), BF16),
            jax.ShapeDtypeStruct((2 * pairs, halo, BLOCK * LANES), BF16),
            jax.ShapeDtypeStruct((2 * pairs, own, LANES), F32),
        ],
        scratch_shapes=[pltpu.VMEM((BLOCK * (own + 1), LANES), F32)] * 4,
        cost_estimate=CHEAP,
        compiler_params=vmem(),
        name="attend_back",
    )(q, kv, skv, go, kvh, kvo, plan, live)


def halo_kernel(
    low_ref, high_ref, nh_ref, wq_ref, w_ref, gm_ref, far_ref, near_ref, gw_ref, block_ref
):
    halo = low_ref.shape[1]
    far = far_ref.shape[1]

    @pl.when(pl.program_id(0) == 0)
    def _():
        gw_ref[...] = jnp.zeros_like(gw_ref)
        grads = gm_ref[...].astype(BF16)
        block_ref[...] = mm(grads[:, :D], wq_ref[...]) + mm(widen_keys(grads[:, D:]), w_ref[...])

    rows = jnp.concatenate(
        [
            jnp.concatenate(
                [
                    ref[head, :, b * LANES : (b + 1) * LANES]
                    for ref in (low_ref, high_ref)
                    for head in range(ref.shape[0])
                ],
                axis=1,
            )
            for b in range(8)
        ],
        axis=0,
    )
    out = (mm(rows, w_ref[...]).reshape(8, halo, D) + block_ref[...][None]).astype(BF16)
    far_ref[...] = out[:, :far]
    near_ref[...] = out[:, far:]
    gw_ref[...] += mm(rows, nh_ref[...].reshape(8 * halo, D), TN)


def halo_back(low, high, nh, w_q, w_kv, gm, far):
    halo = low.shape[1]
    part = lambda v: pl.BlockSpec((v.shape[0], halo, 8 * LANES), lambda i: (0, 0, i))
    return pl.pallas_call(
        halo_kernel,
        grid=(BLOCK // 8,),
        in_specs=[
            part(low),
            part(high),
            pl.BlockSpec((8, halo, D), lambda i: (i, 0, 0)),
            once((D, D)),
            once((2 * D, D)),
            once((halo, 2 * D)),
        ],
        out_specs=[
            pl.BlockSpec((8, far, D), lambda i: (i, 0, 0)),
            pl.BlockSpec((8, halo - far, D), lambda i: (i, 0, 0)),
            pl.BlockSpec((2 * D, D), lambda i: (0, 0)),
        ],
        out_shape=[
            jax.ShapeDtypeStruct((BLOCK, far, D), BF16),
            jax.ShapeDtypeStruct((BLOCK, halo - far, D), BF16),
            jax.ShapeDtypeStruct((2 * D, D), F32),
        ],
        scratch_shapes=[pltpu.VMEM((halo, D), F32)],
        cost_estimate=CHEAP,
        compiler_params=vmem(),
        name="halo_back",
    )(low, high, nh, w_q, w_kv, gm)


def project_kernel(x_ref, gain_ref, wq_ref, wkv_ref, n_ref, q_ref, kv_ref, m_ref, head_ref, tail_ref):
    rows = x_ref.shape[0]
    blocks = rows // BLOCK
    normed = (normalise(x_ref[...].astype(F32)) * gain_ref[...]).astype(BF16)
    n_ref[...] = normed
    q = mm(normed, wq_ref[...], NT).astype(BF16)
    q_ref[...] = q
    kv = mm(normed, wkv_ref[...], NT).astype(BF16)
    kv_ref[...] = kv
    half = lax.broadcasted_iota(jnp.int32, (1, LANES), 1) < HEAD_DIM
    m_ref[:, :D] = jnp.mean(q.astype(F32).reshape(blocks, BLOCK, D), axis=1)
    for pair in range(PAIRS):
        even = kv[:, 2 * pair * LANES : (2 * pair + 1) * LANES]
        odd = kv[:, (2 * pair + 1) * LANES : (2 * pair + 2) * LANES]
        keys = jnp.where(half, even.astype(F32), odd.astype(F32))
        m_ref[:, D + pair * LANES : D + (pair + 1) * LANES] = jnp.mean(
            keys.reshape(blocks, BLOCK, LANES), axis=1
        )
    m_ref[:, 2 * D :] = jnp.mean(normed.astype(F32).reshape(blocks, BLOCK, D), axis=1)
    at = pl.program_id(0)
    ends = head_ref.shape[0] // blocks
    for ref, first in ((head_ref, 0), (tail_ref, pl.num_programs(0) - ends)):

        @pl.when((at >= first) & (at < first + ends))
        def _():
            ref[pl.ds(pl.multiple_of((at - first) * blocks, 8), blocks), :] = m_ref[...]


def project(x, gain, wt_q, wt_kv, ends):
    tok = x.shape[0]
    tile = 8 * BLOCK
    return pl.pallas_call(
        project_kernel,
        grid=(tok // tile,),
        in_specs=[
            pl.BlockSpec((tile, D), lambda i: (i, 0)),
            pl.BlockSpec((1, D), lambda i: (0, 0)),
            pl.BlockSpec((D, D), lambda i: (0, 0)),
            pl.BlockSpec((2 * D, D), lambda i: (0, 0)),
        ],
        out_specs=[
            pl.BlockSpec((tile, D), lambda i: (i, 0)),
            pl.BlockSpec((tile, D), lambda i: (i, 0)),
            pl.BlockSpec((tile, 2 * D), lambda i: (i, 0)),
            pl.BlockSpec((8, 3 * D), lambda i: (i, 0)),
            once((ends, 3 * D)),
            once((ends, 3 * D)),
        ],
        out_shape=[
            jax.ShapeDtypeStruct((tok, D), BF16),
            jax.ShapeDtypeStruct((tok, D), BF16),
            jax.ShapeDtypeStruct((tok, 2 * D), BF16),
            jax.ShapeDtypeStruct((tok // BLOCK, 3 * D), F32),
            jax.ShapeDtypeStruct((ends, 3 * D), F32),
            jax.ShapeDtypeStruct((ends, 3 * D), F32),
        ],
        cost_estimate=CHEAP,
        compiler_params=vmem(),
        name="project",
    )(x, gain, wt_q, wt_kv)


PIECE_ONE = 208
PIECE_TWO = 576
PARTS_TWO = 592


def place(vector, start):
    size = vector.shape[1]
    row = lax.broadcasted_iota(jnp.int32, (size, LANES), 0)
    lane = lax.broadcasted_iota(jnp.int32, (size, LANES), 1)
    pick = (lane == row + start).astype(F32).astype(BF16)
    return mm(jnp.broadcast_to(vector.astype(F32), (16, size)).astype(BF16), pick)


def pack_kernel(
    wqkv_ref, wsort_ref, g1, bo, g2, bi, bd, win_ref, wdown_ref, wout_ref, x_ref,
    one_ref, two_ref, tail_ref,
):
    tail_ref[...] = x_ref[x_ref.shape[0] - tail_ref.shape[0] :, :]
    one_ref[:192, :] = wqkv_ref[...]
    row = place(g1[...], 0) + place(bo[...], 16) + place(g2[...], 32)
    row = row + place(bi[...], 48) + place(bd[...], 112)
    one_ref[192:, :] = jnp.concatenate([wsort_ref[...].astype(F32), row[:8]], axis=0).astype(BF16)
    two_ref[:256, :] = win_ref[...].astype(F32).T.astype(BF16)
    for k in range(4):
        two_ref[256 + k * 64 : 256 + (k + 1) * 64, :] = wdown_ref[:, k * LANES : (k + 1) * LANES]
    two_ref[512:, :] = wout_ref[...]


def pack(w_qkv, w_sort, vectors, w_in, w_down, w_out, x, tail):
    most = 512
    last = x.shape[0] // most - 1
    return pl.pallas_call(
        pack_kernel,
        grid=(1,),
        in_specs=[VMEM] * 10 + [pl.BlockSpec((most, D), lambda i: (last, 0))],
        out_shape=[
            jax.ShapeDtypeStruct((PIECE_ONE, LANES), BF16),
            jax.ShapeDtypeStruct((PIECE_TWO, LANES), BF16),
            jax.ShapeDtypeStruct((tail, D), BF16),
        ],
        cost_estimate=CHEAP,
        compiler_params=vmem(),
        name="pack",
    )(w_qkv.T, w_sort.T, *(v.reshape(1, -1) for v in vectors), w_in, w_down.T, w_out.T, x)


def rows_at(start, size):
    return pl.ds(pl.multiple_of(start * size, size), size)


def each_owner(at_ref, visit):
    def planes(z, carry):
        for other in range(2):
            c = at_ref[2] ^ other
            for h in range(4):
                visit(other == 0, h, z, 2 * z + c, c)
        return carry

    lax.fori_loop(0, 4, planes, 0)


def each_piece(at_ref, mine_ref, other_ref, visit):
    def owner(own, h, z, b, c):
        source = mine_ref if own else other_ref
        visit(h, b, c, source.at[at_ref[0] ^ h, at_ref[1] ^ z])

    each_owner(at_ref, owner)


def widen(vecs, start, size):
    total = 32 * size
    lane = lax.broadcasted_iota(jnp.int32, (LANES, total), 1)
    row = lax.broadcasted_iota(jnp.int32, (LANES, total), 0)
    pick = (row == start + lax.rem(lane, size)).astype(F32).astype(BF16)
    every = mm(vecs, pick)
    owner = lax.broadcasted_iota(jnp.int32, (32, total), 0)
    lane = lax.broadcasted_iota(jnp.int32, (32, total), 1)
    return jnp.sum(jnp.where(owner == lane // size, every, 0.0), axis=0, keepdims=True)


def assemble_kernel(
    at_ref, mine_ref, other_ref, wq_ref, wkv_ref, ws_ref, g1_ref, bo_ref, g2_ref, bi_ref, bd_ref,
    vecs_ref,
):
    def visit(h, b, c, piece):
        lanes = slice(h * LANES, (h + 1) * LANES)
        wq_ref[rows_at(b, 64), lanes] = piece[:64, :]
        wkv_ref[rows_at(2 * b + c, 64), lanes] = piece[64:128, :]
        wkv_ref[rows_at(2 * b + 1 - c, 64), lanes] = piece[128:192, :]
        tail = piece[192:208, :].astype(F32)
        ws_ref[h, rows_at(b, 8), :] = tail[:8]
        vecs_ref[pl.ds(h * 8 + b, 1), :] = tail[8:9]

    each_piece(at_ref, mine_ref, other_ref, visit)
    vecs = vecs_ref[...].astype(BF16)
    g1_ref[...] = widen(vecs, 0, 16)
    bo_ref[...] = widen(vecs, 16, 16)
    g2_ref[...] = widen(vecs, 32, 16)
    bi_ref[...] = widen(vecs, 48, 64)
    bd_ref[...] = widen(vecs, 112, 16)


def assemble(at, mine, other):
    row = jax.ShapeDtypeStruct((1, D), F32)
    return pl.pallas_call(
        assemble_kernel,
        in_specs=[SMEM, VMEM, VMEM],
        out_shape=[
            jax.ShapeDtypeStruct((D, D), BF16),
            jax.ShapeDtypeStruct((2 * D, D), BF16),
            jax.ShapeDtypeStruct((PAIRS, HEAD_DIM, LANES), F32),
            row, row, row, jax.ShapeDtypeStruct((1, FF), F32), row,
        ],
        scratch_shapes=[pltpu.VMEM((32, LANES), F32)],
        cost_estimate=CHEAP,
        compiler_params=vmem(),
        name="assemble",
    )(at, mine, other)


GELU_A = 0.7978845608028654
GELU_B = 0.044715


def feed_tile(x, att, g, bo, g2, bi, bd, win, wdown, wout, acc_in, acc_down, acc_out, sums):
    middle = x.astype(F32) + mm(att, wout[...], NT) + bo
    centre = middle - jnp.mean(middle, axis=-1, keepdims=True)
    spread_ = jnp.mean(centre * centre, axis=-1, keepdims=True)
    inverse = lax.rsqrt(spread_ + EPSILON)
    hat = centre * inverse
    normed = (hat * g2).astype(BF16)
    normed_t = normed.T
    g_t = g.T
    out = jnp.zeros(middle.shape, F32)
    u = jnp.zeros(middle.shape, F32)
    cut = 512
    for k in range(FF // cut):
        cols = slice(k * cut, (k + 1) * cut)
        pre = mm(normed, win[cols, :], NT) + bi[:, cols]
        square = pre * pre
        t = jnp.tanh(GELU_A * pre * (1.0 + GELU_B * square))
        half = 0.5 * (1.0 + t)
        hidden = (pre * half).astype(BF16)
        slope = half + (0.5 * GELU_A) * pre * (1.0 - t * t) * (1.0 + (3.0 * GELU_B) * square)
        g_pre = (mm(g, wdown[:, cols], NN) * slope).astype(BF16)
        out = out + mm(hidden, wdown[:, cols], NT)
        u = u + mm(g_pre, win[cols, :], NN)
        part = mm(normed_t, g_pre)
        for i in range(2):
            acc_in[2 * k + i] += part[:, i * 256 : (i + 1) * 256]
        acc_down[:, cols] += mm(g_t, hidden)
        sums[4:5, cols] += jnp.sum(g_pre.astype(F32), axis=0, keepdims=True)
    gf = g.astype(F32)
    sums[1:2, :D] += jnp.sum(u * hat, axis=0, keepdims=True)
    sums[3:4, :D] += jnp.sum(gf, axis=0, keepdims=True)
    du = u * g2
    inner = jnp.mean(du * hat, axis=-1, keepdims=True)
    g_middle = gf + inverse * (du - jnp.mean(du, axis=-1, keepdims=True) - hat * inner)
    branch = g_middle.astype(BF16)
    sums[0:1, :D] += jnp.sum(branch.astype(F32), axis=0, keepdims=True)
    acc_out[...] += mm(branch.T, att)
    return (middle + out + bd).astype(BF16), g_middle, mm(branch, wout[...], NN).astype(BF16)


def clear(*refs):
    for ref in refs:
        ref[...] = jnp.zeros_like(ref)


def narrow(sums):
    total = jnp.zeros((32, LANES), F32)
    for index, start, size in ((0, 16, 16), (1, 32, 16), (4, 48, 64), (3, 112, 16)):
        width = 32 * size
        owner = lax.broadcasted_iota(jnp.int32, (32, width), 0)
        lane = lax.broadcasted_iota(jnp.int32, (32, width), 1)
        kept = jnp.where(owner == lane // size, sums[index : index + 1, :width], 0.0)
        row = lax.broadcasted_iota(jnp.int32, (width, LANES), 0)
        lane = lax.broadcasted_iota(jnp.int32, (width, LANES), 1)
        pick = (lane == start + lax.rem(row, size)).astype(F32).astype(BF16)
        total = total + mm(kept.astype(BF16), pick)
    return total


def feed_fast_kernel(
    at_ref, x_ref, att_ref, g_ref, bo_ref, g2_ref, bi_ref, bd_ref, mine_ref, other_ref,
    out_ref, gm_ref, ga_ref, keep_ref, send_ref,
    win, wdown, wout, acc_in, acc_down, acc_out, sums, vecs,
):
    @pl.when(pl.program_id(0) == 0)
    def _():
        def visit(h, b, c, piece):
            win[rows_at(b, 256), h * LANES : (h + 1) * LANES] = piece[:256, :]
            for k in range(4):
                lanes = slice(h * 512 + k * LANES, h * 512 + (k + 1) * LANES)
                wdown[rows_at(b, 64), lanes] = piece[256 + k * 64 : 320 + k * 64, :]
            wout[rows_at(b, 64), h * LANES : (h + 1) * LANES] = piece[512:576, :]

        each_piece(at_ref, mine_ref, other_ref, visit)
        clear(acc_in, acc_down, acc_out, sums)

    out_ref[...], gm_ref[...], ga_ref[...] = feed_tile(
        x_ref[...], att_ref[...], g_ref[...], bo_ref[...], g2_ref[...], bi_ref[...], bd_ref[...],
        win, wdown, wout, acc_in, acc_down, acc_out, sums,
    )

    @pl.when(pl.program_id(0) == pl.num_programs(0) - 1)
    def _():
        vecs[...] = narrow(sums)

        def owner(own, h, z, b, c):
            ref = keep_ref if own else send_ref
            for k in range(2):
                ref[h, z, k * LANES : (k + 1) * LANES, :] = acc_in[
                    b, h * LANES : (h + 1) * LANES, k * LANES : (k + 1) * LANES
                ].astype(BF16)
            for k in range(4):
                ref[h, z, 256 + k * 64 : 320 + k * 64, :] = acc_down[
                    rows_at(b, 64), h * 512 + k * LANES : h * 512 + (k + 1) * LANES
                ].astype(BF16)
            ref[h, z, 512:576, :] = acc_out[
                rows_at(b, 64), h * LANES : (h + 1) * LANES
            ].astype(BF16)
            ref[h, z, 576:592, :] = jnp.broadcast_to(
                vecs[pl.ds(h * 8 + b, 1), :], (16, LANES)
            ).astype(BF16)

        each_owner(at_ref, owner)


def feed_fast(at, x, att, g, bo, g2, bi, bd, mine, other):
    tok = x.shape[0]
    tile = 512
    tiled = pl.BlockSpec((tile, D), lambda i: (i, 0))
    parts = (4, 4, PARTS_TWO, LANES)
    return pl.pallas_call(
        feed_fast_kernel,
        grid=(tok // tile,),
        in_specs=[
            SMEM, tiled, tiled, tiled, once((1, D)), once((1, D)), once((1, FF)), once((1, D)),
            once(mine.shape), once(other.shape),
        ],
        out_specs=[tiled, tiled, tiled, once(parts), once(parts)],
        out_shape=[
            jax.ShapeDtypeStruct((tok, D), BF16),
            jax.ShapeDtypeStruct((tok, D), F32),
            jax.ShapeDtypeStruct((tok, D), BF16),
            jax.ShapeDtypeStruct(parts, BF16),
            jax.ShapeDtypeStruct(parts, BF16),
        ],
        scratch_shapes=[
            pltpu.VMEM((FF, D), BF16), pltpu.VMEM((D, FF), BF16), pltpu.VMEM((D, D), BF16),
            pltpu.VMEM((8, D, FF // 8), F32), pltpu.VMEM((D, FF), F32), pltpu.VMEM((D, D), F32),
            pltpu.VMEM((8, FF), F32), pltpu.VMEM((32, LANES), F32),
        ],
        cost_estimate=CHEAP,
        compiler_params=vmem(60),
        name="feed",
    )(at, x, att, g, bo, g2, bi, bd, mine, other)


def feed_slow_kernel(
    x_ref, att_ref, g_ref, bo_ref, g2_ref, bi_ref, bd_ref, win, wdown, wout,
    out_ref, gm_ref, ga_ref, acc_in, acc_down, acc_out, sums,
):
    @pl.when(pl.program_id(0) == 0)
    def _():
        clear(acc_in, acc_down, acc_out, sums)

    out_ref[...], gm_ref[...], ga_ref[...] = feed_tile(
        x_ref[...], att_ref[...], g_ref[...], bo_ref[...], g2_ref[...], bi_ref[...], bd_ref[...],
        win, wdown, wout, acc_in, acc_down, acc_out, sums,
    )


def feed_slow(x, att, g, bo, g2, bi, bd, win, wdown, wout):
    tok = x.shape[0]
    tile = 512
    tiled = pl.BlockSpec((tile, D), lambda i: (i, 0))
    wide, square, rows, cut = (D, FF), (D, D), (8, FF), (8, D, FF // 8)
    return pl.pallas_call(
        feed_slow_kernel,
        grid=(tok // tile,),
        in_specs=[
            tiled, tiled, tiled, once((1, D)), once((1, D)), once((1, FF)), once((1, D)),
            once((FF, D)), once(wide), once(square),
        ],
        out_specs=[tiled, tiled, tiled, once(cut), once(wide), once(square), once(rows)],
        out_shape=[
            jax.ShapeDtypeStruct((tok, D), BF16),
            jax.ShapeDtypeStruct((tok, D), F32),
            jax.ShapeDtypeStruct((tok, D), BF16),
            jax.ShapeDtypeStruct(cut, F32),
            jax.ShapeDtypeStruct(wide, F32),
            jax.ShapeDtypeStruct(square, F32),
            jax.ShapeDtypeStruct(rows, F32),
        ],
        cost_estimate=CHEAP,
        compiler_params=vmem(60),
        name="feed_whole",
    )(x, att, g, bo, g2, bi, bd, win, wdown, wout)


def split_kernel(which, at_ref, keep_ref, got_ref, *outs):
    for r, out in enumerate(outs):
        i = at_ref[which] ^ r
        out[...] = (keep_ref[i].astype(F32) + got_ref[i].astype(F32)).astype(BF16)


def split_sum(at, which, keep, got):
    one, two, rows, lanes = keep.shape
    per = 1 if rows > 400 else 2
    block = pl.BlockSpec((one, per, rows, lanes), lambda i: (0, i, 0, 0))
    return pl.pallas_call(
        functools.partial(split_kernel, which),
        grid=(two // per,),
        in_specs=[SMEM, block, block],
        out_specs=[pl.BlockSpec((per, rows, lanes), lambda i: (i, 0, 0))] * one,
        out_shape=[jax.ShapeDtypeStruct((two, rows, lanes), BF16)] * one,
        cost_estimate=CHEAP,
        compiler_params=vmem(),
        name="split_sum",
    )(at, keep, got)


def merge_kernel(which, at_ref, a_ref, b_ref, c_ref, d_ref, *outs):
    for r, out in enumerate(outs):
        i = at_ref[which] ^ r
        total = a_ref[i].astype(F32) + b_ref[i].astype(F32)
        out[...] = (total + c_ref[i].astype(F32) + d_ref[i].astype(F32)).astype(BF16)


def merge_sum(at, which, pieces):
    count, rows, lanes = pieces[0].shape
    return pl.pallas_call(
        functools.partial(merge_kernel, which),
        in_specs=[SMEM] + [VMEM] * 4,
        out_shape=[jax.ShapeDtypeStruct((rows, lanes), BF16)] * count,
        cost_estimate=CHEAP,
        compiler_params=vmem(),
        name="merge_sum",
    )(at, *pieces)


def last_two_kernel(a_ref, b_ref, c_ref, d_ref, gin_ref, gdown_ref, gout_ref, bo, g2, bi, bd):
    total = a_ref[...].astype(F32) + b_ref[...].astype(F32)
    total = total + c_ref[...].astype(F32) + d_ref[...].astype(F32)
    for k in range(2):
        gin_ref[:, k * LANES : (k + 1) * LANES] = total[k * LANES : (k + 1) * LANES]
    for k in range(4):
        gdown_ref[:, k * LANES : (k + 1) * LANES] = total[256 + k * 64 : 320 + k * 64]
    gout_ref[...] = total[512:576]
    row = total[576:577]
    bo[...], g2[...], bi[...], bd[...] = row[:, 16:32], row[:, 32:48], row[:, 48:112], row[:, 112:]


def last_two(pieces):
    return pl.pallas_call(
        last_two_kernel,
        out_shape=[
            jax.ShapeDtypeStruct((LANES, 256), F32),
            jax.ShapeDtypeStruct((64, 512), F32),
            jax.ShapeDtypeStruct((64, LANES), F32),
            *(jax.ShapeDtypeStruct((1, n), F32) for n in (16, 16, 64, 16)),
        ],
        cost_estimate=CHEAP,
        compiler_params=vmem(),
        name="last_two",
    )(*pieces)


def last_one_kernel(a_ref, b_ref, c_ref, d_ref, gw_ref, gs_ref, g1_ref):
    total = a_ref[...].astype(F32) + b_ref[...].astype(F32)
    total = total + c_ref[...].astype(F32) + d_ref[...].astype(F32)
    gw_ref[...] = total[:192]
    gs_ref[...] = total[192:200]
    g1_ref[...] = total[200:201, :16]


def last_one(pieces):
    return pl.pallas_call(
        last_one_kernel,
        out_shape=[
            jax.ShapeDtypeStruct((192, LANES), F32),
            jax.ShapeDtypeStruct((8, LANES), F32),
            jax.ShapeDtypeStruct((1, 16), F32),
        ],
        cost_estimate=CHEAP,
        compiler_params=vmem(),
        name="last_one",
    )(*pieces)


def widen_keys(gmk):
    half = lax.broadcasted_iota(jnp.int32, (gmk.shape[0], LANES), 1) < HEAD_DIM
    zero = jnp.zeros((gmk.shape[0], LANES), gmk.dtype)
    wide = []
    for pair in range(PAIRS):
        tile = gmk[:, pair * LANES : (pair + 1) * LANES]
        wide += [jnp.where(half, tile, zero), jnp.where(half, zero, tile)]
    return jnp.concatenate(wide, axis=1)


def weight_kernel(
    fast, at_ref, ql_ref, qh_ref, kvl_ref, kvh_ref, n_ref, wq_ref, wkv_ref, gm_ref,
    pa, pb, pc, pd, pe, halo_ref, gain_ref, gs_ref, keep_ref, send_ref, acc_q, acc_kv,
):
    @pl.when(pl.program_id(0) == 0)
    def _():
        means = jnp.concatenate([ref[:, 2 * D :] for ref in (pa, pb, pc, pd, pe)], axis=0)
        means = means.astype(BF16)
        grads = (gm_ref[...] * float(BLOCK)).astype(BF16)
        acc_q[...] = mm(grads[:, :D], means, TN)
        acc_kv[...] = halo_ref[...] + mm(widen_keys(grads[:, D:]), means, TN)

    normed = n_ref[...]
    cut = ql_ref.shape[1]
    for lo, q_ref, kv_ref in ((0, ql_ref, kvl_ref), (cut, qh_ref, kvh_ref)):
        hi = lo + q_ref.shape[1]
        acc_q[lo:hi, :] += mm(q_ref[...].T, normed)
        acc_kv[2 * lo : 2 * hi, :] += mm(kv_ref[...].T, normed)

    @pl.when(pl.program_id(0) == pl.num_programs(0) - 1)
    def _():
        gain = jnp.sum(acc_q[...] * wq_ref[...].astype(F32), axis=0, keepdims=True)
        gain = gain + jnp.sum(acc_kv[...] * wkv_ref[...].astype(F32), axis=0, keepdims=True)
        gain = gain / gain_ref[...]
        if not fast:
            keep_ref[:D, :] = acc_q[...]
            keep_ref[D:, :] = acc_kv[...]
            send_ref[...] = jnp.broadcast_to(gain, (8, D))
            return
        def owner(own, h, z, b, c):
            ref = keep_ref if own else send_ref
            lanes = slice(h * LANES, (h + 1) * LANES)
            ref[z, h, :64, :] = acc_q[rows_at(b, 64), lanes].astype(BF16)
            ref[z, h, 64:128, :] = acc_kv[rows_at(2 * b + c, 64), lanes].astype(BF16)
            ref[z, h, 128:192, :] = acc_kv[rows_at(2 * b + 1 - c, 64), lanes].astype(BF16)
            share = pltpu.roll(
                jnp.broadcast_to(gain[:, lanes], (8, LANES)), lax.rem(LANES - 16 * b, LANES), 1
            )
            ref[z, h, 192:208, :] = jnp.concatenate(
                [gs_ref[h, rows_at(b, 8), :], share], axis=0
            ).astype(BF16)

        each_owner(at_ref, owner)


def weight_back(at, gq, gkv, normed, wt_q, wt_kv, gm, pieces, halo, gain, gsort, fast):
    tok = normed.shape[0]
    tile = 512
    parts = (4, 4, PIECE_ONE, LANES)
    shapes = (parts, parts) if fast else ((3 * D, D), (8, D))
    kind = BF16 if fast else F32
    rows = lambda width: pl.BlockSpec((tile, width), lambda i: (i, 0))
    return pl.pallas_call(
        functools.partial(weight_kernel, fast),
        grid=(tok // tile,),
        in_specs=[
            SMEM, *(rows(v.shape[1]) for v in (*gq, *gkv)), rows(D), once((D, D)),
            once((2 * D, D)), once(gm.shape), *(once(p.shape) for p in pieces),
            once((2 * D, D)), once((1, D)), once(gsort.shape),
        ],
        out_specs=[once(shapes[0]), once(shapes[1])],
        out_shape=[
            jax.ShapeDtypeStruct(shapes[0], kind),
            jax.ShapeDtypeStruct(shapes[1], kind),
        ],
        scratch_shapes=[pltpu.VMEM((D, D), F32), pltpu.VMEM((2 * D, D), F32)],
        cost_estimate=CHEAP,
        compiler_params=vmem(),
        name="weight_back",
    )(at, *gq, *gkv, normed, wt_q, wt_kv, gm, *pieces, halo, gain, gsort)


def inner_kernel(
    ql_ref, qh_ref, kvl_ref, kvh_ref, wq_ref, wkv_ref, gm_ref, fd, fe, out_ref, blocks_ref
):
    rows = ql_ref.shape[0]
    per = rows // BLOCK

    @pl.when(pl.program_id(0) == 0)
    def _():
        own, ends = fd.shape[0], fe.shape[0]
        halo = own + ends
        blocks_ref[...] = gm_ref[halo : halo + own, :] + fd[...].astype(F32)
        blocks_ref[:ends, :] += fe[...].astype(F32)

    cut = ql_ref.shape[1]
    value = mm(ql_ref[...], wq_ref[:cut, :]) + mm(qh_ref[...], wq_ref[cut:, :])
    value = value + mm(kvl_ref[...], wkv_ref[: 2 * cut, :])
    value = value + mm(kvh_ref[...], wkv_ref[2 * cut :, :])
    grads = blocks_ref[pl.ds(pl.multiple_of(pl.program_id(0) * per, per), per), :].astype(BF16)
    block = mm(grads[:, :D], wq_ref[...]) + mm(widen_keys(grads[:, D:]), wkv_ref[...])
    out_ref[...] = value + jnp.broadcast_to(block[:, None, :], (per, BLOCK, D)).reshape(rows, D)


def inner_gradient(gq, gkv, wt_q, wt_kv, gm, far):
    tok = gq[0].shape[0]
    tile = 8 * BLOCK
    rows = lambda width: pl.BlockSpec((tile, width), lambda i: (i, 0))
    return pl.pallas_call(
        inner_kernel,
        grid=(tok // tile,),
        in_specs=[
            *(rows(v.shape[1]) for v in (*gq, *gkv)), once((D, D)), once((2 * D, D)),
            once(gm.shape), *(once(f.shape) for f in far),
        ],
        out_specs=rows(D),
        out_shape=jax.ShapeDtypeStruct((tok, D), F32),
        scratch_shapes=[pltpu.VMEM((tok // BLOCK, 2 * D), F32)],
        cost_estimate=CHEAP,
        compiler_params=vmem(),
        name="inner_gradient",
    )(*gq, *gkv, wt_q, wt_kv, gm, *far)


def finish_kernel(skip, x_ref, u_ref, one_ref, two_ref, g_ref, gain_ref, out_ref, total):
    rows = x_ref.shape[0]
    at = lax.broadcasted_iota(jnp.int32, (rows, rows), 0)
    lane = lax.broadcasted_iota(jnp.int32, (rows, rows), 1)
    order = (lane == lax.rem(at, BLOCK) * 8 + at // BLOCK).astype(F32).astype(BF16)
    total[...] = u_ref[...] + mm(order, one_ref[...].reshape(rows, D))

    @pl.when(pl.program_id(0) >= skip)
    def _():
        total[...] += mm(order, two_ref[...].reshape(rows, D))

    x = x_ref[...].astype(F32)
    centre = x - jnp.mean(x, axis=-1, keepdims=True)
    inverse = lax.rsqrt(jnp.mean(centre * centre, axis=-1, keepdims=True) + EPSILON)
    hat = centre * inverse
    du = total[...] * gain_ref[...]
    inner = jnp.mean(du * hat, axis=-1, keepdims=True)
    out_ref[...] = g_ref[...] + inverse * (
        du - jnp.mean(du, axis=-1, keepdims=True) - hat * inner
    )


def finish(x, u, one, two, g_middle, gain):
    tok = x.shape[0]
    tile = 8 * BLOCK
    skip = (tok // BLOCK - two.shape[1]) // 8
    rows = lambda width: pl.BlockSpec((tile, width), lambda i: (i, 0))
    return pl.pallas_call(
        functools.partial(finish_kernel, skip),
        grid=(tok // tile,),
        in_specs=[
            rows(D), rows(D),
            pl.BlockSpec((BLOCK, 8, D), lambda i: (0, i, 0)),
            pl.BlockSpec((BLOCK, 8, D), lambda i: (0, jnp.maximum(i - skip, 0), 0)),
            rows(D), once((1, D)),
        ],
        out_specs=rows(D),
        out_shape=jax.ShapeDtypeStruct((tok, D), F32),
        scratch_shapes=[pltpu.VMEM((tile, D), F32)],
        cost_estimate=CHEAP,
        compiler_params=vmem(),
        name="finish",
    )(x, u, one, two, g_middle, gain)


class Grid:
    def __init__(self):
        self.heads = lax.axis_size("head")
        self.planes = lax.axis_size("plane")
        self.cycles = 2 * self.planes
        self.head = lax.axis_index("head")
        self.plane = lax.axis_index("plane")
        self.core = lax.axis_index("core")
        self.cycle = 2 * self.plane + self.core
        self.place = self.cycle * self.heads + self.head

    def send(self, value, pairs):
        return lax.ppermute(value, ("head", "plane", "core"), pairs)

    def number(self, head, cycle):
        return head * self.cycles + cycle

    def along(self, steps):
        count = self.heads * self.cycles
        at = lambda place: self.number(place % self.heads, place // self.heads)
        return [(at(i), at(i + steps)) for i in range(count) if 0 <= i + steps < count]

    def swap_head(self, flip):
        return [
            (self.number(h, b), self.number(h ^ flip, b))
            for h in range(self.heads)
            for b in range(self.cycles)
        ]

    def swap_plane(self, flip):
        return [
            (self.number(h, b), self.number(h, b ^ (2 * flip)))
            for h in range(self.heads)
            for b in range(self.cycles)
        ]

    def swap_core(self):
        return [
            (self.number(h, b), self.number(h, b ^ 1))
            for h in range(self.heads)
            for b in range(self.cycles)
        ]


def in_order(pieces, index):
    stacked = jnp.stack(pieces)
    count = len(pieces)
    bit = 1
    while bit < count:
        swapped = jnp.stack([stacked[i ^ bit] for i in range(count)])
        stacked = jnp.where((index & bit) != 0, swapped, stacked)
        bit *= 2
    return stacked


def gather_all(grid, piece):
    got = [piece] + [grid.send(piece, grid.swap_plane(r)) for r in range(1, grid.planes)]
    got = in_order(got, grid.plane)
    got = [got] + [grid.send(got, grid.swap_head(r)) for r in range(1, grid.heads)]
    got = in_order(got, grid.head)
    got = in_order([got, grid.send(got, grid.swap_core())], grid.core)
    got = got.transpose(1, 2, 0, *range(3, got.ndim))
    return got.reshape(grid.heads, grid.cycles, *piece.shape)


def across_planes(parts):
    return lax.all_to_all(parts, "plane", 0, 0, tiled=True)


def across_heads(parts):
    return lax.all_to_all(parts, "head", 0, 0, tiled=True)


def scatter_sum(grid, parts):
    mine = lax.dynamic_index_in_dim(parts, grid.core, 0, keepdims=False)
    other = lax.dynamic_index_in_dim(parts, 1 - grid.core, 0, keepdims=False)
    got = grid.send(other, grid.swap_core())
    total = (mine.astype(F32) + got.astype(F32)).astype(BF16)
    total = jnp.sum(across_heads(total).astype(F32), axis=0).astype(BF16)
    return jnp.sum(across_planes(total).astype(F32), axis=0)


def as_rows(value):
    flat = value.reshape(-1)
    short = -flat.shape[0] % LANES
    return jnp.pad(flat, (0, short)).reshape(-1, LANES)


def by_owner(grid, value):
    columns, rows = value.shape
    cut = value.reshape(grid.planes, 2, columns // grid.cycles, grid.heads, rows // grid.heads)
    return cut.transpose(1, 3, 0, 2, 4)


def vector_by_owner(grid, value):
    cut = value.reshape(grid.heads, grid.planes, 2, -1)
    return cut.transpose(2, 0, 1, 3)


def rows_of(value):
    lead = value.shape[:3]
    flat = value.reshape(*lead, -1)
    short = -flat.shape[-1] % LANES
    flat = jnp.pad(flat, ((0, 0),) * 3 + ((0, short),))
    return flat.reshape(*lead, -1, LANES)


def after(value, *others):
    return lax.optimization_barrier((value, *others))[0]


def weights_slow(grid, vectors, parameters):
    w_qkv, w_sort, w_in, w_down, w_out = parameters
    heads, cycles = grid.heads, grid.cycles
    first = jnp.concatenate([as_rows(w_qkv.T), as_rows(w_sort), as_rows(jnp.concatenate(vectors))])
    wide, sort_rows = as_rows(w_qkv.T).shape[0], as_rows(w_sort).shape[0]
    got = gather_all(grid, first)
    span = w_qkv.shape[1]
    wt_qkv = (
        got[:, :, :wide]
        .reshape(heads, cycles, span, D // heads)
        .transpose(1, 2, 0, 3)
        .reshape(HEADS, 3, HEAD_DIM, D)
    )
    wt_q = wt_qkv[:, 0].reshape(D, D)
    paired = wt_qkv.reshape(PAIRS, 2, 3, HEAD_DIM, D)
    wt_kv = jnp.stack(
        [paired[:, 0, 1], paired[:, 0, 2], paired[:, 1, 2], paired[:, 1, 1]], axis=1
    ).reshape(2 * D, D)
    size = w_sort.shape[0] * w_sort.shape[1]
    w_pairs = (
        got[:, :, wide : wide + sort_rows]
        .reshape(heads, cycles, -1)[:, :, :size]
        .reshape(heads, cycles, *w_sort.shape)
        .transpose(1, 3, 0, 2)
        .reshape(HEAD_DIM, PAIRS, LANES)
        .transpose(1, 0, 2)
        .astype(F32)
    )
    flat = got[:, :, wide + sort_rows :].reshape(heads, cycles, -1)
    sizes = [v.shape[0] for v in vectors]
    cuts = [sum(sizes[:i]) for i in range(len(sizes) + 1)]
    rows = [
        flat[:, :, cuts[i] : cuts[i + 1]].reshape(1, -1).astype(F32) for i in range(len(sizes))
    ]
    second = jnp.concatenate([as_rows(w_in.T), as_rows(w_down.T), as_rows(w_out.T)])
    in_rows, down_rows = as_rows(w_in.T).shape[0], as_rows(w_down.T).shape[0]
    got = gather_all(grid, second)

    def whole(depth, columns, part):
        return (
            part.reshape(heads, cycles, -1)[:, :, : columns // cycles * (depth // heads)]
            .reshape(heads, cycles, columns // cycles, depth // heads)
            .transpose(1, 2, 0, 3)
            .reshape(columns, depth)
        )

    feed = (
        whole(D, FF, got[:, :, :in_rows]),
        whole(FF, D, got[:, :, in_rows : in_rows + down_rows]),
        whole(D, D, got[:, :, in_rows + down_rows :]),
    )
    return wt_q, wt_kv, w_pairs, rows, feed


def matrix(rows, shape):
    flat = rows.reshape(-1)[: shape[0] * shape[1]]
    return flat.reshape(shape[1], shape[0]).T


def gradients_two_slow(grid, acc_in, acc_down, acc_out, sums, parameters, vectors):
    w_qkv, w_sort, w_in, w_down, w_out = parameters
    low = [
        rows_of(by_owner(grid, v.astype(BF16))) for v in (acc_in.transpose(0, 2, 1).reshape(FF, D), acc_down, acc_out)
    ]
    order = ((0, D), (1, D), (4, FF), (3, D))
    small = [vector_by_owner(grid, sums[i, :n]) for i, n in order]
    low.append(rows_of(jnp.concatenate(small, axis=-1).astype(BF16)))
    total = scatter_sum(grid, jnp.concatenate(low, axis=3))
    cuts = [0]
    for item in low:
        cuts.append(cuts[-1] + item.shape[3])
    g_in, g_down, g_out = (
        matrix(total[cuts[i] : cuts[i + 1]], w.shape) for i, w in enumerate((w_in, w_down, w_out))
    )
    flat = total[cuts[3] :].reshape(-1)
    sizes = [v.shape[0] for v in vectors[1:]]
    at = [sum(sizes[:i]) for i in range(5)]
    return g_in, g_down, g_out, *(flat[at[i] : at[i + 1]] for i in range(4))


def gradients_one_slow(grid, both, gain, gsort, parameters, vectors):
    w_qkv, w_sort = parameters[:2]
    q = both[:D].reshape(HEADS, HEAD_DIM, D)
    kv = both[D:].reshape(PAIRS, 4, HEAD_DIM, D)
    k = jnp.stack([kv[:, 0], kv[:, 3]], axis=1).reshape(HEADS, HEAD_DIM, D)
    v = jnp.stack([kv[:, 1], kv[:, 2]], axis=1).reshape(HEADS, HEAD_DIM, D)
    wide = jnp.stack([q, k, v], axis=1).reshape(3 * D, D)
    sort = gsort.transpose(0, 2, 1).reshape(grid.heads, D // grid.heads, grid.planes, 2, -1)
    low = [
        rows_of(by_owner(grid, wide.astype(BF16))),
        rows_of(sort.transpose(3, 0, 2, 1, 4).astype(BF16)),
        rows_of(vector_by_owner(grid, gain[0]).astype(BF16)),
    ]
    total = scatter_sum(grid, jnp.concatenate(low, axis=3))
    one, two = low[0].shape[3], low[0].shape[3] + low[1].shape[3]
    size = w_sort.shape[0] * w_sort.shape[1]
    return (
        matrix(total[:one], w_qkv.shape),
        total[one:two].reshape(-1)[:size].reshape(w_sort.shape),
        total[two:].reshape(-1)[: vectors[0].shape[0]],
    )


def per_device(
    tokens, cotangent, doc_lengths, norm_gain1, w_qkv, w_out, b_out, norm_gain2, w_in, b_in,
    w_down, b_down, w_sort,
):
    grid = Grid()
    heads = grid.heads
    x = tokens[0]
    upstream = cotangent[0]
    tok = x.shape[0]
    own = tok // BLOCK
    context = HALO + own
    window = HALO + own + HALO
    second = HALO - own
    fast = heads == 4 and grid.cycles == 8
    at = jnp.stack([grid.head, grid.plane, grid.core]).astype(jnp.int32)
    vectors = (norm_gain1, b_out, norm_gain2, b_in, b_down)
    parameters = (w_qkv, w_sort, w_in, w_down, w_out)

    three = range(1, 4)
    tail = (DOC_MOST - 1 - own) * BLOCK
    if fast:
        one, two, x_tail = pack(w_qkv, w_sort, vectors, w_in, w_down, w_out, x, tail)
        ones = [one] + [grid.send(one, grid.swap_plane(r)) for r in three]
        ones = jnp.stack(ones)
        ones = [ones] + [grid.send(ones, grid.swap_head(r)) for r in three]
        x_send, x_tail = lax.optimization_barrier((x, x_tail, *ones))[:2]
    else:
        x_send, x_tail = x, x[tok - tail :]
    halo_one = grid.send(x_send, grid.along(1))
    halo_two = grid.send(x_tail, grid.along(2))
    if fast:
        ones = jnp.stack(ones)
        other = grid.send(ones, grid.swap_core())
        two = after(two, other)
        twos = [two] + [grid.send(two, grid.swap_plane(r)) for r in three]
        wt_q, wt_kv, w_pairs, *rows = assemble(at, ones, other)
    else:
        wt_q, wt_kv, w_pairs, rows, feed_weights = weights_slow(grid, vectors, parameters)
        twos = []
    gain_one, bias_out, gain_two, bias_in, bias_down = rows

    begin = grid.place * own
    position = begin - HALO + jnp.arange(window, dtype=jnp.int32)
    doc_ends = jnp.cumsum(doc_lengths, dtype=jnp.int32)
    ended = jnp.sum(
        (doc_ends[None, :] <= position[:, None]).astype(jnp.int32), axis=1, dtype=jnp.int32
    )
    span_end = (grid.cycle + 1) * heads * own
    doc = jnp.where((position >= 0) & (position < span_end), ended, -1)
    fold = window - LANES
    docc = jnp.stack([doc[:LANES], jnp.concatenate([doc[LANES:], doc[fold:LANES]])])
    docn = doc[:, None]
    live = (doc[HALO:context] == doc[HALO - 1 : context - 1]) & (doc[HALO:context] >= 0)
    live = jnp.repeat(live.astype(F32), BLOCK).reshape(tok // LANES, LANES)

    normed, q, kv, means, means_head, means_tail = project(x, gain_one, wt_q, wt_kv, second)
    blocked = lambda value: value.reshape(-1, BLOCK, D)
    (kv_own,) = context_project((blocked(x),), after(gain_one, means), wt_kv, False)
    means_send, means_head, means_tail, docn, docc, live = lax.optimization_barrier(
        (means, means_head, means_tail, docn, docc, live, halo_one, halo_two, kv_own, *twos)
    )[:6]
    pieces = (
        grid.send(means_tail, grid.along(2)),
        grid.send(means_send, grid.along(1)),
        means,
        grid.send(means_send, grid.along(-1)),
        grid.send(means_head, grid.along(-2)),
    )
    kv_halo, normed_halo = context_project(
        (blocked(halo_two), blocked(halo_one)), after(gain_one, kv_own), wt_kv, True
    )
    if fast:
        twos = jnp.stack(lax.optimization_barrier((*twos, *pieces, kv_halo))[:4])
        twos = [twos] + [grid.send(twos, grid.swap_head(r)) for r in three]

    plan, *kept = sink_forward(pieces, after(w_pairs, kv_halo), docn, docc, own, context)
    attended, skv = attend(q, kv, kv_halo, kv_own, plan, live)
    if fast:
        twos = jnp.stack(lax.optimization_barrier((*twos, attended))[:4])
        feed_weights = (twos, grid.send(twos, grid.swap_core()))

    if fast:
        output, g_middle, g_att, keep, send = feed_fast(
            at, x, attended, upstream, bias_out, gain_two, bias_in, bias_down, *feed_weights
        )
        got = grid.send(send, grid.swap_core())
    else:
        output, g_middle, g_att, *sums = feed_slow(
            x, attended, upstream, bias_out, gain_two, bias_in, bias_down, *feed_weights
        )
        g_in, g_down, g_out, g_b_out, g_gain_two, g_b_in, g_b_down = gradients_two_slow(
            grid, *sums, parameters, vectors
        )
        twos = []

    gq_low, gkv_low, gh_low, gplan_low = attend_back(
        q, kv, skv, g_att, kv_halo, kv_own, plan, live, 0, 1
    )
    if fast:
        twos = split_sum(at, 0, after(keep, gh_low), got)
        g_att = after(g_att, *twos)
        twos = [twos[0]] + [grid.send(twos[r], grid.swap_head(r)) for r in three]
    gq_high, gkv_high, gh_high, gplan_high = attend_back(
        q, kv, skv, g_att, kv_halo, kv_own, plan, live, 1, PAIRS - 1
    )
    gq, gkv = (gq_low, gq_high), (gkv_low, gkv_high)
    gmeans, gsort, *sends = sink_backward(
        pieces, w_pairs, *kept, gplan_low, gplan_high, own, context
    )
    if fast:
        twos = merge_sum(at, 1, lax.optimization_barrier((*twos, gmeans))[:4])
        gh_high = after(gh_high, *twos)
        twos = [twos[0]] + [grid.send(twos[r], grid.swap_plane(r)) for r in three]
    gn_far, gn_near, g_kv_halo = halo_back(
        gh_low, gh_high, normed_halo, wt_q, wt_kv, gmeans, second
    )
    sends = lax.optimization_barrier((*sends, gn_near))[:2]
    far = [grid.send(value, grid.along(step)) for value, step in zip(sends, (1, 2))]
    gn_far, gn_near = lax.optimization_barrier((gn_far, gn_near, *far, *twos))[:2]
    back_one = grid.send(gn_near, grid.along(-1))
    back_two = grid.send(gn_far, grid.along(-2))
    gmeans = after(gmeans, gn_near)
    keep, send = weight_back(
        at, gq, gkv, normed, wt_q, wt_kv, gmeans, pieces, g_kv_halo, gain_one, gsort, fast
    )
    if fast:
        got = grid.send(send, grid.swap_core())
        ones = split_sum(at, 1, keep, got)
        waiting = [ones[0]] + [grid.send(ones[r], grid.swap_plane(r)) for r in three]
        inner = inner_gradient((gq[0], after(gq[1], *ones)), gkv, wt_q, wt_kv, gmeans, far)
        ones = merge_sum(at, 0, lax.optimization_barrier((*waiting, inner))[:4])
        ones = [ones[0]] + [grid.send(ones[r], grid.swap_head(r)) for r in three]
    else:
        inner = inner_gradient(gq, gkv, wt_q, wt_kv, gmeans, far)
    input_grad = finish(x, inner, back_one, back_two, g_middle, gain_one)
    if fast:
        g_wqkv, g_sort, g_gain_one = last_one(lax.optimization_barrier((*ones, input_grad))[:4])
        g_in, g_down, g_out, *small = last_two(twos)
        g_wqkv, g_sort, g_down, g_out = g_wqkv.T, g_sort.T, g_down.T, g_out.T
        g_gain_one = g_gain_one[0]
        g_b_out, g_gain_two, g_b_in, g_b_down = (value[0] for value in small)
    else:
        g_wqkv, g_sort, g_gain_one = gradients_one_slow(
            grid, keep, send, gsort, parameters, vectors
        )
    return (
        output[None], input_grad[None], g_gain_one, g_wqkv, g_out, g_b_out, g_gain_two, g_in,
        g_b_in, g_down, g_b_down, g_sort,
    )


def solution(mesh):
    heads, cycles = mesh.shape["head"], mesh.shape["blk"]
    fine = Mesh(mesh.devices.reshape(heads, cycles // 2, 2), ("head", "plane", "core"))
    both = P(("head", "plane", "core"))
    split = P("head", ("plane", "core"))
    stream = P(("plane", "core"), "head", None)
    return jax.shard_map(
        per_device,
        mesh=fine,
        in_specs=(
            stream, stream, P(), both, split, split, both, both, split, both, split, both, split,
        ),
        out_specs=(
            stream, stream, both, split, split, both, both, split, both, split, both, split,
        ),
        check_vma=False,
    )
```

```python
import functools

import jax
import jax.numpy as jnp
from jax import lax
from jax.experimental import pallas as pl
from jax.experimental.pallas import tpu as pltpu
from jax.sharding import Mesh
from jax.sharding import PartitionSpec as P

D = 512
HEADS = 8
HEAD_DIM = 64
FF = 2048
BLOCK = 32
SINK_ITERS = 8
DOC_MOST = 62
LANES = 128
PAIRS = HEADS // 2
HALO = 64
GROUPS = 6
CHEAP = pl.CostEstimate(flops=0, transcendentals=0, bytes_accessed=0)
EPSILON = 1e-05
NEGATIVE = -1e30
FLOOR = -1e20
LOG2E = 1.4426950408889634
TINY = 1e-37
F32 = jnp.float32
BF16 = jnp.bfloat16
NT = (((1,), (1,)), ((), ()))
NN = (((1,), (0,)), ((), ()))
TN = (((0,), (0,)), ((), ()))


def mm(a, b, dims=NN):
    return lax.dot_general(a, b, dims, preferred_element_type=F32)


def vmem(limit=56):
    return pltpu.CompilerParams(vmem_limit_bytes=limit * 1024 * 1024)


def once(shape):
    return pl.BlockSpec(shape, lambda *i: (0,) * len(shape), pipeline_mode=pl.Buffered(1))


def halves(value):
    high = value.astype(BF16)
    return high, (value - high.astype(F32)).astype(BF16)


def mm3(a, b, dims):
    (da,), (db,) = dims[0]
    ah, al = halves(a)
    bh, bl = halves(b)
    return mm(
        jnp.concatenate([ah, al, ah], axis=da), jnp.concatenate([bh, bh, bl], axis=db), dims
    )


def sink_mask(docn_ref, docc_ref, window, context):
    first = context
    fold = window - LANES
    lane = lax.broadcasted_iota(jnp.int32, (1, LANES), 1)
    docn = docn_ref[...]
    row = lax.broadcasted_iota(jnp.int32, (window, 1), 0)
    col = jnp.where((row >= first) & (lane < fold), lane + LANES, lane)
    docc = jnp.where(row >= first, docc_ref[1:2, :], docc_ref[0:1, :])
    return (docn == docc) & (docn >= 0) & (col < row)


def fold_pair(top, low, fold, join):
    lane = lax.broadcasted_iota(jnp.int32, (1, LANES), 1)
    both = join(top, low)
    return jnp.where(lane < fold, top, both), jnp.where(lane < fold, low, both)


def sink_weight(pair, odd):
    lane = lax.broadcasted_iota(jnp.int32, pair.shape, 1)
    zero = jnp.zeros_like(pair)
    if odd:
        return jnp.concatenate([zero, jnp.where(lane >= HEAD_DIM, pair, zero)], axis=0)
    return jnp.concatenate([jnp.where(lane < HEAD_DIM, pair, zero), zero], axis=0)


def refold(keys, fold):
    return jnp.concatenate([keys[LANES:], keys[fold:LANES]], axis=0)


def row_step(values):
    highest = jnp.maximum(jnp.max(values, axis=1, keepdims=True), FLOOR)
    total = jnp.sum(jnp.exp2(values - highest), axis=1, keepdims=True)
    return values - (highest + LOG2E * jnp.log(jnp.maximum(total, TINY)))


def column_step(values, context, fold):
    top, low = values[:context], values[context:]
    h1, h2 = fold_pair(
        jnp.max(top, axis=0, keepdims=True),
        jnp.max(low, axis=0, keepdims=True),
        fold,
        jnp.maximum,
    )
    h1, h2 = jnp.maximum(h1, FLOOR), jnp.maximum(h2, FLOOR)
    e1, e2 = jnp.exp2(top - h1), jnp.exp2(low - h2)
    t1, t2 = fold_pair(
        jnp.sum(e1, axis=0, keepdims=True), jnp.sum(e2, axis=0, keepdims=True), fold, jnp.add
    )
    t1, t2 = jnp.maximum(t1, TINY), jnp.maximum(t2, TINY)
    moved = jnp.concatenate(
        [top - (h1 + LOG2E * jnp.log(t1)), low - (h2 + LOG2E * jnp.log(t2))], axis=0
    )
    scales = jnp.concatenate([jnp.exp2(h1), jnp.exp2(h2), 1.0 / t1, 1.0 / t2], axis=0)
    return moved, e1, e2, scales


def sink_forward_kernel(
    own, context, a, b, c, d, e, w_ref, docn_ref, docc_ref, plan_ref, kept_ref, scale_ref, proj_ref,
    q_ref, k_ref, vals, kept, sems,
):
    window = q_ref.shape[1]
    fold = window - LANES
    at = 0
    for piece in (a, b, c, d, e):
        rows = piece.shape[0]
        for pair in range(PAIRS):
            q_ref[pair, at : at + rows, :] = piece[:, pair * LANES : (pair + 1) * LANES]
            k_ref[pair, at : at + rows, :] = piece[:, D + pair * LANES : D + (pair + 1) * LANES]
        at += rows

    def logits(pair, carry):
        permitted = sink_mask(docn_ref, docc_ref, window, context)
        queries, keys = q_ref[pair], k_ref[pair]
        keys_two = refold(keys, fold)
        for odd in range(2):
            projected = mm3(queries, sink_weight(w_ref[pair], odd), NT)
            proj_ref[2 * pair + odd] = projected
            top = mm3(projected[:context], keys[:LANES], NT)
            low = mm3(projected[context:], keys_two, NT)
            vals[2 * pair + odd] = jnp.where(
                permitted, LOG2E * jnp.concatenate([top, low], axis=0), NEGATIVE
            )
        return carry

    lax.fori_loop(0, PAIRS, logits, 0)

    def send(step):
        return pltpu.make_async_copy(kept.at[step], kept_ref.at[step], sems.at[step])

    def step(turn, carry):
        for head in range(HEADS):
            moved, top, low, scales = column_step(row_step(vals[head]), context, fold)
            kept[turn, head, :context, :] = top
            kept[turn, head, context:, :] = low
            scale_ref[turn, head] = scales
            vals[head] = moved
        send(turn).start()
        return carry

    lax.fori_loop(0, SINK_ITERS, step, 0)
    for head in range(HEADS):
        plan_ref[head] = (
            kept[SINK_ITERS - 1, head, context - own : context, :]
            * scale_ref[SINK_ITERS - 1, head, 2:3, :]
        ).astype(BF16)
    lax.fori_loop(0, SINK_ITERS, lambda turn, carry: (send(turn).wait(), carry)[1], 0)


def sink_backward_kernel(
    own, context, a, b, c, d, e, w_ref, kept_ref, scale_ref, proj, gl_ref, gh_ref,
    gm_ref, gw_ref, sd, se, q_ref, k_ref, vals, gq, gk, kept, sems,
):
    window = q_ref.shape[1]
    fold = window - LANES

    def fetch(step):
        return pltpu.make_async_copy(kept_ref.at[step], kept.at[step], sems.at[step])

    def begin(turn, carry):
        fetch(SINK_ITERS - 1 - turn).start()
        return carry

    lax.fori_loop(0, SINK_ITERS, begin, 0)
    at = 0
    for piece in (a, b, c, d, e):
        rows = piece.shape[0]
        for pair in range(PAIRS):
            q_ref[pair, at : at + rows, :] = piece[:, pair * LANES : (pair + 1) * LANES]
            k_ref[pair, at : at + rows, :] = piece[:, D + pair * LANES : D + (pair + 1) * LANES]
        at += rows

    def back(turn, carry):
        at = SINK_ITERS - 1 - turn
        fetch(at).wait()

        @pl.when(turn == 0)
        def _():
            for head in range(HEADS):
                low = gl_ref.shape[0]
                ref, index = (gl_ref, head) if head < low else (gh_ref, head - low)
                vals[head, : context - own, :] = jnp.zeros((context - own, LANES), F32)
                vals[head, context - own : context, :] = (
                    ref[index]
                    * kept[SINK_ITERS - 1, head, context - own : context, :]
                    * scale_ref[SINK_ITERS - 1, head, 2:3, :]
                )
                vals[head, context:, :] = jnp.zeros((window - context, LANES), F32)

        for head in range(HEADS):
            g1, g2 = vals[head, :context, :], vals[head, context:, :]
            s1, s2 = fold_pair(
                jnp.sum(g1, axis=0, keepdims=True),
                jnp.sum(g2, axis=0, keepdims=True),
                fold,
                jnp.add,
            )
            scales = scale_ref[at, head]
            e1, e2 = kept[at, head, :context, :], kept[at, head, context:, :]
            g1, g2 = g1 - e1 * (s1 * scales[2:3]), g2 - e2 * (s2 * scales[3:4])
            r1, r2 = jnp.sum(g1, axis=1, keepdims=True), jnp.sum(g2, axis=1, keepdims=True)
            vals[head, :context, :] = g1 - (e1 * scales[0:1]) * r1
            vals[head, context:, :] = g2 - (e2 * scales[1:2]) * r2
        return carry

    lax.fori_loop(0, SINK_ITERS, back, 0)

    def products(pair, carry):
        queries, keys = q_ref[pair], k_ref[pair]
        keys_two = refold(keys, fold)
        turned = []
        gq_total = jnp.zeros((window, LANES), F32)
        gk_total = jnp.zeros((window, LANES), F32)
        for odd in range(2):
            head = 2 * pair + odd
            g1, g2 = vals[head, :context, :], vals[head, context:, :]
            against = jnp.concatenate(
                [mm3(g1, keys[:LANES], NN), mm3(g2, keys_two, NN)], axis=0
            )
            gq_total = gq_total + mm3(against, sink_weight(w_ref[pair], odd), NN)
            u1 = mm3(g1, proj[head, :context, :], TN)
            u2 = mm3(g2, proj[head, context:, :], TN)
            gk_total = gk_total + jnp.concatenate(
                [u1[:fold], u1[fold:] + u2[fold:], u2[:fold]], axis=0
            )
            turned.append(mm3(against, queries, TN))
        half = lax.broadcasted_iota(jnp.int32, (HEAD_DIM, LANES), 1) < HEAD_DIM
        gw_ref[pair] = jnp.where(half, turned[0][:HEAD_DIM], turned[1][HEAD_DIM:])
        gq[pair] = gq_total * (1.0 / BLOCK)
        gk[pair] = gk_total * (1.0 / BLOCK)
        return carry

    lax.fori_loop(0, PAIRS, products, 0)
    for pair in range(PAIRS):
        gm_ref[:, pair * LANES : (pair + 1) * LANES] = gq[pair]
        gm_ref[:, D + pair * LANES : D + (pair + 1) * LANES] = gk[pair]
    sd[...] = gm_ref[context : context + d.shape[0], :].astype(BF16)
    se[...] = gm_ref[context + d.shape[0] :, :].astype(BF16)


HBM = pl.BlockSpec(memory_space=pl.ANY)
VMEM = pl.BlockSpec(memory_space=pltpu.VMEM)
SMEM = pl.BlockSpec(memory_space=pltpu.SMEM)


def sink_forward(pieces, weight, docn, docc, own, context):
    window = sum(piece.shape[0] for piece in pieces)
    kept = (SINK_ITERS, HEADS, window, LANES)
    return pl.pallas_call(
        functools.partial(sink_forward_kernel, own, context),
        in_specs=[VMEM] * 8,
        out_specs=[VMEM, HBM, VMEM, VMEM],
        out_shape=[
            jax.ShapeDtypeStruct((HEADS, own, LANES), BF16),
            jax.ShapeDtypeStruct(kept, F32),
            jax.ShapeDtypeStruct((SINK_ITERS, HEADS, 4, LANES), F32),
            jax.ShapeDtypeStruct((HEADS, window, LANES), F32),
        ],
        scratch_shapes=[
            pltpu.VMEM((PAIRS, window, LANES), F32),
            pltpu.VMEM((PAIRS, window, LANES), F32),
            pltpu.VMEM((HEADS, window, LANES), F32),
            pltpu.VMEM(kept, F32),
            pltpu.SemaphoreType.DMA((SINK_ITERS,)),
        ],
        cost_estimate=CHEAP,
        compiler_params=vmem(),
        name="sink_forward",
    )(*pieces, weight, docn, docc)


def sink_backward(pieces, weight, kept, scales, projected, low, high, own, context):
    window = sum(piece.shape[0] for piece in pieces)
    return pl.pallas_call(
        functools.partial(sink_backward_kernel, own, context),
        in_specs=[VMEM] * 6 + [HBM] + [VMEM] * 4,
        out_shape=[
            jax.ShapeDtypeStruct((window, 2 * D), F32),
            jax.ShapeDtypeStruct((PAIRS, HEAD_DIM, LANES), F32),
            *(
                jax.ShapeDtypeStruct((pieces[i].shape[0], 2 * D), BF16)
                for i in (3, 4)
            ),
        ],
        scratch_shapes=[
            *[pltpu.VMEM((PAIRS, window, LANES), F32)] * 2,
            pltpu.VMEM((HEADS, window, LANES), F32),
            *[pltpu.VMEM((PAIRS, window, LANES), F32)] * 2,
            pltpu.VMEM(kept.shape, F32),
            pltpu.SemaphoreType.DMA((SINK_ITERS,)),
        ],
        cost_estimate=CHEAP,
        compiler_params=vmem(),
        name="sink_backward",
    )(*pieces, weight, kept, scales, projected, low, high)


def normalise(values):
    centre = values - jnp.mean(values, axis=-1, keepdims=True)
    spread = jnp.mean(centre * centre, axis=-1, keepdims=True)
    return centre * lax.rsqrt(spread + EPSILON)


def context_kernel(count, keep, *refs):
    gain_ref, w_ref, kvx_ref = refs[count : count + 3]
    x = jnp.concatenate([ref[...].astype(F32) for ref in refs[:count]], axis=0)
    short = -x.shape[0] % 16
    if short:
        x = jnp.concatenate([jnp.zeros((short, 8, D), F32), x], axis=0)
    blocks = x.shape[0]
    normed = normalise(x) * gain_ref[...].reshape(1, 1, D)
    normed = normed.astype(BF16).reshape(blocks * 8, D)
    row = lax.broadcasted_iota(jnp.int32, (LANES, LANES), 0)
    lane = lax.broadcasted_iota(jnp.int32, (LANES, LANES), 1)
    turn = (lane == (row % 16) * 8 + row // 16).astype(F32).astype(BF16)
    turned = [
        mm(turn, normed[i * LANES : (i + 1) * LANES]).astype(BF16) for i in range(blocks // 16)
    ]
    rows = []
    for b in range(8):
        part = jnp.concatenate([part[b * 16 : (b + 1) * 16] for part in turned], axis=0)
        if keep:
            refs[count + 3][b] = part
        rows.append(part)
    rows = jnp.concatenate(rows, axis=0)
    for head in range(0, HEADS, 2):
        out = mm(rows, w_ref[head * LANES : (head + 2) * LANES, :], NT).astype(BF16)
        for b in range(8):
            for e in range(2):
                kvx_ref[head + e, :, b * LANES : (b + 1) * LANES] = out[
                    b * blocks : (b + 1) * blocks, e * LANES : (e + 1) * LANES
                ]


def context_project(values, gain, w_kv, keep):
    blocks = sum(v.shape[0] for v in values)
    blocks += -blocks % 16
    outs = 2 if keep else 1
    return pl.pallas_call(
        functools.partial(context_kernel, len(values), keep),
        grid=(BLOCK // 8,),
        in_specs=[
            *(pl.BlockSpec((v.shape[0], 8, D), lambda i: (0, i, 0)) for v in values),
            pl.BlockSpec((1, D), lambda i: (0, 0)),
            pl.BlockSpec((2 * D, D), lambda i: (0, 0)),
        ],
        out_specs=[
            pl.BlockSpec((HEADS, blocks, 8 * LANES), lambda i: (0, 0, i)),
            pl.BlockSpec((8, blocks, D), lambda i: (i, 0, 0)),
        ][:outs],
        out_shape=[
            jax.ShapeDtypeStruct((HEADS, blocks, BLOCK * LANES), BF16),
            jax.ShapeDtypeStruct((BLOCK, blocks, D), BF16),
        ][:outs],
        cost_estimate=CHEAP,
        compiler_params=vmem(),
        name="context_halo" if keep else "context_own",
    )(*values, gain, w_kv)


def compact(values, lane_block):
    out = values[:BLOCK]
    for j in range(1, 4):
        out = jnp.where(lane_block == j, values[j * BLOCK : (j + 1) * BLOCK], out)
    return out


def spread(values, lane_block):
    zero = jnp.zeros_like(values)
    return jnp.concatenate([jnp.where(lane_block == j, values, zero) for j in range(4)], axis=0)


def softmax_pair(local, chosen, live):
    lane = lax.broadcasted_iota(jnp.int32, (BLOCK, LANES), 1)
    row = lax.broadcasted_iota(jnp.int32, (BLOCK, LANES), 0)
    local = jnp.where(row <= lax.rem(lane, BLOCK), local, NEGATIVE)
    chosen = jnp.where(live, chosen, NEGATIVE)
    highest = jnp.maximum(
        jnp.max(local, axis=0, keepdims=True), jnp.max(chosen, axis=0, keepdims=True)
    )
    el, es = jnp.exp(local - highest), jnp.exp(chosen - highest)
    total = jnp.sum(el, axis=0, keepdims=True) + jnp.sum(es, axis=0, keepdims=True)
    inverse = 1.0 / total
    return el * inverse, es * inverse


def half_mask(first):
    lane = lax.broadcasted_iota(jnp.int32, (LANES, LANES), 1)
    return (lane < HEAD_DIM) if first else (lane >= HEAD_DIM)


def attend_kernel(
    q_ref, kv_ref, kvh_ref, kvo_ref, plan_ref, live_ref, att_ref, skv_ref, even_ref, odd_ref
):
    own = plan_ref.shape[1]
    blocks = kvh_ref.shape[1] + own
    held = (even_ref, odd_ref)
    for e in range(2):
        plan = plan_ref[e][:, :blocks]
        for chunk in range(4):
            lanes = slice(chunk * 8 * LANES, (chunk + 1) * 8 * LANES)
            out = mm(plan, jnp.concatenate([kvh_ref[e, :, lanes], kvo_ref[e, :, lanes]], axis=0))
            for b in range(8):
                at = (chunk * 8 + b) * (own + 1)
                held[e][at : at + own, :] = out[:, b * LANES : (b + 1) * LANES]
    lane_block = lax.broadcasted_iota(jnp.int32, (BLOCK, LANES), 1) // BLOCK
    lane_half = [half_mask(True), half_mask(False)]

    def group(turn, carry):
        chains = [(turn * GROUPS + i, e) for i in range(GROUPS) for e in range(2)]
        starts = [pl.multiple_of(g * LANES, LANES) for g, _ in chains]
        both, scores = [], []
        for (g, e), start in zip(chains, starts):
            local = kv_ref[pl.ds(start, LANES), e * LANES : (e + 1) * LANES]
            chosen = jnp.concatenate(
                [held[e][pl.ds(4 * g + i, BLOCK, stride=own + 1), :] for i in range(4)], axis=0
            ).astype(BF16)
            skv_ref[pl.ds(start, LANES), e * LANES : (e + 1) * LANES] = chosen
            both.append(jnp.concatenate([local, chosen], axis=0))
        for (g, e), start, kv in zip(chains, starts, both):
            q = q_ref[pl.ds(start, LANES), :] * 0.125
            qm = jnp.where(lane_half[e], q, jnp.zeros_like(q))
            out = mm(kv, qm, NT)
            scores.append((compact(out[:LANES], lane_block), compact(out[LANES:], lane_block)))
        weights = []
        for (g, e), (local, chosen) in zip(chains, scores):
            weights.append(softmax_pair(local, chosen, live_ref[pl.ds(g, 1), :] > 0.0))
        outs = []
        for (g, e), kv, (wl, ws) in zip(chains, both, weights):
            wide = jnp.concatenate(
                [spread(wl.astype(BF16), lane_block), spread(ws.astype(BF16), lane_block)], axis=0
            )
            turned = kv.T
            outs.append(mm(turned[HEAD_DIM:] if e == 0 else turned[:HEAD_DIM], wide))
        for i in range(GROUPS):
            att_ref[pl.ds(starts[2 * i], LANES), :] = jnp.concatenate(
                outs[2 * i : 2 * i + 2], axis=0
            ).T.astype(BF16)
        return carry

    lax.fori_loop(0, own // 4 // GROUPS, group, 0)


def attend(q, kv, kvh, kvo, plan, live):
    tok, own, halo = q.shape[0], plan.shape[1], kvh.shape[1]
    return pl.pallas_call(
        attend_kernel,
        grid=(PAIRS,),
        in_specs=[
            pl.BlockSpec((tok, LANES), lambda j: (0, j)),
            pl.BlockSpec((tok, 2 * LANES), lambda j: (0, j)),
            pl.BlockSpec((2, halo, BLOCK * LANES), lambda j: (j, 0, 0)),
            pl.BlockSpec((2, own, BLOCK * LANES), lambda j: (j, 0, 0)),
            pl.BlockSpec((2, own, LANES), lambda j: (j, 0, 0)),
            pl.BlockSpec((tok // LANES, LANES), lambda j: (0, 0)),
        ],
        out_specs=[
            pl.BlockSpec((tok, LANES), lambda j: (0, j)),
            pl.BlockSpec((tok, 2 * LANES), lambda j: (0, j)),
        ],
        out_shape=[
            jax.ShapeDtypeStruct((tok, D), BF16),
            jax.ShapeDtypeStruct((tok, 2 * D), BF16),
        ],
        scratch_shapes=[pltpu.VMEM((BLOCK * (own + 1), LANES), F32)] * 2,
        cost_estimate=CHEAP,
        compiler_params=vmem(),
        name="attend",
    )(q, kv, kvh, kvo, plan, live)


def attend_back_kernel(
    q_ref, kv_ref, skv_ref, go_ref, kvh_ref, kvo_ref, plan_ref, live_ref,
    gq_ref, gkv_ref, gh_ref, gp_ref, even_ref, odd_ref, leven_ref, lodd_ref,
):
    own = plan_ref.shape[1]
    halo = kvh_ref.shape[1]
    blocks = halo + own
    held = (even_ref, odd_ref)
    lheld = (leven_ref, lodd_ref)
    lane_block = lax.broadcasted_iota(jnp.int32, (BLOCK, LANES), 1) // BLOCK
    lane_half = [half_mask(True), half_mask(False)]

    def group(turn, carry):
        chains = [(turn * GROUPS + i, e) for i in range(GROUPS) for e in range(2)]
        starts = [pl.multiple_of(g * LANES, LANES) for g, _ in chains]
        both, right, scores = [], [], []
        for (g, e), start in zip(chains, starts):
            lanes = slice(e * LANES, (e + 1) * LANES)
            rows = pl.ds(start, LANES)
            both.append(jnp.concatenate([kv_ref[rows, lanes], skv_ref[rows, lanes]], axis=0))
            q = q_ref[rows, :] * 0.125
            go = go_ref[rows, :]
            go = jnp.concatenate([go[:, HEAD_DIM:], go[:, :HEAD_DIM]], axis=1)
            qm = jnp.where(lane_half[e], q, jnp.zeros_like(q))
            gm = jnp.where(lane_half[1 - e], go, jnp.zeros_like(go))
            right.append(jnp.concatenate([qm, gm], axis=0))
        for kv, other in zip(both, right):
            out = mm(kv, other, NT)
            scores.append(
                [
                    compact(out[rows, lanes], lane_block)
                    for lanes in (slice(0, LANES), slice(LANES, 2 * LANES))
                    for rows in (slice(0, LANES), slice(LANES, 2 * LANES))
                ]
            )
        wides = []
        for (g, e), (sl, ss, dl, ds) in zip(chains, scores):
            wl, ws = softmax_pair(sl, ss, live_ref[pl.ds(g, 1), :] > 0.0)
            inner = jnp.sum(wl * dl + ws * ds, axis=0, keepdims=True)
            low = [v.astype(BF16) for v in (wl, ws, wl * (dl - inner), ws * (ds - inner))]
            wides.append(low)
        outs = []
        for (g, e), start, kv, other, (wl, ws, gl, gs) in zip(chains, starts, both, right, wides):
            weights = jnp.concatenate([spread(wl, lane_block), spread(ws, lane_block)], axis=0)
            gscore = jnp.concatenate([spread(gl, lane_block), spread(gs, lane_block)], axis=0)
            gboth = mm(jnp.concatenate([gscore, weights], axis=1), other)
            lheld[e][pl.ds(start, LANES), :] = gboth[:LANES]
            for i in range(4):
                held[e][pl.ds(4 * g + i, BLOCK, stride=own + 1), :] = gboth[
                    LANES + i * BLOCK : LANES + (i + 1) * BLOCK
                ]
            turned = kv.T
            outs.append(mm(turned[:HEAD_DIM] if e == 0 else turned[HEAD_DIM:], gscore))
        for i in range(GROUPS):
            gq_ref[pl.ds(starts[2 * i], LANES), :] = (
                jnp.concatenate(outs[2 * i : 2 * i + 2], axis=0).T * 0.125
            ).astype(BF16)
        return carry

    lax.fori_loop(0, own // 4 // GROUPS, group, 0)
    for e in range(2):
        plan = plan_ref[e][:, :blocks]
        gplan = jnp.zeros((own, blocks), F32)
        for chunk in range(4):
            lanes = slice(chunk * 8 * LANES, (chunk + 1) * 8 * LANES)
            grads = jnp.concatenate(
                [
                    held[e][(chunk * 8 + b) * (own + 1) : (chunk * 8 + b) * (own + 1) + own, :]
                    for b in range(8)
                ],
                axis=1,
            ).astype(BF16)
            here = jnp.concatenate([kvh_ref[e, :, lanes], kvo_ref[e, :, lanes]], axis=0)
            gplan = gplan + mm(grads, here, NT)
            gcontext = mm(plan, grads, TN)
            gh_ref[e, :, lanes] = gcontext[:halo].astype(BF16)
            for b in range(8):
                at = (chunk * 8 + b) * (own + 1)
                held[e][at : at + own, :] = gcontext[halo:, b * LANES : (b + 1) * LANES]
        gp_ref[e] = jnp.concatenate([gplan, jnp.zeros((own, LANES - blocks), F32)], axis=1)

    def finish(g, carry):
        start = pl.multiple_of(g * LANES, LANES)
        for e in range(2):
            rest = jnp.concatenate(
                [held[e][pl.ds(4 * g + i, BLOCK, stride=own + 1), :] for i in range(4)], axis=0
            )
            gkv_ref[pl.ds(start, LANES), e * LANES : (e + 1) * LANES] = (
                rest + lheld[e][pl.ds(start, LANES), :]
            ).astype(BF16)
        return carry

    lax.fori_loop(0, own // 4, finish, 0)


def attend_back(q, kv, skv, go, kvh, kvo, plan, live, first, pairs):
    tok, own, halo = q.shape[0], plan.shape[1], kvh.shape[1]
    return pl.pallas_call(
        attend_back_kernel,
        grid=(pairs,),
        in_specs=[
            pl.BlockSpec((tok, LANES), lambda j: (0, j + first)),
            pl.BlockSpec((tok, 2 * LANES), lambda j: (0, j + first)),
            pl.BlockSpec((tok, 2 * LANES), lambda j: (0, j + first)),
            pl.BlockSpec((tok, LANES), lambda j: (0, j + first)),
            pl.BlockSpec((2, halo, BLOCK * LANES), lambda j: (j + first, 0, 0)),
            pl.BlockSpec((2, own, BLOCK * LANES), lambda j: (j + first, 0, 0)),
            pl.BlockSpec((2, own, LANES), lambda j: (j + first, 0, 0)),
            pl.BlockSpec((tok // LANES, LANES), lambda j: (0, 0)),
        ],
        out_specs=[
            pl.BlockSpec((tok, LANES), lambda j: (0, j)),
            pl.BlockSpec((tok, 2 * LANES), lambda j: (0, j)),
            pl.BlockSpec((2, halo, BLOCK * LANES), lambda j: (j, 0, 0)),
            pl.BlockSpec((2, own, LANES), lambda j: (j, 0, 0)),
        ],
        out_shape=[
            jax.ShapeDtypeStruct((tok, pairs * LANES), BF16),
            jax.ShapeDtypeStruct((tok, 2 * pairs * LANES), BF16),
            jax.ShapeDtypeStruct((2 * pairs, halo, BLOCK * LANES), BF16),
            jax.ShapeDtypeStruct((2 * pairs, own, LANES), F32),
        ],
        scratch_shapes=[pltpu.VMEM((BLOCK * (own + 1), LANES), F32)] * 4,
        cost_estimate=CHEAP,
        compiler_params=vmem(),
        name="attend_back",
    )(q, kv, skv, go, kvh, kvo, plan, live)


def halo_kernel(
    low_ref, high_ref, nh_ref, wq_ref, w_ref, gm_ref, far_ref, near_ref, gw_ref, block_ref
):
    halo = low_ref.shape[1]
    far = far_ref.shape[1]

    @pl.when(pl.program_id(0) == 0)
    def _():
        gw_ref[...] = jnp.zeros_like(gw_ref)
        grads = gm_ref[...].astype(BF16)
        block_ref[...] = mm(grads[:, :D], wq_ref[...]) + mm(widen_keys(grads[:, D:]), w_ref[...])

    rows = jnp.concatenate(
        [
            jnp.concatenate(
                [
                    ref[head, :, b * LANES : (b + 1) * LANES]
                    for ref in (low_ref, high_ref)
                    for head in range(ref.shape[0])
                ],
                axis=1,
            )
            for b in range(8)
        ],
        axis=0,
    )
    out = (mm(rows, w_ref[...]).reshape(8, halo, D) + block_ref[...][None]).astype(BF16)
    far_ref[...] = out[:, :far]
    near_ref[...] = out[:, far:]
    gw_ref[...] += mm(rows, nh_ref[...].reshape(8 * halo, D), TN)


def halo_back(low, high, nh, w_q, w_kv, gm, far):
    halo = low.shape[1]
    part = lambda v: pl.BlockSpec((v.shape[0], halo, 8 * LANES), lambda i: (0, 0, i))
    return pl.pallas_call(
        halo_kernel,
        grid=(BLOCK // 8,),
        in_specs=[
            part(low),
            part(high),
            pl.BlockSpec((8, halo, D), lambda i: (i, 0, 0)),
            once((D, D)),
            once((2 * D, D)),
            once((halo, 2 * D)),
        ],
        out_specs=[
            pl.BlockSpec((8, far, D), lambda i: (i, 0, 0)),
            pl.BlockSpec((8, halo - far, D), lambda i: (i, 0, 0)),
            pl.BlockSpec((2 * D, D), lambda i: (0, 0)),
        ],
        out_shape=[
            jax.ShapeDtypeStruct((BLOCK, far, D), BF16),
            jax.ShapeDtypeStruct((BLOCK, halo - far, D), BF16),
            jax.ShapeDtypeStruct((2 * D, D), F32),
        ],
        scratch_shapes=[pltpu.VMEM((halo, D), F32)],
        cost_estimate=CHEAP,
        compiler_params=vmem(),
        name="halo_back",
    )(low, high, nh, w_q, w_kv, gm)


def project_kernel(x_ref, gain_ref, wq_ref, wkv_ref, n_ref, q_ref, kv_ref, m_ref, head_ref, tail_ref):
    rows = x_ref.shape[0]
    blocks = rows // BLOCK
    normed = (normalise(x_ref[...].astype(F32)) * gain_ref[...]).astype(BF16)
    n_ref[...] = normed
    q = mm(normed, wq_ref[...], NT).astype(BF16)
    q_ref[...] = q
    kv = mm(normed, wkv_ref[...], NT).astype(BF16)
    kv_ref[...] = kv
    half = lax.broadcasted_iota(jnp.int32, (1, LANES), 1) < HEAD_DIM
    m_ref[:, :D] = jnp.mean(q.astype(F32).reshape(blocks, BLOCK, D), axis=1)
    for pair in range(PAIRS):
        even = kv[:, 2 * pair * LANES : (2 * pair + 1) * LANES]
        odd = kv[:, (2 * pair + 1) * LANES : (2 * pair + 2) * LANES]
        keys = jnp.where(half, even.astype(F32), odd.astype(F32))
        m_ref[:, D + pair * LANES : D + (pair + 1) * LANES] = jnp.mean(
            keys.reshape(blocks, BLOCK, LANES), axis=1
        )
    m_ref[:, 2 * D :] = jnp.mean(normed.astype(F32).reshape(blocks, BLOCK, D), axis=1)
    at = pl.program_id(0)
    ends = head_ref.shape[0] // blocks
    for ref, first in ((head_ref, 0), (tail_ref, pl.num_programs(0) - ends)):

        @pl.when((at >= first) & (at < first + ends))
        def _():
            ref[pl.ds(pl.multiple_of((at - first) * blocks, 8), blocks), :] = m_ref[...]


def project(x, gain, wt_q, wt_kv, ends):
    tok = x.shape[0]
    tile = 8 * BLOCK
    return pl.pallas_call(
        project_kernel,
        grid=(tok // tile,),
        in_specs=[
            pl.BlockSpec((tile, D), lambda i: (i, 0)),
            pl.BlockSpec((1, D), lambda i: (0, 0)),
            pl.BlockSpec((D, D), lambda i: (0, 0)),
            pl.BlockSpec((2 * D, D), lambda i: (0, 0)),
        ],
        out_specs=[
            pl.BlockSpec((tile, D), lambda i: (i, 0)),
            pl.BlockSpec((tile, D), lambda i: (i, 0)),
            pl.BlockSpec((tile, 2 * D), lambda i: (i, 0)),
            pl.BlockSpec((8, 3 * D), lambda i: (i, 0)),
            once((ends, 3 * D)),
            once((ends, 3 * D)),
        ],
        out_shape=[
            jax.ShapeDtypeStruct((tok, D), BF16),
            jax.ShapeDtypeStruct((tok, D), BF16),
            jax.ShapeDtypeStruct((tok, 2 * D), BF16),
            jax.ShapeDtypeStruct((tok // BLOCK, 3 * D), F32),
            jax.ShapeDtypeStruct((ends, 3 * D), F32),
            jax.ShapeDtypeStruct((ends, 3 * D), F32),
        ],
        cost_estimate=CHEAP,
        compiler_params=vmem(),
        name="project",
    )(x, gain, wt_q, wt_kv)


PIECE_ONE = 208
PIECE_TWO = 576
PARTS_TWO = 592


def place(vector, start):
    size = vector.shape[1]
    row = lax.broadcasted_iota(jnp.int32, (size, LANES), 0)
    lane = lax.broadcasted_iota(jnp.int32, (size, LANES), 1)
    pick = (lane == row + start).astype(F32).astype(BF16)
    return mm(jnp.broadcast_to(vector.astype(F32), (16, size)).astype(BF16), pick)


def pack_kernel(
    wqkv_ref, wsort_ref, g1, bo, g2, bi, bd, win_ref, wdown_ref, wout_ref, x_ref,
    one_ref, two_ref, tail_ref,
):
    tail_ref[...] = x_ref[x_ref.shape[0] - tail_ref.shape[0] :, :]
    one_ref[:192, :] = wqkv_ref[...]
    row = place(g1[...], 0) + place(bo[...], 16) + place(g2[...], 32)
    row = row + place(bi[...], 48) + place(bd[...], 112)
    one_ref[192:, :] = jnp.concatenate([wsort_ref[...].astype(F32), row[:8]], axis=0).astype(BF16)
    two_ref[:256, :] = win_ref[...].astype(F32).T.astype(BF16)
    for k in range(4):
        two_ref[256 + k * 64 : 256 + (k + 1) * 64, :] = wdown_ref[:, k * LANES : (k + 1) * LANES]
    two_ref[512:, :] = wout_ref[...]


def pack(w_qkv, w_sort, vectors, w_in, w_down, w_out, x, tail):
    most = 512
    last = x.shape[0] // most - 1
    return pl.pallas_call(
        pack_kernel,
        grid=(1,),
        in_specs=[VMEM] * 10 + [pl.BlockSpec((most, D), lambda i: (last, 0))],
        out_shape=[
            jax.ShapeDtypeStruct((PIECE_ONE, LANES), BF16),
            jax.ShapeDtypeStruct((PIECE_TWO, LANES), BF16),
            jax.ShapeDtypeStruct((tail, D), BF16),
        ],
        cost_estimate=CHEAP,
        compiler_params=vmem(),
        name="pack",
    )(w_qkv.T, w_sort.T, *(v.reshape(1, -1) for v in vectors), w_in, w_down.T, w_out.T, x)


def rows_at(start, size):
    return pl.ds(pl.multiple_of(start * size, size), size)


def each_owner(at_ref, visit):
    def planes(z, carry):
        for other in range(2):
            c = at_ref[2] ^ other
            for h in range(4):
                visit(other == 0, h, z, 2 * z + c, c)
        return carry

    lax.fori_loop(0, 4, planes, 0)


def each_piece(at_ref, mine_ref, other_ref, visit):
    def owner(own, h, z, b, c):
        source = mine_ref if own else other_ref
        visit(h, b, c, source.at[at_ref[0] ^ h, at_ref[1] ^ z])

    each_owner(at_ref, owner)


def widen(vecs, start, size):
    total = 32 * size
    lane = lax.broadcasted_iota(jnp.int32, (LANES, total), 1)
    row = lax.broadcasted_iota(jnp.int32, (LANES, total), 0)
    pick = (row == start + lax.rem(lane, size)).astype(F32).astype(BF16)
    every = mm(vecs, pick)
    owner = lax.broadcasted_iota(jnp.int32, (32, total), 0)
    lane = lax.broadcasted_iota(jnp.int32, (32, total), 1)
    return jnp.sum(jnp.where(owner == lane // size, every, 0.0), axis=0, keepdims=True)


def assemble_kernel(
    at_ref, mine_ref, other_ref, wq_ref, wkv_ref, ws_ref, g1_ref, bo_ref, g2_ref, bi_ref, bd_ref,
    vecs_ref,
):
    def visit(h, b, c, piece):
        lanes = slice(h * LANES, (h + 1) * LANES)
        wq_ref[rows_at(b, 64), lanes] = piece[:64, :]
        wkv_ref[rows_at(2 * b + c, 64), lanes] = piece[64:128, :]
        wkv_ref[rows_at(2 * b + 1 - c, 64), lanes] = piece[128:192, :]
        tail = piece[192:208, :].astype(F32)
        ws_ref[h, rows_at(b, 8), :] = tail[:8]
        vecs_ref[pl.ds(h * 8 + b, 1), :] = tail[8:9]

    each_piece(at_ref, mine_ref, other_ref, visit)
    vecs = vecs_ref[...].astype(BF16)
    g1_ref[...] = widen(vecs, 0, 16)
    bo_ref[...] = widen(vecs, 16, 16)
    g2_ref[...] = widen(vecs, 32, 16)
    bi_ref[...] = widen(vecs, 48, 64)
    bd_ref[...] = widen(vecs, 112, 16)


def assemble(at, mine, other):
    row = jax.ShapeDtypeStruct((1, D), F32)
    return pl.pallas_call(
        assemble_kernel,
        in_specs=[SMEM, VMEM, VMEM],
        out_shape=[
            jax.ShapeDtypeStruct((D, D), BF16),
            jax.ShapeDtypeStruct((2 * D, D), BF16),
            jax.ShapeDtypeStruct((PAIRS, HEAD_DIM, LANES), F32),
            row, row, row, jax.ShapeDtypeStruct((1, FF), F32), row,
        ],
        scratch_shapes=[pltpu.VMEM((32, LANES), F32)],
        cost_estimate=CHEAP,
        compiler_params=vmem(),
        name="assemble",
    )(at, mine, other)


GELU_A = 0.7978845608028654
GELU_B = 0.044715


def feed_tile(x, att, g, bo, g2, bi, bd, win, wdown, wout, acc_in, acc_down, acc_out, sums):
    middle = x.astype(F32) + mm(att, wout[...], NT) + bo
    centre = middle - jnp.mean(middle, axis=-1, keepdims=True)
    spread_ = jnp.mean(centre * centre, axis=-1, keepdims=True)
    inverse = lax.rsqrt(spread_ + EPSILON)
    hat = centre * inverse
    normed = (hat * g2).astype(BF16)
    normed_t = normed.T
    g_t = g.T
    out = jnp.zeros(middle.shape, F32)
    u = jnp.zeros(middle.shape, F32)
    cut = 512
    for k in range(FF // cut):
        cols = slice(k * cut, (k + 1) * cut)
        pre = mm(normed, win[cols, :], NT) + bi[:, cols]
        square = pre * pre
        t = jnp.tanh(GELU_A * pre * (1.0 + GELU_B * square))
        half = 0.5 * (1.0 + t)
        hidden = (pre * half).astype(BF16)
        slope = half + (0.5 * GELU_A) * pre * (1.0 - t * t) * (1.0 + (3.0 * GELU_B) * square)
        g_pre = (mm(g, wdown[:, cols], NN) * slope).astype(BF16)
        out = out + mm(hidden, wdown[:, cols], NT)
        u = u + mm(g_pre, win[cols, :], NN)
        part = mm(normed_t, g_pre)
        for i in range(2):
            acc_in[2 * k + i] += part[:, i * 256 : (i + 1) * 256]
        acc_down[:, cols] += mm(g_t, hidden)
        sums[4:5, cols] += jnp.sum(g_pre.astype(F32), axis=0, keepdims=True)
    gf = g.astype(F32)
    sums[1:2, :D] += jnp.sum(u * hat, axis=0, keepdims=True)
    sums[3:4, :D] += jnp.sum(gf, axis=0, keepdims=True)
    du = u * g2
    inner = jnp.mean(du * hat, axis=-1, keepdims=True)
    g_middle = gf + inverse * (du - jnp.mean(du, axis=-1, keepdims=True) - hat * inner)
    branch = g_middle.astype(BF16)
    sums[0:1, :D] += jnp.sum(branch.astype(F32), axis=0, keepdims=True)
    acc_out[...] += mm(branch.T, att)
    return (middle + out + bd).astype(BF16), g_middle, mm(branch, wout[...], NN).astype(BF16)


def clear(*refs):
    for ref in refs:
        ref[...] = jnp.zeros_like(ref)


def narrow(sums):
    total = jnp.zeros((32, LANES), F32)
    for index, start, size in ((0, 16, 16), (1, 32, 16), (4, 48, 64), (3, 112, 16)):
        width = 32 * size
        owner = lax.broadcasted_iota(jnp.int32, (32, width), 0)
        lane = lax.broadcasted_iota(jnp.int32, (32, width), 1)
        kept = jnp.where(owner == lane // size, sums[index : index + 1, :width], 0.0)
        row = lax.broadcasted_iota(jnp.int32, (width, LANES), 0)
        lane = lax.broadcasted_iota(jnp.int32, (width, LANES), 1)
        pick = (lane == start + lax.rem(row, size)).astype(F32).astype(BF16)
        total = total + mm(kept.astype(BF16), pick)
    return total


def feed_fast_kernel(
    at_ref, x_ref, att_ref, g_ref, bo_ref, g2_ref, bi_ref, bd_ref, mine_ref, other_ref,
    out_ref, gm_ref, ga_ref, keep_ref, send_ref,
    win, wdown, wout, acc_in, acc_down, acc_out, sums, vecs,
):
    @pl.when(pl.program_id(0) == 0)
    def _():
        def visit(h, b, c, piece):
            win[rows_at(b, 256), h * LANES : (h + 1) * LANES] = piece[:256, :]
            for k in range(4):
                lanes = slice(h * 512 + k * LANES, h * 512 + (k + 1) * LANES)
                wdown[rows_at(b, 64), lanes] = piece[256 + k * 64 : 320 + k * 64, :]
            wout[rows_at(b, 64), h * LANES : (h + 1) * LANES] = piece[512:576, :]

        each_piece(at_ref, mine_ref, other_ref, visit)
        clear(acc_in, acc_down, acc_out, sums)

    out_ref[...], gm_ref[...], ga_ref[...] = feed_tile(
        x_ref[...], att_ref[...], g_ref[...], bo_ref[...], g2_ref[...], bi_ref[...], bd_ref[...],
        win, wdown, wout, acc_in, acc_down, acc_out, sums,
    )

    @pl.when(pl.program_id(0) == pl.num_programs(0) - 1)
    def _():
        vecs[...] = narrow(sums)

        def owner(own, h, z, b, c):
            ref = keep_ref if own else send_ref
            for k in range(2):
                ref[h, z, k * LANES : (k + 1) * LANES, :] = acc_in[
                    b, h * LANES : (h + 1) * LANES, k * LANES : (k + 1) * LANES
                ].astype(BF16)
            for k in range(4):
                ref[h, z, 256 + k * 64 : 320 + k * 64, :] = acc_down[
                    rows_at(b, 64), h * 512 + k * LANES : h * 512 + (k + 1) * LANES
                ].astype(BF16)
            ref[h, z, 512:576, :] = acc_out[
                rows_at(b, 64), h * LANES : (h + 1) * LANES
            ].astype(BF16)
            ref[h, z, 576:592, :] = jnp.broadcast_to(
                vecs[pl.ds(h * 8 + b, 1), :], (16, LANES)
            ).astype(BF16)

        each_owner(at_ref, owner)


def feed_fast(at, x, att, g, bo, g2, bi, bd, mine, other):
    tok = x.shape[0]
    tile = 512
    tiled = pl.BlockSpec((tile, D), lambda i: (i, 0))
    parts = (4, 4, PARTS_TWO, LANES)
    return pl.pallas_call(
        feed_fast_kernel,
        grid=(tok // tile,),
        in_specs=[
            SMEM, tiled, tiled, tiled, once((1, D)), once((1, D)), once((1, FF)), once((1, D)),
            once(mine.shape), once(other.shape),
        ],
        out_specs=[tiled, tiled, tiled, once(parts), once(parts)],
        out_shape=[
            jax.ShapeDtypeStruct((tok, D), BF16),
            jax.ShapeDtypeStruct((tok, D), F32),
            jax.ShapeDtypeStruct((tok, D), BF16),
            jax.ShapeDtypeStruct(parts, BF16),
            jax.ShapeDtypeStruct(parts, BF16),
        ],
        scratch_shapes=[
            pltpu.VMEM((FF, D), BF16), pltpu.VMEM((D, FF), BF16), pltpu.VMEM((D, D), BF16),
            pltpu.VMEM((8, D, FF // 8), F32), pltpu.VMEM((D, FF), F32), pltpu.VMEM((D, D), F32),
            pltpu.VMEM((8, FF), F32), pltpu.VMEM((32, LANES), F32),
        ],
        cost_estimate=CHEAP,
        compiler_params=vmem(60),
        name="feed",
    )(at, x, att, g, bo, g2, bi, bd, mine, other)


def feed_slow_kernel(
    x_ref, att_ref, g_ref, bo_ref, g2_ref, bi_ref, bd_ref, win, wdown, wout,
    out_ref, gm_ref, ga_ref, acc_in, acc_down, acc_out, sums,
):
    @pl.when(pl.program_id(0) == 0)
    def _():
        clear(acc_in, acc_down, acc_out, sums)

    out_ref[...], gm_ref[...], ga_ref[...] = feed_tile(
        x_ref[...], att_ref[...], g_ref[...], bo_ref[...], g2_ref[...], bi_ref[...], bd_ref[...],
        win, wdown, wout, acc_in, acc_down, acc_out, sums,
    )


def feed_slow(x, att, g, bo, g2, bi, bd, win, wdown, wout):
    tok = x.shape[0]
    tile = 512
    tiled = pl.BlockSpec((tile, D), lambda i: (i, 0))
    wide, square, rows, cut = (D, FF), (D, D), (8, FF), (8, D, FF // 8)
    return pl.pallas_call(
        feed_slow_kernel,
        grid=(tok // tile,),
        in_specs=[
            tiled, tiled, tiled, once((1, D)), once((1, D)), once((1, FF)), once((1, D)),
            once((FF, D)), once(wide), once(square),
        ],
        out_specs=[tiled, tiled, tiled, once(cut), once(wide), once(square), once(rows)],
        out_shape=[
            jax.ShapeDtypeStruct((tok, D), BF16),
            jax.ShapeDtypeStruct((tok, D), F32),
            jax.ShapeDtypeStruct((tok, D), BF16),
            jax.ShapeDtypeStruct(cut, F32),
            jax.ShapeDtypeStruct(wide, F32),
            jax.ShapeDtypeStruct(square, F32),
            jax.ShapeDtypeStruct(rows, F32),
        ],
        cost_estimate=CHEAP,
        compiler_params=vmem(60),
        name="feed_whole",
    )(x, att, g, bo, g2, bi, bd, win, wdown, wout)


def split_kernel(which, at_ref, keep_ref, got_ref, *outs):
    for r, out in enumerate(outs):
        i = at_ref[which] ^ r
        out[...] = (keep_ref[i].astype(F32) + got_ref[i].astype(F32)).astype(BF16)


def split_sum(at, which, keep, got):
    one, two, rows, lanes = keep.shape
    per = 1 if rows > 400 else 2
    block = pl.BlockSpec((one, per, rows, lanes), lambda i: (0, i, 0, 0))
    return pl.pallas_call(
        functools.partial(split_kernel, which),
        grid=(two // per,),
        in_specs=[SMEM, block, block],
        out_specs=[pl.BlockSpec((per, rows, lanes), lambda i: (i, 0, 0))] * one,
        out_shape=[jax.ShapeDtypeStruct((two, rows, lanes), BF16)] * one,
        cost_estimate=CHEAP,
        compiler_params=vmem(),
        name="split_sum",
    )(at, keep, got)


def merge_kernel(which, at_ref, a_ref, b_ref, c_ref, d_ref, *outs):
    for r, out in enumerate(outs):
        i = at_ref[which] ^ r
        total = a_ref[i].astype(F32) + b_ref[i].astype(F32)
        out[...] = (total + c_ref[i].astype(F32) + d_ref[i].astype(F32)).astype(BF16)


def merge_sum(at, which, pieces):
    count, rows, lanes = pieces[0].shape
    return pl.pallas_call(
        functools.partial(merge_kernel, which),
        in_specs=[SMEM] + [VMEM] * 4,
        out_shape=[jax.ShapeDtypeStruct((rows, lanes), BF16)] * count,
        cost_estimate=CHEAP,
        compiler_params=vmem(),
        name="merge_sum",
    )(at, *pieces)


def last_two_kernel(a_ref, b_ref, c_ref, d_ref, gin_ref, gdown_ref, gout_ref, bo, g2, bi, bd):
    total = a_ref[...].astype(F32) + b_ref[...].astype(F32)
    total = total + c_ref[...].astype(F32) + d_ref[...].astype(F32)
    for k in range(2):
        gin_ref[:, k * LANES : (k + 1) * LANES] = total[k * LANES : (k + 1) * LANES]
    for k in range(4):
        gdown_ref[:, k * LANES : (k + 1) * LANES] = total[256 + k * 64 : 320 + k * 64]
    gout_ref[...] = total[512:576]
    row = total[576:577]
    bo[...], g2[...], bi[...], bd[...] = row[:, 16:32], row[:, 32:48], row[:, 48:112], row[:, 112:]


def last_two(pieces):
    return pl.pallas_call(
        last_two_kernel,
        out_shape=[
            jax.ShapeDtypeStruct((LANES, 256), F32),
            jax.ShapeDtypeStruct((64, 512), F32),
            jax.ShapeDtypeStruct((64, LANES), F32),
            *(jax.ShapeDtypeStruct((1, n), F32) for n in (16, 16, 64, 16)),
        ],
        cost_estimate=CHEAP,
        compiler_params=vmem(),
        name="last_two",
    )(*pieces)


def last_one_kernel(a_ref, b_ref, c_ref, d_ref, gw_ref, gs_ref, g1_ref):
    total = a_ref[...].astype(F32) + b_ref[...].astype(F32)
    total = total + c_ref[...].astype(F32) + d_ref[...].astype(F32)
    gw_ref[...] = total[:192]
    gs_ref[...] = total[192:200]
    g1_ref[...] = total[200:201, :16]


def last_one(pieces):
    return pl.pallas_call(
        last_one_kernel,
        out_shape=[
            jax.ShapeDtypeStruct((192, LANES), F32),
            jax.ShapeDtypeStruct((8, LANES), F32),
            jax.ShapeDtypeStruct((1, 16), F32),
        ],
        cost_estimate=CHEAP,
        compiler_params=vmem(),
        name="last_one",
    )(*pieces)


def widen_keys(gmk):
    half = lax.broadcasted_iota(jnp.int32, (gmk.shape[0], LANES), 1) < HEAD_DIM
    zero = jnp.zeros((gmk.shape[0], LANES), gmk.dtype)
    wide = []
    for pair in range(PAIRS):
        tile = gmk[:, pair * LANES : (pair + 1) * LANES]
        wide += [jnp.where(half, tile, zero), jnp.where(half, zero, tile)]
    return jnp.concatenate(wide, axis=1)


def weight_kernel(
    fast, at_ref, ql_ref, qh_ref, kvl_ref, kvh_ref, n_ref, wq_ref, wkv_ref, gm_ref,
    pa, pb, pc, pd, pe, halo_ref, gain_ref, gs_ref, keep_ref, send_ref, acc_q, acc_kv,
):
    @pl.when(pl.program_id(0) == 0)
    def _():
        means = jnp.concatenate([ref[:, 2 * D :] for ref in (pa, pb, pc, pd, pe)], axis=0)
        means = means.astype(BF16)
        grads = (gm_ref[...] * float(BLOCK)).astype(BF16)
        acc_q[...] = mm(grads[:, :D], means, TN)
        acc_kv[...] = halo_ref[...] + mm(widen_keys(grads[:, D:]), means, TN)

    normed = n_ref[...]
    cut = ql_ref.shape[1]
    for lo, q_ref, kv_ref in ((0, ql_ref, kvl_ref), (cut, qh_ref, kvh_ref)):
        hi = lo + q_ref.shape[1]
        acc_q[lo:hi, :] += mm(q_ref[...].T, normed)
        acc_kv[2 * lo : 2 * hi, :] += mm(kv_ref[...].T, normed)

    @pl.when(pl.program_id(0) == pl.num_programs(0) - 1)
    def _():
        gain = jnp.sum(acc_q[...] * wq_ref[...].astype(F32), axis=0, keepdims=True)
        gain = gain + jnp.sum(acc_kv[...] * wkv_ref[...].astype(F32), axis=0, keepdims=True)
        gain = gain / gain_ref[...]
        if not fast:
            keep_ref[:D, :] = acc_q[...]
            keep_ref[D:, :] = acc_kv[...]
            send_ref[...] = jnp.broadcast_to(gain, (8, D))
            return
        def owner(own, h, z, b, c):
            ref = keep_ref if own else send_ref
            lanes = slice(h * LANES, (h + 1) * LANES)
            ref[z, h, :64, :] = acc_q[rows_at(b, 64), lanes].astype(BF16)
            ref[z, h, 64:128, :] = acc_kv[rows_at(2 * b + c, 64), lanes].astype(BF16)
            ref[z, h, 128:192, :] = acc_kv[rows_at(2 * b + 1 - c, 64), lanes].astype(BF16)
            share = pltpu.roll(
                jnp.broadcast_to(gain[:, lanes], (8, LANES)), lax.rem(LANES - 16 * b, LANES), 1
            )
            ref[z, h, 192:208, :] = jnp.concatenate(
                [gs_ref[h, rows_at(b, 8), :], share], axis=0
            ).astype(BF16)

        each_owner(at_ref, owner)


def weight_back(at, gq, gkv, normed, wt_q, wt_kv, gm, pieces, halo, gain, gsort, fast):
    tok = normed.shape[0]
    tile = 512
    parts = (4, 4, PIECE_ONE, LANES)
    shapes = (parts, parts) if fast else ((3 * D, D), (8, D))
    kind = BF16 if fast else F32
    rows = lambda width: pl.BlockSpec((tile, width), lambda i: (i, 0))
    return pl.pallas_call(
        functools.partial(weight_kernel, fast),
        grid=(tok // tile,),
        in_specs=[
            SMEM, *(rows(v.shape[1]) for v in (*gq, *gkv)), rows(D), once((D, D)),
            once((2 * D, D)), once(gm.shape), *(once(p.shape) for p in pieces),
            once((2 * D, D)), once((1, D)), once(gsort.shape),
        ],
        out_specs=[once(shapes[0]), once(shapes[1])],
        out_shape=[
            jax.ShapeDtypeStruct(shapes[0], kind),
            jax.ShapeDtypeStruct(shapes[1], kind),
        ],
        scratch_shapes=[pltpu.VMEM((D, D), F32), pltpu.VMEM((2 * D, D), F32)],
        cost_estimate=CHEAP,
        compiler_params=vmem(),
        name="weight_back",
    )(at, *gq, *gkv, normed, wt_q, wt_kv, gm, *pieces, halo, gain, gsort)


def inner_kernel(
    ql_ref, qh_ref, kvl_ref, kvh_ref, wq_ref, wkv_ref, gm_ref, fd, fe, out_ref, blocks_ref
):
    rows = ql_ref.shape[0]
    per = rows // BLOCK

    @pl.when(pl.program_id(0) == 0)
    def _():
        own, ends = fd.shape[0], fe.shape[0]
        halo = own + ends
        blocks_ref[...] = gm_ref[halo : halo + own, :] + fd[...].astype(F32)
        blocks_ref[:ends, :] += fe[...].astype(F32)

    cut = ql_ref.shape[1]
    value = mm(ql_ref[...], wq_ref[:cut, :]) + mm(qh_ref[...], wq_ref[cut:, :])
    value = value + mm(kvl_ref[...], wkv_ref[: 2 * cut, :])
    value = value + mm(kvh_ref[...], wkv_ref[2 * cut :, :])
    grads = blocks_ref[pl.ds(pl.multiple_of(pl.program_id(0) * per, per), per), :].astype(BF16)
    block = mm(grads[:, :D], wq_ref[...]) + mm(widen_keys(grads[:, D:]), wkv_ref[...])
    out_ref[...] = value + jnp.broadcast_to(block[:, None, :], (per, BLOCK, D)).reshape(rows, D)


def inner_gradient(gq, gkv, wt_q, wt_kv, gm, far):
    tok = gq[0].shape[0]
    tile = 8 * BLOCK
    rows = lambda width: pl.BlockSpec((tile, width), lambda i: (i, 0))
    return pl.pallas_call(
        inner_kernel,
        grid=(tok // tile,),
        in_specs=[
            *(rows(v.shape[1]) for v in (*gq, *gkv)), once((D, D)), once((2 * D, D)),
            once(gm.shape), *(once(f.shape) for f in far),
        ],
        out_specs=rows(D),
        out_shape=jax.ShapeDtypeStruct((tok, D), F32),
        scratch_shapes=[pltpu.VMEM((tok // BLOCK, 2 * D), F32)],
        cost_estimate=CHEAP,
        compiler_params=vmem(),
        name="inner_gradient",
    )(*gq, *gkv, wt_q, wt_kv, gm, *far)


def finish_kernel(skip, x_ref, u_ref, one_ref, two_ref, g_ref, gain_ref, out_ref, total):
    rows = x_ref.shape[0]
    at = lax.broadcasted_iota(jnp.int32, (rows, rows), 0)
    lane = lax.broadcasted_iota(jnp.int32, (rows, rows), 1)
    order = (lane == lax.rem(at, BLOCK) * 8 + at // BLOCK).astype(F32).astype(BF16)
    total[...] = u_ref[...] + mm(order, one_ref[...].reshape(rows, D))

    @pl.when(pl.program_id(0) >= skip)
    def _():
        total[...] += mm(order, two_ref[...].reshape(rows, D))

    x = x_ref[...].astype(F32)
    centre = x - jnp.mean(x, axis=-1, keepdims=True)
    inverse = lax.rsqrt(jnp.mean(centre * centre, axis=-1, keepdims=True) + EPSILON)
    hat = centre * inverse
    du = total[...] * gain_ref[...]
    inner = jnp.mean(du * hat, axis=-1, keepdims=True)
    out_ref[...] = g_ref[...] + inverse * (
        du - jnp.mean(du, axis=-1, keepdims=True) - hat * inner
    )


def finish(x, u, one, two, g_middle, gain):
    tok = x.shape[0]
    tile = 8 * BLOCK
    skip = (tok // BLOCK - two.shape[1]) // 8
    rows = lambda width: pl.BlockSpec((tile, width), lambda i: (i, 0))
    return pl.pallas_call(
        functools.partial(finish_kernel, skip),
        grid=(tok // tile,),
        in_specs=[
            rows(D), rows(D),
            pl.BlockSpec((BLOCK, 8, D), lambda i: (0, i, 0)),
            pl.BlockSpec((BLOCK, 8, D), lambda i: (0, jnp.maximum(i - skip, 0), 0)),
            rows(D), once((1, D)),
        ],
        out_specs=rows(D),
        out_shape=jax.ShapeDtypeStruct((tok, D), F32),
        scratch_shapes=[pltpu.VMEM((tile, D), F32)],
        cost_estimate=CHEAP,
        compiler_params=vmem(),
        name="finish",
    )(x, u, one, two, g_middle, gain)


class Grid:
    def __init__(self):
        self.heads = lax.axis_size("head")
        self.planes = lax.axis_size("plane")
        self.cycles = 2 * self.planes
        self.head = lax.axis_index("head")
        self.plane = lax.axis_index("plane")
        self.core = lax.axis_index("core")
        self.cycle = 2 * self.plane + self.core
        self.place = self.cycle * self.heads + self.head

    def send(self, value, pairs):
        return lax.ppermute(value, ("head", "plane", "core"), pairs)

    def number(self, head, cycle):
        return head * self.cycles + cycle

    def along(self, steps):
        count = self.heads * self.cycles
        at = lambda place: self.number(place % self.heads, place // self.heads)
        return [(at(i), at(i + steps)) for i in range(count) if 0 <= i + steps < count]

    def swap_head(self, flip):
        return [
            (self.number(h, b), self.number(h ^ flip, b))
            for h in range(self.heads)
            for b in range(self.cycles)
        ]

    def swap_plane(self, flip):
        return [
            (self.number(h, b), self.number(h, b ^ (2 * flip)))
            for h in range(self.heads)
            for b in range(self.cycles)
        ]

    def swap_core(self):
        return [
            (self.number(h, b), self.number(h, b ^ 1))
            for h in range(self.heads)
            for b in range(self.cycles)
        ]


def in_order(pieces, index):
    stacked = jnp.stack(pieces)
    count = len(pieces)
    bit = 1
    while bit < count:
        swapped = jnp.stack([stacked[i ^ bit] for i in range(count)])
        stacked = jnp.where((index & bit) != 0, swapped, stacked)
        bit *= 2
    return stacked


def gather_all(grid, piece):
    got = [piece] + [grid.send(piece, grid.swap_plane(r)) for r in range(1, grid.planes)]
    got = in_order(got, grid.plane)
    got = [got] + [grid.send(got, grid.swap_head(r)) for r in range(1, grid.heads)]
    got = in_order(got, grid.head)
    got = in_order([got, grid.send(got, grid.swap_core())], grid.core)
    got = got.transpose(1, 2, 0, *range(3, got.ndim))
    return got.reshape(grid.heads, grid.cycles, *piece.shape)


def across_planes(parts):
    return lax.all_to_all(parts, "plane", 0, 0, tiled=True)


def across_heads(parts):
    return lax.all_to_all(parts, "head", 0, 0, tiled=True)


def scatter_sum(grid, parts):
    mine = lax.dynamic_index_in_dim(parts, grid.core, 0, keepdims=False)
    other = lax.dynamic_index_in_dim(parts, 1 - grid.core, 0, keepdims=False)
    got = grid.send(other, grid.swap_core())
    total = (mine.astype(F32) + got.astype(F32)).astype(BF16)
    total = jnp.sum(across_heads(total).astype(F32), axis=0).astype(BF16)
    return jnp.sum(across_planes(total).astype(F32), axis=0)


def as_rows(value):
    flat = value.reshape(-1)
    short = -flat.shape[0] % LANES
    return jnp.pad(flat, (0, short)).reshape(-1, LANES)


def by_owner(grid, value):
    columns, rows = value.shape
    cut = value.reshape(grid.planes, 2, columns // grid.cycles, grid.heads, rows // grid.heads)
    return cut.transpose(1, 3, 0, 2, 4)


def vector_by_owner(grid, value):
    cut = value.reshape(grid.heads, grid.planes, 2, -1)
    return cut.transpose(2, 0, 1, 3)


def rows_of(value):
    lead = value.shape[:3]
    flat = value.reshape(*lead, -1)
    short = -flat.shape[-1] % LANES
    flat = jnp.pad(flat, ((0, 0),) * 3 + ((0, short),))
    return flat.reshape(*lead, -1, LANES)


def after(value, *others):
    return lax.optimization_barrier((value, *others))[0]


def weights_slow(grid, vectors, parameters):
    w_qkv, w_sort, w_in, w_down, w_out = parameters
    heads, cycles = grid.heads, grid.cycles
    first = jnp.concatenate([as_rows(w_qkv.T), as_rows(w_sort), as_rows(jnp.concatenate(vectors))])
    wide, sort_rows = as_rows(w_qkv.T).shape[0], as_rows(w_sort).shape[0]
    got = gather_all(grid, first)
    span = w_qkv.shape[1]
    wt_qkv = (
        got[:, :, :wide]
        .reshape(heads, cycles, span, D // heads)
        .transpose(1, 2, 0, 3)
        .reshape(HEADS, 3, HEAD_DIM, D)
    )
    wt_q = wt_qkv[:, 0].reshape(D, D)
    paired = wt_qkv.reshape(PAIRS, 2, 3, HEAD_DIM, D)
    wt_kv = jnp.stack(
        [paired[:, 0, 1], paired[:, 0, 2], paired[:, 1, 2], paired[:, 1, 1]], axis=1
    ).reshape(2 * D, D)
    size = w_sort.shape[0] * w_sort.shape[1]
    w_pairs = (
        got[:, :, wide : wide + sort_rows]
        .reshape(heads, cycles, -1)[:, :, :size]
        .reshape(heads, cycles, *w_sort.shape)
        .transpose(1, 3, 0, 2)
        .reshape(HEAD_DIM, PAIRS, LANES)
        .transpose(1, 0, 2)
        .astype(F32)
    )
    flat = got[:, :, wide + sort_rows :].reshape(heads, cycles, -1)
    sizes = [v.shape[0] for v in vectors]
    cuts = [sum(sizes[:i]) for i in range(len(sizes) + 1)]
    rows = [
        flat[:, :, cuts[i] : cuts[i + 1]].reshape(1, -1).astype(F32) for i in range(len(sizes))
    ]
    second = jnp.concatenate([as_rows(w_in.T), as_rows(w_down.T), as_rows(w_out.T)])
    in_rows, down_rows = as_rows(w_in.T).shape[0], as_rows(w_down.T).shape[0]
    got = gather_all(grid, second)

    def whole(depth, columns, part):
        return (
            part.reshape(heads, cycles, -1)[:, :, : columns // cycles * (depth // heads)]
            .reshape(heads, cycles, columns // cycles, depth // heads)
            .transpose(1, 2, 0, 3)
            .reshape(columns, depth)
        )

    feed = (
        whole(D, FF, got[:, :, :in_rows]),
        whole(FF, D, got[:, :, in_rows : in_rows + down_rows]),
        whole(D, D, got[:, :, in_rows + down_rows :]),
    )
    return wt_q, wt_kv, w_pairs, rows, feed


def matrix(rows, shape):
    flat = rows.reshape(-1)[: shape[0] * shape[1]]
    return flat.reshape(shape[1], shape[0]).T


def gradients_two_slow(grid, acc_in, acc_down, acc_out, sums, parameters, vectors):
    w_qkv, w_sort, w_in, w_down, w_out = parameters
    low = [
        rows_of(by_owner(grid, v.astype(BF16))) for v in (acc_in.transpose(0, 2, 1).reshape(FF, D), acc_down, acc_out)
    ]
    order = ((0, D), (1, D), (4, FF), (3, D))
    small = [vector_by_owner(grid, sums[i, :n]) for i, n in order]
    low.append(rows_of(jnp.concatenate(small, axis=-1).astype(BF16)))
    total = scatter_sum(grid, jnp.concatenate(low, axis=3))
    cuts = [0]
    for item in low:
        cuts.append(cuts[-1] + item.shape[3])
    g_in, g_down, g_out = (
        matrix(total[cuts[i] : cuts[i + 1]], w.shape) for i, w in enumerate((w_in, w_down, w_out))
    )
    flat = total[cuts[3] :].reshape(-1)
    sizes = [v.shape[0] for v in vectors[1:]]
    at = [sum(sizes[:i]) for i in range(5)]
    return g_in, g_down, g_out, *(flat[at[i] : at[i + 1]] for i in range(4))


def gradients_one_slow(grid, both, gain, gsort, parameters, vectors):
    w_qkv, w_sort = parameters[:2]
    q = both[:D].reshape(HEADS, HEAD_DIM, D)
    kv = both[D:].reshape(PAIRS, 4, HEAD_DIM, D)
    k = jnp.stack([kv[:, 0], kv[:, 3]], axis=1).reshape(HEADS, HEAD_DIM, D)
    v = jnp.stack([kv[:, 1], kv[:, 2]], axis=1).reshape(HEADS, HEAD_DIM, D)
    wide = jnp.stack([q, k, v], axis=1).reshape(3 * D, D)
    sort = gsort.transpose(0, 2, 1).reshape(grid.heads, D // grid.heads, grid.planes, 2, -1)
    low = [
        rows_of(by_owner(grid, wide.astype(BF16))),
        rows_of(sort.transpose(3, 0, 2, 1, 4).astype(BF16)),
        rows_of(vector_by_owner(grid, gain[0]).astype(BF16)),
    ]
    total = scatter_sum(grid, jnp.concatenate(low, axis=3))
    one, two = low[0].shape[3], low[0].shape[3] + low[1].shape[3]
    size = w_sort.shape[0] * w_sort.shape[1]
    return (
        matrix(total[:one], w_qkv.shape),
        total[one:two].reshape(-1)[:size].reshape(w_sort.shape),
        total[two:].reshape(-1)[: vectors[0].shape[0]],
    )


def per_device(
    tokens, cotangent, doc_lengths, norm_gain1, w_qkv, w_out, b_out, norm_gain2, w_in, b_in,
    w_down, b_down, w_sort,
):
    grid = Grid()
    heads = grid.heads
    x = tokens[0]
    upstream = cotangent[0]
    tok = x.shape[0]
    own = tok // BLOCK
    context = HALO + own
    window = HALO + own + HALO
    second = HALO - own
    fast = heads == 4 and grid.cycles == 8
    at = jnp.stack([grid.head, grid.plane, grid.core]).astype(jnp.int32)
    vectors = (norm_gain1, b_out, norm_gain2, b_in, b_down)
    parameters = (w_qkv, w_sort, w_in, w_down, w_out)

    three = range(1, 4)
    tail = (DOC_MOST - 1 - own) * BLOCK
    if fast:
        one, two, x_tail = pack(w_qkv, w_sort, vectors, w_in, w_down, w_out, x, tail)
        ones = [one] + [grid.send(one, grid.swap_plane(r)) for r in three]
        ones = jnp.stack(ones)
        ones = [ones] + [grid.send(ones, grid.swap_head(r)) for r in three]
        x_send, x_tail = lax.optimization_barrier((x, x_tail, *ones))[:2]
    else:
        x_send, x_tail = x, x[tok - tail :]
    halo_one = grid.send(x_send, grid.along(1))
    halo_two = grid.send(x_tail, grid.along(2))
    if fast:
        ones = jnp.stack(ones)
        other = grid.send(ones, grid.swap_core())
        two = after(two, other)
        twos = [two] + [grid.send(two, grid.swap_plane(r)) for r in three]
        wt_q, wt_kv, w_pairs, *rows = assemble(at, ones, other)
    else:
        wt_q, wt_kv, w_pairs, rows, feed_weights = weights_slow(grid, vectors, parameters)
        twos = []
    gain_one, bias_out, gain_two, bias_in, bias_down = rows

    begin = grid.place * own
    position = begin - HALO + jnp.arange(window, dtype=jnp.int32)
    doc_ends = jnp.cumsum(doc_lengths, dtype=jnp.int32)
    ended = jnp.sum(
        (doc_ends[None, :] <= position[:, None]).astype(jnp.int32), axis=1, dtype=jnp.int32
    )
    span_end = (grid.cycle + 1) * heads * own
    doc = jnp.where((position >= 0) & (position < span_end), ended, -1)
    fold = window - LANES
    docc = jnp.stack([doc[:LANES], jnp.concatenate([doc[LANES:], doc[fold:LANES]])])
    docn = doc[:, None]
    live = (doc[HALO:context] == doc[HALO - 1 : context - 1]) & (doc[HALO:context] >= 0)
    live = jnp.repeat(live.astype(F32), BLOCK).reshape(tok // LANES, LANES)

    normed, q, kv, means, means_head, means_tail = project(x, gain_one, wt_q, wt_kv, second)
    blocked = lambda value: value.reshape(-1, BLOCK, D)
    (kv_own,) = context_project((blocked(x),), after(gain_one, means), wt_kv, False)
    means_send, means_head, means_tail, docn, docc, live = lax.optimization_barrier(
        (means, means_head, means_tail, docn, docc, live, halo_one, halo_two, kv_own, *twos)
    )[:6]
    pieces = (
        grid.send(means_tail, grid.along(2)),
        grid.send(means_send, grid.along(1)),
        means,
        grid.send(means_send, grid.along(-1)),
        grid.send(means_head, grid.along(-2)),
    )
    kv_halo, normed_halo = context_project(
        (blocked(halo_two), blocked(halo_one)), after(gain_one, kv_own), wt_kv, True
    )
    if fast:
        twos = jnp.stack(lax.optimization_barrier((*twos, *pieces, kv_halo))[:4])
        twos = [twos] + [grid.send(twos, grid.swap_head(r)) for r in three]

    plan, *kept = sink_forward(pieces, after(w_pairs, kv_halo), docn, docc, own, context)
    attended, skv = attend(q, kv, kv_halo, kv_own, plan, live)
    if fast:
        twos = jnp.stack(lax.optimization_barrier((*twos, attended))[:4])
        feed_weights = (twos, grid.send(twos, grid.swap_core()))

    if fast:
        output, g_middle, g_att, keep, send = feed_fast(
            at, x, attended, upstream, bias_out, gain_two, bias_in, bias_down, *feed_weights
        )
        got = grid.send(send, grid.swap_core())
    else:
        output, g_middle, g_att, *sums = feed_slow(
            x, attended, upstream, bias_out, gain_two, bias_in, bias_down, *feed_weights
        )
        g_in, g_down, g_out, g_b_out, g_gain_two, g_b_in, g_b_down = gradients_two_slow(
            grid, *sums, parameters, vectors
        )
        twos = []

    gq_low, gkv_low, gh_low, gplan_low = attend_back(
        q, kv, skv, g_att, kv_halo, kv_own, plan, live, 0, 1
    )
    if fast:
        twos = split_sum(at, 0, after(keep, gh_low), got)
        g_att = after(g_att, *twos)
        twos = [twos[0]] + [grid.send(twos[r], grid.swap_head(r)) for r in three]
    gq_high, gkv_high, gh_high, gplan_high = attend_back(
        q, kv, skv, g_att, kv_halo, kv_own, plan, live, 1, PAIRS - 1
    )
    gq, gkv = (gq_low, gq_high), (gkv_low, gkv_high)
    gmeans, gsort, *sends = sink_backward(
        pieces, w_pairs, *kept, gplan_low, gplan_high, own, context
    )
    if fast:
        twos = merge_sum(at, 1, lax.optimization_barrier((*twos, gmeans))[:4])
        gh_high = after(gh_high, *twos)
        twos = [twos[0]] + [grid.send(twos[r], grid.swap_plane(r)) for r in three]
    gn_far, gn_near, g_kv_halo = halo_back(
        gh_low, gh_high, normed_halo, wt_q, wt_kv, gmeans, second
    )
    sends = lax.optimization_barrier((*sends, gn_near))[:2]
    far = [grid.send(value, grid.along(step)) for value, step in zip(sends, (1, 2))]
    gn_far, gn_near = lax.optimization_barrier((gn_far, gn_near, *far, *twos))[:2]
    back_one = grid.send(gn_near, grid.along(-1))
    back_two = grid.send(gn_far, grid.along(-2))
    gmeans = after(gmeans, gn_near)
    keep, send = weight_back(
        at, gq, gkv, normed, wt_q, wt_kv, gmeans, pieces, g_kv_halo, gain_one, gsort, fast
    )
    if fast:
        got = grid.send(send, grid.swap_core())
        ones = split_sum(at, 1, keep, got)
        waiting = [ones[0]] + [grid.send(ones[r], grid.swap_plane(r)) for r in three]
        inner = inner_gradient((gq[0], after(gq[1], *ones)), gkv, wt_q, wt_kv, gmeans, far)
        ones = merge_sum(at, 0, lax.optimization_barrier((*waiting, inner))[:4])
        ones = [ones[0]] + [grid.send(ones[r], grid.swap_head(r)) for r in three]
    else:
        inner = inner_gradient(gq, gkv, wt_q, wt_kv, gmeans, far)
    input_grad = finish(x, inner, back_one, back_two, g_middle, gain_one)
    if fast:
        g_wqkv, g_sort, g_gain_one = last_one(lax.optimization_barrier((*ones, input_grad))[:4])
        g_in, g_down, g_out, *small = last_two(twos)
        g_wqkv, g_sort, g_down, g_out = g_wqkv.T, g_sort.T, g_down.T, g_out.T
        g_gain_one = g_gain_one[0]
        g_b_out, g_gain_two, g_b_in, g_b_down = (value[0] for value in small)
    else:
        g_wqkv, g_sort, g_gain_one = gradients_one_slow(
            grid, keep, send, gsort, parameters, vectors
        )
    return (
        output[None], input_grad[None], g_gain_one, g_wqkv, g_out, g_b_out, g_gain_two, g_in,
        g_b_in, g_down, g_b_down, g_sort,
    )


def solution(mesh):
    heads, cycles = mesh.shape["head"], mesh.shape["blk"]
    fine = Mesh(mesh.devices.reshape(heads, cycles // 2, 2), ("head", "plane", "core"))
    both = P(("head", "plane", "core"))
    split = P("head", ("plane", "core"))
    stream = P(("plane", "core"), "head", None)
    return jax.shard_map(
        per_device,
        mesh=fine,
        in_specs=(
            stream, stream, P(), both, split, split, both, both, split, both, split, both, split,
        ),
        out_specs=(
            stream, stream, both, split, split, both, both, split, both, split, both, split,
        ),
        check_vma=False,
    )
```
